32 devices in a mesh: seq: 4 (over y, x), batch: 8 (over z, core).
Axes of the slice: x: 2, y: 2, z: 4, core: 2. Of those that a mesh axis runs over, the one named last changes fastest.
Arguments:
- layer_input: bfloat16 [16, 1024, 1536], P('batch', 'seq'), may hold values from -6 to 6
- cotangent: bfloat16 [16, 1024, 1536], P('batch', 'seq'), may hold values from -6 to 6
- token_mask: int32 [16, 1024], P('batch', 'seq'), may hold values 0 or 1
- document_ids: int32 [16, 1024], P('batch'), may hold values from 0 to 3, never falling along the last dimension, each value on 1 to 512 neighbouring positions
- attn_gain: bfloat16 [1536], P(('seq', 'batch')), may hold values from 0.099609375 to 1.8984375
- w_query: bfloat16 [1536, 1536], P(('seq', 'batch')), may hold values from -0.15625 to 0.15625
- w_key: bfloat16 [1536, 768], P(('seq', 'batch')), may hold values from -0.15625 to 0.15625
- w_value: bfloat16 [1536, 768], P(('seq', 'batch')), may hold values from -0.15625 to 0.15625
- w_output: bfloat16 [1536, 1536], P(('seq', 'batch')), may hold values from -1.75 to 1.75
- mlp_gain: bfloat16 [1536], P(('seq', 'batch')), may hold values from 0.099609375 to 1.8984375
- w_gate: bfloat16 [1536, 4096], P(('seq', 'batch')), may hold values from -0.15625 to 0.15625
- w_up: bfloat16 [1536, 4096], P(('seq', 'batch')), may hold values from -0.15625 to 0.15625
- w_down: bfloat16 [4096, 1536], P(('seq', 'batch')), may hold values from -0.09375 to 0.09375
Outputs:
- layer_output: bfloat16 [16, 1024, 1536], P('batch', 'seq')
- input_grad: bfloat16 [16, 1024, 1536], P('batch', 'seq')
- grad_attn_gain: float32 [1536], P(('seq', 'batch'))
- grad_query: float32 [1536, 1536], P(('seq', 'batch'))
- grad_key: float32 [1536, 768], P(('seq', 'batch'))
- grad_value: float32 [1536, 768], P(('seq', 'batch'))
- grad_output: float32 [1536, 1536], P(('seq', 'batch'))
- grad_mlp_gain: float32 [1536], P(('seq', 'batch'))
- grad_gate: float32 [1536, 4096], P(('seq', 'batch'))
- grad_up: float32 [1536, 4096], P(('seq', 'batch'))
- grad_down: float32 [4096, 1536], P(('seq', 'batch'))
The draws below stay inside these ranges and needn't reach their ends.
Inputs may be any that keep to these rules, and one draw needn't show every extreme that they name: `document_ids`: along each sequence the document numbers never fall; each document holds at most 512 positions, and one holds exactly that many.
All inputs are finite; a program needn't handle non-finite values. No bound on the sum of `token_mask` on one device may be relied on, other than what follows from the above.
Results may differ from the reference program's by a relative error of at most 0.014.
The reference program's roundings to bfloat16 on the way count: a program that leaves them out, or rounds other values in their place, can miss the bound.
Values may be sent and summed in bfloat16 or wider, within the bound.
A program may use at most 320 MiB of HBM per device.

```python
import math
import jax
import jax.numpy as jnp
import numpy as np
from jax import lax

D = 1536
FF = 4096
HEADS = 16
KV = 8
HD = 96
LEN = 1024
SEQS = 16


def touch_ends(drawn, own_key, least, top_value):
    dims = drawn.shape
    index_at = [jax.random.randint(jax.random.fold_in(own_key, axis), (), 0, dims[axis]) for axis in range(len(dims))]
    drawn = drawn.at[tuple(index_at)].set(least)
    longest = dims.index(max(dims))
    index_at[longest] = (index_at[longest] + 1) % dims[longest]
    return drawn.at[tuple(index_at)].set(top_value)


def steps_of(key, extent, cuts, least, high):
    gain = 1.0
    for dim, shards_of in cuts:
        steps = jax.random.uniform(jax.random.fold_in(jax.random.fold_in(key, 6), dim), (shards_of,), jnp.float32, least / len(cuts), high / len(cuts))
        gain = gain * jnp.repeat(jnp.exp(steps), extent[dim] // shards_of).reshape((-1,) + (1,) * (len(extent) - 1 - dim))
    return gain


def split_up(number_of, total, most, skew):
    weights = [(1 << 20) // math.isqrt(rank ** skew) + 1 for rank in range(2, number_of + 1)]
    surplus, counts = total - most - (number_of - 1), [1] * (number_of - 1)
    while surplus > 0:
        movable = [i for i in range(number_of - 1) if counts[i] < most]
        pool, remaining = sum([weights[i] for i in movable]), surplus
        for i in movable:
            addition = min(most - counts[i], max(1, remaining * weights[i] // pool), surplus)
            counts[i] = counts[i] + addition
            surplus = surplus - addition
    return np.array([most] + counts)


def uneven_parts(stream_key, number_of, total, limit, slope):
    if number_of == 2:
        one = jax.random.randint(stream_key, (), max(1, total - limit), min(limit, total - 1) + 1)
        return jnp.stack([one, total - one])
    sizes = jnp.asarray(split_up(number_of, total, limit, slope), jnp.int32)
    couples = (number_of - 1) // 2
    source_of, taker = sizes[1:1 + 2 * couples:2], sizes[2:2 + 2 * couples:2]
    margin = jnp.minimum(source_of - 1, limit - taker)
    shifted = jax.random.randint(jax.random.fold_in(stream_key, 1), (couples,), 0, 1 << 20) % (margin + 1)
    sizes = sizes.at[1:1 + 2 * couples:2].set(source_of - shifted).at[2:2 + 2 * couples:2].set(taker + shifted)
    return sizes[jax.random.permutation(jax.random.fold_in(stream_key, 2), number_of)]


def noise(rng, extent, width, reach, split=(), held_as=jnp.bfloat16):
    array = jax.random.normal(rng, extent, jnp.float32) * width
    if len(split) > 0:
        array = steps_of(rng, extent, split, -0.22, 0.18) * array
    return jnp.clip(array, min=-reach, max=reach).astype(held_as)


def setup_inputs(seed: int = 0) -> dict:
    key_list = jax.random.split(jax.random.key(seed), 14)
    return {
        "layer_input": noise(key_list[0], (SEQS, LEN, D), 1.0, 6.0, ((0, 8), (1, 4))),
        "cotangent": noise(key_list[1], (SEQS, LEN, D), 1.0, 6.0, ((0, 8), (1, 4))),
        "token_mask": touch_ends((jax.random.randint(key_list[2], (SEQS, LEN), 0, 4) < 3).astype(jnp.int32), jax.random.fold_in(key_list[2], 1), 0, 1),
        "document_ids": jax.vmap(lambda own: jnp.searchsorted(jnp.cumsum(uneven_parts(own, 4, LEN, LEN // 2, 0)), jnp.arange(LEN), side="right"))(jax.random.split(key_list[3], SEQS)).reshape((SEQS, LEN)).astype(jnp.int32),
        "attn_gain": jnp.clip(1.0 + 0.18 * jax.random.normal(key_list[4], (D,), jnp.float32), 0.099609375, 1.8984375).astype(jnp.bfloat16),
        "w_query": noise(key_list[5], (D, HEADS * HD), D ** -0.5, 0.15625, ((0, 32),)),
        "w_key": noise(key_list[6], (D, KV * HD), D ** -0.5, 0.15625, ((0, 32),)),
        "w_value": noise(key_list[7], (D, KV * HD), D ** -0.5, 0.15625, ((0, 32),)),
        "w_output": noise(key_list[8], (HEADS * HD, D), (HEADS * HD // 128) ** -0.5, 1.75, ((0, 32),)),
        "mlp_gain": jnp.clip(1.0 + 0.18 * jax.random.normal(key_list[9], (D,), jnp.float32), 0.099609375, 1.8984375).astype(jnp.bfloat16),
        "w_gate": noise(key_list[10], (D, FF), D ** -0.5, 0.15625, ((0, 32),)),
        "w_up": noise(key_list[11], (D, FF), D ** -0.5, 0.15625, ((0, 32),)),
        "w_down": noise(key_list[12], (FF, D), FF ** -0.5, 0.09375, ((0, 32),)),
    }


@jax.custom_vjp
def low(v):
    return lax.optimization_barrier(v.astype(jnp.bfloat16)).astype(jnp.float32)

@jax.custom_vjp
def low_back(v):
    return v

def low_keep(v):
    return (low(v), None)

def low_pass(kept, grad):
    return (grad,)

def back_keep(v):
    return (v, None)

def back_low(kept, grad):
    return (low(grad),)
low.defvjp(low_keep, low_pass)
low_back.defvjp(back_keep, back_low)
EPSILON = 1e-05
ROPE_BASE = 10000.0
HIGHEST = lax.Precision.HIGHEST

def product(left, right):
    return jnp.einsum('...d,de->...e', left, right, precision=HIGHEST)

def inverse_rms(field):
    return lax.rsqrt(lax.optimization_barrier(jnp.mean(field * field, axis=-1, keepdims=True)) + EPSILON)

def half_turn(field):
    middle = field.shape[-1] // 2
    return jnp.concatenate([-field[..., middle:], field[..., :middle]], axis=-1)

def rotary(field, positions):
    middle = field.shape[-1] // 2
    freqs = ROPE_BASE ** (-2.0 * jnp.arange(middle, dtype=jnp.float32) / field.shape[-1])
    angles = positions.astype(jnp.float32)[:, None] * freqs[None, :]
    cosine = jnp.concatenate([jnp.cos(angles), jnp.cos(angles)], axis=-1)[:, None, :]
    sine = jnp.concatenate([jnp.sin(angles), jnp.sin(angles)], axis=-1)[:, None, :]
    return field * cosine + half_turn(field) * sine

def attend(queries, keys, values, documents):
    block = min(512, LEN)
    count = LEN // block
    scale = 1.0 / math.sqrt(HD)
    key_pos = jnp.arange(LEN, dtype=jnp.int32)

    def one_block(index):
        start = (index * block).astype(jnp.int32)
        query_block = lax.dynamic_slice_in_dim(queries, start, block, 1)
        query_docs = lax.dynamic_slice_in_dim(documents, start, block, 1)
        query_pos = start + jnp.arange(block, dtype=jnp.int32)
        scores = low_back(jnp.einsum('gqjhd,gkjd->gjhqk', query_block, keys, precision=HIGHEST) * scale)
        allowed = (key_pos[None, None, :] <= query_pos[None, :, None]) & (query_docs[:, :, None] == documents[:, None, :])
        scores = jnp.where(allowed[:, None, None], scores, -1e+30)
        peak_score = lax.optimization_barrier(jnp.max(scores, axis=-1, keepdims=True))
        weights = jnp.exp(scores - peak_score)
        probs = weights / lax.optimization_barrier(jnp.sum(weights, axis=-1, keepdims=True))
        return jnp.einsum('gjhqk,gkjd->gqjhd', low(probs), values, precision=HIGHEST)
    blocks = lax.map(jax.checkpoint(one_block), jnp.arange(count, dtype=jnp.int32))
    return jnp.moveaxis(blocks, 0, 1).reshape(queries.shape[0], LEN, HEADS * HD)

def block_forward(inputs, documents, attn_gain, w_query, w_key, w_value, w_output, mlp_gain, w_gate, w_up, w_down):
    groups = inputs.shape[0]
    positions = jnp.arange(LEN, dtype=jnp.int32)
    normed = low(inputs * inverse_rms(inputs) * attn_gain)
    queries = low(low_back(product(normed, w_query))).reshape(groups, LEN, HEADS, HD)
    keys = low(low_back(product(normed, w_key))).reshape(groups, LEN, KV, HD)
    values = low(low_back(product(normed, w_value))).reshape(groups, LEN, KV, HD)
    queries = low(rotary(queries, positions)).reshape(groups, LEN, KV, HEADS // KV, HD)
    keys = low(rotary(keys, positions))
    mixed = low(low_back(attend(queries, keys, values, documents)))
    hidden_state = inputs + low_back(product(mixed, w_output))
    normed_two = low(hidden_state * inverse_rms(hidden_state) * mlp_gain)
    gate = low_back(product(normed_two, w_gate))
    upward = low_back(product(normed_two, w_up))
    activated = low(jax.nn.silu(gate) * upward)
    return hidden_state + low_back(product(activated, w_down))

def reference(layer_input, cotangent, token_mask, document_ids, attn_gain, w_query, w_key, w_value, w_output, mlp_gain, w_gate, w_up, w_down):
    weights = tuple((member.astype(jnp.float32) for member in (attn_gain, w_query, w_key, w_value, w_output, mlp_gain, w_gate, w_up, w_down)))
    group_size = math.gcd(SEQS, max(1, 4096 // LEN))
    group_count = SEQS // group_size
    inputs = layer_input.astype(jnp.float32).reshape(group_count, group_size, LEN, D)
    seeds = (cotangent.astype(jnp.float32) * token_mask.astype(jnp.float32)[:, :, None]).reshape(group_count, group_size, LEN, D)
    documents = document_ids.reshape(group_count, group_size, LEN)

    def one_group(running, member):
        block_input, block_seed, block_docs = member

        def forward(field, *params):
            return block_forward(field, block_docs, *params)
        output, pullback = jax.vjp(forward, block_input, *weights)
        gradients = pullback(block_seed)
        running = tuple((total_sum + gradient for total_sum, gradient in zip(running, gradients[1:])))
        return (running, (output.astype(jnp.bfloat16), gradients[0].astype(jnp.bfloat16)))
    start = tuple((jnp.zeros(member.shape, jnp.float32) for member in weights))
    running, (outputs, input_grads) = lax.scan(one_group, start, (inputs, seeds, documents))
    return (outputs.reshape(SEQS, LEN, D), input_grads.reshape(SEQS, LEN, D), running[0], running[1], running[2], running[3], running[4], running[5], running[6], running[7], running[8])
```

```python
import math

import jax
import jax.numpy as jnp
from jax import lax
from jax.sharding import Mesh
from jax.sharding import PartitionSpec as P

HEADS = 16
KV = 8
HD = 96


EPSILON = 1e-05
ROPE_BASE = 10000.0


def inverse_rms(field):
    return lax.rsqrt(jnp.mean(field * field, axis=-1, keepdims=True) + EPSILON)


def half_turn(field):
    middle = field.shape[-1] // 2
    return jnp.concatenate([-field[..., middle:], field[..., :middle]], axis=-1)


def rope_tables(length, width):
    middle = width // 2
    freqs = ROPE_BASE ** (-2.0 * jnp.arange(middle, dtype=jnp.float32) / width)
    angles = jnp.arange(length, dtype=jnp.float32)[:, None] * freqs[None, :]
    cosine = jnp.concatenate([jnp.cos(angles), jnp.cos(angles)], axis=-1)
    sine = jnp.concatenate([jnp.sin(angles), jnp.sin(angles)], axis=-1)
    return (cosine, sine)


def rotate_ahead(field, cosine, sine):
    return field * cosine[:, None, :] + half_turn(field) * sine[:, None, :]


def rotate_behind(field, cosine, sine):
    return field * cosine[:, None, :] - half_turn(field) * sine[:, None, :]


def outer_sum(left, right):
    return lax.dot_general(
        left, right, (((0,), (0,)), ((), ())), preferred_element_type=jnp.float32
    )


def back_product(left, right):
    return lax.dot_general(
        left, right, (((1,), (1,)), ((), ())), preferred_element_type=jnp.float32
    )


def fetch_attention(attn_gain, w_query, w_key, w_value, w_output):
    return (
        lax.all_gather(attn_gain, ("seq", "batch"), axis=0, tiled=True),
        lax.all_gather(w_query, ("seq", "batch"), axis=0, tiled=True),
        lax.all_gather(w_key, ("seq", "batch"), axis=0, tiled=True),
        lax.all_gather(w_value, ("seq", "batch"), axis=0, tiled=True),
        lax.all_gather(w_output, ("seq", "batch"), axis=0, tiled=True),
    )


def fetch_feedforward(mlp_gain, w_gate, w_up, w_down):
    return (
        lax.all_gather(mlp_gain, ("seq", "batch"), axis=0, tiled=True),
        lax.all_gather(w_gate, ("seq", "batch"), axis=0, tiled=True),
        lax.all_gather(w_up, ("seq", "batch"), axis=0, tiled=True),
        lax.all_gather(w_down, ("seq", "batch"), axis=0, tiled=True),
    )


def block_scores(query_block, keys, documents, start, block, scale):
    length = keys.shape[0]
    scores = (
        jnp.einsum("qjhd,kjd->jhqk", query_block, keys, preferred_element_type=jnp.float32) * scale
    )
    key_pos = jnp.arange(length, dtype=jnp.int32)
    query_pos = start + jnp.arange(block, dtype=jnp.int32)
    query_docs = lax.dynamic_slice_in_dim(documents, start, block, 0)
    allowed = (key_pos[None, :] <= query_pos[:, None]) & (query_docs[:, None] == documents[None, :])
    return jnp.where(allowed[None, None], scores, -1e30)


def attention_forward(queries, keys, values, documents, block, scale):
    length = queries.shape[0]
    count = length // block

    def one_block(index):
        start = index * block
        query_block = lax.dynamic_slice_in_dim(queries, start, block, 0)
        scores = block_scores(query_block, keys, documents, start, block, scale)
        peak_score = jnp.max(scores, axis=-1, keepdims=True)
        weights = jnp.exp(scores - peak_score)
        totals = jnp.sum(weights, axis=-1, keepdims=True)
        probs = (weights / totals).astype(jnp.bfloat16)
        result = jnp.einsum("jhqk,kjd->qjhd", probs, values, preferred_element_type=jnp.float32)
        return (
            result.astype(jnp.bfloat16).reshape(block, -1),
            (peak_score + jnp.log(totals))[..., 0],
        )

    results, sums = lax.map(one_block, jnp.arange(count, dtype=jnp.int32))
    return (results.reshape(length, -1), sums)


def attention_backward(queries, keys, values, documents, sums, grad_out, block, scale):
    length = queries.shape[0]
    count = length // block

    def one_block(carry, member):
        grad_keys, grad_values = carry
        index, sums_block = member
        start = index * block
        query_block = lax.dynamic_slice_in_dim(queries, start, block, 0)
        grad_block = lax.dynamic_slice_in_dim(grad_out, start, block, 0)
        scores = block_scores(query_block, keys, documents, start, block, scale)
        probs = jnp.exp(scores - sums_block[..., None])
        grad_probs = jnp.einsum(
            "qjhd,kjd->jhqk", grad_block, values, preferred_element_type=jnp.float32
        )
        centre = jnp.sum(probs * grad_probs, axis=-1, keepdims=True)
        grad_scores = (probs * (grad_probs - centre)).astype(jnp.bfloat16)
        grad_query = (
            jnp.einsum("jhqk,kjd->qjhd", grad_scores, keys, preferred_element_type=jnp.float32)
            * scale
        )
        grad_keys = (
            grad_keys
            + jnp.einsum(
                "jhqk,qjhd->kjd", grad_scores, query_block, preferred_element_type=jnp.float32
            )
            * scale
        )
        grad_values = grad_values + jnp.einsum(
            "jhqk,qjhd->kjd",
            probs.astype(jnp.bfloat16),
            grad_block,
            preferred_element_type=jnp.float32,
        )
        return ((grad_keys, grad_values), grad_query)

    empty = jnp.zeros(keys.shape, jnp.float32)
    (grad_keys, grad_values), grad_query = lax.scan(
        one_block, (empty, empty), (jnp.arange(count, dtype=jnp.int32), sums)
    )
    return (
        grad_query.reshape(length, queries.shape[1] * queries.shape[2], queries.shape[3]),
        grad_keys,
        grad_values,
    )


def body(
    layer_input,
    cotangent,
    token_mask,
    document_ids,
    attn_gain,
    w_query,
    w_key,
    w_value,
    w_output,
    mlp_gain,
    w_gate,
    w_up,
    w_down,
):
    parts = lax.axis_size("seq")
    micro_count = layer_input.shape[0]
    shard = layer_input.shape[1]
    length = shard * parts
    heads_here = HEADS // parts
    kv_here = max(1, KV // parts)
    copies = parts * kv_here // KV
    per_kv = heads_here // kv_here
    block = min(512, length)
    scale = 1.0 / math.sqrt(HD)
    cosine, sine = rope_tables(length, HD)
    attn_set = None
    mlp_set = None
    attn_total = None
    mlp_total = None
    outputs = []
    input_grads = []
    kept = {
        "normed": [],
        "normed_two": [],
        "activated": [],
        "seed_low": [],
        "gate_low": [],
        "up_low": [],
        "grad_low": [],
        "mixed": [],
        "query_back": [],
        "key_back": [],
        "value_back": [],
    }
    gain_one_total = None
    gain_two_total = None
    for micro in range(micro_count):
        attn_set = fetch_attention(attn_gain, w_query, w_key, w_value, w_output)
        mlp_set = fetch_feedforward(mlp_gain, w_gate, w_up, w_down)
        gain_one = attn_set[0].astype(jnp.float32)
        gain_two = mlp_set[0].astype(jnp.float32)
        documents = document_ids[micro]
        inputs = layer_input[micro].astype(jnp.float32)
        inv_one = inverse_rms(inputs)
        unit_one = inputs * inv_one
        normed = (unit_one * gain_one).astype(jnp.bfloat16)
        queries = jnp.dot(normed, attn_set[1], preferred_element_type=jnp.float32).astype(
            jnp.bfloat16
        )
        keys_lin = jnp.dot(normed, attn_set[2], preferred_element_type=jnp.float32).astype(
            jnp.bfloat16
        )
        values_lin = jnp.dot(normed, attn_set[3], preferred_element_type=jnp.float32).astype(
            jnp.bfloat16
        )
        queries = queries.reshape(shard, parts, heads_here * HD)
        key_slots = jnp.repeat(keys_lin.reshape(shard, KV, HD), copies, axis=1).reshape(
            shard, parts, kv_here * HD
        )
        value_slots = jnp.repeat(values_lin.reshape(shard, KV, HD), copies, axis=1).reshape(
            shard, parts, kv_here * HD
        )
        pairs = jnp.concatenate([key_slots, value_slots], axis=-1)
        query_heads, pair_heads = (
            lax.all_to_all(queries, "seq", split_axis=1, concat_axis=0, tiled=True),
            lax.all_to_all(pairs, "seq", split_axis=1, concat_axis=0, tiled=True),
        )
        query_rot = rotate_ahead(
            query_heads.reshape(length, heads_here, HD).astype(jnp.float32), cosine, sine
        )
        query_rot = query_rot.astype(jnp.bfloat16).reshape(length, kv_here, per_kv, HD)
        key_heads = pair_heads[:, 0, : kv_here * HD].reshape(length, kv_here, HD)
        key_rot = rotate_ahead(key_heads.astype(jnp.float32), cosine, sine).astype(jnp.bfloat16)
        value_heads = pair_heads[:, 0, kv_here * HD :].reshape(length, kv_here, HD)
        attended, sums = attention_forward(query_rot, key_rot, value_heads, documents, block, scale)
        mixed = lax.all_to_all(
            attended.reshape(length, 1, heads_here * HD),
            "seq",
            split_axis=0,
            concat_axis=1,
            tiled=True,
        )
        mixed = mixed.reshape(shard, HEADS * HD)
        hidden_state = inputs + jnp.dot(mixed, attn_set[4], preferred_element_type=jnp.float32)
        inv_two = inverse_rms(hidden_state)
        unit_two = hidden_state * inv_two
        normed_two = (unit_two * gain_two).astype(jnp.bfloat16)
        gate = jnp.dot(normed_two, mlp_set[1], preferred_element_type=jnp.float32)
        upward = jnp.dot(normed_two, mlp_set[2], preferred_element_type=jnp.float32)
        sigma = jax.nn.sigmoid(gate)
        activated = (gate * sigma * upward).astype(jnp.bfloat16)
        output = hidden_state + jnp.dot(activated, mlp_set[3], preferred_element_type=jnp.float32)
        outputs.append(output.astype(jnp.bfloat16))
        seed = cotangent[micro].astype(jnp.float32) * token_mask[micro].astype(jnp.float32)[:, None]
        seed_low = seed.astype(jnp.bfloat16)
        grad_act = back_product(seed_low, mlp_set[3])
        grad_up_low = (grad_act * gate * sigma).astype(jnp.bfloat16)
        grad_gate_low = (grad_act * upward * sigma * (1.0 + gate * (1.0 - sigma))).astype(
            jnp.bfloat16
        )
        grad_normed_two = back_product(grad_gate_low, mlp_set[1]) + back_product(
            grad_up_low, mlp_set[2]
        )
        grad_gain_two = jnp.sum(grad_normed_two * unit_two, axis=0)
        scaled_two = grad_normed_two * gain_two
        grad_hidden = seed + inv_two * (
            scaled_two - unit_two * jnp.mean(scaled_two * unit_two, axis=-1, keepdims=True)
        )
        gain_two_total = grad_gain_two if gain_two_total is None else gain_two_total + grad_gain_two
        kept["normed_two"].append(normed_two)
        kept["activated"].append(activated)
        kept["seed_low"].append(seed_low)
        kept["gate_low"].append(grad_gate_low)
        kept["up_low"].append(grad_up_low)
        grad_low = grad_hidden.astype(jnp.bfloat16)
        grad_mixed = (
            back_product(grad_low, attn_set[4])
            .astype(jnp.bfloat16)
            .reshape(shard, parts, heads_here * HD)
        )
        grad_heads = lax.all_to_all(
            grad_mixed, "seq", split_axis=1, concat_axis=0, tiled=True
        ).reshape(length, kv_here, per_kv, HD)
        grad_query_rot, grad_key_rot, grad_values = attention_backward(
            query_rot, key_rot, value_heads, documents, sums, grad_heads, block, scale
        )
        grad_query_heads = (
            rotate_behind(grad_query_rot, cosine, sine)
            .astype(jnp.bfloat16)
            .reshape(length, 1, heads_here * HD)
        )
        grad_key_heads = rotate_behind(grad_key_rot, cosine, sine)
        grad_pairs = jnp.concatenate(
            [
                grad_key_heads.reshape(length, kv_here * HD),
                grad_values.reshape(length, kv_here * HD),
            ],
            axis=-1,
        )
        query_back = lax.all_to_all(
            grad_query_heads, "seq", split_axis=0, concat_axis=1, tiled=True
        ).reshape(shard, HEADS * HD)
        pair_back = lax.all_to_all(
            grad_pairs.reshape(length, 1, 2 * kv_here * HD).astype(jnp.bfloat16),
            "seq",
            split_axis=0,
            concat_axis=1,
            tiled=True,
        ).astype(jnp.float32)
        key_back = pair_back[:, :, : kv_here * HD].reshape(shard, KV, copies, HD).sum(axis=2)
        value_back = pair_back[:, :, kv_here * HD :].reshape(shard, KV, copies, HD).sum(axis=2)
        key_back = key_back.reshape(shard, KV * HD).astype(jnp.bfloat16)
        value_back = value_back.reshape(shard, KV * HD).astype(jnp.bfloat16)
        grad_normed = (
            back_product(query_back, attn_set[1])
            + back_product(key_back, attn_set[2])
            + back_product(value_back, attn_set[3])
        )
        grad_gain_one = jnp.sum(grad_normed * unit_one, axis=0)
        scaled_one = grad_normed * gain_one
        grad_input = grad_hidden + inv_one * (
            scaled_one - unit_one * jnp.mean(scaled_one * unit_one, axis=-1, keepdims=True)
        )
        input_grads.append(grad_input.astype(jnp.bfloat16))
        gain_one_total = grad_gain_one if gain_one_total is None else gain_one_total + grad_gain_one
        kept["normed"].append(normed)
        kept["mixed"].append(mixed)
        kept["grad_low"].append(grad_low)
        kept["query_back"].append(query_back)
        kept["key_back"].append(key_back)
        kept["value_back"].append(value_back)
    rows = {name: jnp.concatenate(values, axis=0) for name, values in kept.items()}
    attn_total = (
        lax.psum_scatter(gain_one_total, ("seq", "batch"), scatter_dimension=0, tiled=True),
        lax.psum_scatter(
            outer_sum(rows["normed"], rows["query_back"]),
            ("seq", "batch"),
            scatter_dimension=0,
            tiled=True,
        ),
        lax.psum_scatter(
            outer_sum(rows["normed"], rows["key_back"]),
            ("seq", "batch"),
            scatter_dimension=0,
            tiled=True,
        ),
        lax.psum_scatter(
            outer_sum(rows["normed"], rows["value_back"]),
            ("seq", "batch"),
            scatter_dimension=0,
            tiled=True,
        ),
        lax.psum_scatter(
            outer_sum(rows["mixed"], rows["grad_low"]),
            ("seq", "batch"),
            scatter_dimension=0,
            tiled=True,
        ),
    )
    mlp_total = (
        lax.psum_scatter(gain_two_total, ("seq", "batch"), scatter_dimension=0, tiled=True),
        lax.psum_scatter(
            outer_sum(rows["normed_two"], rows["gate_low"]),
            ("seq", "batch"),
            scatter_dimension=0,
            tiled=True,
        ),
        lax.psum_scatter(
            outer_sum(rows["normed_two"], rows["up_low"]),
            ("seq", "batch"),
            scatter_dimension=0,
            tiled=True,
        ),
        lax.psum_scatter(
            outer_sum(rows["activated"], rows["seed_low"]),
            ("seq", "batch"),
            scatter_dimension=0,
            tiled=True,
        ),
    )
    return (
        jnp.stack(outputs, axis=0),
        jnp.stack(input_grads, axis=0),
        attn_total[0],
        attn_total[1],
        attn_total[2],
        attn_total[3],
        attn_total[4],
        mlp_total[0],
        mlp_total[1],
        mlp_total[2],
        mlp_total[3],
    )


AXES = ("y", "x", "z", "core")
SIZES = (2, 2, 4, 2)


def route(move):
    pairs = []
    for y in range(2):
        for x in range(2):
            for z in range(4):
                for c in range(2):
                    ty, tx, tz, tc = move(y, x, z, c)
                    pairs.append(
                        (((y * 2 + x) * 4 + z) * 2 + c, ((ty * 2 + tx) * 4 + tz) * 2 + tc)
                    )
    return pairs


def send(value, move):
    return lax.ppermute(value, AXES, route(move))


def to_core(value):
    return send(value, lambda y, x, z, c: (y, x, z, 1 - c))


def to_x(value):
    return send(value, lambda y, x, z, c: (y, 1 - x, z, c))


def to_y(value):
    return send(value, lambda y, x, z, c: (1 - y, x, z, c))


def to_z(value, k):
    return send(value, lambda y, x, z, c: (y, x, z ^ k, c))


def in_order(mine, other, place, axis=0):
    first = jnp.where(place == 0, mine, other)
    second = jnp.where(place == 0, other, mine)
    return jnp.concatenate([first, second], axis=axis)


def pick(value, place, axis=0):
    return lax.dynamic_index_in_dim(value, place, axis, keepdims=False)


def plane_turn(tokens, x):
    got = [
        send(pick(tokens, x ^ a), lambda y, x_, z, c, a=a: (c, x_ ^ a, z, y)) for a in range(2)
    ]
    return in_order(got[0][None], got[1][None], x)


def gather_line(block, z):
    got = [block[None]] + [to_z(block, k)[None] for k in (1, 2, 3)]
    low = in_order(got[0], got[1], z & 1)
    high = in_order(got[2], got[3], z & 1)
    return in_order(low, high, z >> 1)


def gather_all(block, y, x, z, x_first):
    line = gather_line(block, z)
    if x_first:
        pair = in_order(line[None], to_x(line)[None], x)
        return in_order(pair[None], to_y(pair)[None], y).reshape((16,) + block.shape)
    pair = in_order(line[None], to_y(line)[None], y)
    return in_order(pair[:, None], to_x(pair)[:, None], x, axis=1).reshape((16,) + block.shape)


def scatter_all(total, y, x, z, y_first):
    rest = total.shape[1:]
    total = total.reshape((2, 2, 4) + rest)
    low = jnp.bfloat16
    if y_first:
        got = to_y(pick(total, 1 - y).astype(low))
        half = pick(total, y).astype(jnp.float32) + got.astype(jnp.float32)
        got = to_x(pick(half, 1 - x).astype(low))
        line = pick(half, x) + got.astype(jnp.float32)
    else:
        got = to_x(pick(total, 1 - x, 1).astype(low))
        half = pick(total, x, 1).astype(jnp.float32) + got.astype(jnp.float32)
        got = to_y(pick(half, 1 - y).astype(low))
        line = pick(half, y) + got.astype(jnp.float32)
    result = pick(line, z)
    for k in (1, 2, 3):
        result = result + to_z(pick(line, z ^ k).astype(low), k).astype(jnp.float32)
    return result


def add_all(value):
    value = value + to_core(value)
    value = value + to_x(value)
    value = value + to_y(value)
    value = value + to_z(value, 1)
    return value + to_z(value, 2)


def fast_body(
    layer_input,
    cotangent,
    token_mask,
    document_ids,
    attn_gain,
    w_query,
    w_key,
    w_value,
    w_output,
    mlp_gain,
    w_gate,
    w_up,
    w_down,
):
    f32, low = jnp.float32, jnp.bfloat16
    y, x, z, core = (lax.axis_index(name) for name in AXES)
    device = ((y * 2 + x) * 4 + z) * 2 + core
    quarter = layer_input.shape[1]
    half_len = 2 * quarter
    length = 2 * half_len
    width = layer_input.shape[2]
    rows = w_query.shape[0]
    units = w_gate.shape[1]
    heads, kvs = HEADS // 2, KV // 2
    scale = 1.0 / math.sqrt(HD)
    cosine, sine = rope_tables(length, HD)

    own = plane_turn(layer_input, x).reshape(half_len, width)
    masked = cotangent * token_mask.astype(low)[:, :, None]
    seed_low = plane_turn(masked, x).reshape(half_len, width)
    other_docs = to_core(document_ids)
    documents = pick(jnp.where(core == y, document_ids, other_docs), x)

    gains = jnp.stack([attn_gain, mlp_gain])[:, None]
    gains = in_order(gains, to_core(gains), core, axis=1).reshape(1, -1)
    gains = gather_all(gains, y, x, z, True).reshape(16, 2, 2 * rows)
    gains = jnp.moveaxis(gains, 1, 0).reshape(2, width).astype(f32)

    def halves(weight):
        return weight.reshape(rows, 2, -1)

    qkv = jnp.concatenate([halves(w_query), halves(w_key), halves(w_value)], axis=2)
    gate_up = [weight.reshape(rows, -1, 2, 128) for weight in (w_gate, w_up)]

    def swap_in(mine, sent):
        return in_order(mine[None], to_core(sent)[None], core).reshape(2 * rows, -1)

    qkv = swap_in(pick(qkv, core, 1), pick(qkv, 1 - core, 1))
    qkv = gather_all(qkv, y, x, z, True).reshape(width, -1)
    out_w = gather_all(w_output, y, x, z, False).reshape(2, 8, rows, width)
    out_got = to_core(pick(out_w, 1 - core))
    out_w = in_order(pick(out_w, core)[:, None], out_got[:, None], core, axis=1).reshape(-1, width)
    gate_up = [
        swap_in(
            pick(weight, core, 2).reshape(rows, -1), pick(weight, 1 - core, 2).reshape(rows, -1)
        )
        for weight in gate_up
    ]
    gate_w = gather_all(gate_up[0], y, x, z, True).reshape(width, -1)
    up_w = gather_all(gate_up[1], y, x, z, False).reshape(width, -1)
    down_l = gather_all(w_down[:, : width // 2], y, x, z, True).reshape(units // 2, -1)
    down_r = gather_all(w_down[:, width // 2 :], y, x, z, False).reshape(units // 2, -1)
    down_w = jnp.concatenate([down_l, down_r], axis=1)

    def both(mine):
        return in_order(mine, to_core(mine), core)

    def join(part):
        part = part.reshape(2, half_len, width)
        return pick(part, core) + to_core(pick(part, 1 - core))

    inputs = own.astype(f32)
    inv_one = inverse_rms(inputs)
    unit_one = inputs * inv_one
    normed = both((unit_one * gains[0]).astype(low))
    seed_full = both(seed_low)
    qkv_lin = jnp.dot(normed, qkv, preferred_element_type=f32).astype(low)
    q_cols, k_cols = heads * HD, kvs * HD
    query_rot = rotate_ahead(
        qkv_lin[:, :q_cols].reshape(length, heads, HD).astype(f32), cosine, sine
    ).astype(low)
    query_rot = query_rot.reshape(length, kvs, 2, HD)
    key_rot = rotate_ahead(
        qkv_lin[:, q_cols : q_cols + k_cols].reshape(length, kvs, HD).astype(f32), cosine, sine
    ).astype(low)
    value_heads = qkv_lin[:, q_cols + k_cols :].reshape(length, kvs, HD)
    mixed, sums = attention_forward(
        query_rot, key_rot, value_heads, documents, 512, scale
    )
    hidden = inputs + join(jnp.dot(mixed, out_w, preferred_element_type=f32))
    inv_two = inverse_rms(hidden)
    unit_two = hidden * inv_two
    normed_two = both((unit_two * gains[1]).astype(low))
    gate = jnp.dot(normed_two, gate_w, preferred_element_type=f32)
    upward = jnp.dot(normed_two, up_w, preferred_element_type=f32)
    sigma = jax.nn.sigmoid(gate)
    activated = (gate * sigma * upward).astype(low)
    grad_act = back_product(seed_full, down_w)
    up_low = (grad_act * gate * sigma).astype(low)
    gate_low = (grad_act * upward * sigma * (1.0 + gate * (1.0 - sigma))).astype(low)
    grad_down = scatter_all(
        outer_sum(activated, seed_full).astype(low).reshape(16, -1, width), y, x, z, True
    )

    def swap_out(block, shape, axis):
        block = block.reshape(2, rows, -1)
        got = to_core(pick(block, 1 - core))
        mine = pick(block, core)
        return in_order(mine.reshape(shape), got.reshape(shape), core, axis=axis)

    grad_gate = scatter_all(
        outer_sum(normed_two, gate_low).astype(low).reshape(16, 2 * rows, -1), y, x, z, True
    )
    grad_gate = swap_out(grad_gate, (rows, 16, 1, 128), 2).reshape(rows, units)
    grad_up = scatter_all(
        outer_sum(normed_two, up_low).astype(low).reshape(16, 2 * rows, -1), y, x, z, False
    )
    grad_up = swap_out(grad_up, (rows, 16, 1, 128), 2).reshape(rows, units)
    output = hidden + join(jnp.dot(activated, down_w, preferred_element_type=f32))
    output = plane_turn(output.astype(low).reshape(2, quarter, width), x)
    grad_normed_two = join(back_product(gate_low, gate_w) + back_product(up_low, up_w))
    gain_two = add_all(jnp.sum(grad_normed_two * unit_two, axis=0))
    scaled_two = grad_normed_two * gains[1]
    grad_hidden = seed_low.astype(f32) + inv_two * (
        scaled_two - unit_two * jnp.mean(scaled_two * unit_two, axis=-1, keepdims=True)
    )
    grad_low = both(grad_hidden.astype(low))
    grad_out_w = outer_sum(mixed, grad_low).astype(low).reshape(8, 2, rows, width)
    got = to_core(pick(grad_out_w, 1 - core, 1))
    grad_out_w = in_order(pick(grad_out_w, core, 1), got, core)
    grad_output = scatter_all(grad_out_w, y, x, z, False)
    grad_heads = back_product(grad_low, out_w).astype(low).reshape(length, kvs, 2, HD)
    grad_query_rot, grad_key_rot, grad_values = attention_backward(
        query_rot, key_rot, value_heads, documents, sums, grad_heads, 512, scale
    )
    grad_qkv = jnp.concatenate(
        [
            rotate_behind(grad_query_rot, cosine, sine).reshape(length, q_cols),
            rotate_behind(grad_key_rot, cosine, sine).reshape(length, k_cols),
            grad_values.reshape(length, k_cols),
        ],
        axis=1,
    ).astype(low)
    grad_normed = join(back_product(grad_qkv, qkv))
    gain_one = add_all(jnp.sum(grad_normed * unit_one, axis=0))
    scaled_one = grad_normed * gains[0]
    grad_input = grad_hidden + inv_one * (
        scaled_one - unit_one * jnp.mean(scaled_one * unit_one, axis=-1, keepdims=True)
    )
    grad_input = plane_turn(grad_input.astype(low).reshape(2, quarter, width), x)
    grad_w = scatter_all(
        outer_sum(normed, grad_qkv).astype(low).reshape(16, 2 * rows, -1), y, x, z, True
    )
    grad_w = swap_out(grad_w, (rows, 1, 2 * k_cols + q_cols), 1)
    q_grad = grad_w[:, :, :q_cols].reshape(rows, -1)
    k_grad = grad_w[:, :, q_cols : q_cols + k_cols].reshape(rows, -1)
    v_grad = grad_w[:, :, q_cols + k_cols :].reshape(rows, -1)

    def shard_of(total):
        return lax.dynamic_slice_in_dim(total, device * rows, rows, 0)

    return (
        output,
        grad_input,
        shard_of(gain_one),
        q_grad,
        k_grad,
        v_grad,
        grad_output,
        shard_of(gain_two),
        grad_gate,
        grad_up,
        grad_down,
    )


def solution(mesh):
    fast = dict(mesh.shape) == {"seq": 4, "batch": 8}
    if fast:
        grid = Mesh(mesh.devices.reshape(SIZES), AXES)
        seq, batch = ("y", "x"), ("z", "core")
    else:
        grid, seq, batch = mesh, ("seq",), ("batch",)
    weight = P(seq + batch, None)
    gain = P(seq + batch)
    token = P(batch, seq, None)
    return jax.shard_map(
        fast_body if fast else body,
        mesh=grid,
        in_specs=(token, token, P(batch, seq), P(batch, None), gain)
        + (weight,) * 4
        + (gain,)
        + (weight,) * 3,
        out_specs=(token, token, gain) + (weight,) * 4 + (gain,) + (weight,) * 3,
        check_vma=False,
    )
```

```python
import functools
import math

import jax
import jax.numpy as jnp
from jax import lax
from jax.experimental import pallas as pl
from jax.experimental.pallas import tpu as pltpu
from jax.sharding import Mesh
from jax.sharding import PartitionSpec as P

HEADS = 16
KV = 8
HD = 96


EPSILON = 1e-05
ROPE_BASE = 10000.0


def inverse_rms(field):
    return lax.rsqrt(jnp.mean(field * field, axis=-1, keepdims=True) + EPSILON)


def half_turn(field):
    middle = field.shape[-1] // 2
    return jnp.concatenate([-field[..., middle:], field[..., :middle]], axis=-1)


def rope_tables(length, width):
    middle = width // 2
    freqs = ROPE_BASE ** (-2.0 * jnp.arange(middle, dtype=jnp.float32) / width)
    angles = jnp.arange(length, dtype=jnp.float32)[:, None] * freqs[None, :]
    cosine = jnp.concatenate([jnp.cos(angles), jnp.cos(angles)], axis=-1)
    sine = jnp.concatenate([jnp.sin(angles), jnp.sin(angles)], axis=-1)
    return (cosine, sine)


def rotate_ahead(field, cosine, sine):
    return field * cosine[:, None, :] + half_turn(field) * sine[:, None, :]


def rotate_behind(field, cosine, sine):
    return field * cosine[:, None, :] - half_turn(field) * sine[:, None, :]


def outer_sum(left, right):
    return lax.dot_general(
        left, right, (((0,), (0,)), ((), ())), preferred_element_type=jnp.float32
    )


def back_product(left, right):
    return lax.dot_general(
        left, right, (((1,), (1,)), ((), ())), preferred_element_type=jnp.float32
    )


def fetch_attention(attn_gain, w_query, w_key, w_value, w_output):
    return (
        lax.all_gather(attn_gain, ("seq", "batch"), axis=0, tiled=True),
        lax.all_gather(w_query, ("seq", "batch"), axis=0, tiled=True),
        lax.all_gather(w_key, ("seq", "batch"), axis=0, tiled=True),
        lax.all_gather(w_value, ("seq", "batch"), axis=0, tiled=True),
        lax.all_gather(w_output, ("seq", "batch"), axis=0, tiled=True),
    )


def fetch_feedforward(mlp_gain, w_gate, w_up, w_down):
    return (
        lax.all_gather(mlp_gain, ("seq", "batch"), axis=0, tiled=True),
        lax.all_gather(w_gate, ("seq", "batch"), axis=0, tiled=True),
        lax.all_gather(w_up, ("seq", "batch"), axis=0, tiled=True),
        lax.all_gather(w_down, ("seq", "batch"), axis=0, tiled=True),
    )


def block_scores(query_block, keys, documents, start, block, scale):
    length = keys.shape[0]
    scores = (
        jnp.einsum("qjhd,kjd->jhqk", query_block, keys, preferred_element_type=jnp.float32) * scale
    )
    key_pos = jnp.arange(length, dtype=jnp.int32)
    query_pos = start + jnp.arange(block, dtype=jnp.int32)
    query_docs = lax.dynamic_slice_in_dim(documents, start, block, 0)
    allowed = (key_pos[None, :] <= query_pos[:, None]) & (query_docs[:, None] == documents[None, :])
    return jnp.where(allowed[None, None], scores, -1e30)


def attention_forward(queries, keys, values, documents, block, scale):
    length = queries.shape[0]
    count = length // block

    def one_block(index):
        start = index * block
        query_block = lax.dynamic_slice_in_dim(queries, start, block, 0)
        scores = block_scores(query_block, keys, documents, start, block, scale)
        peak_score = jnp.max(scores, axis=-1, keepdims=True)
        weights = jnp.exp(scores - peak_score)
        totals = jnp.sum(weights, axis=-1, keepdims=True)
        probs = (weights / totals).astype(jnp.bfloat16)
        result = jnp.einsum("jhqk,kjd->qjhd", probs, values, preferred_element_type=jnp.float32)
        return (
            result.astype(jnp.bfloat16).reshape(block, -1),
            (peak_score + jnp.log(totals))[..., 0],
        )

    results, sums = lax.map(one_block, jnp.arange(count, dtype=jnp.int32))
    return (results.reshape(length, -1), sums)


def attention_backward(queries, keys, values, documents, sums, grad_out, block, scale):
    length = queries.shape[0]
    count = length // block

    def one_block(carry, member):
        grad_keys, grad_values = carry
        index, sums_block = member
        start = index * block
        query_block = lax.dynamic_slice_in_dim(queries, start, block, 0)
        grad_block = lax.dynamic_slice_in_dim(grad_out, start, block, 0)
        scores = block_scores(query_block, keys, documents, start, block, scale)
        probs = jnp.exp(scores - sums_block[..., None])
        grad_probs = jnp.einsum(
            "qjhd,kjd->jhqk", grad_block, values, preferred_element_type=jnp.float32
        )
        centre = jnp.sum(probs * grad_probs, axis=-1, keepdims=True)
        grad_scores = (probs * (grad_probs - centre)).astype(jnp.bfloat16)
        grad_query = (
            jnp.einsum("jhqk,kjd->qjhd", grad_scores, keys, preferred_element_type=jnp.float32)
            * scale
        )
        grad_keys = (
            grad_keys
            + jnp.einsum(
                "jhqk,qjhd->kjd", grad_scores, query_block, preferred_element_type=jnp.float32
            )
            * scale
        )
        grad_values = grad_values + jnp.einsum(
            "jhqk,qjhd->kjd",
            probs.astype(jnp.bfloat16),
            grad_block,
            preferred_element_type=jnp.float32,
        )
        return ((grad_keys, grad_values), grad_query)

    empty = jnp.zeros(keys.shape, jnp.float32)
    (grad_keys, grad_values), grad_query = lax.scan(
        one_block, (empty, empty), (jnp.arange(count, dtype=jnp.int32), sums)
    )
    return (
        grad_query.reshape(length, queries.shape[1] * queries.shape[2], queries.shape[3]),
        grad_keys,
        grad_values,
    )


def body(
    layer_input,
    cotangent,
    token_mask,
    document_ids,
    attn_gain,
    w_query,
    w_key,
    w_value,
    w_output,
    mlp_gain,
    w_gate,
    w_up,
    w_down,
):
    parts = lax.axis_size("seq")
    micro_count = layer_input.shape[0]
    shard = layer_input.shape[1]
    length = shard * parts
    heads_here = HEADS // parts
    kv_here = max(1, KV // parts)
    copies = parts * kv_here // KV
    per_kv = heads_here // kv_here
    block = min(512, length)
    scale = 1.0 / math.sqrt(HD)
    cosine, sine = rope_tables(length, HD)
    attn_set = None
    mlp_set = None
    attn_total = None
    mlp_total = None
    outputs = []
    input_grads = []
    kept = {
        "normed": [],
        "normed_two": [],
        "activated": [],
        "seed_low": [],
        "gate_low": [],
        "up_low": [],
        "grad_low": [],
        "mixed": [],
        "query_back": [],
        "key_back": [],
        "value_back": [],
    }
    gain_one_total = None
    gain_two_total = None
    for micro in range(micro_count):
        attn_set = fetch_attention(attn_gain, w_query, w_key, w_value, w_output)
        mlp_set = fetch_feedforward(mlp_gain, w_gate, w_up, w_down)
        gain_one = attn_set[0].astype(jnp.float32)
        gain_two = mlp_set[0].astype(jnp.float32)
        documents = document_ids[micro]
        inputs = layer_input[micro].astype(jnp.float32)
        inv_one = inverse_rms(inputs)
        unit_one = inputs * inv_one
        normed = (unit_one * gain_one).astype(jnp.bfloat16)
        queries = jnp.dot(normed, attn_set[1], preferred_element_type=jnp.float32).astype(
            jnp.bfloat16
        )
        keys_lin = jnp.dot(normed, attn_set[2], preferred_element_type=jnp.float32).astype(
            jnp.bfloat16
        )
        values_lin = jnp.dot(normed, attn_set[3], preferred_element_type=jnp.float32).astype(
            jnp.bfloat16
        )
        queries = queries.reshape(shard, parts, heads_here * HD)
        key_slots = jnp.repeat(keys_lin.reshape(shard, KV, HD), copies, axis=1).reshape(
            shard, parts, kv_here * HD
        )
        value_slots = jnp.repeat(values_lin.reshape(shard, KV, HD), copies, axis=1).reshape(
            shard, parts, kv_here * HD
        )
        pairs = jnp.concatenate([key_slots, value_slots], axis=-1)
        query_heads, pair_heads = (
            lax.all_to_all(queries, "seq", split_axis=1, concat_axis=0, tiled=True),
            lax.all_to_all(pairs, "seq", split_axis=1, concat_axis=0, tiled=True),
        )
        query_rot = rotate_ahead(
            query_heads.reshape(length, heads_here, HD).astype(jnp.float32), cosine, sine
        )
        query_rot = query_rot.astype(jnp.bfloat16).reshape(length, kv_here, per_kv, HD)
        key_heads = pair_heads[:, 0, : kv_here * HD].reshape(length, kv_here, HD)
        key_rot = rotate_ahead(key_heads.astype(jnp.float32), cosine, sine).astype(jnp.bfloat16)
        value_heads = pair_heads[:, 0, kv_here * HD :].reshape(length, kv_here, HD)
        attended, sums = attention_forward(query_rot, key_rot, value_heads, documents, block, scale)
        mixed = lax.all_to_all(
            attended.reshape(length, 1, heads_here * HD),
            "seq",
            split_axis=0,
            concat_axis=1,
            tiled=True,
        )
        mixed = mixed.reshape(shard, HEADS * HD)
        hidden_state = inputs + jnp.dot(mixed, attn_set[4], preferred_element_type=jnp.float32)
        inv_two = inverse_rms(hidden_state)
        unit_two = hidden_state * inv_two
        normed_two = (unit_two * gain_two).astype(jnp.bfloat16)
        gate = jnp.dot(normed_two, mlp_set[1], preferred_element_type=jnp.float32)
        upward = jnp.dot(normed_two, mlp_set[2], preferred_element_type=jnp.float32)
        sigma = jax.nn.sigmoid(gate)
        activated = (gate * sigma * upward).astype(jnp.bfloat16)
        output = hidden_state + jnp.dot(activated, mlp_set[3], preferred_element_type=jnp.float32)
        outputs.append(output.astype(jnp.bfloat16))
        seed = cotangent[micro].astype(jnp.float32) * token_mask[micro].astype(jnp.float32)[:, None]
        seed_low = seed.astype(jnp.bfloat16)
        grad_act = back_product(seed_low, mlp_set[3])
        grad_up_low = (grad_act * gate * sigma).astype(jnp.bfloat16)
        grad_gate_low = (grad_act * upward * sigma * (1.0 + gate * (1.0 - sigma))).astype(
            jnp.bfloat16
        )
        grad_normed_two = back_product(grad_gate_low, mlp_set[1]) + back_product(
            grad_up_low, mlp_set[2]
        )
        grad_gain_two = jnp.sum(grad_normed_two * unit_two, axis=0)
        scaled_two = grad_normed_two * gain_two
        grad_hidden = seed + inv_two * (
            scaled_two - unit_two * jnp.mean(scaled_two * unit_two, axis=-1, keepdims=True)
        )
        gain_two_total = grad_gain_two if gain_two_total is None else gain_two_total + grad_gain_two
        kept["normed_two"].append(normed_two)
        kept["activated"].append(activated)
        kept["seed_low"].append(seed_low)
        kept["gate_low"].append(grad_gate_low)
        kept["up_low"].append(grad_up_low)
        grad_low = grad_hidden.astype(jnp.bfloat16)
        grad_mixed = (
            back_product(grad_low, attn_set[4])
            .astype(jnp.bfloat16)
            .reshape(shard, parts, heads_here * HD)
        )
        grad_heads = lax.all_to_all(
            grad_mixed, "seq", split_axis=1, concat_axis=0, tiled=True
        ).reshape(length, kv_here, per_kv, HD)
        grad_query_rot, grad_key_rot, grad_values = attention_backward(
            query_rot, key_rot, value_heads, documents, sums, grad_heads, block, scale
        )
        grad_query_heads = (
            rotate_behind(grad_query_rot, cosine, sine)
            .astype(jnp.bfloat16)
            .reshape(length, 1, heads_here * HD)
        )
        grad_key_heads = rotate_behind(grad_key_rot, cosine, sine)
        grad_pairs = jnp.concatenate(
            [
                grad_key_heads.reshape(length, kv_here * HD),
                grad_values.reshape(length, kv_here * HD),
            ],
            axis=-1,
        )
        query_back = lax.all_to_all(
            grad_query_heads, "seq", split_axis=0, concat_axis=1, tiled=True
        ).reshape(shard, HEADS * HD)
        pair_back = lax.all_to_all(
            grad_pairs.reshape(length, 1, 2 * kv_here * HD).astype(jnp.bfloat16),
            "seq",
            split_axis=0,
            concat_axis=1,
            tiled=True,
        ).astype(jnp.float32)
        key_back = pair_back[:, :, : kv_here * HD].reshape(shard, KV, copies, HD).sum(axis=2)
        value_back = pair_back[:, :, kv_here * HD :].reshape(shard, KV, copies, HD).sum(axis=2)
        key_back = key_back.reshape(shard, KV * HD).astype(jnp.bfloat16)
        value_back = value_back.reshape(shard, KV * HD).astype(jnp.bfloat16)
        grad_normed = (
            back_product(query_back, attn_set[1])
            + back_product(key_back, attn_set[2])
            + back_product(value_back, attn_set[3])
        )
        grad_gain_one = jnp.sum(grad_normed * unit_one, axis=0)
        scaled_one = grad_normed * gain_one
        grad_input = grad_hidden + inv_one * (
            scaled_one - unit_one * jnp.mean(scaled_one * unit_one, axis=-1, keepdims=True)
        )
        input_grads.append(grad_input.astype(jnp.bfloat16))
        gain_one_total = grad_gain_one if gain_one_total is None else gain_one_total + grad_gain_one
        kept["normed"].append(normed)
        kept["mixed"].append(mixed)
        kept["grad_low"].append(grad_low)
        kept["query_back"].append(query_back)
        kept["key_back"].append(key_back)
        kept["value_back"].append(value_back)
    rows = {name: jnp.concatenate(values, axis=0) for name, values in kept.items()}
    attn_total = (
        lax.psum_scatter(gain_one_total, ("seq", "batch"), scatter_dimension=0, tiled=True),
        lax.psum_scatter(
            outer_sum(rows["normed"], rows["query_back"]),
            ("seq", "batch"),
            scatter_dimension=0,
            tiled=True,
        ),
        lax.psum_scatter(
            outer_sum(rows["normed"], rows["key_back"]),
            ("seq", "batch"),
            scatter_dimension=0,
            tiled=True,
        ),
        lax.psum_scatter(
            outer_sum(rows["normed"], rows["value_back"]),
            ("seq", "batch"),
            scatter_dimension=0,
            tiled=True,
        ),
        lax.psum_scatter(
            outer_sum(rows["mixed"], rows["grad_low"]),
            ("seq", "batch"),
            scatter_dimension=0,
            tiled=True,
        ),
    )
    mlp_total = (
        lax.psum_scatter(gain_two_total, ("seq", "batch"), scatter_dimension=0, tiled=True),
        lax.psum_scatter(
            outer_sum(rows["normed_two"], rows["gate_low"]),
            ("seq", "batch"),
            scatter_dimension=0,
            tiled=True,
        ),
        lax.psum_scatter(
            outer_sum(rows["normed_two"], rows["up_low"]),
            ("seq", "batch"),
            scatter_dimension=0,
            tiled=True,
        ),
        lax.psum_scatter(
            outer_sum(rows["activated"], rows["seed_low"]),
            ("seq", "batch"),
            scatter_dimension=0,
            tiled=True,
        ),
    )
    return (
        jnp.stack(outputs, axis=0),
        jnp.stack(input_grads, axis=0),
        attn_total[0],
        attn_total[1],
        attn_total[2],
        attn_total[3],
        attn_total[4],
        mlp_total[0],
        mlp_total[1],
        mlp_total[2],
        mlp_total[3],
    )


QB = 256
SPAN = 768


def turned(field, back):
    middle = HD // 2
    left, right = field[:, :middle], field[:, middle:]
    if back:
        return jnp.concatenate([right, -left], axis=1)
    return jnp.concatenate([-right, left], axis=1)


def spun(field, cosine, sine, back=False):
    field = field.astype(jnp.float32)
    return field * cosine + turned(field, back) * sine


def nt(left, right):
    return lax.dot_general(left, right, (((1,), (1,)), ((), ())), preferred_element_type=jnp.float32)


def nn(left, right):
    return jnp.dot(left, right, preferred_element_type=jnp.float32)


def tn(left, right):
    return lax.dot_general(left, right, (((0,), (0,)), ((), ())), preferred_element_type=jnp.float32)


def head(ref, rows, number):
    return ref[rows, HD * number : HD * (number + 1)]


def ahead_kernel(heads, kvs, q_ref, kv_ref, cos_ref, sin_ref, row_ref, col_ref, out_ref, keys):
    low, f32 = jnp.bfloat16, jnp.float32
    step = pl.program_id(0)
    everything = pl.ds(0, kv_ref.shape[0])

    @pl.when(step == 0)
    def _():
        for j in range(kvs):
            keys[j] = spun(head(kv_ref, everything, j), cos_ref[...], sin_ref[...]).astype(low)

    start = pl.multiple_of(step * QB, QB)
    base = pl.multiple_of(jnp.maximum(start + QB - SPAN, 0), QB)
    here, span = pl.ds(start, QB), pl.ds(base, SPAN)
    place = start + lax.broadcasted_iota(jnp.int32, (QB, SPAN), 0)
    key_place = base + lax.broadcasted_iota(jnp.int32, (QB, SPAN), 1)
    allowed = (key_place <= place) & (col_ref[here, :] == row_ref[:, span])
    bias = jnp.where(allowed, 0.0, -1e30).astype(f32)
    scale = (1.0 / math.sqrt(HD)) * math.log2(math.e)
    cosine, sine = cos_ref[here, :], sin_ref[here, :]
    results = []
    for h in range(heads):
        j = h * kvs // heads
        query = spun(head(q_ref, here, h), cosine, sine).astype(low)
        scores = nt(query, keys[j, span, :]) * scale + bias
        peak = jnp.max(scores, axis=1, keepdims=True)
        weights = jnp.exp2(scores - peak)
        total = jnp.sum(weights, axis=1, keepdims=True)
        probs = (weights * (1.0 / total)).astype(low)
        results.append(nn(probs, head(kv_ref, span, kvs + j)).astype(low))
    out_ref[...] = jnp.concatenate(results, axis=1)


def behind_kernel(
    heads, kvs, q_ref, kv_ref, grad_ref, cos_ref, sin_ref, row_ref, col_ref, gq_ref, gkv_ref, keys, gks, gvs
):
    low, f32 = jnp.bfloat16, jnp.float32
    step = pl.program_id(0)
    everything = pl.ds(0, kv_ref.shape[0])

    @pl.when(step == 0)
    def _():
        for j in range(kvs):
            keys[j] = spun(head(kv_ref, everything, j), cos_ref[...], sin_ref[...]).astype(low)
        gks[...] = jnp.zeros_like(gks)
        gvs[...] = jnp.zeros_like(gvs)

    start = pl.multiple_of(step * QB, QB)
    base = pl.multiple_of(jnp.maximum(start + QB - SPAN, 0), QB)
    here, span = pl.ds(start, QB), pl.ds(base, SPAN)
    key_place = base + lax.broadcasted_iota(jnp.int32, (SPAN, QB), 0)
    place = start + lax.broadcasted_iota(jnp.int32, (SPAN, QB), 1)
    allowed = (key_place <= place) & (col_ref[span, :] == row_ref[:, here])
    bias = jnp.where(allowed, 0.0, -1e30).astype(f32)
    width = 1.0 / math.sqrt(HD)
    scale = width * math.log2(math.e)
    cosine, sine = cos_ref[here, :], sin_ref[here, :]
    results = []
    for h in range(heads):
        j = h * kvs // heads
        query = spun(head(q_ref, here, h), cosine, sine).astype(low)
        key, value = keys[j, span, :], head(kv_ref, span, kvs + j)
        grad = head(grad_ref, here, h)
        scores = nt(key, query) * scale + bias
        peak = jnp.max(scores, axis=0, keepdims=True)
        weights = jnp.exp2(scores - peak)
        total = jnp.sum(weights, axis=0, keepdims=True)
        probs = weights * (1.0 / total)
        slope = nt(value, grad)
        centre = jnp.sum(probs * slope, axis=0, keepdims=True)
        gs = (probs * (slope - centre)).astype(low)
        gvs[j, span, :] += nn(probs.astype(low), grad)
        gks[j, span, :] += nn(gs, query)
        results.append(spun(tn(gs, key) * width, cosine, sine, True).astype(low))
    gq_ref[...] = jnp.concatenate(results, axis=1)

    @pl.when(step == pl.num_programs(0) - 1)
    def _():
        gk = [spun(gks[j] * width, cos_ref[...], sin_ref[...], True).astype(low) for j in range(kvs)]
        gv = [gvs[j].astype(low) for j in range(kvs)]
        gkv_ref[...] = jnp.concatenate(gk + gv, axis=1)


def whole(shape):
    return pl.BlockSpec(shape, lambda i: (0,) * len(shape))


def attend_ahead(heads, kvs, q, kv, cosine, sine, row, col):
    length = q.shape[0]
    return pl.pallas_call(
        functools.partial(ahead_kernel, heads, kvs),
        grid=(length // QB,),
        in_specs=[whole(v.shape) for v in (q, kv, cosine, sine, row, col)],
        out_specs=pl.BlockSpec((QB, heads * HD), lambda i: (i, 0)),
        out_shape=jax.ShapeDtypeStruct((length, heads * HD), jnp.bfloat16),
        scratch_shapes=[pltpu.VMEM((kvs, length, HD), jnp.bfloat16)],
        compiler_params=pltpu.CompilerParams(vmem_limit_bytes=48 << 20),
        cost_estimate=pl.CostEstimate(flops=4 * heads * length * SPAN * HD, bytes_accessed=6 << 20, transcendentals=heads * length * SPAN),
    )(q, kv, cosine, sine, row, col)


def attend_behind(heads, kvs, q, kv, grad, cosine, sine, row, col):
    length = q.shape[0]
    return pl.pallas_call(
        functools.partial(behind_kernel, heads, kvs),
        grid=(length // QB,),
        in_specs=[whole(v.shape) for v in (q, kv, grad, cosine, sine, row, col)],
        out_specs=[
            pl.BlockSpec((QB, heads * HD), lambda i: (i, 0)),
            pl.BlockSpec((length, 2 * kvs * HD), lambda i: (0, 0)),
        ],
        out_shape=[
            jax.ShapeDtypeStruct((length, heads * HD), jnp.bfloat16),
            jax.ShapeDtypeStruct((length, 2 * kvs * HD), jnp.bfloat16),
        ],
        scratch_shapes=[
            pltpu.VMEM((kvs, length, HD), jnp.bfloat16),
            pltpu.VMEM((kvs, length, HD), jnp.float32),
            pltpu.VMEM((kvs, length, HD), jnp.float32),
        ],
        compiler_params=pltpu.CompilerParams(vmem_limit_bytes=48 << 20),
        cost_estimate=pl.CostEstimate(flops=10 * heads * length * SPAN * HD, bytes_accessed=9 << 20, transcendentals=heads * length * SPAN),
    )(q, kv, grad, cosine, sine, row, col)


AXES = ("y", "x", "zh", "zl", "core")
BITS = {"y": 16, "x": 8, "zh": 4, "zl": 2, "core": 1}


def hop(value, *names):
    flip = sum(BITS[name] for name in names)
    return lax.ppermute(value, AXES, [(i, i ^ flip) for i in range(32)])


def after(value, *others):
    return lax.optimization_barrier((value,) + others)[0]


def in_order(mine, other, place, axis=0):
    first = jnp.where(place == 0, mine, other)
    second = jnp.where(place == 0, other, mine)
    return jnp.concatenate([first, second], axis=axis)


def pick(value, place, axis=0):
    return lax.dynamic_index_in_dim(value, place, axis, keepdims=False)


def plane_turn(tokens, x):
    got = []
    for flip in range(2):
        pairs = []
        for i in range(32):
            y_i, x_i, z_i, core_i = i // 16, i // 8 % 2, i // 2 % 4, i % 2
            pairs.append((i, core_i * 16 + (x_i ^ flip) * 8 + z_i * 2 + y_i))
        got.append(lax.ppermute(pick(tokens, x ^ flip), AXES, pairs)[None])
    return in_order(got[0], got[1], x)


def gather_line(block, zh, zl):
    got = [block[None]] + [hop(block, *names)[None] for names in (("zl",), ("zh",), ("zh", "zl"))]
    return in_order(in_order(got[0], got[1], zl), in_order(got[2], got[3], zl), zh)


def plane_out(line, x_first):
    return hop(line, "x" if x_first else "y")


def plane_pair(line, got, y, x, x_first):
    if x_first:
        return in_order(line[None], got[None], x)[None]
    return in_order(line[None], got[None], y)[:, None]


def plane_rest(pair, y, x, x_first):
    if x_first:
        done = in_order(pair, hop(pair, "y"), y)
    else:
        done = in_order(pair, hop(pair, "x"), x, axis=1)
    return done.reshape((4,) + done.shape[2:])


def gather_plane(line, y, x, x_first):
    pair = plane_pair(line, plane_out(line, x_first), y, x, x_first)
    return plane_rest(pair, y, x, x_first)


def plane_send(total, y, x, y_first):
    total = total.reshape((2, 2) + total.shape[1:])
    if y_first:
        return pick(total, y), hop(pick(total, 1 - y), "y")
    return pick(total, x, 1), hop(pick(total, 1 - x, 1), "x")


def plane_sum(kept, got, y, x, y_first):
    f32, low = jnp.float32, jnp.bfloat16
    half = kept.astype(f32) + got.astype(f32)
    if y_first:
        return pick(half, x) + hop(pick(half, 1 - x).astype(low), "x").astype(f32)
    return pick(half, y) + hop(pick(half, 1 - y).astype(low), "y").astype(f32)


def scatter_line(line, zh, zl):
    f32, low = jnp.float32, jnp.bfloat16
    place = zh * 2 + zl
    result = pick(line, place)
    for k, names in ((1, ("zl",)), (2, ("zh",)), (3, ("zh", "zl"))):
        result = result + hop(pick(line, place ^ k).astype(low), *names).astype(f32)
    return result


def scatter_pairs(line, zh):
    return pick(line, zh) + hop(pick(line, 1 - zh).astype(jnp.bfloat16), "zh").astype(jnp.float32)


def add_all(value):
    for name in ("core", "x", "y", "zl", "zh"):
        value = value + hop(value, name)
    return value


def fast_body(
    layer_input,
    cotangent,
    token_mask,
    document_ids,
    attn_gain,
    w_query,
    w_key,
    w_value,
    w_output,
    mlp_gain,
    w_gate,
    w_up,
    w_down,
):
    f32, low = jnp.float32, jnp.bfloat16
    y, x, zh, zl, core = (lax.axis_index(name) for name in AXES)
    device = sum(lax.axis_index(name) * BITS[name] for name in AXES)
    quarter, width = layer_input.shape[1:]
    half_len = 2 * quarter
    length = 2 * half_len
    rows = w_query.shape[0]
    units = w_gate.shape[1]
    heads, kvs = HEADS // 2, KV // 2
    cosine, sine = rope_tables(length, HD)

    def swap_in(mine, sent):
        return in_order(mine[None], hop(sent, "core")[None], core)

    def halves(weight):
        return weight.reshape(rows, 2, -1)

    def both(mine):
        return in_order(mine, hop(mine, "core"), core)

    def join(part):
        part = part.reshape(2, half_len, width)
        return pick(part, core) + hop(pick(part, 1 - core), "core")

    query_w = halves(w_query)
    pair_w = jnp.concatenate([halves(w_key), halves(w_value)], axis=2)
    query_w, pair_w = (
        swap_in(pick(w, core, 1), pick(w, 1 - core, 1)).reshape(2 * rows, -1)
        for w in (query_w, pair_w)
    )
    own = plane_turn(layer_input, x).reshape(half_len, width)
    masked = cotangent * token_mask.astype(low)[:, :, None]
    masked = after(masked, own)
    seed_low = plane_turn(masked, x).reshape(half_len, width)
    gains = jnp.stack([attn_gain, mlp_gain])[:, None]
    gains = in_order(gains, hop(gains, "core"), core, axis=1).reshape(1, -1)
    gains = gather_plane(gather_line(gains, zh, zl), y, x, True).reshape(16, 2, 2 * rows)
    gains = jnp.moveaxis(gains, 1, 0).reshape(2, width).astype(f32)
    documents = pick(jnp.where(core == y, document_ids, hop(document_ids, "core")), x)
    row, col = documents[None, :], documents[:, None]
    query_w = gather_line(query_w, zh, zl)
    pair_w = gather_line(pair_w, zh, zl)

    hidden_ws = []
    for weight in (w_gate, w_up):
        weight = weight.reshape(rows, units // 512, 2, 2, 128)
        mine, sent = (
            jnp.moveaxis(pick(weight, place, 3), 2, 0).reshape(2, rows, -1)
            for place in (core, 1 - core)
        )
        block = jnp.stack([mine, hop(sent, "core")])
        block = jnp.where(core == 0, block, block[::-1])
        block = after(jnp.moveaxis(block, 0, 1), query_w, pair_w)
        block = in_order(pick(block, zl)[None], hop(pick(block, 1 - zl), "zl")[None], zl)
        block = block.reshape(4 * rows, -1)
        hidden_ws.append(in_order(block, hop(block, "zh"), zh))
    down_ws = []
    for columns in (slice(0, width // 2), slice(width // 2, width)):
        block = after(w_down[:, columns], query_w, pair_w)
        down_ws.append(in_order(block, hop(block, "zh"), zh))
    out_w = gather_line(after(w_output, query_w, pair_w), zh, zl)

    query_w = gather_plane(query_w, y, x, True).reshape(width, -1)
    pair_w = gather_plane(pair_w, y, x, False).reshape(width, -1)
    lines = [out_w] + hidden_ws + down_ws
    ways = [True, True, False, True, False]
    lines = [after(line, query_w, pair_w) for line in lines]
    outs = [plane_out(line, way) for line, way in zip(lines, ways)]

    inputs = own.astype(f32)
    inv_one = inverse_rms(inputs)
    unit_one = inputs * inv_one
    normed = both((unit_one * gains[0]).astype(low))
    query = nn(normed, query_w).astype(low)
    pair = nn(normed, pair_w).astype(low)
    mixed = attend_ahead(heads, kvs, query, pair, cosine, sine, row, col)

    pairs = [
        plane_pair(line, after(got, mixed), y, x, way)
        for line, got, way in zip(lines, outs, ways)
    ]
    out_w = plane_rest(pairs[0], y, x, True).reshape(2, 8, rows, width)
    out_got = hop(pick(out_w, 1 - core), "core")
    out_w = in_order(pick(out_w, core)[:, None], out_got[:, None], core, axis=1).reshape(-1, width)
    gate_w, up_w, down_l, down_r = (
        plane_rest(pair_, y, x, way) for pair_, way in zip(pairs[1:], ways[1:])
    )
    gate_w, up_w = gate_w.reshape(width, -1), up_w.reshape(width, -1)
    down_w = jnp.concatenate([down_l, down_r], axis=-1).reshape(-1, width)

    hidden = inputs + join(nn(mixed, out_w))
    inv_two = inverse_rms(hidden)
    unit_two = hidden * inv_two

    def spread(mine):
        far = hop(mine, "zl")
        return (
            jnp.concatenate([mine, hop(mine, "core")]),
            jnp.concatenate([far, hop(far, "core")]),
        )

    seeds = spread(after(seed_low, query_w, pair_w))
    normed_two = spread((unit_two * gains[1]).astype(low))

    def ahead_and_back(tokens, seed):
        gate, upward, grad_act = nn(tokens, gate_w), nn(tokens, up_w), nt(seed, down_w)
        sigma = jax.nn.sigmoid(gate)
        activated = (gate * sigma * upward).astype(low)
        up_low = (grad_act * gate * sigma).astype(low)
        gate_low = (grad_act * upward * sigma * (1.0 + gate * (1.0 - sigma))).astype(low)
        back = nt(gate_low, gate_w) + nt(up_low, up_w)
        return activated, gate_low, up_low, nn(activated, down_w), back

    near = ahead_and_back(normed_two[0], seeds[0])
    far_tokens = after(normed_two[1], near[4])
    far = ahead_and_back(far_tokens, seeds[1])

    def fold(part):
        return part[:half_len] + hop(part[half_len:], "core")

    theirs = fold(far[4]).astype(low)
    back = hop(theirs, "zl")
    near_low, far_low = (
        tuple(after(v, theirs) for v in parts[:3]) for parts in (near, far)
    )
    grad_down = (tn(near_low[0], seeds[0]) + tn(far_low[0], seeds[1])).astype(low)
    grad_gate = (tn(normed_two[0], near_low[1]) + tn(far_tokens, far_low[1])).astype(low)
    grad_up = (tn(normed_two[0], near_low[2]) + tn(far_tokens, far_low[2])).astype(low)
    totals = [
        grad_gate.reshape(4, 2, 2, 2 * rows, -1),
        grad_up.reshape(4, 2, 2, 2 * rows, -1),
        grad_down[:, : width // 2].reshape(4, 2, -1, width // 2),
        grad_down[:, width // 2 :].reshape(4, 2, -1, width // 2),
    ]
    kepts = [plane_send(total, y, x, way) for total, way in zip(totals, ways[1:])]

    grad_normed_two = fold(near[4]) + back.astype(f32)
    scaled_two = grad_normed_two * gains[1]
    grad_hidden = seed_low.astype(f32) + inv_two * (
        scaled_two - unit_two * jnp.mean(scaled_two * unit_two, axis=-1, keepdims=True)
    )
    grad_low = both(grad_hidden.astype(low))
    grad_heads = nt(grad_low, out_w).astype(low)
    grad_heads = after(grad_heads, *totals)

    ahead_low = after(fold(far[3]).astype(low), back)
    output = hidden + fold(near[3]) + hop(ahead_low, "zl").astype(f32)
    gain_two = jnp.sum(grad_normed_two * unit_two, axis=0)

    grad_query, grad_pair = attend_behind(
        heads, kvs, query, pair, grad_heads, cosine, sine, row, col
    )
    output = after(output.astype(low), grad_query)
    output = plane_turn(output.reshape(2, quarter, width), x)
    part = nt(grad_query, query_w) + nt(grad_pair, pair_w)
    grad_out_w = tn(mixed, grad_low).astype(low).reshape(8, 2, rows, width)
    got = hop(pick(grad_out_w, 1 - core, 1), "core")
    grad_out_w = in_order(pick(grad_out_w, core, 1), got, core).reshape(4, 4, rows, width)
    tails = [
        tn(normed, grad_query).astype(low).reshape(4, 4, 2 * rows, -1),
        tn(normed, grad_pair).astype(low).reshape(4, 4, 2 * rows, -1),
        grad_out_w[..., : width // 2],
        grad_out_w[..., width // 2 :],
    ]
    tail_ways = [True, False, True, False]
    tail_kepts = [plane_send(total, y, x, way) for total, way in zip(tails, tail_ways)]
    sums = [
        scatter_pairs(plane_sum(kept, after(got, part), y, x, way), zh)
        for (kept, got), way in zip(kepts, ways[1:])
    ]
    grad_normed = join(part)
    scaled_one = grad_normed * gains[0]
    grad_input = grad_hidden + inv_one * (
        scaled_one - unit_one * jnp.mean(scaled_one * unit_one, axis=-1, keepdims=True)
    )
    grad_input = plane_turn(grad_input.astype(low).reshape(2, quarter, width), x)
    gain_one = add_all(jnp.stack([jnp.sum(grad_normed * unit_one, axis=0), gain_two]))
    tail_sums = [
        scatter_line(plane_sum(kept, got, y, x, way), zh, zl)
        for (kept, got), way in zip(tail_kepts, tail_ways)
    ]

    hidden_grads = []
    for total in sums[:2]:
        total = in_order(pick(total, zl)[None], hop(pick(total, 1 - zl), "zl")[None], zl)
        total = total.reshape(2, 2, rows, -1)
        total = swap_in(pick(total, core, 1), pick(total, 1 - core, 1))
        total = jnp.transpose(total.reshape(2, 2, rows, -1, 128), (2, 3, 1, 0, 4))
        hidden_grads.append(total.reshape(rows, units))
    grad_down = jnp.concatenate(sums[2:], axis=1)
    grad_output = jnp.concatenate(tail_sums[2:], axis=1)
    moved = []
    for total in tail_sums[:2]:
        total = total.reshape(2, rows, -1)
        moved.append(swap_in(pick(total, core), pick(total, 1 - core)))
    q_grad = jnp.moveaxis(moved[0], 0, 1).reshape(rows, -1)
    k_grad, v_grad = (
        jnp.moveaxis(part_, 0, 1).reshape(rows, -1)
        for part_ in (moved[1][:, :, : kvs * HD], moved[1][:, :, kvs * HD :])
    )
    gain_one = lax.dynamic_slice_in_dim(gain_one, device * rows, rows, 1)

    return (
        output,
        grad_input,
        gain_one[0],
        q_grad,
        k_grad,
        v_grad,
        grad_output,
        gain_one[1],
        hidden_grads[0],
        hidden_grads[1],
        grad_down,
    )


def solution(mesh):
    fast = dict(mesh.shape) == {"seq": 4, "batch": 8}
    if fast:
        grid = Mesh(mesh.devices.reshape((2,) * 5), AXES)
        seq, batch = ("y", "x"), ("zh", "zl", "core")
    else:
        grid, seq, batch = mesh, ("seq",), ("batch",)
    weight = P(seq + batch, None)
    gain = P(seq + batch)
    token = P(batch, seq, None)
    return jax.shard_map(
        fast_body if fast else body,
        mesh=grid,
        in_specs=(token, token, P(batch, seq), P(batch, None), gain)
        + (weight,) * 4
        + (gain,)
        + (weight,) * 3,
        out_specs=(token, token, gain) + (weight,) * 4 + (gain,) + (weight,) * 3,
        check_vma=False,
    )
```

```python
import functools
import math

import jax
import jax.numpy as jnp
from jax import lax
from jax.experimental import pallas as pl
from jax.experimental.pallas import tpu as pltpu
from jax.sharding import Mesh
from jax.sharding import PartitionSpec as P

HEADS = 16
KV = 8
HD = 96


EPSILON = 1e-05
ROPE_BASE = 10000.0


def inverse_rms(field):
    return lax.rsqrt(jnp.mean(field * field, axis=-1, keepdims=True) + EPSILON)


def half_turn(field):
    middle = field.shape[-1] // 2
    return jnp.concatenate([-field[..., middle:], field[..., :middle]], axis=-1)


def rope_tables(length, width):
    middle = width // 2
    freqs = ROPE_BASE ** (-2.0 * jnp.arange(middle, dtype=jnp.float32) / width)
    angles = jnp.arange(length, dtype=jnp.float32)[:, None] * freqs[None, :]
    cosine = jnp.concatenate([jnp.cos(angles), jnp.cos(angles)], axis=-1)
    sine = jnp.concatenate([jnp.sin(angles), jnp.sin(angles)], axis=-1)
    return (cosine, sine)


def rotate_ahead(field, cosine, sine):
    return field * cosine[:, None, :] + half_turn(field) * sine[:, None, :]


def rotate_behind(field, cosine, sine):
    return field * cosine[:, None, :] - half_turn(field) * sine[:, None, :]


def outer_sum(left, right):
    return lax.dot_general(
        left, right, (((0,), (0,)), ((), ())), preferred_element_type=jnp.float32
    )


def back_product(left, right):
    return lax.dot_general(
        left, right, (((1,), (1,)), ((), ())), preferred_element_type=jnp.float32
    )


def fetch_attention(attn_gain, w_query, w_key, w_value, w_output):
    return (
        lax.all_gather(attn_gain, ("seq", "batch"), axis=0, tiled=True),
        lax.all_gather(w_query, ("seq", "batch"), axis=0, tiled=True),
        lax.all_gather(w_key, ("seq", "batch"), axis=0, tiled=True),
        lax.all_gather(w_value, ("seq", "batch"), axis=0, tiled=True),
        lax.all_gather(w_output, ("seq", "batch"), axis=0, tiled=True),
    )


def fetch_feedforward(mlp_gain, w_gate, w_up, w_down):
    return (
        lax.all_gather(mlp_gain, ("seq", "batch"), axis=0, tiled=True),
        lax.all_gather(w_gate, ("seq", "batch"), axis=0, tiled=True),
        lax.all_gather(w_up, ("seq", "batch"), axis=0, tiled=True),
        lax.all_gather(w_down, ("seq", "batch"), axis=0, tiled=True),
    )


def block_scores(query_block, keys, documents, start, block, scale):
    length = keys.shape[0]
    scores = (
        jnp.einsum("qjhd,kjd->jhqk", query_block, keys, preferred_element_type=jnp.float32) * scale
    )
    key_pos = jnp.arange(length, dtype=jnp.int32)
    query_pos = start + jnp.arange(block, dtype=jnp.int32)
    query_docs = lax.dynamic_slice_in_dim(documents, start, block, 0)
    allowed = (key_pos[None, :] <= query_pos[:, None]) & (query_docs[:, None] == documents[None, :])
    return jnp.where(allowed[None, None], scores, -1e30)


def attention_forward(queries, keys, values, documents, block, scale):
    length = queries.shape[0]
    count = length // block

    def one_block(index):
        start = index * block
        query_block = lax.dynamic_slice_in_dim(queries, start, block, 0)
        scores = block_scores(query_block, keys, documents, start, block, scale)
        peak_score = jnp.max(scores, axis=-1, keepdims=True)
        weights = jnp.exp(scores - peak_score)
        totals = jnp.sum(weights, axis=-1, keepdims=True)
        probs = (weights / totals).astype(jnp.bfloat16)
        result = jnp.einsum("jhqk,kjd->qjhd", probs, values, preferred_element_type=jnp.float32)
        return (
            result.astype(jnp.bfloat16).reshape(block, -1),
            (peak_score + jnp.log(totals))[..., 0],
        )

    results, sums = lax.map(one_block, jnp.arange(count, dtype=jnp.int32))
    return (results.reshape(length, -1), sums)


def attention_backward(queries, keys, values, documents, sums, grad_out, block, scale):
    length = queries.shape[0]
    count = length // block

    def one_block(carry, member):
        grad_keys, grad_values = carry
        index, sums_block = member
        start = index * block
        query_block = lax.dynamic_slice_in_dim(queries, start, block, 0)
        grad_block = lax.dynamic_slice_in_dim(grad_out, start, block, 0)
        scores = block_scores(query_block, keys, documents, start, block, scale)
        probs = jnp.exp(scores - sums_block[..., None])
        grad_probs = jnp.einsum(
            "qjhd,kjd->jhqk", grad_block, values, preferred_element_type=jnp.float32
        )
        centre = jnp.sum(probs * grad_probs, axis=-1, keepdims=True)
        grad_scores = (probs * (grad_probs - centre)).astype(jnp.bfloat16)
        grad_query = (
            jnp.einsum("jhqk,kjd->qjhd", grad_scores, keys, preferred_element_type=jnp.float32)
            * scale
        )
        grad_keys = (
            grad_keys
            + jnp.einsum(
                "jhqk,qjhd->kjd", grad_scores, query_block, preferred_element_type=jnp.float32
            )
            * scale
        )
        grad_values = grad_values + jnp.einsum(
            "jhqk,qjhd->kjd",
            probs.astype(jnp.bfloat16),
            grad_block,
            preferred_element_type=jnp.float32,
        )
        return ((grad_keys, grad_values), grad_query)

    empty = jnp.zeros(keys.shape, jnp.float32)
    (grad_keys, grad_values), grad_query = lax.scan(
        one_block, (empty, empty), (jnp.arange(count, dtype=jnp.int32), sums)
    )
    return (
        grad_query.reshape(length, queries.shape[1] * queries.shape[2], queries.shape[3]),
        grad_keys,
        grad_values,
    )


def body(
    layer_input,
    cotangent,
    token_mask,
    document_ids,
    attn_gain,
    w_query,
    w_key,
    w_value,
    w_output,
    mlp_gain,
    w_gate,
    w_up,
    w_down,
):
    parts = lax.axis_size("seq")
    micro_count = layer_input.shape[0]
    shard = layer_input.shape[1]
    length = shard * parts
    heads_here = HEADS // parts
    kv_here = max(1, KV // parts)
    copies = parts * kv_here // KV
    per_kv = heads_here // kv_here
    block = min(512, length)
    scale = 1.0 / math.sqrt(HD)
    cosine, sine = rope_tables(length, HD)
    attn_set = None
    mlp_set = None
    attn_total = None
    mlp_total = None
    outputs = []
    input_grads = []
    kept = {
        "normed": [],
        "normed_two": [],
        "activated": [],
        "seed_low": [],
        "gate_low": [],
        "up_low": [],
        "grad_low": [],
        "mixed": [],
        "query_back": [],
        "key_back": [],
        "value_back": [],
    }
    gain_one_total = None
    gain_two_total = None
    for micro in range(micro_count):
        attn_set = fetch_attention(attn_gain, w_query, w_key, w_value, w_output)
        mlp_set = fetch_feedforward(mlp_gain, w_gate, w_up, w_down)
        gain_one = attn_set[0].astype(jnp.float32)
        gain_two = mlp_set[0].astype(jnp.float32)
        documents = document_ids[micro]
        inputs = layer_input[micro].astype(jnp.float32)
        inv_one = inverse_rms(inputs)
        unit_one = inputs * inv_one
        normed = (unit_one * gain_one).astype(jnp.bfloat16)
        queries = jnp.dot(normed, attn_set[1], preferred_element_type=jnp.float32).astype(
            jnp.bfloat16
        )
        keys_lin = jnp.dot(normed, attn_set[2], preferred_element_type=jnp.float32).astype(
            jnp.bfloat16
        )
        values_lin = jnp.dot(normed, attn_set[3], preferred_element_type=jnp.float32).astype(
            jnp.bfloat16
        )
        queries = queries.reshape(shard, parts, heads_here * HD)
        key_slots = jnp.repeat(keys_lin.reshape(shard, KV, HD), copies, axis=1).reshape(
            shard, parts, kv_here * HD
        )
        value_slots = jnp.repeat(values_lin.reshape(shard, KV, HD), copies, axis=1).reshape(
            shard, parts, kv_here * HD
        )
        pairs = jnp.concatenate([key_slots, value_slots], axis=-1)
        query_heads, pair_heads = (
            lax.all_to_all(queries, "seq", split_axis=1, concat_axis=0, tiled=True),
            lax.all_to_all(pairs, "seq", split_axis=1, concat_axis=0, tiled=True),
        )
        query_rot = rotate_ahead(
            query_heads.reshape(length, heads_here, HD).astype(jnp.float32), cosine, sine
        )
        query_rot = query_rot.astype(jnp.bfloat16).reshape(length, kv_here, per_kv, HD)
        key_heads = pair_heads[:, 0, : kv_here * HD].reshape(length, kv_here, HD)
        key_rot = rotate_ahead(key_heads.astype(jnp.float32), cosine, sine).astype(jnp.bfloat16)
        value_heads = pair_heads[:, 0, kv_here * HD :].reshape(length, kv_here, HD)
        attended, sums = attention_forward(query_rot, key_rot, value_heads, documents, block, scale)
        mixed = lax.all_to_all(
            attended.reshape(length, 1, heads_here * HD),
            "seq",
            split_axis=0,
            concat_axis=1,
            tiled=True,
        )
        mixed = mixed.reshape(shard, HEADS * HD)
        hidden_state = inputs + jnp.dot(mixed, attn_set[4], preferred_element_type=jnp.float32)
        inv_two = inverse_rms(hidden_state)
        unit_two = hidden_state * inv_two
        normed_two = (unit_two * gain_two).astype(jnp.bfloat16)
        gate = jnp.dot(normed_two, mlp_set[1], preferred_element_type=jnp.float32)
        upward = jnp.dot(normed_two, mlp_set[2], preferred_element_type=jnp.float32)
        sigma = jax.nn.sigmoid(gate)
        activated = (gate * sigma * upward).astype(jnp.bfloat16)
        output = hidden_state + jnp.dot(activated, mlp_set[3], preferred_element_type=jnp.float32)
        outputs.append(output.astype(jnp.bfloat16))
        seed = cotangent[micro].astype(jnp.float32) * token_mask[micro].astype(jnp.float32)[:, None]
        seed_low = seed.astype(jnp.bfloat16)
        grad_act = back_product(seed_low, mlp_set[3])
        grad_up_low = (grad_act * gate * sigma).astype(jnp.bfloat16)
        grad_gate_low = (grad_act * upward * sigma * (1.0 + gate * (1.0 - sigma))).astype(
            jnp.bfloat16
        )
        grad_normed_two = back_product(grad_gate_low, mlp_set[1]) + back_product(
            grad_up_low, mlp_set[2]
        )
        grad_gain_two = jnp.sum(grad_normed_two * unit_two, axis=0)
        scaled_two = grad_normed_two * gain_two
        grad_hidden = seed + inv_two * (
            scaled_two - unit_two * jnp.mean(scaled_two * unit_two, axis=-1, keepdims=True)
        )
        gain_two_total = grad_gain_two if gain_two_total is None else gain_two_total + grad_gain_two
        kept["normed_two"].append(normed_two)
        kept["activated"].append(activated)
        kept["seed_low"].append(seed_low)
        kept["gate_low"].append(grad_gate_low)
        kept["up_low"].append(grad_up_low)
        grad_low = grad_hidden.astype(jnp.bfloat16)
        grad_mixed = (
            back_product(grad_low, attn_set[4])
            .astype(jnp.bfloat16)
            .reshape(shard, parts, heads_here * HD)
        )
        grad_heads = lax.all_to_all(
            grad_mixed, "seq", split_axis=1, concat_axis=0, tiled=True
        ).reshape(length, kv_here, per_kv, HD)
        grad_query_rot, grad_key_rot, grad_values = attention_backward(
            query_rot, key_rot, value_heads, documents, sums, grad_heads, block, scale
        )
        grad_query_heads = (
            rotate_behind(grad_query_rot, cosine, sine)
            .astype(jnp.bfloat16)
            .reshape(length, 1, heads_here * HD)
        )
        grad_key_heads = rotate_behind(grad_key_rot, cosine, sine)
        grad_pairs = jnp.concatenate(
            [
                grad_key_heads.reshape(length, kv_here * HD),
                grad_values.reshape(length, kv_here * HD),
            ],
            axis=-1,
        )
        query_back = lax.all_to_all(
            grad_query_heads, "seq", split_axis=0, concat_axis=1, tiled=True
        ).reshape(shard, HEADS * HD)
        pair_back = lax.all_to_all(
            grad_pairs.reshape(length, 1, 2 * kv_here * HD).astype(jnp.bfloat16),
            "seq",
            split_axis=0,
            concat_axis=1,
            tiled=True,
        ).astype(jnp.float32)
        key_back = pair_back[:, :, : kv_here * HD].reshape(shard, KV, copies, HD).sum(axis=2)
        value_back = pair_back[:, :, kv_here * HD :].reshape(shard, KV, copies, HD).sum(axis=2)
        key_back = key_back.reshape(shard, KV * HD).astype(jnp.bfloat16)
        value_back = value_back.reshape(shard, KV * HD).astype(jnp.bfloat16)
        grad_normed = (
            back_product(query_back, attn_set[1])
            + back_product(key_back, attn_set[2])
            + back_product(value_back, attn_set[3])
        )
        grad_gain_one = jnp.sum(grad_normed * unit_one, axis=0)
        scaled_one = grad_normed * gain_one
        grad_input = grad_hidden + inv_one * (
            scaled_one - unit_one * jnp.mean(scaled_one * unit_one, axis=-1, keepdims=True)
        )
        input_grads.append(grad_input.astype(jnp.bfloat16))
        gain_one_total = grad_gain_one if gain_one_total is None else gain_one_total + grad_gain_one
        kept["normed"].append(normed)
        kept["mixed"].append(mixed)
        kept["grad_low"].append(grad_low)
        kept["query_back"].append(query_back)
        kept["key_back"].append(key_back)
        kept["value_back"].append(value_back)
    rows = {name: jnp.concatenate(values, axis=0) for name, values in kept.items()}
    attn_total = (
        lax.psum_scatter(gain_one_total, ("seq", "batch"), scatter_dimension=0, tiled=True),
        lax.psum_scatter(
            outer_sum(rows["normed"], rows["query_back"]),
            ("seq", "batch"),
            scatter_dimension=0,
            tiled=True,
        ),
        lax.psum_scatter(
            outer_sum(rows["normed"], rows["key_back"]),
            ("seq", "batch"),
            scatter_dimension=0,
            tiled=True,
        ),
        lax.psum_scatter(
            outer_sum(rows["normed"], rows["value_back"]),
            ("seq", "batch"),
            scatter_dimension=0,
            tiled=True,
        ),
        lax.psum_scatter(
            outer_sum(rows["mixed"], rows["grad_low"]),
            ("seq", "batch"),
            scatter_dimension=0,
            tiled=True,
        ),
    )
    mlp_total = (
        lax.psum_scatter(gain_two_total, ("seq", "batch"), scatter_dimension=0, tiled=True),
        lax.psum_scatter(
            outer_sum(rows["normed_two"], rows["gate_low"]),
            ("seq", "batch"),
            scatter_dimension=0,
            tiled=True,
        ),
        lax.psum_scatter(
            outer_sum(rows["normed_two"], rows["up_low"]),
            ("seq", "batch"),
            scatter_dimension=0,
            tiled=True,
        ),
        lax.psum_scatter(
            outer_sum(rows["activated"], rows["seed_low"]),
            ("seq", "batch"),
            scatter_dimension=0,
            tiled=True,
        ),
    )
    return (
        jnp.stack(outputs, axis=0),
        jnp.stack(input_grads, axis=0),
        attn_total[0],
        attn_total[1],
        attn_total[2],
        attn_total[3],
        attn_total[4],
        mlp_total[0],
        mlp_total[1],
        mlp_total[2],
        mlp_total[3],
    )


AXES = ("y", "x", "zh", "zl", "core")
BITS = {"y": 16, "x": 8, "zh": 4, "zl": 2, "core": 1}
MESH = pl.DeviceIdType.MESH


def coordinates():
    return tuple(lax.axis_index(name) for name in AXES)


def peer(me, *names):
    return tuple(1 - at if name in names else at for name, at in zip(AXES, me))


def greet(me, groups):
    barrier = pltpu.get_barrier_semaphore()
    for names in groups:
        pl.semaphore_signal(barrier, 1, device_id=peer(me, *names), device_id_type=MESH)
    pl.semaphore_wait(barrier, len(groups))


class Mover:
    def __init__(self, me, sends, recvs):
        self.me, self.sends, self.recvs, self.used = me, sends, recvs, 0
        self.started = []

    def next(self):
        number = self.used
        self.used += 1
        assert number < self.sends.shape[0]
        return number

    def copy(self, src, dst, *names, device=None):
        number = self.next()
        return pltpu.make_async_remote_copy(
            src_ref=src,
            dst_ref=dst,
            send_sem=self.sends.at[number],
            recv_sem=self.recvs.at[number],
            device_id=peer(self.me, *names) if device is None else device,
            device_id_type=MESH,
        )

    def send(self, src, dst, *names):
        made = self.copy(src, dst, *names)
        made.start()
        self.started.append(made)
        return made

    def local(self, src, dst):
        made = self.quiet(src, dst)
        made.start()
        return made

    def quiet(self, src, dst):
        number = self.next()
        return pltpu.make_async_copy(src, dst, self.recvs.at[number])

    def finish(self):
        for made in self.started:
            made.wait_send()


HEAD_GROUPS = (
    ("core",),
    ("zl",),
    ("zh",),
    ("zh", "zl"),
    ("zl", "core"),
    ("x",),
    ("y",),
    ("y", "core"),
    ("y", "core", "x"),
)
LINE = (("zl",), ("zh",), ("zh", "zl"))


def turn_start(move, me, src, dst):
    y, x, zh, zl, core = me
    stays = y == core
    made = []
    for flip in (1, 0):
        place = x if flip == 0 else 1 - x
        from_, to = src.at[place], dst.at[x]
        copy = move.copy(from_, to, device=(core, place, zh, zl, y))
        if flip == 0:
            own = move.quiet(from_, to)
            pl.when(stays)(own.start)
            pl.when(jnp.logical_not(stays))(copy.start)
            made.append((copy, own))
        else:
            copy.start()
            made.append((copy, None))
    return made


def turn_end(me, made):
    stays = me[0] == me[4]
    for copy, own in made:
        if own is None:
            copy.wait()
        else:
            pl.when(stays)(own.wait)
            pl.when(jnp.logical_not(stays))(copy.wait)


def head_kernel(
    x_in,
    g_in,
    qkv_in,
    gate_in,
    up_in,
    down_in,
    out_in,
    gain_in,
    docs_in,
    x_out,
    g_out,
    qkv_w,
    gate_w,
    up_w,
    down_w,
    out_w,
    gains,
    docs_out,
    sends,
    recvs,
):
    me = coordinates()
    y, x, zh, zl, core = me
    s, z = y * 2 + x, zh * 2 + zl
    half = qkv_w.shape[-1] // 2
    left, right = pl.ds(0, half), pl.ds(half, half)
    greet(me, HEAD_GROUPS)
    move = Mover(me, sends, recvs)

    own = [
        move.local(qkv_in.at[core], qkv_w.at[s, z, core]),
        move.local(gain_in, gains.at[s, z, core]),
        move.local(gate_in.at[zl, core], gate_w.at[s, zh, zl, core]),
        move.local(up_in.at[zl, core], up_w.at[s, zh, zl, core]),
        move.local(down_in, down_w.at[s, zh]),
    ]
    first = [
        move.send(qkv_in.at[1 - core], qkv_w.at[s, z, core], "core"),
        move.send(gain_in, gains.at[s, z, core], "core"),
    ]
    docs = move.send(docs_in, docs_out, "core")
    x_turn = turn_start(move, me, x_in, x_out)
    own[0].wait()
    own[1].wait()
    first[0].wait_recv()
    first[1].wait_recv()
    line = [move.send(qkv_w.at[s, z], qkv_w.at[s, z], *names) for names in LINE]
    line += [move.send(gains.at[s, z], gains.at[s, z], *names) for names in LINE]
    g_turn = turn_start(move, me, g_in, g_out)

    spread = []
    for src, dst in ((gate_in, gate_w), (up_in, up_w)):
        for names in (("core",), ("zl",), ("zl", "core")):
            to_zl = 1 - zl if "zl" in names else zl
            to_core = 1 - core if "core" in names else core
            spread.append(move.send(src.at[to_zl, to_core], dst.at[s, zh, zl, core], *names))
    mine = y == core
    other = jnp.logical_not(mine)
    out_own = move.quiet(out_in, out_w.at[x, z, core])
    out_sent = move.copy(out_in, out_w.at[x, z, core], "core")
    pl.when(mine)(out_own.start)
    pl.when(other)(out_sent.start)

    for made in line:
        made.wait_recv()
    hops = plane_start(move, qkv_w, s, (left, right))
    hops += [move.send(gains.at[s], gains.at[s], "x")]
    for made in own[2:]:
        made.wait()
    for made in spread:
        made.wait_recv()
    pairs = [
        move.send(ref.at[s, zh], ref.at[s, zh], "zh") for ref in (gate_w, up_w, down_w)
    ]
    out_line = [move.copy(out_w.at[x, z], out_w.at[x, z], *names) for names in LINE]
    pl.when(other)(out_sent.wait_send)

    @pl.when(mine)
    def _():
        out_own.wait()
        out_sent.wait_recv()
        for made in out_line:
            made.start()

    rest = plane_pass(move, hops[:4], qkv_w, y, x, (left, right))
    hops[4].wait_recv()
    xs = pl.ds(2 * y, 2)
    rest.append(move.send(gains.at[xs], gains.at[xs], "y"))
    turn_end(me, x_turn)
    turn_end(me, g_turn)
    docs.wait_recv()
    for made in rest + pairs:
        made.wait_recv()

    @pl.when(mine)
    def _():
        for made in out_line:
            made.wait()

    move.finish()


def plane_start(move, ref, s, parts):
    made = []
    for part in parts:
        piece = ref.at[s] if part is None else ref.at[s, ..., part]
        made += [move.send(piece, piece, "x"), move.send(piece, piece, "y")]
    return made


def plane_pass(move, made, ref, y, x, parts):
    made[0].wait_recv()
    first = ref.at[2 * y + 1 - x, ..., parts[0]]
    rest = [move.send(first, first, "y")]
    made[3].wait_recv()
    second = ref.at[2 * (1 - y) + x, ..., parts[1]]
    rest.append(move.send(second, second, "x"))
    made[1].wait_recv()
    made[2].wait_recv()
    return rest


def fetch_head(x_in, g_in, qkv, gate, up, down, out, gain, docs):
    low = jnp.bfloat16
    rows = qkv.shape[1]
    shapes = [
        jax.ShapeDtypeStruct(x_in.shape, low),
        jax.ShapeDtypeStruct(g_in.shape, low),
        jax.ShapeDtypeStruct((4, 4, 2) + qkv.shape[1:], low),
        jax.ShapeDtypeStruct((4, 2, 2, 2) + gate.shape[2:], low),
        jax.ShapeDtypeStruct((4, 2, 2, 2) + up.shape[2:], low),
        jax.ShapeDtypeStruct((4, 2) + down.shape, low),
        jax.ShapeDtypeStruct((2, 4, 2) + out.shape, low),
        jax.ShapeDtypeStruct((4, 4, 2) + gain.shape, gain.dtype),
        jax.ShapeDtypeStruct(docs.shape, docs.dtype),
    ]
    hbm = pl.BlockSpec(memory_space=pl.ANY)
    return pl.pallas_call(
        head_kernel,
        in_specs=[hbm] * 9,
        out_specs=[hbm] * 9,
        out_shape=shapes,
        scratch_shapes=[pltpu.SemaphoreType.DMA((48,)), pltpu.SemaphoreType.DMA((48,))],
        compiler_params=pltpu.CompilerParams(collective_id=1, has_side_effects=True),
        name="head",
    )(x_in, g_in, qkv, gate, up, down, out, gain, docs)


QB = 256
SPAN = 768


def turned(field, back):
    middle = HD // 2
    left, right = field[:, :middle], field[:, middle:]
    if back:
        return jnp.concatenate([right, -left], axis=1)
    return jnp.concatenate([-right, left], axis=1)


def spun(field, cosine, sine, back=False):
    field = field.astype(jnp.float32)
    return field * cosine + turned(field, back) * sine


def nt(left, right):
    return lax.dot_general(left, right, (((1,), (1,)), ((), ())), preferred_element_type=jnp.float32)


def nn(left, right):
    return jnp.dot(left, right, preferred_element_type=jnp.float32)


def tn(left, right):
    return lax.dot_general(left, right, (((0,), (0,)), ((), ())), preferred_element_type=jnp.float32)


def head(ref, rows, number):
    return ref[rows, HD * number : HD * (number + 1)]


def ahead_block(heads, kvs, step, qkv_ref, cos_ref, sin_ref, row_ref, col_ref, out_ref, keys):
    low, f32 = jnp.bfloat16, jnp.float32
    start = pl.multiple_of(step * QB, QB)
    base = pl.multiple_of(jnp.maximum(start + QB - SPAN, 0), QB)
    here, span = pl.ds(start, QB), pl.ds(base, SPAN)
    key_place = base + lax.broadcasted_iota(jnp.int32, (SPAN, QB), 0)
    place = start + lax.broadcasted_iota(jnp.int32, (SPAN, QB), 1)
    allowed = (key_place <= place) & (col_ref[span, :] == row_ref[:, here])
    bias = jnp.where(allowed, 0.0, -1e30).astype(f32)
    scale = (1.0 / math.sqrt(HD)) * math.log2(math.e)
    cosine, sine = cos_ref[here, :], sin_ref[here, :]
    results = []
    for h in range(heads):
        j = h * kvs // heads
        query = spun(head(qkv_ref, here, h), cosine, sine).astype(low)
        scores = nt(keys[j, span, :], query) * scale + bias
        peak = jnp.max(scores, axis=0, keepdims=True)
        weights = jnp.exp2(scores - peak)
        total = jnp.sum(weights, axis=0, keepdims=True)
        probs = (weights * (1.0 / total)).astype(low)
        results.append(tn(probs, head(qkv_ref, span, heads + kvs + j)).astype(low))
    out_ref[here, :] = jnp.concatenate(results, axis=1)


def ahead_kernel(
    heads,
    kvs,
    qkv_ref,
    cos_ref,
    sin_ref,
    row_ref,
    col_ref,
    out_in,
    gate_in,
    up_in,
    down_in,
    seed_in,
    mixed_ref,
    out_w,
    gate_w,
    up_w,
    down_w,
    seeds,
    keys,
    sends,
    recvs,
):
    me = coordinates()
    y, x, zh, zl, core = me
    s = 2 * y + x
    mine = y == core
    other = jnp.logical_not(mine)
    greet(me, (("x",), ("y",), ("core",), ("zl",)))
    move = Mover(me, sends, recvs)
    seed_own = move.local(seed_in, seeds.at[0])
    seed_moves = [
        move.send(seed_in, seeds.at[1], "core"),
        move.send(seed_in, seeds.at[2], "zl"),
    ]
    out_x = move.copy(out_w.at[x], out_w.at[x], "x")
    out_y = [move.copy(out_w.at[at], out_w.at[at], "y") for at in (x, 1 - x)]

    @pl.when(mine)
    def _():
        out_x.start()
        out_y[0].start()

    wide = gate_w.shape[-1]
    gate_hops = plane_start(move, gate_w, s, (pl.ds(0, wide // 2), pl.ds(wide // 2, wide // 2)))
    up_hops = plane_start(move, up_w, s, (pl.ds(0, wide // 2), pl.ds(wide // 2, wide // 2)))
    deep = down_w.shape[-1]
    down_hops = plane_start(move, down_w, s, (pl.ds(0, deep // 2), pl.ds(deep // 2, deep // 2)))
    everything = pl.ds(0, qkv_ref.shape[0])
    for j in range(kvs):
        keys[j] = spun(head(qkv_ref, everything, heads + j), cos_ref[...], sin_ref[...]).astype(
            jnp.bfloat16
        )

    def block(step, carry):
        ahead_block(
            heads, kvs, step, qkv_ref, cos_ref, sin_ref, row_ref, col_ref, mixed_ref, keys
        )

        @pl.when(step == 1)
        def _():
            @pl.when(mine)
            def _():
                out_x.wait_recv()
                out_y[1].start()

        return carry

    lax.fori_loop(0, qkv_ref.shape[0] // QB, block, 0)
    seed_moves[1].wait_recv()
    seed_moves.append(move.send(seeds.at[2], seeds.at[3], "core"))
    rest = []
    for made, ref, size in (
        (gate_hops, gate_w, wide), (up_hops, up_w, wide), (down_hops, down_w, deep)
    ):
        parts = (pl.ds(0, size // 2), pl.ds(size // 2, size // 2))
        rest += plane_pass(move, made, ref, y, x, parts)

    @pl.when(mine)
    def _():
        out_x.wait_send()
        for made in out_y:
            made.wait_send()

    @pl.when(other)
    def _():
        for made in out_y:
            made.wait_recv()

    seed_own.wait()
    seed_moves[0].wait_recv()
    seed_moves[2].wait_recv()
    for made in rest:
        made.wait_recv()
    move.finish()


def behind_kernel(
    heads, kvs, qkv_ref, grad_ref, cos_ref, sin_ref, row_ref, col_ref, gq_ref, gkv_ref, keys, gks, gvs
):
    low, f32 = jnp.bfloat16, jnp.float32
    step = pl.program_id(0)
    everything = pl.ds(0, qkv_ref.shape[0])

    @pl.when(step == 0)
    def _():
        for j in range(kvs):
            keys[j] = spun(head(qkv_ref, everything, heads + j), cos_ref[...], sin_ref[...]).astype(low)
        gks[...] = jnp.zeros_like(gks)
        gvs[...] = jnp.zeros_like(gvs)

    start = pl.multiple_of(step * QB, QB)
    base = pl.multiple_of(jnp.maximum(start + QB - SPAN, 0), QB)
    here, span = pl.ds(start, QB), pl.ds(base, SPAN)
    key_place = base + lax.broadcasted_iota(jnp.int32, (SPAN, QB), 0)
    place = start + lax.broadcasted_iota(jnp.int32, (SPAN, QB), 1)
    allowed = (key_place <= place) & (col_ref[span, :] == row_ref[:, here])
    bias = jnp.where(allowed, 0.0, -1e30).astype(f32)
    width = 1.0 / math.sqrt(HD)
    scale = width * math.log2(math.e)
    cosine, sine = cos_ref[here, :], sin_ref[here, :]
    results = []
    for h in range(heads):
        j = h * kvs // heads
        query = spun(head(qkv_ref, here, h), cosine, sine).astype(low)
        key, value = keys[j, span, :], head(qkv_ref, span, heads + kvs + j)
        grad = head(grad_ref, here, h)
        scores = nt(key, query) * scale + bias
        peak = jnp.max(scores, axis=0, keepdims=True)
        weights = jnp.exp2(scores - peak)
        total = jnp.sum(weights, axis=0, keepdims=True)
        probs = weights * (1.0 / total)
        slope = nt(value, grad)
        centre = jnp.sum(probs * slope, axis=0, keepdims=True)
        gs = (probs * (slope - centre)).astype(low)
        gvs[j, span, :] += nn(probs.astype(low), grad)
        gks[j, span, :] += nn(gs, query)
        results.append(spun(tn(gs, key) * width, cosine, sine, True).astype(low))
    gq_ref[...] = jnp.concatenate(results, axis=1)

    @pl.when(step == pl.num_programs(0) - 1)
    def _():
        gk = [spun(gks[j] * width, cos_ref[...], sin_ref[...], True).astype(low) for j in range(kvs)]
        gv = [gvs[j].astype(low) for j in range(kvs)]
        gkv_ref[...] = jnp.concatenate(gk + gv, axis=1)


def whole(shape):
    return pl.BlockSpec(shape, lambda i: (0,) * len(shape))


def attend_ahead(heads, kvs, qkv, cosine, sine, row, col, seed, out_w, gate_w, up_w, down_w):
    length = qkv.shape[0]
    hbm = pl.BlockSpec(memory_space=pl.ANY)
    vmem = pl.BlockSpec(memory_space=pltpu.VMEM)
    weights = (out_w, gate_w, up_w, down_w)
    return pl.pallas_call(
        functools.partial(ahead_kernel, heads, kvs),
        in_specs=[vmem] * 5 + [hbm] * 5,
        out_specs=[vmem] + [hbm] * 5,
        out_shape=[jax.ShapeDtypeStruct((length, heads * HD), jnp.bfloat16)]
        + [jax.ShapeDtypeStruct(w.shape, w.dtype) for w in weights]
        + [jax.ShapeDtypeStruct((4,) + seed.shape, seed.dtype)],
        input_output_aliases={5: 1, 6: 2, 7: 3, 8: 4},
        scratch_shapes=[
            pltpu.VMEM((kvs, length, HD), jnp.bfloat16),
            pltpu.SemaphoreType.DMA((32,)),
            pltpu.SemaphoreType.DMA((32,)),
        ],
        compiler_params=pltpu.CompilerParams(
            collective_id=2, has_side_effects=True, vmem_limit_bytes=48 << 20
        ),
        cost_estimate=pl.CostEstimate(
            flops=4 * heads * length * SPAN * HD,
            bytes_accessed=6 << 20,
            transcendentals=heads * length * SPAN,
        ),
        name="ahead",
    )(qkv, cosine, sine, row, col, *weights, seed)


def attend_behind(heads, kvs, qkv, grad, cosine, sine, row, col):
    length = qkv.shape[0]
    return pl.pallas_call(
        functools.partial(behind_kernel, heads, kvs),
        grid=(length // QB,),
        in_specs=[whole(v.shape) for v in (qkv, grad, cosine, sine, row, col)],
        out_specs=[
            pl.BlockSpec((QB, heads * HD), lambda i: (i, 0)),
            pl.BlockSpec((length, 2 * kvs * HD), lambda i: (0, 0)),
        ],
        out_shape=[
            jax.ShapeDtypeStruct((length, heads * HD), jnp.bfloat16),
            jax.ShapeDtypeStruct((length, 2 * kvs * HD), jnp.bfloat16),
        ],
        scratch_shapes=[
            pltpu.VMEM((kvs, length, HD), jnp.bfloat16),
            pltpu.VMEM((kvs, length, HD), jnp.float32),
            pltpu.VMEM((kvs, length, HD), jnp.float32),
        ],
        compiler_params=pltpu.CompilerParams(vmem_limit_bytes=48 << 20),
        cost_estimate=pl.CostEstimate(flops=10 * heads * length * SPAN * HD, bytes_accessed=9 << 20, transcendentals=heads * length * SPAN),
    )(qkv, grad, cosine, sine, row, col)


def hop(value, *names):
    flip = sum(BITS[name] for name in names)
    return lax.ppermute(value, AXES, [(i, i ^ flip) for i in range(32)])


def after(value, *others):
    return lax.optimization_barrier((value,) + others)[0]


def in_order(mine, other, place, axis=0):
    first = jnp.where(place == 0, mine, other)
    second = jnp.where(place == 0, other, mine)
    return jnp.concatenate([first, second], axis=axis)


def pick(value, place, axis=0):
    return lax.dynamic_index_in_dim(value, place, axis, keepdims=False)


def plane_turn(tokens, x):
    got = []
    for flip in range(2):
        pairs = []
        for i in range(32):
            y_i, x_i, z_i, core_i = i // 16, i // 8 % 2, i // 2 % 4, i % 2
            pairs.append((i, core_i * 16 + (x_i ^ flip) * 8 + z_i * 2 + y_i))
        got.append(lax.ppermute(pick(tokens, x ^ flip), AXES, pairs)[None])
    return in_order(got[0], got[1], x)


def gather_line(block, zh, zl):
    got = [block[None]] + [hop(block, *names)[None] for names in (("zl",), ("zh",), ("zh", "zl"))]
    return in_order(in_order(got[0], got[1], zl), in_order(got[2], got[3], zl), zh)


def plane_out(line, x_first):
    return hop(line, "x" if x_first else "y")


def plane_pair(line, got, y, x, x_first):
    if x_first:
        return in_order(line[None], got[None], x)[None]
    return in_order(line[None], got[None], y)[:, None]


def plane_rest(pair, y, x, x_first):
    if x_first:
        done = in_order(pair, hop(pair, "y"), y)
    else:
        done = in_order(pair, hop(pair, "x"), x, axis=1)
    return done.reshape((4,) + done.shape[2:])


def gather_plane(line, y, x, x_first):
    pair = plane_pair(line, plane_out(line, x_first), y, x, x_first)
    return plane_rest(pair, y, x, x_first)


def plane_send(total, y, x, y_first):
    total = total.reshape((2, 2) + total.shape[1:])
    if y_first:
        return pick(total, y), hop(pick(total, 1 - y), "y")
    return pick(total, x, 1), hop(pick(total, 1 - x, 1), "x")


def plane_sum(kept, got, y, x, y_first):
    f32, low = jnp.float32, jnp.bfloat16
    half = kept.astype(f32) + got.astype(f32)
    if y_first:
        return pick(half, x) + hop(pick(half, 1 - x).astype(low), "x").astype(f32)
    return pick(half, y) + hop(pick(half, 1 - y).astype(low), "y").astype(f32)


def scatter_line(line, zh, zl):
    f32, low = jnp.float32, jnp.bfloat16
    place = zh * 2 + zl
    result = pick(line, place)
    for k, names in ((1, ("zl",)), (2, ("zh",)), (3, ("zh", "zl"))):
        result = result + hop(pick(line, place ^ k).astype(low), *names).astype(f32)
    return result


def scatter_pairs(line, zh):
    return pick(line, zh) + hop(pick(line, 1 - zh).astype(jnp.bfloat16), "zh").astype(jnp.float32)


def add_all(value):
    for name in ("core", "x", "y", "zl", "zh"):
        value = value + hop(value, name)
    return value


def fast_body(
    layer_input,
    cotangent,
    token_mask,
    document_ids,
    attn_gain,
    w_query,
    w_key,
    w_value,
    w_output,
    mlp_gain,
    w_gate,
    w_up,
    w_down,
):
    f32, low = jnp.float32, jnp.bfloat16
    y, x, zh, zl, core = (lax.axis_index(name) for name in AXES)
    device = sum(lax.axis_index(name) * BITS[name] for name in AXES)
    quarter, width = layer_input.shape[1:]
    half_len = 2 * quarter
    length = 2 * half_len
    rows = w_query.shape[0]
    units = w_gate.shape[1]
    heads, kvs = HEADS // 2, KV // 2
    cosine, sine = rope_tables(length, HD)

    def swap_in(mine, sent):
        return in_order(mine[None], hop(sent, "core")[None], core)

    def halves(weight):
        return weight.reshape(rows, 2, -1)

    def both(mine):
        return in_order(mine, hop(mine, "core"), core)

    def join(part):
        part = part.reshape(2, half_len, width)
        return pick(part, core) + hop(pick(part, 1 - core), "core")

    masked = cotangent * token_mask.astype(low)[:, :, None]
    qkv = jnp.concatenate([halves(w) for w in (w_query, w_key, w_value)], axis=2)
    qkv = jnp.moveaxis(qkv, 1, 0)
    gate_in, up_in = (
        jnp.transpose(w.reshape(rows, units // 512, 2, 2, 128), (2, 3, 0, 1, 4)).reshape(
            2, 2, rows, -1
        )
        for w in (w_gate, w_up)
    )
    gain = jnp.concatenate([attn_gain, mlp_gain]).astype(f32)
    gain = jnp.broadcast_to(jnp.pad(gain, (0, 128 - 2 * rows)), (8, 128))
    own, seed_low, qkv_w, gate_w, up_w, down_w, out_w, gains, docs = fetch_head(
        layer_input, masked, qkv, gate_in, up_in, w_down, w_output, gain, document_ids
    )
    own, seed_low = own.reshape(half_len, width), seed_low.reshape(half_len, width)
    gains = gains[..., 0, : 2 * rows].reshape(32, 2, rows)
    gains = jnp.moveaxis(gains, 1, 0).reshape(2, width)
    documents = pick(jnp.where(core == y, document_ids, docs), x)
    row, col = documents[None, :], documents[:, None]
    qkv_w = qkv_w.reshape(width, -1)

    inputs = own.astype(f32)
    inv_one = inverse_rms(inputs)
    unit_one = inputs * inv_one
    normed = both((unit_one * gains[0]).astype(low))
    pair = nn(normed, qkv_w).astype(low)
    mixed, out_w, gate_w, up_w, down_w, seeds = attend_ahead(
        heads, kvs, pair, cosine, sine, row, col, seed_low, out_w, gate_w, up_w, down_w
    )
    out_w, down_w = out_w.reshape(-1, width), down_w.reshape(-1, width)
    gate_w, up_w = gate_w.reshape(width, -1), up_w.reshape(width, -1)

    hidden = inputs + join(nn(mixed, out_w))
    inv_two = inverse_rms(hidden)
    unit_two = hidden * inv_two

    def spread(mine):
        far = hop(mine, "zl")
        return (
            jnp.concatenate([mine, hop(mine, "core")]),
            jnp.concatenate([far, hop(far, "core")]),
        )

    seeds = seeds.reshape(2, length, width)
    normed_two = spread((unit_two * gains[1]).astype(low))

    def ahead_and_back(tokens, seed):
        gate, upward, grad_act = nn(tokens, gate_w), nn(tokens, up_w), nt(seed, down_w)
        sigma = jax.nn.sigmoid(gate)
        activated = (gate * sigma * upward).astype(low)
        up_low = (grad_act * gate * sigma).astype(low)
        gate_low = (grad_act * upward * sigma * (1.0 + gate * (1.0 - sigma))).astype(low)
        back = nt(gate_low, gate_w) + nt(up_low, up_w)
        return activated, gate_low, up_low, nn(activated, down_w), back

    near = ahead_and_back(normed_two[0], seeds[0])
    far_tokens = after(normed_two[1], near[4])
    far = ahead_and_back(far_tokens, seeds[1])

    def fold(part):
        return part[:half_len] + hop(part[half_len:], "core")

    theirs = fold(far[4]).astype(low)
    back = hop(theirs, "zl")
    near_low, far_low = (
        tuple(after(v, theirs) for v in parts[:3]) for parts in (near, far)
    )
    grad_down = (tn(near_low[0], seeds[0]) + tn(far_low[0], seeds[1])).astype(low)
    grad_gate = (tn(normed_two[0], near_low[1]) + tn(far_tokens, far_low[1])).astype(low)
    grad_up = (tn(normed_two[0], near_low[2]) + tn(far_tokens, far_low[2])).astype(low)
    totals = [
        grad_gate.reshape(4, 2, 2, 2 * rows, -1),
        grad_up.reshape(4, 2, 2, 2 * rows, -1),
        grad_down[:, : width // 2].reshape(4, 2, -1, width // 2),
        grad_down[:, width // 2 :].reshape(4, 2, -1, width // 2),
    ]
    ways = [True, False, True, False]
    kepts = [plane_send(total, y, x, way) for total, way in zip(totals, ways)]

    grad_normed_two = fold(near[4]) + back.astype(f32)
    scaled_two = grad_normed_two * gains[1]
    grad_hidden = seed_low.astype(f32) + inv_two * (
        scaled_two - unit_two * jnp.mean(scaled_two * unit_two, axis=-1, keepdims=True)
    )
    grad_low = both(grad_hidden.astype(low))
    grad_heads = nt(grad_low, out_w).astype(low)
    grad_heads = after(grad_heads, *totals)

    ahead_low = after(fold(far[3]).astype(low), back)
    output = hidden + fold(near[3]) + hop(ahead_low, "zl").astype(f32)
    gain_two = jnp.sum(grad_normed_two * unit_two, axis=0)

    grad_query, grad_pair = attend_behind(
        heads, kvs, pair, grad_heads, cosine, sine, row, col
    )
    output = after(output.astype(low), grad_query)
    output = plane_turn(output.reshape(2, quarter, width), x)
    cols = heads * HD
    part = nt(grad_query, qkv_w[:, :cols]) + nt(grad_pair, qkv_w[:, cols:])
    grad_out_w = tn(mixed, grad_low).astype(low).reshape(8, 2, rows, width)
    got = hop(pick(grad_out_w, 1 - core, 1), "core")
    grad_out_w = in_order(pick(grad_out_w, core, 1), got, core).reshape(4, 4, rows, width)
    tails = [
        tn(normed, grad_query).astype(low).reshape(4, 4, 2 * rows, -1),
        tn(normed, grad_pair).astype(low).reshape(4, 4, 2 * rows, -1),
        grad_out_w[..., : width // 2],
        grad_out_w[..., width // 2 :],
    ]
    tail_ways = [True, False, True, False]
    tail_kepts = [plane_send(total, y, x, way) for total, way in zip(tails, tail_ways)]
    sums = [
        scatter_pairs(plane_sum(kept, after(got, part), y, x, way), zh)
        for (kept, got), way in zip(kepts, ways)
    ]
    grad_normed = join(part)
    scaled_one = grad_normed * gains[0]
    grad_input = grad_hidden + inv_one * (
        scaled_one - unit_one * jnp.mean(scaled_one * unit_one, axis=-1, keepdims=True)
    )
    grad_input = plane_turn(grad_input.astype(low).reshape(2, quarter, width), x)
    gain_one = add_all(jnp.stack([jnp.sum(grad_normed * unit_one, axis=0), gain_two]))
    tail_sums = [
        scatter_line(plane_sum(kept, got, y, x, way), zh, zl)
        for (kept, got), way in zip(tail_kepts, tail_ways)
    ]

    hidden_grads = []
    for total in sums[:2]:
        total = in_order(pick(total, zl)[None], hop(pick(total, 1 - zl), "zl")[None], zl)
        total = total.reshape(2, 2, rows, -1)
        total = swap_in(pick(total, core, 1), pick(total, 1 - core, 1))
        total = jnp.transpose(total.reshape(2, 2, rows, -1, 128), (2, 3, 1, 0, 4))
        hidden_grads.append(total.reshape(rows, units))
    grad_down = jnp.concatenate(sums[2:], axis=1)
    grad_output = jnp.concatenate(tail_sums[2:], axis=1)
    moved = []
    for total in tail_sums[:2]:
        total = total.reshape(2, rows, -1)
        moved.append(swap_in(pick(total, core), pick(total, 1 - core)))
    q_grad = jnp.moveaxis(moved[0], 0, 1).reshape(rows, -1)
    k_grad, v_grad = (
        jnp.moveaxis(part_, 0, 1).reshape(rows, -1)
        for part_ in (moved[1][:, :, : kvs * HD], moved[1][:, :, kvs * HD :])
    )
    gain_one = lax.dynamic_slice_in_dim(gain_one, device * rows, rows, 1)

    return (
        output,
        grad_input,
        gain_one[0],
        q_grad,
        k_grad,
        v_grad,
        grad_output,
        gain_one[1],
        hidden_grads[0],
        hidden_grads[1],
        grad_down,
    )


def solution(mesh):
    fast = dict(mesh.shape) == {"seq": 4, "batch": 8}
    if fast:
        grid = Mesh(mesh.devices.reshape((2,) * 5), AXES)
        seq, batch = ("y", "x"), ("zh", "zl", "core")
    else:
        grid, seq, batch = mesh, ("seq",), ("batch",)
    weight = P(seq + batch, None)
    gain = P(seq + batch)
    token = P(batch, seq, None)
    return jax.shard_map(
        fast_body if fast else body,
        mesh=grid,
        in_specs=(token, token, P(batch, seq), P(batch, None), gain)
        + (weight,) * 4
        + (gain,)
        + (weight,) * 3,
        out_specs=(token, token, gain) + (weight,) * 4 + (gain,) + (weight,) * 3,
        check_vma=False,
    )
```

```python
import functools
import math

import jax
import jax.numpy as jnp
from jax import lax
from jax.experimental import pallas as pl
from jax.experimental.pallas import tpu as pltpu
from jax.sharding import Mesh
from jax.sharding import PartitionSpec as P

HEADS = 16
KV = 8
HD = 96


EPSILON = 1e-05
ROPE_BASE = 10000.0


def inverse_rms(field):
    return lax.rsqrt(jnp.mean(field * field, axis=-1, keepdims=True) + EPSILON)


def half_turn(field):
    middle = field.shape[-1] // 2
    return jnp.concatenate([-field[..., middle:], field[..., :middle]], axis=-1)


def rope_tables(length, width):
    middle = width // 2
    freqs = ROPE_BASE ** (-2.0 * jnp.arange(middle, dtype=jnp.float32) / width)
    angles = jnp.arange(length, dtype=jnp.float32)[:, None] * freqs[None, :]
    cosine = jnp.concatenate([jnp.cos(angles), jnp.cos(angles)], axis=-1)
    sine = jnp.concatenate([jnp.sin(angles), jnp.sin(angles)], axis=-1)
    return (cosine, sine)


def rotate_ahead(field, cosine, sine):
    return field * cosine[:, None, :] + half_turn(field) * sine[:, None, :]


def rotate_behind(field, cosine, sine):
    return field * cosine[:, None, :] - half_turn(field) * sine[:, None, :]


def outer_sum(left, right):
    return lax.dot_general(
        left, right, (((0,), (0,)), ((), ())), preferred_element_type=jnp.float32
    )


def back_product(left, right):
    return lax.dot_general(
        left, right, (((1,), (1,)), ((), ())), preferred_element_type=jnp.float32
    )


def fetch_attention(attn_gain, w_query, w_key, w_value, w_output):
    return (
        lax.all_gather(attn_gain, ("seq", "batch"), axis=0, tiled=True),
        lax.all_gather(w_query, ("seq", "batch"), axis=0, tiled=True),
        lax.all_gather(w_key, ("seq", "batch"), axis=0, tiled=True),
        lax.all_gather(w_value, ("seq", "batch"), axis=0, tiled=True),
        lax.all_gather(w_output, ("seq", "batch"), axis=0, tiled=True),
    )


def fetch_feedforward(mlp_gain, w_gate, w_up, w_down):
    return (
        lax.all_gather(mlp_gain, ("seq", "batch"), axis=0, tiled=True),
        lax.all_gather(w_gate, ("seq", "batch"), axis=0, tiled=True),
        lax.all_gather(w_up, ("seq", "batch"), axis=0, tiled=True),
        lax.all_gather(w_down, ("seq", "batch"), axis=0, tiled=True),
    )


def block_scores(query_block, keys, documents, start, block, scale):
    length = keys.shape[0]
    scores = (
        jnp.einsum("qjhd,kjd->jhqk", query_block, keys, preferred_element_type=jnp.float32) * scale
    )
    key_pos = jnp.arange(length, dtype=jnp.int32)
    query_pos = start + jnp.arange(block, dtype=jnp.int32)
    query_docs = lax.dynamic_slice_in_dim(documents, start, block, 0)
    allowed = (key_pos[None, :] <= query_pos[:, None]) & (query_docs[:, None] == documents[None, :])
    return jnp.where(allowed[None, None], scores, -1e30)


def attention_forward(queries, keys, values, documents, block, scale):
    length = queries.shape[0]
    count = length // block

    def one_block(index):
        start = index * block
        query_block = lax.dynamic_slice_in_dim(queries, start, block, 0)
        scores = block_scores(query_block, keys, documents, start, block, scale)
        peak_score = jnp.max(scores, axis=-1, keepdims=True)
        weights = jnp.exp(scores - peak_score)
        totals = jnp.sum(weights, axis=-1, keepdims=True)
        probs = (weights / totals).astype(jnp.bfloat16)
        result = jnp.einsum("jhqk,kjd->qjhd", probs, values, preferred_element_type=jnp.float32)
        return (
            result.astype(jnp.bfloat16).reshape(block, -1),
            (peak_score + jnp.log(totals))[..., 0],
        )

    results, sums = lax.map(one_block, jnp.arange(count, dtype=jnp.int32))
    return (results.reshape(length, -1), sums)


def attention_backward(queries, keys, values, documents, sums, grad_out, block, scale):
    length = queries.shape[0]
    count = length // block

    def one_block(carry, member):
        grad_keys, grad_values = carry
        index, sums_block = member
        start = index * block
        query_block = lax.dynamic_slice_in_dim(queries, start, block, 0)
        grad_block = lax.dynamic_slice_in_dim(grad_out, start, block, 0)
        scores = block_scores(query_block, keys, documents, start, block, scale)
        probs = jnp.exp(scores - sums_block[..., None])
        grad_probs = jnp.einsum(
            "qjhd,kjd->jhqk", grad_block, values, preferred_element_type=jnp.float32
        )
        centre = jnp.sum(probs * grad_probs, axis=-1, keepdims=True)
        grad_scores = (probs * (grad_probs - centre)).astype(jnp.bfloat16)
        grad_query = (
            jnp.einsum("jhqk,kjd->qjhd", grad_scores, keys, preferred_element_type=jnp.float32)
            * scale
        )
        grad_keys = (
            grad_keys
            + jnp.einsum(
                "jhqk,qjhd->kjd", grad_scores, query_block, preferred_element_type=jnp.float32
            )
            * scale
        )
        grad_values = grad_values + jnp.einsum(
            "jhqk,qjhd->kjd",
            probs.astype(jnp.bfloat16),
            grad_block,
            preferred_element_type=jnp.float32,
        )
        return ((grad_keys, grad_values), grad_query)

    empty = jnp.zeros(keys.shape, jnp.float32)
    (grad_keys, grad_values), grad_query = lax.scan(
        one_block, (empty, empty), (jnp.arange(count, dtype=jnp.int32), sums)
    )
    return (
        grad_query.reshape(length, queries.shape[1] * queries.shape[2], queries.shape[3]),
        grad_keys,
        grad_values,
    )


def body(
    layer_input,
    cotangent,
    token_mask,
    document_ids,
    attn_gain,
    w_query,
    w_key,
    w_value,
    w_output,
    mlp_gain,
    w_gate,
    w_up,
    w_down,
):
    parts = lax.axis_size("seq")
    micro_count = layer_input.shape[0]
    shard = layer_input.shape[1]
    length = shard * parts
    heads_here = HEADS // parts
    kv_here = max(1, KV // parts)
    copies = parts * kv_here // KV
    per_kv = heads_here // kv_here
    block = min(512, length)
    scale = 1.0 / math.sqrt(HD)
    cosine, sine = rope_tables(length, HD)
    attn_set = None
    mlp_set = None
    attn_total = None
    mlp_total = None
    outputs = []
    input_grads = []
    kept = {
        "normed": [],
        "normed_two": [],
        "activated": [],
        "seed_low": [],
        "gate_low": [],
        "up_low": [],
        "grad_low": [],
        "mixed": [],
        "query_back": [],
        "key_back": [],
        "value_back": [],
    }
    gain_one_total = None
    gain_two_total = None
    for micro in range(micro_count):
        attn_set = fetch_attention(attn_gain, w_query, w_key, w_value, w_output)
        mlp_set = fetch_feedforward(mlp_gain, w_gate, w_up, w_down)
        gain_one = attn_set[0].astype(jnp.float32)
        gain_two = mlp_set[0].astype(jnp.float32)
        documents = document_ids[micro]
        inputs = layer_input[micro].astype(jnp.float32)
        inv_one = inverse_rms(inputs)
        unit_one = inputs * inv_one
        normed = (unit_one * gain_one).astype(jnp.bfloat16)
        queries = jnp.dot(normed, attn_set[1], preferred_element_type=jnp.float32).astype(
            jnp.bfloat16
        )
        keys_lin = jnp.dot(normed, attn_set[2], preferred_element_type=jnp.float32).astype(
            jnp.bfloat16
        )
        values_lin = jnp.dot(normed, attn_set[3], preferred_element_type=jnp.float32).astype(
            jnp.bfloat16
        )
        queries = queries.reshape(shard, parts, heads_here * HD)
        key_slots = jnp.repeat(keys_lin.reshape(shard, KV, HD), copies, axis=1).reshape(
            shard, parts, kv_here * HD
        )
        value_slots = jnp.repeat(values_lin.reshape(shard, KV, HD), copies, axis=1).reshape(
            shard, parts, kv_here * HD
        )
        pairs = jnp.concatenate([key_slots, value_slots], axis=-1)
        query_heads, pair_heads = (
            lax.all_to_all(queries, "seq", split_axis=1, concat_axis=0, tiled=True),
            lax.all_to_all(pairs, "seq", split_axis=1, concat_axis=0, tiled=True),
        )
        query_rot = rotate_ahead(
            query_heads.reshape(length, heads_here, HD).astype(jnp.float32), cosine, sine
        )
        query_rot = query_rot.astype(jnp.bfloat16).reshape(length, kv_here, per_kv, HD)
        key_heads = pair_heads[:, 0, : kv_here * HD].reshape(length, kv_here, HD)
        key_rot = rotate_ahead(key_heads.astype(jnp.float32), cosine, sine).astype(jnp.bfloat16)
        value_heads = pair_heads[:, 0, kv_here * HD :].reshape(length, kv_here, HD)
        attended, sums = attention_forward(query_rot, key_rot, value_heads, documents, block, scale)
        mixed = lax.all_to_all(
            attended.reshape(length, 1, heads_here * HD),
            "seq",
            split_axis=0,
            concat_axis=1,
            tiled=True,
        )
        mixed = mixed.reshape(shard, HEADS * HD)
        hidden_state = inputs + jnp.dot(mixed, attn_set[4], preferred_element_type=jnp.float32)
        inv_two = inverse_rms(hidden_state)
        unit_two = hidden_state * inv_two
        normed_two = (unit_two * gain_two).astype(jnp.bfloat16)
        gate = jnp.dot(normed_two, mlp_set[1], preferred_element_type=jnp.float32)
        upward = jnp.dot(normed_two, mlp_set[2], preferred_element_type=jnp.float32)
        sigma = jax.nn.sigmoid(gate)
        activated = (gate * sigma * upward).astype(jnp.bfloat16)
        output = hidden_state + jnp.dot(activated, mlp_set[3], preferred_element_type=jnp.float32)
        outputs.append(output.astype(jnp.bfloat16))
        seed = cotangent[micro].astype(jnp.float32) * token_mask[micro].astype(jnp.float32)[:, None]
        seed_low = seed.astype(jnp.bfloat16)
        grad_act = back_product(seed_low, mlp_set[3])
        grad_up_low = (grad_act * gate * sigma).astype(jnp.bfloat16)
        grad_gate_low = (grad_act * upward * sigma * (1.0 + gate * (1.0 - sigma))).astype(
            jnp.bfloat16
        )
        grad_normed_two = back_product(grad_gate_low, mlp_set[1]) + back_product(
            grad_up_low, mlp_set[2]
        )
        grad_gain_two = jnp.sum(grad_normed_two * unit_two, axis=0)
        scaled_two = grad_normed_two * gain_two
        grad_hidden = seed + inv_two * (
            scaled_two - unit_two * jnp.mean(scaled_two * unit_two, axis=-1, keepdims=True)
        )
        gain_two_total = grad_gain_two if gain_two_total is None else gain_two_total + grad_gain_two
        kept["normed_two"].append(normed_two)
        kept["activated"].append(activated)
        kept["seed_low"].append(seed_low)
        kept["gate_low"].append(grad_gate_low)
        kept["up_low"].append(grad_up_low)
        grad_low = grad_hidden.astype(jnp.bfloat16)
        grad_mixed = (
            back_product(grad_low, attn_set[4])
            .astype(jnp.bfloat16)
            .reshape(shard, parts, heads_here * HD)
        )
        grad_heads = lax.all_to_all(
            grad_mixed, "seq", split_axis=1, concat_axis=0, tiled=True
        ).reshape(length, kv_here, per_kv, HD)
        grad_query_rot, grad_key_rot, grad_values = attention_backward(
            query_rot, key_rot, value_heads, documents, sums, grad_heads, block, scale
        )
        grad_query_heads = (
            rotate_behind(grad_query_rot, cosine, sine)
            .astype(jnp.bfloat16)
            .reshape(length, 1, heads_here * HD)
        )
        grad_key_heads = rotate_behind(grad_key_rot, cosine, sine)
        grad_pairs = jnp.concatenate(
            [
                grad_key_heads.reshape(length, kv_here * HD),
                grad_values.reshape(length, kv_here * HD),
            ],
            axis=-1,
        )
        query_back = lax.all_to_all(
            grad_query_heads, "seq", split_axis=0, concat_axis=1, tiled=True
        ).reshape(shard, HEADS * HD)
        pair_back = lax.all_to_all(
            grad_pairs.reshape(length, 1, 2 * kv_here * HD).astype(jnp.bfloat16),
            "seq",
            split_axis=0,
            concat_axis=1,
            tiled=True,
        ).astype(jnp.float32)
        key_back = pair_back[:, :, : kv_here * HD].reshape(shard, KV, copies, HD).sum(axis=2)
        value_back = pair_back[:, :, kv_here * HD :].reshape(shard, KV, copies, HD).sum(axis=2)
        key_back = key_back.reshape(shard, KV * HD).astype(jnp.bfloat16)
        value_back = value_back.reshape(shard, KV * HD).astype(jnp.bfloat16)
        grad_normed = (
            back_product(query_back, attn_set[1])
            + back_product(key_back, attn_set[2])
            + back_product(value_back, attn_set[3])
        )
        grad_gain_one = jnp.sum(grad_normed * unit_one, axis=0)
        scaled_one = grad_normed * gain_one
        grad_input = grad_hidden + inv_one * (
            scaled_one - unit_one * jnp.mean(scaled_one * unit_one, axis=-1, keepdims=True)
        )
        input_grads.append(grad_input.astype(jnp.bfloat16))
        gain_one_total = grad_gain_one if gain_one_total is None else gain_one_total + grad_gain_one
        kept["normed"].append(normed)
        kept["mixed"].append(mixed)
        kept["grad_low"].append(grad_low)
        kept["query_back"].append(query_back)
        kept["key_back"].append(key_back)
        kept["value_back"].append(value_back)
    rows = {name: jnp.concatenate(values, axis=0) for name, values in kept.items()}
    attn_total = (
        lax.psum_scatter(gain_one_total, ("seq", "batch"), scatter_dimension=0, tiled=True),
        lax.psum_scatter(
            outer_sum(rows["normed"], rows["query_back"]),
            ("seq", "batch"),
            scatter_dimension=0,
            tiled=True,
        ),
        lax.psum_scatter(
            outer_sum(rows["normed"], rows["key_back"]),
            ("seq", "batch"),
            scatter_dimension=0,
            tiled=True,
        ),
        lax.psum_scatter(
            outer_sum(rows["normed"], rows["value_back"]),
            ("seq", "batch"),
            scatter_dimension=0,
            tiled=True,
        ),
        lax.psum_scatter(
            outer_sum(rows["mixed"], rows["grad_low"]),
            ("seq", "batch"),
            scatter_dimension=0,
            tiled=True,
        ),
    )
    mlp_total = (
        lax.psum_scatter(gain_two_total, ("seq", "batch"), scatter_dimension=0, tiled=True),
        lax.psum_scatter(
            outer_sum(rows["normed_two"], rows["gate_low"]),
            ("seq", "batch"),
            scatter_dimension=0,
            tiled=True,
        ),
        lax.psum_scatter(
            outer_sum(rows["normed_two"], rows["up_low"]),
            ("seq", "batch"),
            scatter_dimension=0,
            tiled=True,
        ),
        lax.psum_scatter(
            outer_sum(rows["activated"], rows["seed_low"]),
            ("seq", "batch"),
            scatter_dimension=0,
            tiled=True,
        ),
    )
    return (
        jnp.stack(outputs, axis=0),
        jnp.stack(input_grads, axis=0),
        attn_total[0],
        attn_total[1],
        attn_total[2],
        attn_total[3],
        attn_total[4],
        mlp_total[0],
        mlp_total[1],
        mlp_total[2],
        mlp_total[3],
    )


AXES = ("y", "x", "zh", "zl", "core")
BITS = {"y": 16, "x": 8, "zh": 4, "zl": 2, "core": 1}
MESH = pl.DeviceIdType.MESH


def coordinates():
    return tuple(lax.axis_index(name) for name in AXES)


def peer(me, *names):
    return tuple(1 - at if name in names else at for name, at in zip(AXES, me))


def greet(me, groups):
    barrier = pltpu.get_barrier_semaphore()
    for names in groups:
        pl.semaphore_signal(barrier, 1, device_id=peer(me, *names), device_id_type=MESH)
    pl.semaphore_wait(barrier, len(groups))


class Mover:
    def __init__(self, me, sends, recvs):
        self.me, self.sends, self.recvs, self.used = me, sends, recvs, 0
        self.started = []

    def next(self):
        number = self.used
        self.used += 1
        assert number < self.sends.shape[0]
        return number

    def copy(self, src, dst, *names, device=None):
        number = self.next()
        return pltpu.make_async_remote_copy(
            src_ref=src,
            dst_ref=dst,
            send_sem=self.sends.at[number],
            recv_sem=self.recvs.at[number],
            device_id=peer(self.me, *names) if device is None else device,
            device_id_type=MESH,
        )

    def later(self, src, dst, *names):
        made = self.copy(src, dst, *names)
        self.started.append(made)
        return made

    def send(self, src, dst, *names):
        made = self.later(src, dst, *names)
        made.start()
        return made

    def local(self, src, dst):
        made = self.quiet(src, dst)
        made.start()
        return made

    def quiet(self, src, dst):
        number = self.next()
        return pltpu.make_async_copy(src, dst, self.recvs.at[number])

    def finish(self):
        for made in self.started:
            made.wait_send()


HEAD_GROUPS = (
    ("core",),
    ("zl",),
    ("zh",),
    ("zh", "zl"),
    ("zl", "core"),
    ("x",),
    ("y",),
    ("y", "core"),
    ("y", "core", "x"),
)
LINE = (("zl",), ("zh",), ("zh", "zl"))


def turn_start(move, me, src, dst):
    y, x, zh, zl, core = me
    stays = y == core
    made = []
    for flip in (1, 0):
        place = x if flip == 0 else 1 - x
        from_, to = src.at[place], dst.at[x]
        copy = move.copy(from_, to, device=(core, place, zh, zl, y))
        if flip == 0:
            own = move.quiet(from_, to)
            pl.when(stays)(own.start)
            pl.when(jnp.logical_not(stays))(copy.start)
            made.append((copy, own))
        else:
            copy.start()
            made.append((copy, None))
    return made


def turn_end(me, made):
    stays = me[0] == me[4]
    for copy, own in made:
        if own is None:
            copy.wait()
        else:
            pl.when(stays)(own.wait)
            pl.when(jnp.logical_not(stays))(copy.wait)


def plane_make(move, ref, s, parts):
    made = []
    for part in parts:
        piece = ref.at[s, ..., part]
        made += [move.later(piece, piece, "x"), move.later(piece, piece, "y")]
    return made


def plane_start(move, ref, s, parts):
    made = plane_make(move, ref, s, parts)
    for one in made:
        one.start()
    return made


def plane_pass(move, made, ref, y, x, parts):
    made[0].wait_recv()
    first = ref.at[2 * y + 1 - x, ..., parts[0]]
    rest = [move.send(first, first, "y")]
    made[3].wait_recv()
    second = ref.at[2 * (1 - y) + x, ..., parts[1]]
    rest.append(move.send(second, second, "x"))
    made[1].wait_recv()
    made[2].wait_recv()
    return rest


def by_rows(count, chunk, work):
    def step(i, carry):
        work(pl.ds(pl.multiple_of(i * chunk, chunk), chunk))
        return carry

    lax.fori_loop(0, count // chunk, step, 0)


class PlaneSum:
    def __init__(self, move, total, held, y, x):
        self.move, self.total = move, total
        self.own, self.mid, self.far, self.near, self.last = (held.at[i] for i in range(5))
        half = total.shape[-1] // 2
        self.left, self.right = pl.ds(0, half), pl.ds(half, half)
        self.at = (2 * y + x, 2 * y + 1 - x, 2 * (1 - y) + x, 2 * (1 - y) + 1 - x)

    def start(self):
        move, total, left, right = self.move, self.total, self.left, self.right
        s, sx, sy, sd = self.at
        self.far_moves = [
            move.send(total.at[sd, :, left], self.far.at[:, left], "y"),
            move.send(total.at[sd, :, right], self.far.at[:, right], "x"),
        ]
        self.loads = [
            move.local(total.at[s], self.own),
            move.local(total.at[sx, :, left], self.mid.at[:, left]),
            move.local(total.at[sy, :, right], self.mid.at[:, right]),
        ]
        self.near_moves = [
            move.copy(total.at[sy, :, left], self.near.at[:, left], "y"),
            move.copy(total.at[sx, :, right], self.near.at[:, right], "x"),
        ]
        self.last_moves = [
            move.copy(self.mid.at[:, left], self.last.at[:, left], "x"),
            move.copy(self.mid.at[:, right], self.last.at[:, right], "y"),
        ]

    def start_near(self):
        for made in self.near_moves:
            made.start()

    def pass_on(self):
        for made in self.loads[1:]:
            made.wait()
        for made in self.far_moves:
            made.wait_recv()
        rows = self.mid.shape[0]
        mid, far = self.mid, self.far

        def work(at):
            added = mid[at, :].astype(jnp.float32) + far[at, :].astype(jnp.float32)
            mid[at, :] = added.astype(jnp.bfloat16)

        by_rows(rows, 16, work)
        for made in self.last_moves:
            made.start()

    def end(self, write):
        self.loads[0].wait()
        for made in self.near_moves + self.last_moves:
            made.wait()
        own, near, last = self.own, self.near, self.last

        def work(at):
            value = own[at, :].astype(jnp.float32) + near[at, :].astype(jnp.float32)
            write(at, value + last[at, :].astype(jnp.float32))

        by_rows(own.shape[0], 16, work)


def tail_kernel(
    gate_in,
    up_in,
    down_in,
    qkv_in,
    out_in,
    y_in,
    x_in,
    gain_in,
    gate_out,
    up_out,
    down_out,
    qkv_out,
    out_out,
    y_out,
    x_out,
    gain_out,
    pair_low,
    pair_got,
    down_low,
    down_got,
    quarter,
    qkv_held,
    qkv_sum,
    qkv_low,
    qkv_got,
    out_got,
    out_low,
    out_x,
    out_line,
    out_line_got,
    rows_sent,
    gain_got,
    sends,
    recvs,
):
    f32, low = jnp.float32, jnp.bfloat16
    me = coordinates()
    y, x, zh, zl, core = me
    z = 2 * zh + zl
    mine = y == core
    other = jnp.logical_not(mine)
    greet(me, HEAD_GROUPS)
    move = Mover(me, sends, recvs)
    qkv = PlaneSum(move, qkv_in, qkv_held, y, x)
    qkv.start()
    out_y = move.copy(out_in, out_got, "y")
    pl.when(other)(out_y.start)
    qkv.start_near()

    pair_rows = pair_got.shape[1]

    def lower(src, dst, skip, count):
        def work(at):
            dst[at, :] = src[skip, at, :].astype(low)

        by_rows(count, 32, work)

    pairs = []
    for i, src in enumerate((gate_in, up_in)):
        lower(src, pair_low.at[i], 1 - zh, pair_rows)
        pairs.append(move.send(pair_low.at[i], pair_got.at[i], "zh"))
    lower(down_in, down_low, 1 - zh, down_low.shape[0])
    pairs.append(move.send(down_low, down_got, "zh"))

    gain_out[...] = gain_in[...]
    for turn, name in enumerate(("core", "x", "y", "zl", "zh")):
        made = move.copy(gain_out, gain_got.at[turn], name)
        made.start()
        made.wait()
        gain_out[...] = gain_out[...] + gain_got[turn]

    qkv.pass_on()
    out_shape = out_in.shape
    blocks = [(a, b) for a in range(out_shape[1]) for b in range(out_shape[2])]

    out_x_move = move.copy(out_low.at[1 - x], out_x, "x")

    @pl.when(mine)
    def _():
        out_y.wait_recv()

        def half(at_x):
            def work(i, carry):
                a, b = i // out_shape[2], i % out_shape[2]
                value = out_in[at_x, a, b].astype(f32) + out_got[at_x, a, b].astype(f32)
                out_low[at_x, a, b] = value.astype(low)
                return carry

            lax.fori_loop(0, len(blocks), work, 0)

        half(1 - x)
        out_x_move.start()
        half(x)

    y_turn = turn_start(move, me, y_in, y_out)
    x_turn = turn_start(move, me, x_in, x_out)

    spread = []
    for i, (src, dst) in enumerate(((gate_in, gate_out), (up_in, up_out))):
        pairs[i].wait_recv()
        got, full = pair_got.at[i], quarter.at[i]

        def work(at, src=src, got=got, full=full):
            full[at, :] = src[zh, at, :] + got[at, :].astype(f32)

        by_rows(pair_rows, 32, work)
        count = pair_rows // 4
        for names in (("core",), ("zl",), ("zl", "core")):
            to_zl = 1 - zl if "zl" in names else zl
            to_core = 1 - core if "core" in names else core
            start = pl.multiple_of((2 * to_zl + to_core) * count, count)
            spread.append(move.send(full.at[pl.ds(start, count)], dst.at[zl, core], *names))
        start = pl.multiple_of((2 * zl + core) * count, count)
        dst[zl, core] = full[pl.ds(start, count), :]
    pairs[2].wait_recv()

    def work(at):
        down_out[at, :] = down_in[zh, at, :] + down_got[at, :].astype(f32)

    by_rows(down_out.shape[0], 32, work)

    def keep(at, value):
        qkv_sum[at, :] = value
        qkv_low[at, :] = value.astype(low)

    qkv.end(keep)
    count = qkv_got.shape[1]
    line = []
    for k, names in enumerate(LINE):
        to = z ^ (1, 2, 3)[k]
        start = pl.multiple_of(to * count, count)
        line.append(move.send(qkv_low.at[pl.ds(start, count)], qkv_got.at[k], *names))

    out_moves = []
    for k, names in enumerate(LINE):
        to = z ^ (1, 2, 3)[k]
        out_moves.append(move.copy(out_line.at[to], out_line_got.at[k], *names))

    @pl.when(mine)
    def _():
        out_x_move.wait()

        def work(i, carry):
            a, b = i // out_shape[2], i % out_shape[2]
            value = out_low[x, a, b].astype(f32) + out_x[a, b].astype(f32)
            out_line[a, b] = value.astype(low)
            return carry

        lax.fori_loop(0, len(blocks), work, 0)
        for made in out_moves:
            made.start()

    for made in line:
        made.wait_recv()
    start = pl.multiple_of(z * count, count)
    total = qkv_sum[pl.ds(start, count), :]
    for k in range(3):
        total = total + qkv_got[k].astype(f32)
    rows = count // 2
    qkv_sum[pl.ds(0, count), :] = total
    theirs = pl.multiple_of((1 - core) * rows, rows)
    swap = move.send(qkv_sum.at[pl.ds(theirs, rows)], qkv_out.at[core], "core")
    qkv_out[core] = qkv_sum[pl.ds(pl.multiple_of(core * rows, rows), rows), :]

    out_swap = move.copy(rows_sent, out_out, "core")

    @pl.when(mine)
    def _():
        for made in out_moves:
            made.wait()
        for at in range(2):
            total = out_line[z, at].astype(f32)
            for k in range(3):
                total = total + out_line_got[k, at].astype(f32)

            @pl.when(core == at)
            def _(total=total):
                out_out[...] = total

            @pl.when(core != at)
            def _(total=total):
                rows_sent[...] = total

        out_swap.start()
        out_swap.wait_send()

    @pl.when(other)
    def _():
        out_y.wait_send()
        out_swap.wait_recv()

    turn_end(me, y_turn)
    turn_end(me, x_turn)
    swap.wait_recv()
    for made in spread:
        made.wait_recv()
    move.finish()


def sum_tail(gate, up, down, qkv, out, y_in, x_in, gain):
    f32, low = jnp.float32, jnp.bfloat16
    hbm = pl.BlockSpec(memory_space=pl.ANY)
    vmem = pl.BlockSpec(memory_space=pltpu.VMEM)
    wide, width = gate.shape[-1], qkv.shape[-1]
    rows = qkv.shape[1] // 8
    pair_rows, down_rows = gate.shape[1], down.shape[1]
    return pl.pallas_call(
        tail_kernel,
        in_specs=[vmem, vmem, vmem, hbm, vmem, hbm, hbm, vmem],
        out_specs=[vmem] * 5 + [hbm, hbm, vmem],
        out_shape=[
            jax.ShapeDtypeStruct((2, 2, rows, wide), f32),
            jax.ShapeDtypeStruct((2, 2, rows, wide), f32),
            jax.ShapeDtypeStruct((down_rows, width), f32),
            jax.ShapeDtypeStruct((2, rows, width), f32),
            jax.ShapeDtypeStruct((rows, width), f32),
            jax.ShapeDtypeStruct(y_in.shape, low),
            jax.ShapeDtypeStruct(x_in.shape, low),
            jax.ShapeDtypeStruct(gain.shape, f32),
        ],
        scratch_shapes=[
            pltpu.VMEM((2, pair_rows, wide), low),
            pltpu.VMEM((2, pair_rows, wide), low),
            pltpu.VMEM((down_rows, width), low),
            pltpu.VMEM((down_rows, width), low),
            pltpu.VMEM((2, pair_rows, wide), f32),
            pltpu.VMEM((5,) + qkv.shape[1:], low),
            pltpu.VMEM(qkv.shape[1:], f32),
            pltpu.VMEM(qkv.shape[1:], low),
            pltpu.VMEM((3, 2 * rows, width), low),
            pltpu.VMEM(out.shape, low),
            pltpu.VMEM(out.shape, low),
            pltpu.VMEM(out.shape[1:], low),
            pltpu.VMEM(out.shape[1:], low),
            pltpu.VMEM((3,) + out.shape[2:], low),
            pltpu.VMEM((rows, width), f32),
            pltpu.VMEM((5,) + gain.shape, f32),
            pltpu.SemaphoreType.DMA((48,)),
            pltpu.SemaphoreType.DMA((48,)),
        ],
        compiler_params=pltpu.CompilerParams(
            collective_id=4, has_side_effects=True, vmem_limit_bytes=56 << 20
        ),
        name="tail",
    )(gate, up, down, qkv, out, y_in, x_in, gain)


QB = 256
SPAN = 768


def turned(field, back):
    middle = HD // 2
    left, right = field[:, :middle], field[:, middle:]
    if back:
        return jnp.concatenate([right, -left], axis=1)
    return jnp.concatenate([-right, left], axis=1)


def spun(field, cosine, sine, back=False):
    field = field.astype(jnp.float32)
    return field * cosine + turned(field, back) * sine


def nt(left, right):
    return lax.dot_general(left, right, (((1,), (1,)), ((), ())), preferred_element_type=jnp.float32)


def nn(left, right):
    return jnp.dot(left, right, preferred_element_type=jnp.float32)


def tn(left, right):
    return lax.dot_general(left, right, (((0,), (0,)), ((), ())), preferred_element_type=jnp.float32)


def head(ref, rows, number):
    return ref[rows, HD * number : HD * (number + 1)]


def ahead_block(
    heads, kvs, step, size, qkv_ref, cos_ref, sin_ref, row_ref, col_ref, out_ref, keys
):
    low, f32 = jnp.bfloat16, jnp.float32
    start, base = step * QB, (step + 1) * QB - size
    if not isinstance(step, int):
        start, base = pl.multiple_of(start, QB), pl.multiple_of(base, QB)
    here, span = pl.ds(start, QB), pl.ds(base, size)
    key_place = base + lax.broadcasted_iota(jnp.int32, (size, QB), 0)
    place = start + lax.broadcasted_iota(jnp.int32, (size, QB), 1)
    allowed = (key_place <= place) & (col_ref[span, :] == row_ref[:, here])
    bias = jnp.where(allowed, 0.0, -1e30).astype(f32)
    scale = (1.0 / math.sqrt(HD)) * math.log2(math.e)
    cosine, sine = cos_ref[here, :], sin_ref[here, :]
    results = []
    for h in range(heads):
        j = h * kvs // heads
        query = spun(head(qkv_ref, here, h), cosine, sine).astype(low)
        scores = nt(keys[j, span, :], query) * scale + bias
        peak = jnp.max(scores, axis=0, keepdims=True)
        weights = jnp.exp2(scores - peak)
        total = jnp.sum(weights, axis=0, keepdims=True)
        probs = (weights * (1.0 / total)).astype(low)
        results.append(tn(probs, head(qkv_ref, span, heads + kvs + j)).astype(low))
    out_ref[here, :] = jnp.concatenate(results, axis=1)


def behind_block(
    heads,
    kvs,
    step,
    size,
    qkv_ref,
    grad_ref,
    cos_ref,
    sin_ref,
    row_ref,
    col_ref,
    gq_ref,
    keys,
    gks,
    gvs,
):
    low, f32 = jnp.bfloat16, jnp.float32
    start, base = step * QB, (step + 1) * QB - size
    if not isinstance(step, int):
        start, base = pl.multiple_of(start, QB), pl.multiple_of(base, QB)
    here, span = pl.ds(start, QB), pl.ds(base, size)
    key_place = base + lax.broadcasted_iota(jnp.int32, (size, QB), 0)
    place = start + lax.broadcasted_iota(jnp.int32, (size, QB), 1)
    allowed = (key_place <= place) & (col_ref[span, :] == row_ref[:, here])
    bias = jnp.where(allowed, 0.0, -1e30).astype(f32)
    width = 1.0 / math.sqrt(HD)
    scale = width * math.log2(math.e)
    cosine, sine = cos_ref[here, :], sin_ref[here, :]
    results = []
    for h in range(heads):
        j = h * kvs // heads
        query = spun(head(qkv_ref, here, h), cosine, sine).astype(low)
        key, value = keys[j, span, :], head(qkv_ref, span, heads + kvs + j)
        grad = head(grad_ref, here, h)
        scores = nt(key, query) * scale + bias
        peak = jnp.max(scores, axis=0, keepdims=True)
        weights = jnp.exp2(scores - peak)
        total = jnp.sum(weights, axis=0, keepdims=True)
        probs = weights * (1.0 / total)
        slope = nt(value, grad)
        centre = jnp.sum(probs * slope, axis=0, keepdims=True)
        gs = (probs * (slope - centre)).astype(low)
        gvs[j, span, :] += nn(probs.astype(low), grad)
        gks[j, span, :] += nn(gs, query)
        results.append(spun(tn(gs, key) * width, cosine, sine, True).astype(low))
    gq_ref[here, :] = jnp.concatenate(results, axis=1)


def behind_kernel(
    heads,
    kvs,
    qkv_ref,
    grad_ref,
    cos_ref,
    sin_ref,
    row_ref,
    col_ref,
    gate_in,
    up_in,
    down_in,
    gq_ref,
    gkv_ref,
    gate_out,
    up_out,
    down_out,
    keys,
    gks,
    gvs,
    gate_held,
    up_held,
    down_held,
    sends,
    recvs,
):
    low = jnp.bfloat16
    me = coordinates()
    y, x = me[0], me[1]
    greet(me, (("x",), ("y",)))
    move = Mover(me, sends, recvs)
    sums = [
        PlaneSum(move, total, held, y, x)
        for total, held in ((gate_in, gate_held), (up_in, up_held), (down_in, down_held))
    ]
    for plane in sums:
        plane.start()
    everything = pl.ds(0, qkv_ref.shape[0])
    for j in range(kvs):
        keys[j] = spun(head(qkv_ref, everything, heads + j), cos_ref[...], sin_ref[...]).astype(low)
    gks[...] = jnp.zeros_like(gks)
    gvs[...] = jnp.zeros_like(gvs)

    def block(step, carry):
        @pl.when(step == 2)
        def _():
            for plane in sums:
                plane.start_near()

        @pl.when(step == 3)
        def _():
            for plane in sums:
                plane.pass_on()

        work(step, SPAN)
        return carry

    def work(step, size):
        behind_block(
            heads, kvs, step, size, qkv_ref, grad_ref, cos_ref, sin_ref, row_ref, col_ref, gq_ref,
            keys, gks, gvs,
        )

    for step in range(SPAN // QB - 1):
        work(step, (step + 1) * QB)
    lax.fori_loop(SPAN // QB - 1, qkv_ref.shape[0] // QB, block, 0)
    width = 1.0 / math.sqrt(HD)
    gk = [
        spun(gks[j] * width, cos_ref[...], sin_ref[...], True).astype(low) for j in range(kvs)
    ]
    gv = [gvs[j].astype(low) for j in range(kvs)]
    gkv_ref[...] = jnp.concatenate(gk + gv, axis=1)
    for plane, out in zip(sums, (gate_out, up_out, down_out)):

        def write(at, value, out=out):
            out[at, :] = value

        plane.end(write)
    move.finish()


def attend_behind(heads, kvs, qkv, grad, cosine, sine, row, col, gate, up, down):
    low, f32 = jnp.bfloat16, jnp.float32
    length = qkv.shape[0]
    hbm = pl.BlockSpec(memory_space=pl.ANY)
    vmem = pl.BlockSpec(memory_space=pltpu.VMEM)
    totals = (gate, up, down)
    return pl.pallas_call(
        functools.partial(behind_kernel, heads, kvs),
        in_specs=[vmem] * 6 + [hbm] * 3,
        out_specs=[vmem] * 5,
        out_shape=[
            jax.ShapeDtypeStruct((length, heads * HD), low),
            jax.ShapeDtypeStruct((length, 2 * kvs * HD), low),
        ]
        + [jax.ShapeDtypeStruct(total.shape[1:], f32) for total in totals],
        scratch_shapes=[
            pltpu.VMEM((kvs, length, HD), low),
            pltpu.VMEM((kvs, length, HD), f32),
            pltpu.VMEM((kvs, length, HD), f32),
        ]
        + [pltpu.VMEM((5,) + total.shape[1:], low) for total in totals]
        + [pltpu.SemaphoreType.DMA((32,)), pltpu.SemaphoreType.DMA((32,))],
        compiler_params=pltpu.CompilerParams(
            collective_id=3, has_side_effects=True, vmem_limit_bytes=56 << 20
        ),
        cost_estimate=pl.CostEstimate(
            flops=10 * heads * length * SPAN * HD,
            bytes_accessed=9 << 20,
            transcendentals=heads * length * SPAN,
        ),
        name="behind",
    )(qkv, grad, cosine, sine, row, col, *totals)


def bands(size):
    return (pl.ds(0, size // 2), pl.ds(size // 2, size // 2))


def first_kernel(
    heads,
    kvs,
    x_in,
    g_in,
    qkv_in,
    gate_in,
    up_in,
    down_in,
    out_in,
    gain_in,
    docs_in,
    cos_ref,
    sin_ref,
    x_own,
    normed,
    qkv,
    mixed,
    hidden,
    qkv_w,
    out_w,
    gain_rows,
    seeds,
    tokens,
    gate_w,
    up_w,
    down_w,
    docs,
    row,
    col,
    gains,
    keys,
    part,
    part_got,
    sends,
    recvs,
):
    f32, low = jnp.float32, jnp.bfloat16
    me = coordinates()
    y, x, zh, zl, core = me
    s, z = y * 2 + x, zh * 2 + zl
    mine = y == core
    other = jnp.logical_not(mine)
    width = qkv_w.shape[-1]
    length = qkv.shape[0]
    half_len = length // 2
    greet(me, HEAD_GROUPS)
    move = Mover(me, sends, recvs)

    own = [
        move.local(qkv_in.at[core], qkv_w.at[s, z, core]),
        move.local(gain_in, gains.at[s, z, core]),
    ]
    first = [
        move.send(qkv_in.at[1 - core], qkv_w.at[s, z, core], "core"),
        move.send(gain_in, gains.at[s, z, core], "core"),
    ]
    docs_move = move.send(docs_in, docs, "core")
    x_turn = turn_start(move, me, x_in, x_own)
    for made in own:
        made.wait()
    for made in first:
        made.wait_recv()
    line = [move.send(gains.at[s, z], gains.at[s, z], *names) for names in LINE]
    line += [move.send(qkv_w.at[s, z], qkv_w.at[s, z], *names) for names in LINE]

    own = [
        move.local(gate_in.at[zl, core], gate_w.at[s, zh, zl, core]),
        move.local(up_in.at[zl, core], up_w.at[s, zh, zl, core]),
        move.local(down_in, down_w.at[s, zh]),
    ]
    spread = []
    for src, dst in ((gate_in, gate_w), (up_in, up_w)):
        for names in (("core",), ("zl",), ("zl", "core")):
            to_zl = 1 - zl if "zl" in names else zl
            to_core = 1 - core if "core" in names else core
            spread.append(move.send(src.at[to_zl, to_core], dst.at[s, zh, zl, core], *names))
    out_own = move.quiet(out_in, out_w.at[x, z, core])
    out_sent = move.copy(out_in, out_w.at[x, z, core], "core")
    pl.when(mine)(out_own.start)
    pl.when(other)(out_sent.start)

    for made in line[:3]:
        made.wait_recv()
    gain_hops = [move.send(gains.at[s], gains.at[s], *names) for names in (("x",), ("y",))]
    turn_end(me, x_turn)
    gain_hops[0].wait_recv()
    sx = 2 * y + 1 - x
    gain_hops.append(move.send(gains.at[sx], gains.at[sx], "y"))
    for made in line[3:]:
        made.wait_recv()
    qkv_hops = plane_start(move, qkv_w, s, bands(width))

    out_line = [move.copy(out_w.at[x, z], out_w.at[x, z], *names) for names in LINE]
    pl.when(other)(out_sent.wait_send)

    @pl.when(mine)
    def _():
        out_own.wait()
        out_sent.wait_recv()
        for made in out_line:
            made.start()

    for made in own:
        made.wait()
    for made in spread:
        made.wait_recv()
    pairs = [
        move.send(ref.at[s, zh], ref.at[s, zh], "zh") for ref in (gate_w, up_w, down_w)
    ]

    for made in gain_hops[1:]:
        made.wait_recv()
    count = out_in.shape[0]
    for i in range(2):
        gain_rows[pl.ds(i, 1), :] = jnp.concatenate(
            [
                gains[a, b, c, 0:1, i * count : (i + 1) * count]
                for a in range(4)
                for b in range(4)
                for c in range(2)
            ],
            axis=1,
        )

    quarter = half_len // 2
    for q in range(2):

        def norm(at, q=q):
            field = x_own[q, at, :].astype(f32)
            inverse = lax.rsqrt(jnp.mean(field * field, axis=1, keepdims=True) + EPSILON)
            rows = pl.ds(pl.multiple_of(q * quarter + at.start, 16), at.size)
            normed[core, rows, :] = (field * inverse * gain_rows[0:1, :]).astype(low)

        by_rows(quarter, 16, norm)
    normed_move = move.send(normed.at[core], normed.at[core], "core")
    docs_move.wait_recv()
    row[...] = jnp.where(mine, docs_in[x], docs[x])
    col[...] = jnp.transpose(jnp.broadcast_to(row[...], (8, length)))[:, 0:1]

    qkv_rest = plane_pass(move, qkv_hops, qkv_w, y, x, bands(width))
    out_x = move.copy(out_w.at[x], out_w.at[x], "x")
    out_y = [move.copy(out_w.at[at], out_w.at[at], "y") for at in (x, 1 - x)]

    @pl.when(mine)
    def _():
        for made in out_line:
            made.wait()
        out_x.start()
        out_y[0].start()

    wides = [
        (ref.at[:, at], bands(ref.shape[-1]))
        for at in (zh, 1 - zh)
        for ref in (gate_w, up_w, down_w)
    ]
    hops = [plane_make(move, ref, s, parts) for ref, parts in wides]

    def start_some(which):
        for i in which:
            for made in hops[i]:
                made.start()

    normed_move.wait_recv()
    for made in qkv_rest:
        made.wait_recv()
    g_turn = turn_start(move, me, g_in, seeds.at[0])
    start_some((0,))
    weight = qkv_w.reshape(width, width)
    for i in range(length // QB):
        at = pl.ds(i * QB % half_len, QB)
        qkv[pl.ds(i * QB, QB), :] = nn(normed[i * QB // half_len, at, :], weight[...]).astype(low)
    start_some((1, 2))
    seed_moves = [
        move.later(seeds.at[0], seeds.at[1], "core"),
        move.later(seeds.at[0], seeds.at[2], "zl"),
    ]

    everything = pl.ds(0, length)
    for j in range(kvs):
        keys[j] = spun(head(qkv, everything, heads + j), cos_ref[...], sin_ref[...]).astype(low)

    def work(step, size):
        ahead_block(heads, kvs, step, size, qkv, cos_ref, sin_ref, row, col, mixed, keys)

    def block(step, carry):
        @pl.when(step == SPAN // QB - 1)
        def _():
            turn_end(me, g_turn)
            for made in seed_moves:
                made.start()
            for made in pairs[:2]:
                made.wait_recv()
            start_some((3, 4))

        work(step, SPAN)
        return carry

    work(0, QB)

    @pl.when(mine)
    def _():
        out_x.wait_recv()
        out_y[1].start()

    for step in range(1, SPAN // QB - 1):
        work(step, (step + 1) * QB)
    lax.fori_loop(SPAN // QB - 1, length // QB, block, 0)
    pairs[2].wait_recv()
    start_some((5,))
    rest = []

    def pass_some(which):
        for i in which:
            rest.extend(plane_pass(move, hops[i], wides[i][0], y, x, wides[i][1]))

    @pl.when(mine)
    def _():
        out_x.wait_send()
        for made in out_y:
            made.wait_send()

    @pl.when(other)
    def _():
        for made in out_y:
            made.wait_recv()

    out_weight = out_w.reshape(width // 2, width)
    theirs, ours = (pl.multiple_of(c * half_len, half_len) for c in (1 - core, core))

    def project(start):
        for i in range(half_len // QB):
            at = pl.ds(pl.multiple_of(start + i * QB, QB), QB)
            part[pl.ds(i * QB, QB), :] = nn(mixed[at, :], out_weight[...])

    project(theirs)
    part_move = move.copy(part, part_got, "core")
    part_move.start()
    pass_some((0, 1, 2))
    for i in range(half_len // QB):
        at = pl.ds(pl.multiple_of(ours + i * QB, QB), QB)
        hidden[pl.ds(i * QB, QB), :] = nn(mixed[at, :], out_weight[...])
    part_move.wait()
    for q in range(2):

        def norm(at, q=q):
            rows = pl.ds(pl.multiple_of(q * quarter + at.start, 16), at.size)
            field = x_own[q, at, :].astype(f32) + (hidden[rows, :] + part_got[rows, :])
            hidden[rows, :] = field
            inverse = lax.rsqrt(jnp.mean(field * field, axis=1, keepdims=True) + EPSILON)
            tokens[0, rows, :] = (field * inverse * gain_rows[1:2, :]).astype(low)

        by_rows(quarter, 16, norm)
    token_moves = [
        move.send(tokens.at[0], tokens.at[2], "zl"),
        move.send(tokens.at[0], tokens.at[1], "core"),
    ]
    seed_moves[1].wait_recv()
    seed_moves.append(move.send(seeds.at[2], seeds.at[3], "core"))
    pass_some((3, 4, 5))
    token_moves[0].wait_recv()
    token_moves.append(move.send(tokens.at[2], tokens.at[3], "core"))
    for made in rest + seed_moves[::2] + token_moves[1:]:
        made.wait_recv()
    move.finish()


def first_part(heads, kvs, x_in, g_in, qkv, gate, up, down, out, gain, docs, cosine, sine):
    f32, low = jnp.float32, jnp.bfloat16
    rows, width = out.shape
    half_len = 2 * x_in.shape[1]
    length = 2 * half_len
    hbm = pl.BlockSpec(memory_space=pl.ANY)
    vmem = pl.BlockSpec(memory_space=pltpu.VMEM)

    def made(shape, dtype=low):
        return jax.ShapeDtypeStruct(shape, dtype)

    return pl.pallas_call(
        functools.partial(first_kernel, heads, kvs),
        in_specs=[hbm] * 8 + [vmem] * 3,
        out_specs=[vmem] * 9 + [vmem] + [hbm] * 3,
        out_shape=[
            made(x_in.shape),
            made((2, half_len, width)),
            made((length, width)),
            made((length, heads * HD)),
            made((half_len, width), f32),
            made((4, 4, 2) + qkv.shape[1:]),
            made((2, 4, 2) + out.shape),
            made((2, width), f32),
            made((4,) + x_in.shape),
            made((4, half_len, width)),
            made((4, 2, 2, 2) + gate.shape[2:]),
            made((4, 2, 2, 2) + up.shape[2:]),
            made((4, 2) + down.shape),
        ],
        scratch_shapes=[
            pltpu.VMEM(docs.shape, docs.dtype),
            pltpu.VMEM(docs.shape[1:], docs.dtype),
            pltpu.VMEM(docs.shape[:0:-1], docs.dtype),
            pltpu.VMEM((4, 4, 2) + gain.shape, f32),
            pltpu.VMEM((kvs, length, HD), low),
            pltpu.VMEM((half_len, width), f32),
            pltpu.VMEM((half_len, width), f32),
            pltpu.SemaphoreType.DMA((96,)),
            pltpu.SemaphoreType.DMA((96,)),
        ],
        compiler_params=pltpu.CompilerParams(
            collective_id=1, has_side_effects=True, vmem_limit_bytes=60 << 20
        ),
        name="first",
    )(x_in, g_in, qkv, gate, up, down, out, gain, docs, cosine, sine)


def hop(value, *names):
    flip = sum(BITS[name] for name in names)
    return lax.ppermute(value, AXES, [(i, i ^ flip) for i in range(32)])


def after(value, *others):
    return lax.optimization_barrier((value,) + others)[0]


def in_order(mine, other, place, axis=0):
    first = jnp.where(place == 0, mine, other)
    second = jnp.where(place == 0, other, mine)
    return jnp.concatenate([first, second], axis=axis)


def pick(value, place, axis=0):
    return lax.dynamic_index_in_dim(value, place, axis, keepdims=False)


def fast_body(
    layer_input,
    cotangent,
    token_mask,
    document_ids,
    attn_gain,
    w_query,
    w_key,
    w_value,
    w_output,
    mlp_gain,
    w_gate,
    w_up,
    w_down,
):
    f32, low = jnp.float32, jnp.bfloat16
    y, x, zh, zl, core = (lax.axis_index(name) for name in AXES)
    device = sum(lax.axis_index(name) * BITS[name] for name in AXES)
    quarter, width = layer_input.shape[1:]
    half_len = 2 * quarter
    length = 2 * half_len
    rows = w_query.shape[0]
    units = w_gate.shape[1]
    heads, kvs = HEADS // 2, KV // 2
    cosine, sine = rope_tables(length, HD)

    def swap_in(mine, sent):
        return in_order(mine[None], hop(sent, "core")[None], core)

    def halves(weight):
        return weight.reshape(rows, 2, -1)

    def both(mine):
        return in_order(mine, hop(mine, "core"), core)

    def join(part):
        part = part.reshape(2, half_len, width)
        return pick(part, core) + hop(pick(part, 1 - core), "core")

    masked = cotangent * token_mask.astype(low)[:, :, None]
    qkv = jnp.concatenate([halves(w) for w in (w_query, w_key, w_value)], axis=2)
    qkv = jnp.moveaxis(qkv, 1, 0)
    gate_in, up_in = (
        jnp.transpose(w.reshape(rows, units // 512, 2, 2, 128), (2, 3, 0, 1, 4)).reshape(
            2, 2, rows, -1
        )
        for w in (w_gate, w_up)
    )
    gain = jnp.concatenate([attn_gain, mlp_gain]).astype(f32)
    gain = jnp.broadcast_to(jnp.pad(gain, (0, 128 - 2 * rows)), (8, 128))
    own, normed, pair, mixed, hidden, qkv_w, out_w, gains, seeds, tokens, gate_w, up_w, down_w = (
        first_part(
            heads,
            kvs,
            layer_input,
            masked,
            qkv,
            gate_in,
            up_in,
            w_down,
            w_output,
            gain,
            document_ids[:, None],
            cosine,
            sine,
        )
    )
    normed = normed.reshape(length, width)
    qkv_w, out_w = qkv_w.reshape(width, -1), out_w.reshape(-1, width)
    gate_w, up_w = gate_w.reshape(width, -1), up_w.reshape(width, -1)
    down_w = down_w.reshape(-1, width)
    seed_low = seeds[0].reshape(half_len, width)
    seeds = seeds.reshape(2, length, width)
    normed_two = tokens.reshape(2, length, width)
    documents = pick(jnp.where(core == y, document_ids, hop(document_ids, "core")), x)
    row, col = documents[None, :], documents[:, None]
    inputs = own.reshape(half_len, width).astype(f32)
    inv_one = inverse_rms(inputs)
    unit_one = inputs * inv_one
    inv_two = inverse_rms(hidden)
    unit_two = hidden * inv_two

    def ahead_and_back(tokens, seed):
        gate, upward, grad_act = nn(tokens, gate_w), nn(tokens, up_w), nt(seed, down_w)
        sigma = jax.nn.sigmoid(gate)
        activated = (gate * sigma * upward).astype(low)
        up_low = (grad_act * gate * sigma).astype(low)
        gate_low = (grad_act * upward * sigma * (1.0 + gate * (1.0 - sigma))).astype(low)
        back = nt(gate_low, gate_w) + nt(up_low, up_w)
        return activated, gate_low, up_low, nn(activated, down_w), back

    near = ahead_and_back(normed_two[0], seeds[0])
    far_tokens = after(normed_two[1], near[4])
    far = ahead_and_back(far_tokens, seeds[1])

    def fold(part):
        return part[:half_len] + hop(part[half_len:], "core")

    theirs = fold(far[4]).astype(low)
    back = hop(theirs, "zl")
    near_low, far_low = (
        tuple(after(v, theirs) for v in parts[:3]) for parts in (near, far)
    )
    grad_down = (tn(near_low[0], seeds[0]) + tn(far_low[0], seeds[1])).astype(low)
    grad_gate = (tn(normed_two[0], near_low[1]) + tn(far_tokens, far_low[1])).astype(low)
    grad_up = (tn(normed_two[0], near_low[2]) + tn(far_tokens, far_low[2])).astype(low)
    totals = [
        grad_gate.reshape(4, -1, units // 4),
        grad_up.reshape(4, -1, units // 4),
        grad_down.reshape(4, -1, width),
    ]

    grad_normed_two = fold(near[4]) + back.astype(f32)
    scaled_two = grad_normed_two * gains[1]
    grad_hidden = seed_low.astype(f32) + inv_two * (
        scaled_two - unit_two * jnp.mean(scaled_two * unit_two, axis=-1, keepdims=True)
    )
    grad_low = both(grad_hidden.astype(low))
    grad_heads = nt(grad_low, out_w).astype(low)
    grad_heads = after(grad_heads, *totals)

    ahead_low = after(fold(far[3]).astype(low), back)
    output = hidden + fold(near[3]) + hop(ahead_low, "zl").astype(f32)
    gain_two = jnp.sum(grad_normed_two * unit_two, axis=0)

    grad_query, grad_pair, *sums = attend_behind(
        heads, kvs, pair, grad_heads, cosine, sine, row, col, *totals
    )
    cols = heads * HD
    part = nt(grad_query, qkv_w[:, :cols]) + nt(grad_pair, qkv_w[:, cols:])
    grad_out_w = tn(mixed, grad_low).astype(low).reshape(2, 4, 2, rows, width)
    grad_qkv = jnp.concatenate(
        [tn(normed, grad_query).astype(low), tn(normed, grad_pair).astype(low)], axis=1
    )
    grad_normed = join(part)
    scaled_one = grad_normed * gains[0]
    grad_input = grad_hidden + inv_one * (
        scaled_one - unit_one * jnp.mean(scaled_one * unit_one, axis=-1, keepdims=True)
    )
    gain = jnp.stack([jnp.sum(grad_normed * unit_one, axis=0), gain_two])
    hidden_grads = [None, None]
    hidden_grads[0], hidden_grads[1], grad_down, grad_qkv, grad_output, output, grad_input, gain = (
        sum_tail(
            sums[0].reshape(2, -1, units // 4),
            sums[1].reshape(2, -1, units // 4),
            sums[2].reshape(2, -1, width),
            grad_qkv.reshape(4, -1, width),
            grad_out_w,
            output.astype(low).reshape(2, quarter, width),
            grad_input.astype(low).reshape(2, quarter, width),
            gain,
        )
    )
    hidden_grads = [
        jnp.transpose(total.reshape(2, 2, rows, -1, 128), (2, 3, 0, 1, 4)).reshape(rows, units)
        for total in hidden_grads
    ]

    def columns(start, size):
        return jnp.moveaxis(grad_qkv[:, :, start : start + size], 0, 1).reshape(rows, -1)

    q_grad = columns(0, cols)
    k_grad = columns(cols, kvs * HD)
    v_grad = columns(cols + kvs * HD, kvs * HD)
    gain_one = lax.dynamic_slice_in_dim(gain, device * rows, rows, 1)

    return (
        output,
        grad_input,
        gain_one[0],
        q_grad,
        k_grad,
        v_grad,
        grad_output,
        gain_one[1],
        hidden_grads[0],
        hidden_grads[1],
        grad_down,
    )


def solution(mesh):
    fast = dict(mesh.shape) == {"seq": 4, "batch": 8}
    if fast:
        grid = Mesh(mesh.devices.reshape((2,) * 5), AXES)
        seq, batch = ("y", "x"), ("zh", "zl", "core")
    else:
        grid, seq, batch = mesh, ("seq",), ("batch",)
    weight = P(seq + batch, None)
    gain = P(seq + batch)
    token = P(batch, seq, None)
    return jax.shard_map(
        fast_body if fast else body,
        mesh=grid,
        in_specs=(token, token, P(batch, seq), P(batch, None), gain)
        + (weight,) * 4
        + (gain,)
        + (weight,) * 3,
        out_specs=(token, token, gain) + (weight,) * 4 + (gain,) + (weight,) * 3,
        check_vma=False,
    )
```

```python
import functools
import math

import jax
import jax.numpy as jnp
from jax import lax
from jax.experimental import pallas as pl
from jax.experimental.pallas import tpu as pltpu
from jax.sharding import Mesh
from jax.sharding import PartitionSpec as P

HEADS = 16
KV = 8
HD = 96


EPSILON = 1e-05
ROPE_BASE = 10000.0


def inverse_rms(field):
    return lax.rsqrt(jnp.mean(field * field, axis=-1, keepdims=True) + EPSILON)


def half_turn(field):
    middle = field.shape[-1] // 2
    return jnp.concatenate([-field[..., middle:], field[..., :middle]], axis=-1)


def rope_tables(length, width):
    middle = width // 2
    freqs = ROPE_BASE ** (-2.0 * jnp.arange(middle, dtype=jnp.float32) / width)
    angles = jnp.arange(length, dtype=jnp.float32)[:, None] * freqs[None, :]
    cosine = jnp.concatenate([jnp.cos(angles), jnp.cos(angles)], axis=-1)
    sine = jnp.concatenate([jnp.sin(angles), jnp.sin(angles)], axis=-1)
    return (cosine, sine)


def rotate_ahead(field, cosine, sine):
    return field * cosine[:, None, :] + half_turn(field) * sine[:, None, :]


def rotate_behind(field, cosine, sine):
    return field * cosine[:, None, :] - half_turn(field) * sine[:, None, :]


def outer_sum(left, right):
    return lax.dot_general(
        left, right, (((0,), (0,)), ((), ())), preferred_element_type=jnp.float32
    )


def back_product(left, right):
    return lax.dot_general(
        left, right, (((1,), (1,)), ((), ())), preferred_element_type=jnp.float32
    )


def fetch_attention(attn_gain, w_query, w_key, w_value, w_output):
    return (
        lax.all_gather(attn_gain, ("seq", "batch"), axis=0, tiled=True),
        lax.all_gather(w_query, ("seq", "batch"), axis=0, tiled=True),
        lax.all_gather(w_key, ("seq", "batch"), axis=0, tiled=True),
        lax.all_gather(w_value, ("seq", "batch"), axis=0, tiled=True),
        lax.all_gather(w_output, ("seq", "batch"), axis=0, tiled=True),
    )


def fetch_feedforward(mlp_gain, w_gate, w_up, w_down):
    return (
        lax.all_gather(mlp_gain, ("seq", "batch"), axis=0, tiled=True),
        lax.all_gather(w_gate, ("seq", "batch"), axis=0, tiled=True),
        lax.all_gather(w_up, ("seq", "batch"), axis=0, tiled=True),
        lax.all_gather(w_down, ("seq", "batch"), axis=0, tiled=True),
    )


def block_scores(query_block, keys, documents, start, block, scale):
    length = keys.shape[0]
    scores = (
        jnp.einsum("qjhd,kjd->jhqk", query_block, keys, preferred_element_type=jnp.float32) * scale
    )
    key_pos = jnp.arange(length, dtype=jnp.int32)
    query_pos = start + jnp.arange(block, dtype=jnp.int32)
    query_docs = lax.dynamic_slice_in_dim(documents, start, block, 0)
    allowed = (key_pos[None, :] <= query_pos[:, None]) & (query_docs[:, None] == documents[None, :])
    return jnp.where(allowed[None, None], scores, -1e30)


def attention_forward(queries, keys, values, documents, block, scale):
    length = queries.shape[0]
    count = length // block

    def one_block(index):
        start = index * block
        query_block = lax.dynamic_slice_in_dim(queries, start, block, 0)
        scores = block_scores(query_block, keys, documents, start, block, scale)
        peak_score = jnp.max(scores, axis=-1, keepdims=True)
        weights = jnp.exp(scores - peak_score)
        totals = jnp.sum(weights, axis=-1, keepdims=True)
        probs = (weights / totals).astype(jnp.bfloat16)
        result = jnp.einsum("jhqk,kjd->qjhd", probs, values, preferred_element_type=jnp.float32)
        return (
            result.astype(jnp.bfloat16).reshape(block, -1),
            (peak_score + jnp.log(totals))[..., 0],
        )

    results, sums = lax.map(one_block, jnp.arange(count, dtype=jnp.int32))
    return (results.reshape(length, -1), sums)


def attention_backward(queries, keys, values, documents, sums, grad_out, block, scale):
    length = queries.shape[0]
    count = length // block

    def one_block(carry, member):
        grad_keys, grad_values = carry
        index, sums_block = member
        start = index * block
        query_block = lax.dynamic_slice_in_dim(queries, start, block, 0)
        grad_block = lax.dynamic_slice_in_dim(grad_out, start, block, 0)
        scores = block_scores(query_block, keys, documents, start, block, scale)
        probs = jnp.exp(scores - sums_block[..., None])
        grad_probs = jnp.einsum(
            "qjhd,kjd->jhqk", grad_block, values, preferred_element_type=jnp.float32
        )
        centre = jnp.sum(probs * grad_probs, axis=-1, keepdims=True)
        grad_scores = (probs * (grad_probs - centre)).astype(jnp.bfloat16)
        grad_query = (
            jnp.einsum("jhqk,kjd->qjhd", grad_scores, keys, preferred_element_type=jnp.float32)
            * scale
        )
        grad_keys = (
            grad_keys
            + jnp.einsum(
                "jhqk,qjhd->kjd", grad_scores, query_block, preferred_element_type=jnp.float32
            )
            * scale
        )
        grad_values = grad_values + jnp.einsum(
            "jhqk,qjhd->kjd",
            probs.astype(jnp.bfloat16),
            grad_block,
            preferred_element_type=jnp.float32,
        )
        return ((grad_keys, grad_values), grad_query)

    empty = jnp.zeros(keys.shape, jnp.float32)
    (grad_keys, grad_values), grad_query = lax.scan(
        one_block, (empty, empty), (jnp.arange(count, dtype=jnp.int32), sums)
    )
    return (
        grad_query.reshape(length, queries.shape[1] * queries.shape[2], queries.shape[3]),
        grad_keys,
        grad_values,
    )


def body(
    layer_input,
    cotangent,
    token_mask,
    document_ids,
    attn_gain,
    w_query,
    w_key,
    w_value,
    w_output,
    mlp_gain,
    w_gate,
    w_up,
    w_down,
):
    parts = lax.axis_size("seq")
    micro_count = layer_input.shape[0]
    shard = layer_input.shape[1]
    length = shard * parts
    heads_here = HEADS // parts
    kv_here = max(1, KV // parts)
    copies = parts * kv_here // KV
    per_kv = heads_here // kv_here
    block = min(512, length)
    scale = 1.0 / math.sqrt(HD)
    cosine, sine = rope_tables(length, HD)
    attn_set = None
    mlp_set = None
    attn_total = None
    mlp_total = None
    outputs = []
    input_grads = []
    kept = {
        "normed": [],
        "normed_two": [],
        "activated": [],
        "seed_low": [],
        "gate_low": [],
        "up_low": [],
        "grad_low": [],
        "mixed": [],
        "query_back": [],
        "key_back": [],
        "value_back": [],
    }
    gain_one_total = None
    gain_two_total = None
    for micro in range(micro_count):
        attn_set = fetch_attention(attn_gain, w_query, w_key, w_value, w_output)
        mlp_set = fetch_feedforward(mlp_gain, w_gate, w_up, w_down)
        gain_one = attn_set[0].astype(jnp.float32)
        gain_two = mlp_set[0].astype(jnp.float32)
        documents = document_ids[micro]
        inputs = layer_input[micro].astype(jnp.float32)
        inv_one = inverse_rms(inputs)
        unit_one = inputs * inv_one
        normed = (unit_one * gain_one).astype(jnp.bfloat16)
        queries = jnp.dot(normed, attn_set[1], preferred_element_type=jnp.float32).astype(
            jnp.bfloat16
        )
        keys_lin = jnp.dot(normed, attn_set[2], preferred_element_type=jnp.float32).astype(
            jnp.bfloat16
        )
        values_lin = jnp.dot(normed, attn_set[3], preferred_element_type=jnp.float32).astype(
            jnp.bfloat16
        )
        queries = queries.reshape(shard, parts, heads_here * HD)
        key_slots = jnp.repeat(keys_lin.reshape(shard, KV, HD), copies, axis=1).reshape(
            shard, parts, kv_here * HD
        )
        value_slots = jnp.repeat(values_lin.reshape(shard, KV, HD), copies, axis=1).reshape(
            shard, parts, kv_here * HD
        )
        pairs = jnp.concatenate([key_slots, value_slots], axis=-1)
        query_heads, pair_heads = (
            lax.all_to_all(queries, "seq", split_axis=1, concat_axis=0, tiled=True),
            lax.all_to_all(pairs, "seq", split_axis=1, concat_axis=0, tiled=True),
        )
        query_rot = rotate_ahead(
            query_heads.reshape(length, heads_here, HD).astype(jnp.float32), cosine, sine
        )
        query_rot = query_rot.astype(jnp.bfloat16).reshape(length, kv_here, per_kv, HD)
        key_heads = pair_heads[:, 0, : kv_here * HD].reshape(length, kv_here, HD)
        key_rot = rotate_ahead(key_heads.astype(jnp.float32), cosine, sine).astype(jnp.bfloat16)
        value_heads = pair_heads[:, 0, kv_here * HD :].reshape(length, kv_here, HD)
        attended, sums = attention_forward(query_rot, key_rot, value_heads, documents, block, scale)
        mixed = lax.all_to_all(
            attended.reshape(length, 1, heads_here * HD),
            "seq",
            split_axis=0,
            concat_axis=1,
            tiled=True,
        )
        mixed = mixed.reshape(shard, HEADS * HD)
        hidden_state = inputs + jnp.dot(mixed, attn_set[4], preferred_element_type=jnp.float32)
        inv_two = inverse_rms(hidden_state)
        unit_two = hidden_state * inv_two
        normed_two = (unit_two * gain_two).astype(jnp.bfloat16)
        gate = jnp.dot(normed_two, mlp_set[1], preferred_element_type=jnp.float32)
        upward = jnp.dot(normed_two, mlp_set[2], preferred_element_type=jnp.float32)
        sigma = jax.nn.sigmoid(gate)
        activated = (gate * sigma * upward).astype(jnp.bfloat16)
        output = hidden_state + jnp.dot(activated, mlp_set[3], preferred_element_type=jnp.float32)
        outputs.append(output.astype(jnp.bfloat16))
        seed = cotangent[micro].astype(jnp.float32) * token_mask[micro].astype(jnp.float32)[:, None]
        seed_low = seed.astype(jnp.bfloat16)
        grad_act = back_product(seed_low, mlp_set[3])
        grad_up_low = (grad_act * gate * sigma).astype(jnp.bfloat16)
        grad_gate_low = (grad_act * upward * sigma * (1.0 + gate * (1.0 - sigma))).astype(
            jnp.bfloat16
        )
        grad_normed_two = back_product(grad_gate_low, mlp_set[1]) + back_product(
            grad_up_low, mlp_set[2]
        )
        grad_gain_two = jnp.sum(grad_normed_two * unit_two, axis=0)
        scaled_two = grad_normed_two * gain_two
        grad_hidden = seed + inv_two * (
            scaled_two - unit_two * jnp.mean(scaled_two * unit_two, axis=-1, keepdims=True)
        )
        gain_two_total = grad_gain_two if gain_two_total is None else gain_two_total + grad_gain_two
        kept["normed_two"].append(normed_two)
        kept["activated"].append(activated)
        kept["seed_low"].append(seed_low)
        kept["gate_low"].append(grad_gate_low)
        kept["up_low"].append(grad_up_low)
        grad_low = grad_hidden.astype(jnp.bfloat16)
        grad_mixed = (
            back_product(grad_low, attn_set[4])
            .astype(jnp.bfloat16)
            .reshape(shard, parts, heads_here * HD)
        )
        grad_heads = lax.all_to_all(
            grad_mixed, "seq", split_axis=1, concat_axis=0, tiled=True
        ).reshape(length, kv_here, per_kv, HD)
        grad_query_rot, grad_key_rot, grad_values = attention_backward(
            query_rot, key_rot, value_heads, documents, sums, grad_heads, block, scale
        )
        grad_query_heads = (
            rotate_behind(grad_query_rot, cosine, sine)
            .astype(jnp.bfloat16)
            .reshape(length, 1, heads_here * HD)
        )
        grad_key_heads = rotate_behind(grad_key_rot, cosine, sine)
        grad_pairs = jnp.concatenate(
            [
                grad_key_heads.reshape(length, kv_here * HD),
                grad_values.reshape(length, kv_here * HD),
            ],
            axis=-1,
        )
        query_back = lax.all_to_all(
            grad_query_heads, "seq", split_axis=0, concat_axis=1, tiled=True
        ).reshape(shard, HEADS * HD)
        pair_back = lax.all_to_all(
            grad_pairs.reshape(length, 1, 2 * kv_here * HD).astype(jnp.bfloat16),
            "seq",
            split_axis=0,
            concat_axis=1,
            tiled=True,
        ).astype(jnp.float32)
        key_back = pair_back[:, :, : kv_here * HD].reshape(shard, KV, copies, HD).sum(axis=2)
        value_back = pair_back[:, :, kv_here * HD :].reshape(shard, KV, copies, HD).sum(axis=2)
        key_back = key_back.reshape(shard, KV * HD).astype(jnp.bfloat16)
        value_back = value_back.reshape(shard, KV * HD).astype(jnp.bfloat16)
        grad_normed = (
            back_product(query_back, attn_set[1])
            + back_product(key_back, attn_set[2])
            + back_product(value_back, attn_set[3])
        )
        grad_gain_one = jnp.sum(grad_normed * unit_one, axis=0)
        scaled_one = grad_normed * gain_one
        grad_input = grad_hidden + inv_one * (
            scaled_one - unit_one * jnp.mean(scaled_one * unit_one, axis=-1, keepdims=True)
        )
        input_grads.append(grad_input.astype(jnp.bfloat16))
        gain_one_total = grad_gain_one if gain_one_total is None else gain_one_total + grad_gain_one
        kept["normed"].append(normed)
        kept["mixed"].append(mixed)
        kept["grad_low"].append(grad_low)
        kept["query_back"].append(query_back)
        kept["key_back"].append(key_back)
        kept["value_back"].append(value_back)
    rows = {name: jnp.concatenate(values, axis=0) for name, values in kept.items()}
    attn_total = (
        lax.psum_scatter(gain_one_total, ("seq", "batch"), scatter_dimension=0, tiled=True),
        lax.psum_scatter(
            outer_sum(rows["normed"], rows["query_back"]),
            ("seq", "batch"),
            scatter_dimension=0,
            tiled=True,
        ),
        lax.psum_scatter(
            outer_sum(rows["normed"], rows["key_back"]),
            ("seq", "batch"),
            scatter_dimension=0,
            tiled=True,
        ),
        lax.psum_scatter(
            outer_sum(rows["normed"], rows["value_back"]),
            ("seq", "batch"),
            scatter_dimension=0,
            tiled=True,
        ),
        lax.psum_scatter(
            outer_sum(rows["mixed"], rows["grad_low"]),
            ("seq", "batch"),
            scatter_dimension=0,
            tiled=True,
        ),
    )
    mlp_total = (
        lax.psum_scatter(gain_two_total, ("seq", "batch"), scatter_dimension=0, tiled=True),
        lax.psum_scatter(
            outer_sum(rows["normed_two"], rows["gate_low"]),
            ("seq", "batch"),
            scatter_dimension=0,
            tiled=True,
        ),
        lax.psum_scatter(
            outer_sum(rows["normed_two"], rows["up_low"]),
            ("seq", "batch"),
            scatter_dimension=0,
            tiled=True,
        ),
        lax.psum_scatter(
            outer_sum(rows["activated"], rows["seed_low"]),
            ("seq", "batch"),
            scatter_dimension=0,
            tiled=True,
        ),
    )
    return (
        jnp.stack(outputs, axis=0),
        jnp.stack(input_grads, axis=0),
        attn_total[0],
        attn_total[1],
        attn_total[2],
        attn_total[3],
        attn_total[4],
        mlp_total[0],
        mlp_total[1],
        mlp_total[2],
        mlp_total[3],
    )


AXES = ("y", "x", "zh", "zl", "core")
BITS = {"y": 16, "x": 8, "zh": 4, "zl": 2, "core": 1}
MESH = pl.DeviceIdType.MESH


def coordinates():
    return tuple(lax.axis_index(name) for name in AXES)


def peer(me, *names):
    return tuple(1 - at if name in names else at for name, at in zip(AXES, me))


def greet(me, groups):
    barrier = pltpu.get_barrier_semaphore()
    for names in groups:
        pl.semaphore_signal(barrier, 1, device_id=peer(me, *names), device_id_type=MESH)
    pl.semaphore_wait(barrier, len(groups))


class Mover:
    def __init__(self, me, sends, recvs):
        self.me, self.sends, self.recvs, self.used = me, sends, recvs, 0
        self.started = []

    def next(self):
        number = self.used
        self.used += 1
        assert number < self.sends.shape[0]
        return number

    def copy(self, src, dst, *names, device=None):
        number = self.next()
        return pltpu.make_async_remote_copy(
            src_ref=src,
            dst_ref=dst,
            send_sem=self.sends.at[number],
            recv_sem=self.recvs.at[number],
            device_id=peer(self.me, *names) if device is None else device,
            device_id_type=MESH,
        )

    def later(self, src, dst, *names):
        made = self.copy(src, dst, *names)
        self.started.append(made)
        return made

    def send(self, src, dst, *names):
        made = self.later(src, dst, *names)
        made.start()
        return made

    def local(self, src, dst):
        made = self.quiet(src, dst)
        made.start()
        return made

    def quiet(self, src, dst):
        number = self.next()
        return pltpu.make_async_copy(src, dst, self.recvs.at[number])

    def finish(self):
        for made in self.started:
            made.wait_send()


HEAD_GROUPS = (
    ("core",),
    ("zl",),
    ("zh",),
    ("zh", "zl"),
    ("zl", "core"),
    ("x",),
    ("y",),
    ("y", "core"),
    ("y", "core", "x"),
)
LINE = (("zl",), ("zh",), ("zh", "zl"))


def turn_start(move, me, src, dst):
    y, x, zh, zl, core = me
    stays = y == core
    made = []
    for flip in (1, 0):
        place = x if flip == 0 else 1 - x
        from_, to = src.at[place], dst.at[x]
        copy = move.copy(from_, to, device=(core, place, zh, zl, y))
        if flip == 0:
            own = move.quiet(from_, to)
            pl.when(stays)(own.start)
            pl.when(jnp.logical_not(stays))(copy.start)
            made.append((copy, own))
        else:
            copy.start()
            made.append((copy, None))
    return made


def turn_end(me, made):
    stays = me[0] == me[4]
    for copy, own in made:
        if own is None:
            copy.wait()
        else:
            pl.when(stays)(own.wait)
            pl.when(jnp.logical_not(stays))(copy.wait)


def plane_make(move, ref, s, parts):
    made = []
    for part in parts:
        piece = ref.at[s, ..., part]
        made += [move.later(piece, piece, "x"), move.later(piece, piece, "y")]
    return made


def plane_start(move, ref, s, parts):
    made = plane_make(move, ref, s, parts)
    for one in made:
        one.start()
    return made


def plane_pass(move, made, ref, y, x, parts):
    made[0].wait_recv()
    first = ref.at[2 * y + 1 - x, ..., parts[0]]
    rest = [move.send(first, first, "y")]
    made[3].wait_recv()
    second = ref.at[2 * (1 - y) + x, ..., parts[1]]
    rest.append(move.send(second, second, "x"))
    made[1].wait_recv()
    made[2].wait_recv()
    return rest


def by_rows(count, chunk, work):
    def step(i, carry):
        work(pl.ds(pl.multiple_of(i * chunk, chunk), chunk))
        return carry

    lax.fori_loop(0, count // chunk, step, 0)


class PlaneSum:
    def __init__(self, move, total, held, y, x):
        self.move, self.total = move, total
        self.mid, self.far, self.near, self.last = (held.at[i] for i in range(4))
        self.own = self.far
        half = total.shape[-1] // 2
        self.left, self.right = pl.ds(0, half), pl.ds(half, half)
        self.at = (2 * y + x, 2 * y + 1 - x, 2 * (1 - y) + x, 2 * (1 - y) + 1 - x)

    def start(self):
        move, total, left, right = self.move, self.total, self.left, self.right
        s, sx, sy, sd = self.at
        self.far_moves = [
            move.send(total.at[sd, :, left], self.far.at[:, left], "y"),
            move.send(total.at[sd, :, right], self.far.at[:, right], "x"),
        ]
        self.loads = [
            move.local(total.at[sx, :, left], self.mid.at[:, left]),
            move.local(total.at[sy, :, right], self.mid.at[:, right]),
        ]
        self.own_load = move.quiet(total.at[s], self.own)
        self.near_moves = [
            move.copy(total.at[sy, :, left], self.near.at[:, left], "y"),
            move.copy(total.at[sx, :, right], self.near.at[:, right], "x"),
        ]
        self.last_moves = [
            move.copy(self.mid.at[:, left], self.last.at[:, left], "x"),
            move.copy(self.mid.at[:, right], self.last.at[:, right], "y"),
        ]

    def start_near(self):
        for made in self.near_moves:
            made.start()

    def pass_on(self):
        for made in self.loads:
            made.wait()
        for made in self.far_moves:
            made.wait_recv()
        rows = self.mid.shape[0]
        mid, far = self.mid, self.far

        def work(at):
            added = mid[at, :].astype(jnp.float32) + far[at, :].astype(jnp.float32)
            mid[at, :] = added.astype(jnp.bfloat16)

        by_rows(rows, 16, work)
        for made in self.last_moves:
            made.start()
        self.own_load.start()

    def end(self, write):
        if self.own_load is not None:
            self.own_load.wait()
        for made in self.near_moves + self.last_moves:
            made.wait()
        own, near, last = self.own, self.near, self.last

        def work(at):
            value = own[at, :].astype(jnp.float32) + near[at, :].astype(jnp.float32)
            write(at, value + last[at, :].astype(jnp.float32))

        by_rows(own.shape[0], 16, work)


class PlaneSumHere(PlaneSum):
    def __init__(self, move, total, held, y, x):
        self.move, self.total = move, total
        self.far, self.near, self.last = (held.at[i] for i in range(3))
        half = total.shape[-1] // 2
        self.left, self.right = left, right = pl.ds(0, half), pl.ds(half, half)
        self.at = s, sx, sy, sd = (2 * y + x, 2 * y + 1 - x, 2 * (1 - y) + x, 3 - 2 * y - x)
        self.own, self.mids = total.at[s], (total.at[sx], total.at[sy])
        self.far_moves = [
            move.later(total.at[sd, :, left], self.far.at[:, left], "y"),
            move.later(total.at[sd, :, right], self.far.at[:, right], "x"),
        ]
        self.near_moves = [
            move.copy(total.at[sy, :, left], self.near.at[:, left], "y"),
            move.copy(total.at[sx, :, right], self.near.at[:, right], "x"),
        ]
        self.last_moves = [
            move.copy(total.at[sx, :, left], self.last.at[:, left], "x"),
            move.copy(total.at[sy, :, right], self.last.at[:, right], "y"),
        ]
        self.own_load = None

    def start(self):
        for made in self.far_moves:
            made.start()

    def pass_on(self):
        for made in self.far_moves:
            made.wait_recv()
        far = self.far

        def work(at):
            for mid, part in zip(self.mids, (self.left, self.right)):
                added = mid[at, part].astype(jnp.float32) + far[at, part].astype(jnp.float32)
                mid[at, part] = added.astype(jnp.bfloat16)

        by_rows(far.shape[0], 16, work)
        for made in self.last_moves:
            made.start()


def tail_kernel(
    gate_in,
    up_in,
    down_in,
    grad_in,
    normed,
    qkv_w,
    x_own,
    steep,
    gain_rows,
    gain_two,
    out_in,
    y_in,
    gate_out,
    up_out,
    down_out,
    qkv_out,
    out_out,
    y_out,
    x_out,
    gain_out,
    pair_low,
    pair_got,
    down_low,
    down_got,
    quarter,
    part,
    part_got,
    x_low,
    qkv_in,
    qkv_held,
    qkv_sum,
    qkv_low,
    qkv_got,
    out_got,
    out_x,
    out_line,
    out_line_got,
    rows_sent,
    gain_got,
    sends,
    recvs,
):
    f32, low = jnp.float32, jnp.bfloat16
    me = coordinates()
    y, x, zh, zl, core = me
    z = 2 * zh + zl
    mine = y == core
    other = jnp.logical_not(mine)
    greet(me, HEAD_GROUPS)
    move = Mover(me, sends, recvs)
    qkv = PlaneSumHere(move, qkv_in, qkv_held, y, x)
    out_y = move.copy(out_in, out_got, "y")
    half_len = part.shape[0]
    block_rows = qkv_in.shape[1]

    def weigh(at):
        lanes = pl.ds(pl.multiple_of(at * block_rows, 128), block_rows)
        total = tn(normed[0, :, lanes], grad_in[pl.ds(0, half_len), :])
        total = total + tn(normed[1, :, lanes], grad_in[pl.ds(half_len, half_len), :])
        qkv_in[at] = total.astype(low)

    weigh(qkv.at[3])
    qkv.start()

    weigh(qkv.at[1])
    weigh(qkv.at[2])
    qkv.start_near()

    pair_rows = pair_got.shape[1]

    def lower(src, dst, skip, count):
        def work(at):
            dst[at, :] = src[skip, at, :].astype(low)

        by_rows(count, 32, work)

    pairs = []
    for i, src in enumerate((gate_in, up_in)):
        lower(src, pair_low.at[i], 1 - zh, pair_rows)
        pairs.append(move.send(pair_low.at[i], pair_got.at[i], "zh"))
    lower(down_in, down_low, 1 - zh, down_low.shape[0])
    pairs.append(move.send(down_low, down_got, "zh"))

    theirs, ours = (pl.multiple_of(c * half_len, half_len) for c in (1 - core, core))

    def project(start):
        for i in range(half_len // QB):
            at = pl.ds(pl.multiple_of(start + i * QB, QB), QB)
            part[pl.ds(i * QB, QB), :] = nt(grad_in[at, :], qkv_w[...])

    project(theirs)
    part_move = move.copy(part, part_got, "core")
    part_move.start()
    weigh(qkv.at[0])
    qkv.pass_on()
    pl.when(other)(out_y.start)
    y_turn = turn_start(move, me, y_in, y_out)
    part_move.wait()
    project(ours)
    gain_out[...] = jnp.zeros_like(gain_out)
    gain_out[1:2, :] = gain_two[...]
    piece = half_len // 2
    for q in range(2):

        def norm_back(at, q=q):
            every = pl.ds(pl.multiple_of(q * piece + at.start, 16), at.size)
            grad = part[every, :] + part_got[every, :]
            field = x_own[q, at, :].astype(f32)
            inverse = lax.rsqrt(jnp.mean(field * field, axis=1, keepdims=True) + EPSILON)
            unit = field * inverse
            gain_out[0:1, :] += jnp.sum(grad * unit, axis=0, keepdims=True)
            scaled = grad * gain_rows[0:1, :]
            centre = jnp.mean(scaled * unit, axis=1, keepdims=True)
            value = steep[every, :] + inverse * (scaled - unit * centre)
            x_low[q, at, :] = value.astype(low)

        by_rows(piece, 16, norm_back)
    x_turn = turn_start(move, me, x_low, x_out)

    gain_moves = [
        move.copy(gain_out, gain_got.at[turn], name)
        for turn, name in enumerate(("core", "x", "y", "zl", "zh"))
    ]

    def gain_round(turn):
        if turn > 0:
            gain_moves[turn - 1].wait()
            gain_out[...] = gain_out[...] + gain_got[turn - 1]
        if turn < len(gain_moves):
            gain_moves[turn].start()

    gain_round(0)
    out_shape = out_in.shape
    blocks = [(a, b) for a in range(out_shape[1]) for b in range(out_shape[2])]

    def keep(at, value):
        qkv_sum[at, :] = value
        qkv_low[at, :] = value.astype(low)

    qkv.end(keep)
    count = qkv_got.shape[1]
    line = []
    for k, names in enumerate(LINE):
        to = z ^ (1, 2, 3)[k]
        start = pl.multiple_of(to * count, count)
        line.append(move.send(qkv_low.at[pl.ds(start, count)], qkv_got.at[k], *names))

    gain_round(1)

    out_x_move = move.copy(out_got.at[1 - x], out_x, "x")

    @pl.when(mine)
    def _():
        out_y.wait_recv()

        def half(at_x):
            def work(i, carry):
                a, b = i // out_shape[2], i % out_shape[2]
                value = out_in[at_x, a, b].astype(f32) + out_got[at_x, a, b].astype(f32)
                out_got[at_x, a, b] = value.astype(low)
                return carry

            lax.fori_loop(0, len(blocks), work, 0)

        half(1 - x)
        out_x_move.start()
        half(x)

    gain_round(2)

    spread = []
    for i, (src, dst) in enumerate(((gate_in, gate_out), (up_in, up_out))):
        pairs[i].wait_recv()
        got, full = pair_got.at[i], quarter.at[i]

        def work(at, src=src, got=got, full=full):
            full[at, :] = src[zh, at, :] + got[at, :].astype(f32)

        by_rows(pair_rows, 32, work)
        share = pair_rows // 4
        for names in (("core",), ("zl",), ("zl", "core")):
            to_zl = 1 - zl if "zl" in names else zl
            to_core = 1 - core if "core" in names else core
            start = pl.multiple_of((2 * to_zl + to_core) * share, share)
            spread.append(move.send(full.at[pl.ds(start, share)], dst.at[zl, core], *names))
        start = pl.multiple_of((2 * zl + core) * share, share)
        dst[zl, core] = full[pl.ds(start, share), :]
    pairs[2].wait_recv()

    def work(at):
        down_out[at, :] = down_in[zh, at, :] + down_got[at, :].astype(f32)

    by_rows(down_out.shape[0], 32, work)

    gain_round(3)
    out_moves = []
    for k, names in enumerate(LINE):
        to = z ^ (1, 2, 3)[k]
        out_moves.append(move.copy(out_line.at[to], out_line_got.at[k], *names))

    @pl.when(mine)
    def _():
        out_x_move.wait()

        def work(i, carry):
            a, b = i // out_shape[2], i % out_shape[2]
            value = out_got[x, a, b].astype(f32) + out_x[a, b].astype(f32)
            out_line[a, b] = value.astype(low)
            return carry

        lax.fori_loop(0, len(blocks), work, 0)
        for made in out_moves:
            made.start()

    gain_round(4)
    for made in line:
        made.wait_recv()
    start = pl.multiple_of(z * count, count)
    total = qkv_sum[pl.ds(start, count), :]
    for k in range(3):
        total = total + qkv_got[k].astype(f32)
    rows = count // 2
    qkv_sum[pl.ds(0, count), :] = total
    theirs = pl.multiple_of((1 - core) * rows, rows)
    swap = move.send(qkv_sum.at[pl.ds(theirs, rows)], qkv_out.at[core], "core")
    qkv_out[core] = qkv_sum[pl.ds(pl.multiple_of(core * rows, rows), rows), :]

    out_swap = move.copy(rows_sent, out_out, "core")

    @pl.when(mine)
    def _():
        for made in out_moves:
            made.wait()
        for at in range(2):
            total = out_line[z, at].astype(f32)
            for k in range(3):
                total = total + out_line_got[k, at].astype(f32)

            @pl.when(core == at)
            def _(total=total):
                out_out[...] = total

            @pl.when(core != at)
            def _(total=total):
                rows_sent[...] = total

        out_swap.start()
        out_swap.wait_send()

    @pl.when(other)
    def _():
        out_y.wait_send()
        out_swap.wait_recv()

    gain_round(5)
    turn_end(me, y_turn)
    turn_end(me, x_turn)
    swap.wait_recv()
    for made in spread:
        made.wait_recv()
    move.finish()


def sum_tail(gate, up, down, grad, normed, qkv_w, x_own, steep, gain_rows, gain_two, out, y_in):
    f32, low = jnp.float32, jnp.bfloat16
    hbm = pl.BlockSpec(memory_space=pl.ANY)
    vmem = pl.BlockSpec(memory_space=pltpu.VMEM)
    wide, width = gate.shape[-1], grad.shape[-1]
    rows = out.shape[-2]
    half_len = steep.shape[0]
    pair_rows, down_rows = gate.shape[1], down.shape[1]
    return pl.pallas_call(
        tail_kernel,
        in_specs=[vmem] * 11 + [hbm],
        out_specs=[vmem] * 5 + [hbm, hbm, vmem],
        out_shape=[
            jax.ShapeDtypeStruct((2, 2, rows, wide), f32),
            jax.ShapeDtypeStruct((2, 2, rows, wide), f32),
            jax.ShapeDtypeStruct((down_rows, width), f32),
            jax.ShapeDtypeStruct((2, rows, width), f32),
            jax.ShapeDtypeStruct((rows, width), f32),
            jax.ShapeDtypeStruct(y_in.shape, low),
            jax.ShapeDtypeStruct(y_in.shape, low),
            jax.ShapeDtypeStruct((2, width), f32),
        ],
        input_output_aliases={},
        scratch_shapes=[
            pltpu.VMEM((2, pair_rows, wide), low),
            pltpu.VMEM((2, pair_rows, wide), low),
            pltpu.VMEM((down_rows, width), low),
            pltpu.VMEM((down_rows, width), low),
            pltpu.VMEM((2, pair_rows, wide), f32),
            pltpu.VMEM((half_len, width), f32),
            pltpu.VMEM((half_len, width), f32),
            pltpu.VMEM(y_in.shape, low),
            pltpu.VMEM((4, 8 * rows, width), low),
            pltpu.VMEM((3, 8 * rows, width), low),
            pltpu.VMEM((8 * rows, width), f32),
            pltpu.VMEM((8 * rows, width), low),
            pltpu.VMEM((3, 2 * rows, width), low),
            pltpu.VMEM(out.shape, low),
            pltpu.VMEM(out.shape[1:], low),
            pltpu.VMEM(out.shape[1:], low),
            pltpu.VMEM((3,) + out.shape[2:], low),
            pltpu.VMEM((rows, width), f32),
            pltpu.VMEM((5, 2, width), f32),
            pltpu.SemaphoreType.DMA((48,)),
            pltpu.SemaphoreType.DMA((48,)),
        ],
        compiler_params=pltpu.CompilerParams(
            collective_id=4, has_side_effects=True, vmem_limit_bytes=63 << 20
        ),
        name="tail",
    )(gate, up, down, grad, normed, qkv_w, x_own, steep, gain_rows, gain_two, out, y_in)


QB = 256
SPAN = 768


def turned(field, back):
    middle = HD // 2
    left, right = field[:, :middle], field[:, middle:]
    if back:
        return jnp.concatenate([right, -left], axis=1)
    return jnp.concatenate([-right, left], axis=1)


def spun(field, cosine, sine, back=False):
    field = field.astype(jnp.float32)
    return field * cosine + turned(field, back) * sine


def nt(left, right):
    return lax.dot_general(left, right, (((1,), (1,)), ((), ())), preferred_element_type=jnp.float32)


def nn(left, right):
    return jnp.dot(left, right, preferred_element_type=jnp.float32)


def tn(left, right):
    return lax.dot_general(left, right, (((0,), (0,)), ((), ())), preferred_element_type=jnp.float32)


def head(ref, rows, number):
    return ref[rows, HD * number : HD * (number + 1)]


def ahead_block(
    heads, kvs, step, size, qkv_ref, cos_ref, sin_ref, row_ref, col_ref, out_ref, keys
):
    low, f32 = jnp.bfloat16, jnp.float32
    start, base = step * QB, (step + 1) * QB - size
    if not isinstance(step, int):
        start, base = pl.multiple_of(start, QB), pl.multiple_of(base, QB)
    here, span = pl.ds(start, QB), pl.ds(base, size)
    key_place = base + lax.broadcasted_iota(jnp.int32, (size, QB), 0)
    place = start + lax.broadcasted_iota(jnp.int32, (size, QB), 1)
    allowed = (key_place <= place) & (col_ref[span, :] == row_ref[:, here])
    bias = jnp.where(allowed, 0.0, -1e30).astype(f32)
    scale = (1.0 / math.sqrt(HD)) * math.log2(math.e)
    cosine, sine = cos_ref[here, :], sin_ref[here, :]
    results = []
    for h in range(heads):
        j = h * kvs // heads
        query = spun(head(qkv_ref, here, h), cosine, sine).astype(low)
        scores = nt(keys[j, span, :], query) * scale + bias
        peak = jnp.max(scores, axis=0, keepdims=True)
        weights = jnp.exp2(scores - peak)
        total = jnp.sum(weights, axis=0, keepdims=True)
        probs = (weights * (1.0 / total)).astype(low)
        results.append(tn(probs, head(qkv_ref, span, heads + kvs + j)).astype(low))
    out_ref[here, :] = jnp.concatenate(results, axis=1)


def behind_block(
    heads,
    kvs,
    step,
    size,
    qkv_ref,
    grad_ref,
    cos_ref,
    sin_ref,
    row_ref,
    col_ref,
    gq_ref,
    keys,
    gks,
    gvs,
):
    low, f32 = jnp.bfloat16, jnp.float32
    start, base = step * QB, (step + 1) * QB - size
    if not isinstance(step, int):
        start, base = pl.multiple_of(start, QB), pl.multiple_of(base, QB)
    here, span = pl.ds(start, QB), pl.ds(base, size)
    key_place = base + lax.broadcasted_iota(jnp.int32, (size, QB), 0)
    place = start + lax.broadcasted_iota(jnp.int32, (size, QB), 1)
    allowed = (key_place <= place) & (col_ref[span, :] == row_ref[:, here])
    bias = jnp.where(allowed, 0.0, -1e30).astype(f32)
    width = 1.0 / math.sqrt(HD)
    scale = width * math.log2(math.e)
    cosine, sine = cos_ref[here, :], sin_ref[here, :]
    results = []
    for h in range(heads):
        j = h * kvs // heads
        query = spun(head(qkv_ref, here, h), cosine, sine).astype(low)
        key, value = keys[j, span, :], head(qkv_ref, span, heads + kvs + j)
        grad = head(grad_ref, here, h)
        scores = nt(key, query) * scale + bias
        peak = jnp.max(scores, axis=0, keepdims=True)
        weights = jnp.exp2(scores - peak)
        total = jnp.sum(weights, axis=0, keepdims=True)
        probs = weights * (1.0 / total)
        slope = nt(value, grad)
        centre = jnp.sum(probs * slope, axis=0, keepdims=True)
        gs = (probs * (slope - centre)).astype(low)
        gvs[j, span, :] += nn(probs.astype(low), grad)
        gks[j, span, :] += nn(gs, query)
        results.append(spun(tn(gs, key) * width, cosine, sine, True).astype(low))
    gq_ref[here, : HD * heads] = jnp.concatenate(results, axis=1)


def behind_kernel(
    heads,
    kvs,
    qkv_ref,
    mixed,
    hidden,
    seed,
    back_own,
    back,
    ahead_own,
    ahead_far,
    out_w,
    gain_rows,
    cos_ref,
    sin_ref,
    row_ref,
    col_ref,
    gate_in,
    up_in,
    down_in,
    grad_ref,
    steep,
    steep_low,
    y_low,
    out_grad,
    gain_ref,
    gate_out,
    up_out,
    down_out,
    ahead_got,
    keys,
    gks,
    gvs,
    gate_held,
    up_held,
    down_held,
    sends,
    recvs,
):
    f32, low = jnp.float32, jnp.bfloat16
    me = coordinates()
    y, x, zh, zl, core = me
    greet(me, (("x",), ("y",), ("core",), ("zl",)))
    move = Mover(me, sends, recvs)
    sums = [
        PlaneSum(move, total, held, y, x)
        for total, held in ((gate_in, gate_held), (up_in, up_held), (down_in, down_held))
    ]
    for plane in sums:
        plane.start()
    ahead_move = move.send(ahead_far, ahead_got, "zl")
    gain_ref[...] = jnp.zeros_like(gain_ref)
    half_len = hidden.shape[0]

    def norm_back(at):
        grad = back_own[at, :] + back[at, :].astype(f32)
        field = hidden[at, :]
        inverse = lax.rsqrt(jnp.mean(field * field, axis=1, keepdims=True) + EPSILON)
        unit = field * inverse
        gain_ref[...] += jnp.sum(grad * unit, axis=0, keepdims=True)
        scaled = grad * gain_rows[1:2, :]
        centre = jnp.mean(scaled * unit, axis=1, keepdims=True)
        value = seed[at, :].astype(f32) + inverse * (scaled - unit * centre)
        steep[at, :] = value
        steep_low[core, at, :] = value.astype(low)

    by_rows(half_len, 16, norm_back)
    swap = move.send(steep_low.at[core], steep_low.at[core], "core")
    everything = pl.ds(0, qkv_ref.shape[0])
    for j in range(kvs):
        keys[j] = spun(head(qkv_ref, everything, heads + j), cos_ref[...], sin_ref[...]).astype(low)
    gks[...] = jnp.zeros_like(gks)
    gvs[...] = jnp.zeros_like(gvs)
    swap.wait_recv()
    per = half_len // QB
    for i in range(2 * per):
        at = pl.ds(i % per * QB, QB)
        grad_ref[pl.ds(i * QB, QB), : heads * HD] = nt(steep_low[i // per, at, :], out_w[...]).astype(low)
    for plane in sums:
        plane.start_near()

    def block(step, carry):
        @pl.when(step == SPAN // QB - 1)
        def _():
            for plane in sums:
                plane.pass_on()

        work(step, SPAN)
        return carry

    def work(step, size):
        behind_block(
            heads, kvs, step, size, qkv_ref, grad_ref, cos_ref, sin_ref, row_ref, col_ref,
            grad_ref, keys, gks, gvs,
        )

    for step in range(SPAN // QB - 1):
        work(step, (step + 1) * QB)
    lax.fori_loop(SPAN // QB - 1, qkv_ref.shape[0] // QB, block, 0)
    width = 1.0 / math.sqrt(HD)
    gk = [
        spun(gks[j] * width, cos_ref[...], sin_ref[...], True).astype(low) for j in range(kvs)
    ]
    gv = [gvs[j].astype(low) for j in range(kvs)]
    grad_ref[:, HD * heads :] = jnp.concatenate(gk + gv, axis=1)
    rows = mixed.shape[1] // 4
    for i in range(4):
        lanes = pl.ds(i * rows, rows)
        total = tn(mixed[pl.ds(0, half_len), lanes], steep_low[0])
        total = total + tn(mixed[pl.ds(half_len, half_len), lanes], steep_low[1])
        out_grad[pl.ds(i * rows, rows), :] = total.astype(low)
    ahead_move.wait_recv()
    quarter = half_len // 2
    for q in range(2):

        def add(at, q=q):
            every = pl.ds(pl.multiple_of(q * quarter + at.start, 16), at.size)
            value = hidden[every, :] + ahead_own[every, :] + ahead_got[q, at, :].astype(f32)
            ahead_got[q, at, :] = value.astype(low)

        by_rows(quarter, 16, add)
    stored = move.local(ahead_got, y_low)
    for plane, out in zip(sums, (gate_out, up_out, down_out)):

        def write(at, value, out=out):
            out[at, :] = value

        plane.end(write)
    stored.wait()
    move.finish()


def attend_behind(heads, kvs, *operands):
    f32, low = jnp.float32, jnp.bfloat16
    qkv, mixed, hidden = operands[:3]
    totals = operands[-3:]
    length, width = qkv.shape
    half_len = length // 2
    hbm = pl.BlockSpec(memory_space=pl.ANY)
    vmem = pl.BlockSpec(memory_space=pltpu.VMEM)

    def made(*shape, dtype=low):
        return jax.ShapeDtypeStruct(shape, dtype)

    return pl.pallas_call(
        functools.partial(behind_kernel, heads, kvs),
        in_specs=[vmem] * 7 + [hbm] + [vmem] * 6 + [hbm] * 3,
        out_specs=[vmem] * 3 + [hbm] + [vmem] * 5,
        out_shape=[
            made(length, width),
            made(half_len, width, dtype=f32),
            made(2, half_len, width),
            made(2, half_len // 2, width),
            made(heads * HD, width),
            made(1, width, dtype=f32),
        ]
        + [made(*total.shape[1:], dtype=f32) for total in totals],
        scratch_shapes=[
            pltpu.VMEM((2, half_len // 2, width), low),
            pltpu.VMEM((kvs, length, HD), low),
            pltpu.VMEM((kvs, length, HD), f32),
            pltpu.VMEM((kvs, length, HD), f32),
        ]
        + [pltpu.VMEM((4,) + total.shape[1:], low) for total in totals]
        + [pltpu.SemaphoreType.DMA((40,)), pltpu.SemaphoreType.DMA((40,))],
        compiler_params=pltpu.CompilerParams(
            collective_id=3, has_side_effects=True, vmem_limit_bytes=63 << 20
        ),
        cost_estimate=pl.CostEstimate(
            flops=10 * heads * length * SPAN * HD,
            bytes_accessed=9 << 20,
            transcendentals=heads * length * SPAN,
        ),
        name="behind",
    )(*operands)


def bands(size):
    return (pl.ds(0, size // 2), pl.ds(size // 2, size // 2))


def first_kernel(
    heads,
    kvs,
    x_in,
    g_in,
    qkv_in,
    gate_in,
    up_in,
    down_in,
    out_in,
    gain_in,
    docs_in,
    cos_ref,
    sin_ref,
    x_own,
    normed,
    qkv,
    mixed,
    hidden,
    qkv_w,
    out_w,
    gain_rows,
    seeds,
    tokens,
    gate_w,
    up_w,
    down_w,
    docs,
    row,
    col,
    gains,
    keys,
    part,
    part_got,
    sends,
    recvs,
):
    f32, low = jnp.float32, jnp.bfloat16
    me = coordinates()
    y, x, zh, zl, core = me
    s, z = y * 2 + x, zh * 2 + zl
    mine = y == core
    other = jnp.logical_not(mine)
    width = qkv_w.shape[-1]
    length = qkv.shape[0]
    half_len = length // 2
    greet(me, HEAD_GROUPS)
    move = Mover(me, sends, recvs)

    own = [
        move.local(qkv_in.at[core], qkv_w.at[s, z, core]),
        move.local(gain_in, gains.at[s, z, core]),
    ]
    first = [
        move.send(qkv_in.at[1 - core], qkv_w.at[s, z, core], "core"),
        move.send(gain_in, gains.at[s, z, core], "core"),
    ]
    docs_move = move.send(docs_in, docs, "core")
    x_turn = turn_start(move, me, x_in, x_own)
    for made in own:
        made.wait()
    for made in first:
        made.wait_recv()
    line = [move.send(gains.at[s, z], gains.at[s, z], *names) for names in LINE]
    line += [move.send(qkv_w.at[s, z], qkv_w.at[s, z], *names) for names in LINE]

    own = [
        move.local(gate_in.at[zl, core], gate_w.at[s, zh, zl, core]),
        move.local(up_in.at[zl, core], up_w.at[s, zh, zl, core]),
        move.local(down_in, down_w.at[s, zh]),
    ]
    spread = []
    for src, dst in ((gate_in, gate_w), (up_in, up_w)):
        for names in (("core",), ("zl",), ("zl", "core")):
            to_zl = 1 - zl if "zl" in names else zl
            to_core = 1 - core if "core" in names else core
            spread.append(move.send(src.at[to_zl, to_core], dst.at[s, zh, zl, core], *names))
    out_own = move.quiet(out_in, out_w.at[x, z, core])
    out_sent = move.copy(out_in, out_w.at[x, z, core], "core")
    pl.when(mine)(out_own.start)
    pl.when(other)(out_sent.start)

    for made in line[:3]:
        made.wait_recv()
    gain_hops = [move.send(gains.at[s], gains.at[s], *names) for names in (("x",), ("y",))]
    turn_end(me, x_turn)
    gain_hops[0].wait_recv()
    sx = 2 * y + 1 - x
    gain_hops.append(move.send(gains.at[sx], gains.at[sx], "y"))
    for made in line[3:]:
        made.wait_recv()
    qkv_hops = plane_start(move, qkv_w, s, bands(width))

    out_line = [move.copy(out_w.at[x, z], out_w.at[x, z], *names) for names in LINE]
    pl.when(other)(out_sent.wait_send)

    @pl.when(mine)
    def _():
        out_own.wait()
        out_sent.wait_recv()
        for made in out_line:
            made.start()

    for made in own:
        made.wait()
    for made in spread:
        made.wait_recv()
    pairs = [
        move.send(ref.at[s, zh], ref.at[s, zh], "zh") for ref in (gate_w, up_w, down_w)
    ]

    for made in gain_hops[1:]:
        made.wait_recv()
    count = out_in.shape[0]
    for i in range(2):
        gain_rows[pl.ds(i, 1), :] = jnp.concatenate(
            [
                gains[a, b, c, 0:1, i * count : (i + 1) * count]
                for a in range(4)
                for b in range(4)
                for c in range(2)
            ],
            axis=1,
        )

    quarter = half_len // 2
    for q in range(2):

        def norm(at, q=q):
            field = x_own[q, at, :].astype(f32)
            inverse = lax.rsqrt(jnp.mean(field * field, axis=1, keepdims=True) + EPSILON)
            rows = pl.ds(pl.multiple_of(q * quarter + at.start, 16), at.size)
            normed[core, rows, :] = (field * inverse * gain_rows[0:1, :]).astype(low)

        by_rows(quarter, 16, norm)
    normed_move = move.send(normed.at[core], normed.at[core], "core")
    docs_move.wait_recv()
    row[...] = jnp.where(mine, docs_in[x], docs[x])
    col[...] = jnp.transpose(jnp.broadcast_to(row[...], (8, length)))[:, 0:1]

    qkv_rest = plane_pass(move, qkv_hops, qkv_w, y, x, bands(width))
    out_x = move.copy(out_w.at[x], out_w.at[x], "x")
    out_y = [move.copy(out_w.at[at], out_w.at[at], "y") for at in (x, 1 - x)]

    @pl.when(mine)
    def _():
        for made in out_line:
            made.wait()
        out_x.start()
        out_y[0].start()

    wides = [
        (ref.at[:, at], bands(ref.shape[-1]))
        for at in (zh, 1 - zh)
        for ref in (gate_w, up_w, down_w)
    ]
    hops = [plane_make(move, ref, s, parts) for ref, parts in wides]

    def start_some(which):
        for i in which:
            for made in hops[i]:
                made.start()

    normed_move.wait_recv()
    for made in qkv_rest:
        made.wait_recv()
    g_turn = turn_start(move, me, g_in, seeds.at[0])
    start_some((0,))
    weight = qkv_w.reshape(width, width)
    for i in range(length // QB):
        at = pl.ds(i * QB % half_len, QB)
        qkv[pl.ds(i * QB, QB), :] = nn(normed[i * QB // half_len, at, :], weight[...]).astype(low)
    start_some((1, 2))
    seed_moves = [
        move.later(seeds.at[0], seeds.at[1], "core"),
        move.later(seeds.at[0], seeds.at[2], "zl"),
    ]

    everything = pl.ds(0, length)
    for j in range(kvs):
        keys[j] = spun(head(qkv, everything, heads + j), cos_ref[...], sin_ref[...]).astype(low)

    def work(step, size):
        ahead_block(heads, kvs, step, size, qkv, cos_ref, sin_ref, row, col, mixed, keys)

    def block(step, carry):
        @pl.when(step == SPAN // QB - 1)
        def _():
            turn_end(me, g_turn)
            for made in seed_moves:
                made.start()
            for made in pairs[:2]:
                made.wait_recv()
            start_some((3, 4))

        work(step, SPAN)
        return carry

    work(0, QB)

    @pl.when(mine)
    def _():
        out_x.wait_recv()
        out_y[1].start()

    for step in range(1, SPAN // QB - 1):
        work(step, (step + 1) * QB)
    lax.fori_loop(SPAN // QB - 1, length // QB, block, 0)
    pairs[2].wait_recv()
    start_some((5,))
    rest = []

    def pass_some(which):
        for i in which:
            rest.extend(plane_pass(move, hops[i], wides[i][0], y, x, wides[i][1]))

    @pl.when(mine)
    def _():
        out_x.wait_send()
        for made in out_y:
            made.wait_send()

    @pl.when(other)
    def _():
        for made in out_y:
            made.wait_recv()

    out_weight = out_w.reshape(width // 2, width)
    theirs, ours = (pl.multiple_of(c * half_len, half_len) for c in (1 - core, core))

    def project(start):
        for i in range(half_len // QB):
            at = pl.ds(pl.multiple_of(start + i * QB, QB), QB)
            part[pl.ds(i * QB, QB), :] = nn(mixed[at, :], out_weight[...])

    project(theirs)
    part_move = move.copy(part, part_got, "core")
    part_move.start()
    pass_some((0, 1, 2))
    for i in range(half_len // QB):
        at = pl.ds(pl.multiple_of(ours + i * QB, QB), QB)
        hidden[pl.ds(i * QB, QB), :] = nn(mixed[at, :], out_weight[...])
    part_move.wait()
    for q in range(2):

        def norm(at, q=q):
            rows = pl.ds(pl.multiple_of(q * quarter + at.start, 16), at.size)
            field = x_own[q, at, :].astype(f32) + (hidden[rows, :] + part_got[rows, :])
            hidden[rows, :] = field
            inverse = lax.rsqrt(jnp.mean(field * field, axis=1, keepdims=True) + EPSILON)
            tokens[0, rows, :] = (field * inverse * gain_rows[1:2, :]).astype(low)

        by_rows(quarter, 16, norm)
    token_moves = [
        move.send(tokens.at[0], tokens.at[2], "zl"),
        move.send(tokens.at[0], tokens.at[1], "core"),
    ]
    seed_moves[1].wait_recv()
    seed_moves.append(move.send(seeds.at[2], seeds.at[3], "core"))
    pass_some((3, 4, 5))
    token_moves[0].wait_recv()
    token_moves.append(move.send(tokens.at[2], tokens.at[3], "core"))
    for made in rest + seed_moves[::2] + token_moves[1:]:
        made.wait_recv()
    move.finish()


def first_part(heads, kvs, x_in, g_in, qkv, gate, up, down, out, gain, docs, cosine, sine):
    f32, low = jnp.float32, jnp.bfloat16
    rows, width = out.shape
    half_len = 2 * x_in.shape[1]
    length = 2 * half_len
    hbm = pl.BlockSpec(memory_space=pl.ANY)
    vmem = pl.BlockSpec(memory_space=pltpu.VMEM)

    def made(shape, dtype=low):
        return jax.ShapeDtypeStruct(shape, dtype)

    return pl.pallas_call(
        functools.partial(first_kernel, heads, kvs),
        in_specs=[hbm] * 8 + [vmem] * 3,
        out_specs=[vmem] * 9 + [vmem] + [hbm] * 3,
        out_shape=[
            made(x_in.shape),
            made((2, half_len, width)),
            made((length, width)),
            made((length, heads * HD)),
            made((half_len, width), f32),
            made((4, 4, 2) + qkv.shape[1:]),
            made((2, 4, 2) + out.shape),
            made((2, width), f32),
            made((4,) + x_in.shape),
            made((4, half_len, width)),
            made((4, 2, 2, 2) + gate.shape[2:]),
            made((4, 2, 2, 2) + up.shape[2:]),
            made((4, 2) + down.shape),
        ],
        scratch_shapes=[
            pltpu.VMEM(docs.shape, docs.dtype),
            pltpu.VMEM(docs.shape[1:], docs.dtype),
            pltpu.VMEM(docs.shape[:0:-1], docs.dtype),
            pltpu.VMEM((4, 4, 2) + gain.shape, f32),
            pltpu.VMEM((kvs, length, HD), low),
            pltpu.VMEM((half_len, width), f32),
            pltpu.VMEM((half_len, width), f32),
            pltpu.SemaphoreType.DMA((96,)),
            pltpu.SemaphoreType.DMA((96,)),
        ],
        compiler_params=pltpu.CompilerParams(
            collective_id=1, has_side_effects=True, vmem_limit_bytes=60 << 20
        ),
        name="first",
    )(x_in, g_in, qkv, gate, up, down, out, gain, docs, cosine, sine)


def hidden_kernel(
    tokens,
    seeds,
    gate_w,
    up_w,
    down_w,
    act_out,
    gate_out,
    up_out,
    back_own,
    back_far,
    ahead_own,
    ahead_far,
    backs,
    aheads,
    back_got,
    ahead_got,
    sends,
    recvs,
):
    f32, low = jnp.float32, jnp.bfloat16
    me = coordinates()
    move = Mover(me, sends, recvs)

    @pl.when(pl.program_id(0) == 0)
    def _():
        greet(me, (("core",),))

    half_len = backs.shape[1]
    per = half_len // QB
    i = pl.program_id(0)
    moves = [
        (
            move.copy(backs.at[1], back_got.at[turn], "core"),
            move.copy(aheads.at[1], ahead_got.at[turn], "core"),
        )
        for turn in range(2)
    ]

    def fold(turn, back_ref, ahead_ref):
        for made in moves[turn]:
            made.wait()

        def work(at):
            back_ref[at, :] = (backs[0, at, :] + back_got[turn, at, :]).astype(back_ref.dtype)
            ahead_ref[at, :] = (aheads[0, at, :] + ahead_got[turn, at, :]).astype(ahead_ref.dtype)

        by_rows(half_len, 16, work)

    slot = 3 - i // per
    rows = pl.ds(pl.multiple_of(i % per * QB, QB), QB)
    token, seed = tokens[...], seeds[...]
    gate, upward = nn(token, gate_w[...]), nn(token, up_w[...])
    sigma = 1.0 / (1.0 + jnp.exp(-gate))
    silu = gate * sigma
    activated = (silu * upward).astype(low)
    act_out[...] = activated
    grad = nt(seed, down_w[...])
    up_low = (grad * silu).astype(low)
    gate_low = (grad * upward * sigma * (1.0 + gate * (1.0 - sigma))).astype(low)
    up_out[...] = up_low
    gate_out[...] = gate_low
    aheads[slot % 2, rows, :] = nn(activated, down_w[...])
    backs[slot % 2, rows, :] = nt(gate_low, gate_w[...]) + nt(up_low, up_w[...])
    for turn in range(2):

        @pl.when(i == (2 * turn + 1) * per - 1)
        def _(turn=turn):
            for made in moves[turn]:
                made.start()

    @pl.when(i == 2 * per - 1)
    def _():
        fold(0, back_far, ahead_far)

    @pl.when(i == 4 * per - 1)
    def _():
        fold(1, back_own, ahead_own)


def hidden_part(tokens, seeds, gate_w, up_w, down_w):
    f32, low = jnp.float32, jnp.bfloat16
    half_len, width = tokens.shape[1:]
    wide = gate_w.shape[1]
    per = half_len // QB
    vmem = pl.BlockSpec(memory_space=pltpu.VMEM)

    def banded(columns):
        return pl.BlockSpec((QB, columns), lambda i: ((3 - i // per) * per + i % per, 0))

    def made(rows, columns, dtype=low):
        return jax.ShapeDtypeStruct((rows, columns), dtype)

    return pl.pallas_call(
        hidden_kernel,
        grid=(4 * per,),
        in_specs=[banded(width)] * 2 + [vmem] * 3,
        out_specs=[banded(wide)] * 3 + [vmem] * 4,
        out_shape=[made(4 * half_len, wide)] * 3
        + [
            made(half_len, width, f32),
            made(half_len, width),
            made(half_len, width, f32),
            made(half_len, width),
        ],
        scratch_shapes=[
            pltpu.VMEM((2, half_len, width), f32),
            pltpu.VMEM((2, half_len, width), f32),
            pltpu.VMEM((2, half_len, width), f32),
            pltpu.VMEM((2, half_len, width), f32),
            pltpu.SemaphoreType.DMA((4,)),
            pltpu.SemaphoreType.DMA((4,)),
        ],
        compiler_params=pltpu.CompilerParams(
            collective_id=2, has_side_effects=True, vmem_limit_bytes=63 << 20
        ),
        cost_estimate=pl.CostEstimate(
            flops=2 * 6 * 4 * half_len * width * wide,
            bytes_accessed=40 << 20,
            transcendentals=4 * half_len * wide,
        ),
        name="hidden",
    )(tokens.reshape(-1, width), seeds.reshape(-1, width), gate_w, up_w, down_w)


def hop(value, *names):
    flip = sum(BITS[name] for name in names)
    return lax.ppermute(value, AXES, [(i, i ^ flip) for i in range(32)])


def after(value, *others):
    return lax.optimization_barrier((value,) + others)[0]


def in_order(mine, other, place, axis=0):
    first = jnp.where(place == 0, mine, other)
    second = jnp.where(place == 0, other, mine)
    return jnp.concatenate([first, second], axis=axis)


def pick(value, place, axis=0):
    return lax.dynamic_index_in_dim(value, place, axis, keepdims=False)


def fast_body(
    layer_input,
    cotangent,
    token_mask,
    document_ids,
    attn_gain,
    w_query,
    w_key,
    w_value,
    w_output,
    mlp_gain,
    w_gate,
    w_up,
    w_down,
):
    f32, low = jnp.float32, jnp.bfloat16
    y, x, zh, zl, core = (lax.axis_index(name) for name in AXES)
    device = sum(lax.axis_index(name) * BITS[name] for name in AXES)
    quarter, width = layer_input.shape[1:]
    half_len = 2 * quarter
    length = 2 * half_len
    rows = w_query.shape[0]
    units = w_gate.shape[1]
    heads, kvs = HEADS // 2, KV // 2
    cosine, sine = rope_tables(length, HD)

    def halves(weight):
        return weight.reshape(rows, 2, -1)

    masked = cotangent * token_mask.astype(low)[:, :, None]
    qkv = jnp.concatenate([halves(w) for w in (w_query, w_key, w_value)], axis=2)
    qkv = jnp.moveaxis(qkv, 1, 0)
    gate_in, up_in = (
        jnp.transpose(w.reshape(rows, units // 512, 2, 2, 128), (2, 3, 0, 1, 4)).reshape(
            2, 2, rows, -1
        )
        for w in (w_gate, w_up)
    )
    gain = jnp.concatenate([attn_gain, mlp_gain]).astype(f32)
    gain = jnp.broadcast_to(jnp.pad(gain, (0, 128 - 2 * rows)), (8, 128))
    own, normed, pair, mixed, hidden, qkv_w, out_w, gains, seeds, tokens, gate_w, up_w, down_w = (
        first_part(
            heads,
            kvs,
            layer_input,
            masked,
            qkv,
            gate_in,
            up_in,
            w_down,
            w_output,
            gain,
            document_ids[:, None],
            cosine,
            sine,
        )
    )
    qkv_w, out_w = qkv_w.reshape(width, -1), out_w.reshape(-1, width)
    gate_w, up_w = gate_w.reshape(width, -1), up_w.reshape(width, -1)
    down_w = down_w.reshape(-1, width)
    seeds = seeds.reshape(4, half_len, width)
    documents = pick(jnp.where(core == y, document_ids, hop(document_ids, "core")), x)
    row, col = documents[None, :], documents[:, None]
    activated, gate_low, up_low, back_own, back_far, ahead_own, ahead_far = hidden_part(
        tokens, seeds, gate_w, up_w, down_w
    )
    back = hop(back_far, "zl")
    flat_tokens, flat_seeds = tokens.reshape(-1, width), seeds.reshape(-1, width)
    grad_gate = tn(flat_tokens, gate_low).astype(low)
    grad_up = tn(flat_tokens, up_low).astype(low)
    grad_down = tn(activated, flat_seeds).astype(low)
    totals = [
        grad_gate.reshape(4, -1, units // 4),
        grad_up.reshape(4, -1, units // 4),
        grad_down.reshape(4, -1, width),
    ]
    back = after(back, *totals)
    grad_qkv, steep, _, y_low, grad_out_w, gain_two, *sums = attend_behind(
        heads,
        kvs,
        pair,
        mixed,
        hidden,
        seeds[0],
        back_own,
        back,
        ahead_own,
        ahead_far.reshape(2, quarter, width),
        out_w,
        gains,
        cosine,
        sine,
        row,
        col,
        *totals,
    )
    hidden_grads = [None, None]
    hidden_grads[0], hidden_grads[1], grad_down, grad_qkv, grad_output, output, grad_input, gain = (
        sum_tail(
            sums[0].reshape(2, -1, units // 4),
            sums[1].reshape(2, -1, units // 4),
            sums[2].reshape(2, -1, width),
            grad_qkv,
            normed,
            qkv_w,
            own,
            steep,
            gains,
            gain_two,
            grad_out_w.reshape(2, 4, 2, rows, width),
            y_low,
        )
    )
    hidden_grads = [
        jnp.transpose(total.reshape(2, 2, rows, -1, 128), (2, 3, 0, 1, 4)).reshape(rows, units)
        for total in hidden_grads
    ]
    cols = heads * HD

    def columns(start, size):
        return jnp.moveaxis(grad_qkv[:, :, start : start + size], 0, 1).reshape(rows, -1)

    q_grad = columns(0, cols)
    k_grad = columns(cols, kvs * HD)
    v_grad = columns(cols + kvs * HD, kvs * HD)
    gain_one = lax.dynamic_slice_in_dim(gain, device * rows, rows, 1)

    return (
        output,
        grad_input,
        gain_one[0],
        q_grad,
        k_grad,
        v_grad,
        grad_output,
        gain_one[1],
        hidden_grads[0],
        hidden_grads[1],
        grad_down,
    )


def solution(mesh):
    fast = dict(mesh.shape) == {"seq": 4, "batch": 8}
    if fast:
        grid = Mesh(mesh.devices.reshape((2,) * 5), AXES)
        seq, batch = ("y", "x"), ("zh", "zl", "core")
    else:
        grid, seq, batch = mesh, ("seq",), ("batch",)
    weight = P(seq + batch, None)
    gain = P(seq + batch)
    token = P(batch, seq, None)
    return jax.shard_map(
        fast_body if fast else body,
        mesh=grid,
        in_specs=(token, token, P(batch, seq), P(batch, None), gain)
        + (weight,) * 4
        + (gain,)
        + (weight,) * 3,
        out_specs=(token, token, gain) + (weight,) * 4 + (gain,) + (weight,) * 3,
        check_vma=False,
    )
```

```python
import functools
import math

import jax
import jax.numpy as jnp
from jax import lax
from jax.experimental import pallas as pl
from jax.experimental.pallas import tpu as pltpu
from jax.sharding import Mesh
from jax.sharding import PartitionSpec as P

HEADS = 16
KV = 8
HD = 96


EPSILON = 1e-05
ROPE_BASE = 10000.0


def inverse_rms(field):
    return lax.rsqrt(jnp.mean(field * field, axis=-1, keepdims=True) + EPSILON)


def half_turn(field):
    middle = field.shape[-1] // 2
    return jnp.concatenate([-field[..., middle:], field[..., :middle]], axis=-1)


def rope_tables(length, width):
    middle = width // 2
    freqs = ROPE_BASE ** (-2.0 * jnp.arange(middle, dtype=jnp.float32) / width)
    angles = jnp.arange(length, dtype=jnp.float32)[:, None] * freqs[None, :]
    cosine = jnp.concatenate([jnp.cos(angles), jnp.cos(angles)], axis=-1)
    sine = jnp.concatenate([jnp.sin(angles), jnp.sin(angles)], axis=-1)
    return (cosine, sine)


def rotate_ahead(field, cosine, sine):
    return field * cosine[:, None, :] + half_turn(field) * sine[:, None, :]


def rotate_behind(field, cosine, sine):
    return field * cosine[:, None, :] - half_turn(field) * sine[:, None, :]


def outer_sum(left, right):
    return lax.dot_general(
        left, right, (((0,), (0,)), ((), ())), preferred_element_type=jnp.float32
    )


def back_product(left, right):
    return lax.dot_general(
        left, right, (((1,), (1,)), ((), ())), preferred_element_type=jnp.float32
    )


def fetch_attention(attn_gain, w_query, w_key, w_value, w_output):
    return (
        lax.all_gather(attn_gain, ("seq", "batch"), axis=0, tiled=True),
        lax.all_gather(w_query, ("seq", "batch"), axis=0, tiled=True),
        lax.all_gather(w_key, ("seq", "batch"), axis=0, tiled=True),
        lax.all_gather(w_value, ("seq", "batch"), axis=0, tiled=True),
        lax.all_gather(w_output, ("seq", "batch"), axis=0, tiled=True),
    )


def fetch_feedforward(mlp_gain, w_gate, w_up, w_down):
    return (
        lax.all_gather(mlp_gain, ("seq", "batch"), axis=0, tiled=True),
        lax.all_gather(w_gate, ("seq", "batch"), axis=0, tiled=True),
        lax.all_gather(w_up, ("seq", "batch"), axis=0, tiled=True),
        lax.all_gather(w_down, ("seq", "batch"), axis=0, tiled=True),
    )


def block_scores(query_block, keys, documents, start, block, scale):
    length = keys.shape[0]
    scores = (
        jnp.einsum("qjhd,kjd->jhqk", query_block, keys, preferred_element_type=jnp.float32) * scale
    )
    key_pos = jnp.arange(length, dtype=jnp.int32)
    query_pos = start + jnp.arange(block, dtype=jnp.int32)
    query_docs = lax.dynamic_slice_in_dim(documents, start, block, 0)
    allowed = (key_pos[None, :] <= query_pos[:, None]) & (query_docs[:, None] == documents[None, :])
    return jnp.where(allowed[None, None], scores, -1e30)


def attention_forward(queries, keys, values, documents, block, scale):
    length = queries.shape[0]
    count = length // block

    def one_block(index):
        start = index * block
        query_block = lax.dynamic_slice_in_dim(queries, start, block, 0)
        scores = block_scores(query_block, keys, documents, start, block, scale)
        peak_score = jnp.max(scores, axis=-1, keepdims=True)
        weights = jnp.exp(scores - peak_score)
        totals = jnp.sum(weights, axis=-1, keepdims=True)
        probs = (weights / totals).astype(jnp.bfloat16)
        result = jnp.einsum("jhqk,kjd->qjhd", probs, values, preferred_element_type=jnp.float32)
        return (
            result.astype(jnp.bfloat16).reshape(block, -1),
            (peak_score + jnp.log(totals))[..., 0],
        )

    results, sums = lax.map(one_block, jnp.arange(count, dtype=jnp.int32))
    return (results.reshape(length, -1), sums)


def attention_backward(queries, keys, values, documents, sums, grad_out, block, scale):
    length = queries.shape[0]
    count = length // block

    def one_block(carry, member):
        grad_keys, grad_values = carry
        index, sums_block = member
        start = index * block
        query_block = lax.dynamic_slice_in_dim(queries, start, block, 0)
        grad_block = lax.dynamic_slice_in_dim(grad_out, start, block, 0)
        scores = block_scores(query_block, keys, documents, start, block, scale)
        probs = jnp.exp(scores - sums_block[..., None])
        grad_probs = jnp.einsum(
            "qjhd,kjd->jhqk", grad_block, values, preferred_element_type=jnp.float32
        )
        centre = jnp.sum(probs * grad_probs, axis=-1, keepdims=True)
        grad_scores = (probs * (grad_probs - centre)).astype(jnp.bfloat16)
        grad_query = (
            jnp.einsum("jhqk,kjd->qjhd", grad_scores, keys, preferred_element_type=jnp.float32)
            * scale
        )
        grad_keys = (
            grad_keys
            + jnp.einsum(
                "jhqk,qjhd->kjd", grad_scores, query_block, preferred_element_type=jnp.float32
            )
            * scale
        )
        grad_values = grad_values + jnp.einsum(
            "jhqk,qjhd->kjd",
            probs.astype(jnp.bfloat16),
            grad_block,
            preferred_element_type=jnp.float32,
        )
        return ((grad_keys, grad_values), grad_query)

    empty = jnp.zeros(keys.shape, jnp.float32)
    (grad_keys, grad_values), grad_query = lax.scan(
        one_block, (empty, empty), (jnp.arange(count, dtype=jnp.int32), sums)
    )
    return (
        grad_query.reshape(length, queries.shape[1] * queries.shape[2], queries.shape[3]),
        grad_keys,
        grad_values,
    )


def body(
    layer_input,
    cotangent,
    token_mask,
    document_ids,
    attn_gain,
    w_query,
    w_key,
    w_value,
    w_output,
    mlp_gain,
    w_gate,
    w_up,
    w_down,
):
    parts = lax.axis_size("seq")
    micro_count = layer_input.shape[0]
    shard = layer_input.shape[1]
    length = shard * parts
    heads_here = HEADS // parts
    kv_here = max(1, KV // parts)
    copies = parts * kv_here // KV
    per_kv = heads_here // kv_here
    block = min(512, length)
    scale = 1.0 / math.sqrt(HD)
    cosine, sine = rope_tables(length, HD)
    attn_set = None
    mlp_set = None
    attn_total = None
    mlp_total = None
    outputs = []
    input_grads = []
    kept = {
        "normed": [],
        "normed_two": [],
        "activated": [],
        "seed_low": [],
        "gate_low": [],
        "up_low": [],
        "grad_low": [],
        "mixed": [],
        "query_back": [],
        "key_back": [],
        "value_back": [],
    }
    gain_one_total = None
    gain_two_total = None
    for micro in range(micro_count):
        attn_set = fetch_attention(attn_gain, w_query, w_key, w_value, w_output)
        mlp_set = fetch_feedforward(mlp_gain, w_gate, w_up, w_down)
        gain_one = attn_set[0].astype(jnp.float32)
        gain_two = mlp_set[0].astype(jnp.float32)
        documents = document_ids[micro]
        inputs = layer_input[micro].astype(jnp.float32)
        inv_one = inverse_rms(inputs)
        unit_one = inputs * inv_one
        normed = (unit_one * gain_one).astype(jnp.bfloat16)
        queries = jnp.dot(normed, attn_set[1], preferred_element_type=jnp.float32).astype(
            jnp.bfloat16
        )
        keys_lin = jnp.dot(normed, attn_set[2], preferred_element_type=jnp.float32).astype(
            jnp.bfloat16
        )
        values_lin = jnp.dot(normed, attn_set[3], preferred_element_type=jnp.float32).astype(
            jnp.bfloat16
        )
        queries = queries.reshape(shard, parts, heads_here * HD)
        key_slots = jnp.repeat(keys_lin.reshape(shard, KV, HD), copies, axis=1).reshape(
            shard, parts, kv_here * HD
        )
        value_slots = jnp.repeat(values_lin.reshape(shard, KV, HD), copies, axis=1).reshape(
            shard, parts, kv_here * HD
        )
        pairs = jnp.concatenate([key_slots, value_slots], axis=-1)
        query_heads, pair_heads = (
            lax.all_to_all(queries, "seq", split_axis=1, concat_axis=0, tiled=True),
            lax.all_to_all(pairs, "seq", split_axis=1, concat_axis=0, tiled=True),
        )
        query_rot = rotate_ahead(
            query_heads.reshape(length, heads_here, HD).astype(jnp.float32), cosine, sine
        )
        query_rot = query_rot.astype(jnp.bfloat16).reshape(length, kv_here, per_kv, HD)
        key_heads = pair_heads[:, 0, : kv_here * HD].reshape(length, kv_here, HD)
        key_rot = rotate_ahead(key_heads.astype(jnp.float32), cosine, sine).astype(jnp.bfloat16)
        value_heads = pair_heads[:, 0, kv_here * HD :].reshape(length, kv_here, HD)
        attended, sums = attention_forward(query_rot, key_rot, value_heads, documents, block, scale)
        mixed = lax.all_to_all(
            attended.reshape(length, 1, heads_here * HD),
            "seq",
            split_axis=0,
            concat_axis=1,
            tiled=True,
        )
        mixed = mixed.reshape(shard, HEADS * HD)
        hidden_state = inputs + jnp.dot(mixed, attn_set[4], preferred_element_type=jnp.float32)
        inv_two = inverse_rms(hidden_state)
        unit_two = hidden_state * inv_two
        normed_two = (unit_two * gain_two).astype(jnp.bfloat16)
        gate = jnp.dot(normed_two, mlp_set[1], preferred_element_type=jnp.float32)
        upward = jnp.dot(normed_two, mlp_set[2], preferred_element_type=jnp.float32)
        sigma = jax.nn.sigmoid(gate)
        activated = (gate * sigma * upward).astype(jnp.bfloat16)
        output = hidden_state + jnp.dot(activated, mlp_set[3], preferred_element_type=jnp.float32)
        outputs.append(output.astype(jnp.bfloat16))
        seed = cotangent[micro].astype(jnp.float32) * token_mask[micro].astype(jnp.float32)[:, None]
        seed_low = seed.astype(jnp.bfloat16)
        grad_act = back_product(seed_low, mlp_set[3])
        grad_up_low = (grad_act * gate * sigma).astype(jnp.bfloat16)
        grad_gate_low = (grad_act * upward * sigma * (1.0 + gate * (1.0 - sigma))).astype(
            jnp.bfloat16
        )
        grad_normed_two = back_product(grad_gate_low, mlp_set[1]) + back_product(
            grad_up_low, mlp_set[2]
        )
        grad_gain_two = jnp.sum(grad_normed_two * unit_two, axis=0)
        scaled_two = grad_normed_two * gain_two
        grad_hidden = seed + inv_two * (
            scaled_two - unit_two * jnp.mean(scaled_two * unit_two, axis=-1, keepdims=True)
        )
        gain_two_total = grad_gain_two if gain_two_total is None else gain_two_total + grad_gain_two
        kept["normed_two"].append(normed_two)
        kept["activated"].append(activated)
        kept["seed_low"].append(seed_low)
        kept["gate_low"].append(grad_gate_low)
        kept["up_low"].append(grad_up_low)
        grad_low = grad_hidden.astype(jnp.bfloat16)
        grad_mixed = (
            back_product(grad_low, attn_set[4])
            .astype(jnp.bfloat16)
            .reshape(shard, parts, heads_here * HD)
        )
        grad_heads = lax.all_to_all(
            grad_mixed, "seq", split_axis=1, concat_axis=0, tiled=True
        ).reshape(length, kv_here, per_kv, HD)
        grad_query_rot, grad_key_rot, grad_values = attention_backward(
            query_rot, key_rot, value_heads, documents, sums, grad_heads, block, scale
        )
        grad_query_heads = (
            rotate_behind(grad_query_rot, cosine, sine)
            .astype(jnp.bfloat16)
            .reshape(length, 1, heads_here * HD)
        )
        grad_key_heads = rotate_behind(grad_key_rot, cosine, sine)
        grad_pairs = jnp.concatenate(
            [
                grad_key_heads.reshape(length, kv_here * HD),
                grad_values.reshape(length, kv_here * HD),
            ],
            axis=-1,
        )
        query_back = lax.all_to_all(
            grad_query_heads, "seq", split_axis=0, concat_axis=1, tiled=True
        ).reshape(shard, HEADS * HD)
        pair_back = lax.all_to_all(
            grad_pairs.reshape(length, 1, 2 * kv_here * HD).astype(jnp.bfloat16),
            "seq",
            split_axis=0,
            concat_axis=1,
            tiled=True,
        ).astype(jnp.float32)
        key_back = pair_back[:, :, : kv_here * HD].reshape(shard, KV, copies, HD).sum(axis=2)
        value_back = pair_back[:, :, kv_here * HD :].reshape(shard, KV, copies, HD).sum(axis=2)
        key_back = key_back.reshape(shard, KV * HD).astype(jnp.bfloat16)
        value_back = value_back.reshape(shard, KV * HD).astype(jnp.bfloat16)
        grad_normed = (
            back_product(query_back, attn_set[1])
            + back_product(key_back, attn_set[2])
            + back_product(value_back, attn_set[3])
        )
        grad_gain_one = jnp.sum(grad_normed * unit_one, axis=0)
        scaled_one = grad_normed * gain_one
        grad_input = grad_hidden + inv_one * (
            scaled_one - unit_one * jnp.mean(scaled_one * unit_one, axis=-1, keepdims=True)
        )
        input_grads.append(grad_input.astype(jnp.bfloat16))
        gain_one_total = grad_gain_one if gain_one_total is None else gain_one_total + grad_gain_one
        kept["normed"].append(normed)
        kept["mixed"].append(mixed)
        kept["grad_low"].append(grad_low)
        kept["query_back"].append(query_back)
        kept["key_back"].append(key_back)
        kept["value_back"].append(value_back)
    rows = {name: jnp.concatenate(values, axis=0) for name, values in kept.items()}
    attn_total = (
        lax.psum_scatter(gain_one_total, ("seq", "batch"), scatter_dimension=0, tiled=True),
        lax.psum_scatter(
            outer_sum(rows["normed"], rows["query_back"]),
            ("seq", "batch"),
            scatter_dimension=0,
            tiled=True,
        ),
        lax.psum_scatter(
            outer_sum(rows["normed"], rows["key_back"]),
            ("seq", "batch"),
            scatter_dimension=0,
            tiled=True,
        ),
        lax.psum_scatter(
            outer_sum(rows["normed"], rows["value_back"]),
            ("seq", "batch"),
            scatter_dimension=0,
            tiled=True,
        ),
        lax.psum_scatter(
            outer_sum(rows["mixed"], rows["grad_low"]),
            ("seq", "batch"),
            scatter_dimension=0,
            tiled=True,
        ),
    )
    mlp_total = (
        lax.psum_scatter(gain_two_total, ("seq", "batch"), scatter_dimension=0, tiled=True),
        lax.psum_scatter(
            outer_sum(rows["normed_two"], rows["gate_low"]),
            ("seq", "batch"),
            scatter_dimension=0,
            tiled=True,
        ),
        lax.psum_scatter(
            outer_sum(rows["normed_two"], rows["up_low"]),
            ("seq", "batch"),
            scatter_dimension=0,
            tiled=True,
        ),
        lax.psum_scatter(
            outer_sum(rows["activated"], rows["seed_low"]),
            ("seq", "batch"),
            scatter_dimension=0,
            tiled=True,
        ),
    )
    return (
        jnp.stack(outputs, axis=0),
        jnp.stack(input_grads, axis=0),
        attn_total[0],
        attn_total[1],
        attn_total[2],
        attn_total[3],
        attn_total[4],
        mlp_total[0],
        mlp_total[1],
        mlp_total[2],
        mlp_total[3],
    )


AXES = ("y", "x", "zh", "zl", "core")
BITS = {"y": 16, "x": 8, "zh": 4, "zl": 2, "core": 1}
MESH = pl.DeviceIdType.MESH


def coordinates():
    return tuple(lax.axis_index(name) for name in AXES)


def peer(me, *names):
    return tuple(1 - at if name in names else at for name, at in zip(AXES, me))


def greet(me, groups):
    barrier = pltpu.get_barrier_semaphore()
    for names in groups:
        pl.semaphore_signal(barrier, 1, device_id=peer(me, *names), device_id_type=MESH)
    pl.semaphore_wait(barrier, len(groups))


class Mover:
    def __init__(self, me, sends, recvs):
        self.me, self.sends, self.recvs, self.used = me, sends, recvs, 0
        self.started = []

    def next(self):
        number = self.used
        self.used += 1
        assert number < self.sends.shape[0]
        return number

    def copy(self, src, dst, *names, device=None):
        number = self.next()
        return pltpu.make_async_remote_copy(
            src_ref=src,
            dst_ref=dst,
            send_sem=self.sends.at[number],
            recv_sem=self.recvs.at[number],
            device_id=peer(self.me, *names) if device is None else device,
            device_id_type=MESH,
        )

    def later(self, src, dst, *names):
        made = self.copy(src, dst, *names)
        self.started.append(made)
        return made

    def send(self, src, dst, *names):
        made = self.later(src, dst, *names)
        made.start()
        return made

    def local(self, src, dst):
        made = self.quiet(src, dst)
        made.start()
        return made

    def quiet(self, src, dst):
        number = self.next()
        return pltpu.make_async_copy(src, dst, self.recvs.at[number])

    def finish(self):
        for made in self.started:
            made.wait_send()


HEAD_GROUPS = (
    ("core",),
    ("zl",),
    ("zh",),
    ("zh", "zl"),
    ("zl", "core"),
    ("x",),
    ("y",),
    ("y", "core"),
    ("y", "core", "x"),
)
LINE = (("zl",), ("zh",), ("zh", "zl"))


def turn_start(move, me, src, dst):
    y, x, zh, zl, core = me
    stays = y == core
    made = []
    for flip in (1, 0):
        place = x if flip == 0 else 1 - x
        from_, to = src.at[place], dst.at[x]
        copy = move.copy(from_, to, device=(core, place, zh, zl, y))
        if flip == 0:
            own = move.quiet(from_, to)
            pl.when(stays)(own.start)
            pl.when(jnp.logical_not(stays))(copy.start)
            made.append((copy, own))
        else:
            copy.start()
            made.append((copy, None))
    return made


def turn_end(me, made):
    stays = me[0] == me[4]
    for copy, own in made:
        if own is None:
            copy.wait()
        else:
            pl.when(stays)(own.wait)
            pl.when(jnp.logical_not(stays))(copy.wait)


def plane_make(move, ref, s, parts):
    made = []
    for part in parts:
        piece = ref.at[s, ..., part]
        made += [move.later(piece, piece, "x"), move.later(piece, piece, "y")]
    return made


def plane_start(move, ref, s, parts):
    made = plane_make(move, ref, s, parts)
    for one in made:
        one.start()
    return made


def plane_pass(move, made, ref, y, x, parts):
    made[0].wait_recv()
    first = ref.at[2 * y + 1 - x, ..., parts[0]]
    rest = [move.send(first, first, "y")]
    made[3].wait_recv()
    second = ref.at[2 * (1 - y) + x, ..., parts[1]]
    rest.append(move.send(second, second, "x"))
    made[1].wait_recv()
    made[2].wait_recv()
    return rest


def by_rows(count, chunk, work):
    def step(i, carry):
        work(pl.ds(pl.multiple_of(i * chunk, chunk), chunk))
        return carry

    lax.fori_loop(0, count // chunk, step, 0)


class PlaneSum:
    def __init__(self, move, total, held, y, x):
        self.move, self.total = move, total
        self.mid, self.far, self.near, self.last = (held.at[i] for i in range(4))
        self.own = self.far
        half = total.shape[-1] // 2
        self.left, self.right = pl.ds(0, half), pl.ds(half, half)
        self.at = (2 * y + x, 2 * y + 1 - x, 2 * (1 - y) + x, 2 * (1 - y) + 1 - x)

    def start(self):
        move, total, left, right = self.move, self.total, self.left, self.right
        s, sx, sy, sd = self.at
        self.far_moves = [
            move.send(total.at[sd, :, left], self.far.at[:, left], "y"),
            move.send(total.at[sd, :, right], self.far.at[:, right], "x"),
        ]
        self.loads = [
            move.local(total.at[sx, :, left], self.mid.at[:, left]),
            move.local(total.at[sy, :, right], self.mid.at[:, right]),
        ]
        self.own_load = move.quiet(total.at[s], self.own)
        self.near_moves = [
            move.copy(total.at[sy, :, left], self.near.at[:, left], "y"),
            move.copy(total.at[sx, :, right], self.near.at[:, right], "x"),
        ]
        self.last_moves = [
            move.copy(self.mid.at[:, left], self.last.at[:, left], "x"),
            move.copy(self.mid.at[:, right], self.last.at[:, right], "y"),
        ]

    def start_near(self):
        for made in self.near_moves:
            made.start()

    def pass_on(self):
        for made in self.loads:
            made.wait()
        for made in self.far_moves:
            made.wait_recv()
        rows = self.mid.shape[0]
        mid, far = self.mid, self.far

        def work(at):
            added = mid[at, :].astype(jnp.float32) + far[at, :].astype(jnp.float32)
            mid[at, :] = added.astype(jnp.bfloat16)

        by_rows(rows, 16, work)
        for made in self.last_moves:
            made.start()
        self.own_load.start()

    def end(self, write):
        if self.own_load is not None:
            self.own_load.wait()
        for made in self.near_moves + self.last_moves:
            made.wait()
        own, near, last = self.own, self.near, self.last

        def work(at):
            value = own[at, :].astype(jnp.float32) + near[at, :].astype(jnp.float32)
            write(at, value + last[at, :].astype(jnp.float32))

        by_rows(own.shape[0], 16, work)


class PlaneSumHere(PlaneSum):
    def __init__(self, move, total, held, y, x):
        self.move, self.total = move, total
        self.far, self.near, self.last = (held.at[i] for i in range(3))
        half = total.shape[-1] // 2
        self.left, self.right = left, right = pl.ds(0, half), pl.ds(half, half)
        self.at = s, sx, sy, sd = (2 * y + x, 2 * y + 1 - x, 2 * (1 - y) + x, 3 - 2 * y - x)
        self.own, self.mids = total.at[s], (total.at[sx], total.at[sy])
        self.far_moves = [
            move.later(total.at[sd, :, left], self.far.at[:, left], "y"),
            move.later(total.at[sd, :, right], self.far.at[:, right], "x"),
        ]
        self.near_moves = [
            move.copy(total.at[sy, :, left], self.near.at[:, left], "y"),
            move.copy(total.at[sx, :, right], self.near.at[:, right], "x"),
        ]
        self.last_moves = [
            move.copy(total.at[sx, :, left], self.last.at[:, left], "x"),
            move.copy(total.at[sy, :, right], self.last.at[:, right], "y"),
        ]
        self.own_load = None

    def start(self):
        for made in self.far_moves:
            made.start()

    def pass_on(self):
        for made in self.far_moves:
            made.wait_recv()
        far = self.far

        def work(at):
            for mid, part in zip(self.mids, (self.left, self.right)):
                added = mid[at, part].astype(jnp.float32) + far[at, part].astype(jnp.float32)
                mid[at, part] = added.astype(jnp.bfloat16)

        by_rows(far.shape[0], 16, work)
        for made in self.last_moves:
            made.start()


def tail_kernel(
    gate_in,
    up_in,
    down_in,
    grad_in,
    normed,
    qkv_w,
    x_own,
    steep,
    gain_rows,
    gain_two,
    out_in,
    y_in,
    gate_out,
    up_out,
    down_out,
    qkv_out,
    out_out,
    y_out,
    x_out,
    gain_out,
    pair_low,
    pair_got,
    down_low,
    down_got,
    quarter,
    part,
    part_got,
    x_low,
    qkv_in,
    qkv_held,
    qkv_sum,
    qkv_low,
    qkv_got,
    out_got,
    out_x,
    out_line,
    out_line_got,
    rows_sent,
    gain_got,
    sends,
    recvs,
):
    f32, low = jnp.float32, jnp.bfloat16
    me = coordinates()
    y, x, zh, zl, core = me
    z = 2 * zh + zl
    mine = y == core
    other = jnp.logical_not(mine)
    greet(me, HEAD_GROUPS)
    move = Mover(me, sends, recvs)
    qkv = PlaneSumHere(move, qkv_in, qkv_held, y, x)
    out_y = move.copy(out_in, out_got, "y")
    half_len = part.shape[0]
    block_rows = qkv_in.shape[1]

    def weigh(at):
        lanes = pl.ds(pl.multiple_of(at * block_rows, 128), block_rows)
        total = tn(normed[0, :, lanes], grad_in[pl.ds(0, half_len), :])
        total = total + tn(normed[1, :, lanes], grad_in[pl.ds(half_len, half_len), :])
        qkv_in[at] = total.astype(low)

    weigh(qkv.at[3])
    qkv.start()

    weigh(qkv.at[1])
    weigh(qkv.at[2])
    qkv.start_near()

    pair_rows = pair_got.shape[1]

    def lower(src, dst, skip, count):
        def work(at):
            dst[at, :] = src[skip, at, :].astype(low)

        by_rows(count, 32, work)

    pairs = []
    for i, src in enumerate((gate_in, up_in)):
        lower(src, pair_low.at[i], 1 - zh, pair_rows)
        pairs.append(move.send(pair_low.at[i], pair_got.at[i], "zh"))
    lower(down_in, down_low, 1 - zh, down_low.shape[0])
    pairs.append(move.send(down_low, down_got, "zh"))

    theirs, ours = (pl.multiple_of(c * half_len, half_len) for c in (1 - core, core))

    def project(start):
        for i in range(half_len // QB):
            at = pl.ds(pl.multiple_of(start + i * QB, QB), QB)
            part[pl.ds(i * QB, QB), :] = nt(grad_in[at, :], qkv_w[...])

    project(theirs)
    part_move = move.copy(part, part_got, "core")
    part_move.start()
    weigh(qkv.at[0])
    qkv.pass_on()
    pl.when(other)(out_y.start)
    y_turn = turn_start(move, me, y_in, y_out)
    part_move.wait()
    project(ours)
    gain_out[...] = jnp.zeros_like(gain_out)
    gain_out[1:2, :] = gain_two[...]
    piece = half_len // 2
    for q in range(2):

        def norm_back(at, q=q):
            every = pl.ds(pl.multiple_of(q * piece + at.start, 16), at.size)
            grad = part[every, :] + part_got[every, :]
            field = x_own[q, at, :].astype(f32)
            inverse = lax.rsqrt(jnp.mean(field * field, axis=1, keepdims=True) + EPSILON)
            unit = field * inverse
            gain_out[0:1, :] += jnp.sum(grad * unit, axis=0, keepdims=True)
            scaled = grad * gain_rows[0:1, :]
            centre = jnp.mean(scaled * unit, axis=1, keepdims=True)
            value = steep[every, :] + inverse * (scaled - unit * centre)
            x_low[q, at, :] = value.astype(low)

        by_rows(piece, 16, norm_back)
    x_turn = turn_start(move, me, x_low, x_out)

    gain_moves = [
        move.copy(gain_out, gain_got.at[turn], name)
        for turn, name in enumerate(("core", "x", "y", "zl", "zh"))
    ]

    def gain_round(turn):
        if turn > 0:
            gain_moves[turn - 1].wait()
            gain_out[...] = gain_out[...] + gain_got[turn - 1]
        if turn < len(gain_moves):
            gain_moves[turn].start()

    gain_round(0)
    out_shape = out_in.shape
    blocks = [(a, b) for a in range(out_shape[1]) for b in range(out_shape[2])]

    def keep(at, value):
        qkv_sum[at, :] = value
        qkv_low[at, :] = value.astype(low)

    qkv.end(keep)
    count = qkv_got.shape[1]
    line = []
    for k, names in enumerate(LINE):
        to = z ^ (1, 2, 3)[k]
        start = pl.multiple_of(to * count, count)
        line.append(move.send(qkv_low.at[pl.ds(start, count)], qkv_got.at[k], *names))

    gain_round(1)

    out_x_move = move.copy(out_got.at[1 - x], out_x, "x")

    @pl.when(mine)
    def _():
        out_y.wait_recv()

        def half(at_x):
            def work(i, carry):
                a, b = i // out_shape[2], i % out_shape[2]
                value = out_in[at_x, a, b].astype(f32) + out_got[at_x, a, b].astype(f32)
                out_got[at_x, a, b] = value.astype(low)
                return carry

            lax.fori_loop(0, len(blocks), work, 0)

        half(1 - x)
        out_x_move.start()
        half(x)

    gain_round(2)

    spread = []
    for i, (src, dst) in enumerate(((gate_in, gate_out), (up_in, up_out))):
        pairs[i].wait_recv()
        got, full = pair_got.at[i], quarter.at[i]

        def work(at, src=src, got=got, full=full):
            full[at, :] = src[zh, at, :] + got[at, :].astype(f32)

        by_rows(pair_rows, 32, work)
        share = pair_rows // 4
        for names in (("core",), ("zl",), ("zl", "core")):
            to_zl = 1 - zl if "zl" in names else zl
            to_core = 1 - core if "core" in names else core
            start = pl.multiple_of((2 * to_zl + to_core) * share, share)
            spread.append(move.send(full.at[pl.ds(start, share)], dst.at[zl, core], *names))
        start = pl.multiple_of((2 * zl + core) * share, share)
        dst[zl, core] = full[pl.ds(start, share), :]
    pairs[2].wait_recv()

    def work(at):
        down_out[at, :] = down_in[zh, at, :] + down_got[at, :].astype(f32)

    by_rows(down_out.shape[0], 32, work)

    gain_round(3)
    out_moves = []
    for k, names in enumerate(LINE):
        to = z ^ (1, 2, 3)[k]
        out_moves.append(move.copy(out_line.at[to], out_line_got.at[k], *names))

    @pl.when(mine)
    def _():
        out_x_move.wait()

        def work(i, carry):
            a, b = i // out_shape[2], i % out_shape[2]
            value = out_got[x, a, b].astype(f32) + out_x[a, b].astype(f32)
            out_line[a, b] = value.astype(low)
            return carry

        lax.fori_loop(0, len(blocks), work, 0)
        for made in out_moves:
            made.start()

    gain_round(4)
    for made in line:
        made.wait_recv()
    start = pl.multiple_of(z * count, count)
    total = qkv_sum[pl.ds(start, count), :]
    for k in range(3):
        total = total + qkv_got[k].astype(f32)
    rows = count // 2
    qkv_sum[pl.ds(0, count), :] = total
    theirs = pl.multiple_of((1 - core) * rows, rows)
    swap = move.send(qkv_sum.at[pl.ds(theirs, rows)], qkv_out.at[core], "core")
    qkv_out[core] = qkv_sum[pl.ds(pl.multiple_of(core * rows, rows), rows), :]

    out_swap = move.copy(rows_sent, out_out, "core")

    @pl.when(mine)
    def _():
        for made in out_moves:
            made.wait()
        for at in range(2):
            total = out_line[z, at].astype(f32)
            for k in range(3):
                total = total + out_line_got[k, at].astype(f32)

            @pl.when(core == at)
            def _(total=total):
                out_out[...] = total

            @pl.when(core != at)
            def _(total=total):
                rows_sent[...] = total

        out_swap.start()
        out_swap.wait_send()

    @pl.when(other)
    def _():
        out_y.wait_send()
        out_swap.wait_recv()

    gain_round(5)
    turn_end(me, y_turn)
    turn_end(me, x_turn)
    swap.wait_recv()
    for made in spread:
        made.wait_recv()
    move.finish()


def sum_tail(gate, up, down, grad, normed, qkv_w, x_own, steep, gain_rows, gain_two, out, y_in):
    f32, low = jnp.float32, jnp.bfloat16
    hbm = pl.BlockSpec(memory_space=pl.ANY)
    vmem = pl.BlockSpec(memory_space=pltpu.VMEM)
    wide, width = gate.shape[-1], grad.shape[-1]
    rows = out.shape[-2]
    half_len = steep.shape[0]
    pair_rows, down_rows = gate.shape[1], down.shape[1]
    return pl.pallas_call(
        tail_kernel,
        in_specs=[vmem] * 11 + [hbm],
        out_specs=[vmem] * 5 + [hbm, hbm, vmem],
        out_shape=[
            jax.ShapeDtypeStruct((2, 2, rows, wide), f32),
            jax.ShapeDtypeStruct((2, 2, rows, wide), f32),
            jax.ShapeDtypeStruct((down_rows, width), f32),
            jax.ShapeDtypeStruct((2, rows, width), f32),
            jax.ShapeDtypeStruct((rows, width), f32),
            jax.ShapeDtypeStruct(y_in.shape, low),
            jax.ShapeDtypeStruct(y_in.shape, low),
            jax.ShapeDtypeStruct((2, width), f32),
        ],
        input_output_aliases={},
        scratch_shapes=[
            pltpu.VMEM((2, pair_rows, wide), low),
            pltpu.VMEM((2, pair_rows, wide), low),
            pltpu.VMEM((down_rows, width), low),
            pltpu.VMEM((down_rows, width), low),
            pltpu.VMEM((2, pair_rows, wide), f32),
            pltpu.VMEM((half_len, width), f32),
            pltpu.VMEM((half_len, width), f32),
            pltpu.VMEM(y_in.shape, low),
            pltpu.VMEM((4, 8 * rows, width), low),
            pltpu.VMEM((3, 8 * rows, width), low),
            pltpu.VMEM((8 * rows, width), f32),
            pltpu.VMEM((8 * rows, width), low),
            pltpu.VMEM((3, 2 * rows, width), low),
            pltpu.VMEM(out.shape, low),
            pltpu.VMEM(out.shape[1:], low),
            pltpu.VMEM(out.shape[1:], low),
            pltpu.VMEM((3,) + out.shape[2:], low),
            pltpu.VMEM((rows, width), f32),
            pltpu.VMEM((5, 2, width), f32),
            pltpu.SemaphoreType.DMA((48,)),
            pltpu.SemaphoreType.DMA((48,)),
        ],
        compiler_params=pltpu.CompilerParams(
            collective_id=4, has_side_effects=True, vmem_limit_bytes=63 << 20
        ),
        name="tail",
    )(gate, up, down, grad, normed, qkv_w, x_own, steep, gain_rows, gain_two, out, y_in)


QB = 256
SPAN = 768


def turned(field, back):
    middle = HD // 2
    left, right = field[:, :middle], field[:, middle:]
    if back:
        return jnp.concatenate([right, -left], axis=1)
    return jnp.concatenate([-right, left], axis=1)


def spun(field, cosine, sine, back=False):
    field = field.astype(jnp.float32)
    return field * cosine + turned(field, back) * sine


def nt(left, right):
    return lax.dot_general(left, right, (((1,), (1,)), ((), ())), preferred_element_type=jnp.float32)


def nn(left, right):
    return jnp.dot(left, right, preferred_element_type=jnp.float32)


def tn(left, right):
    return lax.dot_general(left, right, (((0,), (0,)), ((), ())), preferred_element_type=jnp.float32)


def head(ref, rows, number):
    return ref[rows, HD * number : HD * (number + 1)]


def ahead_block(
    heads, kvs, step, size, qkv_ref, cos_ref, sin_ref, row_ref, col_ref, out_ref, keys
):
    low, f32 = jnp.bfloat16, jnp.float32
    start, base = step * QB, (step + 1) * QB - size
    if not isinstance(step, int):
        start, base = pl.multiple_of(start, QB), pl.multiple_of(base, QB)
    here, span = pl.ds(start, QB), pl.ds(base, size)
    key_place = base + lax.broadcasted_iota(jnp.int32, (size, QB), 0)
    place = start + lax.broadcasted_iota(jnp.int32, (size, QB), 1)
    allowed = (key_place <= place) & (col_ref[span, :] == row_ref[:, here])
    bias = jnp.where(allowed, 0.0, -1e30).astype(f32)
    scale = (1.0 / math.sqrt(HD)) * math.log2(math.e)
    cosine, sine = cos_ref[here, :], sin_ref[here, :]
    results = []
    for h in range(heads):
        j = h * kvs // heads
        query = spun(head(qkv_ref, here, h), cosine, sine).astype(low)
        scores = nt(keys[j, span, :], query) * scale + bias
        peak = jnp.max(scores, axis=0, keepdims=True)
        weights = jnp.exp2(scores - peak)
        total = jnp.sum(weights, axis=0, keepdims=True)
        probs = (weights * (1.0 / total)).astype(low)
        results.append(tn(probs, head(qkv_ref, span, heads + kvs + j)).astype(low))
    out_ref[here, :] = jnp.concatenate(results, axis=1)


def behind_block(
    heads,
    kvs,
    step,
    size,
    qkv_ref,
    grad_ref,
    cos_ref,
    sin_ref,
    row_ref,
    col_ref,
    gq_ref,
    keys,
    gks,
    gvs,
):
    low, f32 = jnp.bfloat16, jnp.float32
    start, base = step * QB, (step + 1) * QB - size
    if not isinstance(step, int):
        start, base = pl.multiple_of(start, QB), pl.multiple_of(base, QB)
    here, span = pl.ds(start, QB), pl.ds(base, size)
    key_place = base + lax.broadcasted_iota(jnp.int32, (size, QB), 0)
    place = start + lax.broadcasted_iota(jnp.int32, (size, QB), 1)
    allowed = (key_place <= place) & (col_ref[span, :] == row_ref[:, here])
    bias = jnp.where(allowed, 0.0, -1e30).astype(f32)
    width = 1.0 / math.sqrt(HD)
    scale = width * math.log2(math.e)
    cosine, sine = cos_ref[here, :], sin_ref[here, :]
    results = []
    for h in range(heads):
        j = h * kvs // heads
        query = spun(head(qkv_ref, here, h), cosine, sine).astype(low)
        key, value = keys[j, span, :], head(qkv_ref, span, heads + kvs + j)
        grad = head(grad_ref, here, h)
        scores = nt(key, query) * scale + bias
        peak = jnp.max(scores, axis=0, keepdims=True)
        weights = jnp.exp2(scores - peak)
        total = jnp.sum(weights, axis=0, keepdims=True)
        probs = weights * (1.0 / total)
        slope = nt(value, grad)
        centre = jnp.sum(probs * slope, axis=0, keepdims=True)
        gs = (probs * (slope - centre)).astype(low)
        gvs[j, span, :] += nn(probs.astype(low), grad)
        gks[j, span, :] += nn(gs, query)
        results.append(spun(tn(gs, key) * width, cosine, sine, True).astype(low))
    gq_ref[here, : HD * heads] = jnp.concatenate(results, axis=1)


def behind_kernel(
    heads,
    kvs,
    hidden,
    seed,
    back_own,
    gain_rows,
    cos_ref,
    sin_ref,
    row_ref,
    col_ref,
    qkv_in,
    mixed_in,
    out_in,
    back_far,
    ahead_own,
    ahead_far,
    tokens,
    seeds,
    act_in,
    gate_in,
    up_in,
    grad_ref,
    steep,
    gain_ref,
    y_low,
    out_grad,
    gate_out,
    up_out,
    down_out,
    steep_low,
    back_got,
    ahead_got,
    gate_sum,
    up_sum,
    down_sum,
    gate_held,
    up_held,
    down_held,
    sends,
    recvs,
):
    f32, low = jnp.float32, jnp.bfloat16
    me = coordinates()
    y, x, zh, zl, core = me
    greet(me, (("x",), ("y",), ("core",), ("zl",)))
    move = Mover(me, sends, recvs)
    back_move = move.send(back_far, back_got, "zl")
    ahead_move = move.later(ahead_far, ahead_got, "zl")
    swap = move.later(steep_low.at[core], steep_low.at[core], "core")
    gate, up, down = sums = [
        PlaneSumHere(move, total, held, y, x)
        for total, held in (
            (gate_sum, gate_held), (up_sum, up_held), (down_sum, down_held)
        )
    ]
    s, sx, sy, sd = gate.at
    order = (sd, sx, sy, s)
    half_len, width = hidden.shape
    count, wide = gate_in.shape
    block = gate_sum.shape[1]

    def wide_part(gates, ups, pieces):
        def column(i):
            lanes = pl.ds(pl.multiple_of(order[i] * block, 128), block)
            return move.quiet(tokens.at[:, lanes], pieces.at[i % 2])

        columns = [column(i) for i in range(4)]
        columns[0].start()
        loads = [move.local(gate_in, gates), move.local(up_in, ups)]
        for i in range(4):
            columns[i].wait()
            if i < 3:
                columns[i + 1].start()
            if i == 0:
                loads[0].wait()
            gate_sum[order[i]] = tn(pieces[i % 2], gates[...]).astype(low)
            if i == 0:
                gate.start()
                loads[1].wait()
            up_sum[order[i]] = tn(pieces[i % 2], ups[...]).astype(low)
            if i == 0:
                up.start()
            if i == 2:
                gate.start_near()
                up.start_near()

    pl.run_scoped(
        wide_part,
        pltpu.VMEM((count, wide), low),
        pltpu.VMEM((count, wide), low),
        pltpu.VMEM((2, count, block), low),
    )
    deep = down_sum.shape[1]

    def deep_part(rows, pieces):
        def column(i):
            lanes = pl.ds(pl.multiple_of(order[i] * deep, 128), deep)
            return move.quiet(act_in.at[:, lanes], pieces.at[i % 2])

        columns = [column(i) for i in range(4)]
        columns[0].start()
        move.local(seeds, rows).wait()
        for i in range(4):
            columns[i].wait()
            if i < 3:
                columns[i + 1].start()
            down_sum[order[i]] = tn(pieces[i % 2], rows[...]).astype(low)
            if i == 0:
                down.start()
            if i == 2:
                down.start_near()

    pl.run_scoped(
        deep_part,
        pltpu.VMEM((count, width), low),
        pltpu.VMEM((2, count, deep), low),
    )
    gate.pass_on()
    up.pass_on()

    def heads_part(qkv_ref, out_w, keys, gks, gvs):
        loads = [move.local(qkv_in, qkv_ref), move.local(out_in, out_w)]
        gain_ref[...] = jnp.zeros_like(gain_ref)
        back_move.wait_recv()
        ahead_move.start()

        def norm_back(at):
            grad = back_own[at, :] + back_got[at, :].astype(f32)
            field = hidden[at, :]
            inverse = lax.rsqrt(jnp.mean(field * field, axis=1, keepdims=True) + EPSILON)
            unit = field * inverse
            gain_ref[...] += jnp.sum(grad * unit, axis=0, keepdims=True)
            scaled = grad * gain_rows[1:2, :]
            centre = jnp.mean(scaled * unit, axis=1, keepdims=True)
            value = seed[at, :].astype(f32) + inverse * (scaled - unit * centre)
            steep[at, :] = value
            steep_low[core, at, :] = value.astype(low)

        by_rows(half_len, 16, norm_back)
        swap.start()
        for made in loads:
            made.wait()
        everything = pl.ds(0, 2 * half_len)
        for j in range(kvs):
            keys[j] = spun(
                head(qkv_ref, everything, heads + j), cos_ref[...], sin_ref[...]
            ).astype(low)
        gks[...] = jnp.zeros_like(gks)
        gvs[...] = jnp.zeros_like(gvs)
        swap.wait_recv()
        per = half_len // QB
        for i in range(2 * per):
            at = pl.ds(i % per * QB, QB)
            part = nt(steep_low[i // per, at, :], out_w[...]).astype(low)
            grad_ref[pl.ds(i * QB, QB), : heads * HD] = part
        down.pass_on()

        def work(step, size):
            behind_block(
                heads, kvs, step, size, qkv_ref, grad_ref, cos_ref, sin_ref, row_ref, col_ref,
                grad_ref, keys, gks, gvs,
            )

        def one(step, carry):
            work(step, SPAN)
            return carry

        for step in range(SPAN // QB - 1):
            work(step, (step + 1) * QB)
        lax.fori_loop(SPAN // QB - 1, 2 * half_len // QB, one, 0)
        scale = 1.0 / math.sqrt(HD)
        gk = [
            spun(gks[j] * scale, cos_ref[...], sin_ref[...], True).astype(low)
            for j in range(kvs)
        ]
        gv = [gvs[j].astype(low) for j in range(kvs)]
        grad_ref[:, HD * heads :] = jnp.concatenate(gk + gv, axis=1)

    pl.run_scoped(
        heads_part,
        pltpu.VMEM(qkv_in.shape, low),
        pltpu.VMEM(out_in.shape, low),
        pltpu.VMEM((kvs, 2 * half_len, HD), low),
        pltpu.VMEM((kvs, 2 * half_len, HD), f32),
        pltpu.VMEM((kvs, 2 * half_len, HD), f32),
    )

    def last_part(mixed, own, out_made, gate_made, up_made, down_made):
        loads = [move.local(mixed_in, mixed), move.local(ahead_own, own)]
        loads[0].wait()
        rows = mixed.shape[1] // 4
        for i in range(4):
            lanes = pl.ds(i * rows, rows)
            total = tn(mixed[pl.ds(0, half_len), lanes], steep_low[0])
            total = total + tn(mixed[pl.ds(half_len, half_len), lanes], steep_low[1])
            out_made[pl.ds(i * rows, rows), :] = total.astype(low)
        stores = [move.local(out_made, out_grad)]
        ahead_move.wait_recv()
        loads[1].wait()
        quarter = half_len // 2
        for q in range(2):

            def add(at, q=q):
                every = pl.ds(pl.multiple_of(q * quarter + at.start, 16), at.size)
                value = hidden[every, :] + own[every, :] + ahead_got[q, at, :].astype(f32)
                ahead_got[q, at, :] = value.astype(low)

            by_rows(quarter, 16, add)
        stores.append(move.local(ahead_got, y_low))
        for plane, made, out in zip(
            sums, (gate_made, up_made, down_made), (gate_out, up_out, down_out)
        ):

            def write(at, value, made=made):
                made[at, :] = value

            plane.end(write)
            stores.append(move.local(made, out))
        for made in stores:
            made.wait()

    pl.run_scoped(
        last_part,
        pltpu.VMEM(mixed_in.shape, low),
        pltpu.VMEM((half_len, width), f32),
        pltpu.VMEM(out_grad.shape, low),
        pltpu.VMEM(gate_out.shape, f32),
        pltpu.VMEM(up_out.shape, f32),
        pltpu.VMEM(down_out.shape, f32),
    )
    move.finish()


def attend_behind(heads, kvs, *operands):
    f32, low = jnp.float32, jnp.bfloat16
    half_len, width = operands[0].shape
    length = 2 * half_len
    wide = operands[-1].shape[1]
    hbm = pl.BlockSpec(memory_space=pl.ANY)
    vmem = pl.BlockSpec(memory_space=pltpu.VMEM)
    shapes = [(width // 4, wide), (width // 4, wide), (wide // 4, width)]

    def made(*shape, dtype=low):
        return jax.ShapeDtypeStruct(shape, dtype)

    return pl.pallas_call(
        functools.partial(behind_kernel, heads, kvs),
        in_specs=[vmem] * 8 + [hbm] * 11,
        out_specs=[vmem] * 3 + [hbm] * 5,
        out_shape=[
            made(length, width),
            made(half_len, width, dtype=f32),
            made(1, width, dtype=f32),
            made(2, half_len // 2, width),
            made(heads * HD, width),
        ]
        + [made(*shape, dtype=f32) for shape in shapes],
        scratch_shapes=[
            pltpu.VMEM((2, half_len, width), low),
            pltpu.VMEM((half_len, width), low),
            pltpu.VMEM((2, half_len // 2, width), low),
        ]
        + [pltpu.VMEM((4,) + shape, low) for shape in shapes]
        + [pltpu.VMEM((3,) + shape, low) for shape in shapes]
        + [pltpu.SemaphoreType.DMA((64,)), pltpu.SemaphoreType.DMA((64,))],
        compiler_params=pltpu.CompilerParams(
            collective_id=3, has_side_effects=True, vmem_limit_bytes=63 << 20
        ),
        cost_estimate=pl.CostEstimate(
            flops=10 * heads * length * SPAN * HD,
            bytes_accessed=9 << 20,
            transcendentals=heads * length * SPAN,
        ),
        name="behind",
    )(*operands)


def bands(size):
    return (pl.ds(0, size // 2), pl.ds(size // 2, size // 2))


def first_kernel(
    heads,
    kvs,
    x_in,
    g_in,
    qkv_in,
    gate_in,
    up_in,
    down_in,
    out_in,
    gain_in,
    docs_in,
    cos_ref,
    sin_ref,
    x_own,
    normed,
    qkv,
    mixed,
    hidden,
    qkv_w,
    out_w,
    gain_rows,
    seeds,
    tokens,
    gate_w,
    up_w,
    down_w,
    docs,
    row,
    col,
    gains,
    keys,
    part,
    part_got,
    sends,
    recvs,
):
    f32, low = jnp.float32, jnp.bfloat16
    me = coordinates()
    y, x, zh, zl, core = me
    s, z = y * 2 + x, zh * 2 + zl
    mine = y == core
    other = jnp.logical_not(mine)
    width = qkv_w.shape[-1]
    length = qkv.shape[0]
    half_len = length // 2
    greet(me, HEAD_GROUPS)
    move = Mover(me, sends, recvs)

    wides = [
        (ref.at[:, at], bands(ref.shape[-1]))
        for at in (zh, 1 - zh)
        for ref in (gate_w, up_w, down_w)
    ]
    hops = [plane_make(move, ref, s, parts) for ref, parts in wides]
    rest = []

    def start_some(which):
        for i in which:
            for made in hops[i]:
                made.start()

    def pass_some(which):
        for i in which:
            rest.extend(plane_pass(move, hops[i], wides[i][0], y, x, wides[i][1]))

    down_own = move.local(down_in, down_w.at[s, zh])
    own = [
        move.local(qkv_in.at[core], qkv_w.at[s, z, core]),
        move.local(gain_in, gains.at[s, z, core]),
    ]
    first = [
        move.send(qkv_in.at[1 - core], qkv_w.at[s, z, core], "core"),
        move.send(gain_in, gains.at[s, z, core], "core"),
    ]
    docs_move = move.send(docs_in, docs, "core")
    x_turn = turn_start(move, me, x_in, x_own)
    for made in own:
        made.wait()
    for made in first:
        made.wait_recv()
    line = [move.send(gains.at[s, z], gains.at[s, z], *names) for names in LINE]
    line += [move.send(qkv_w.at[s, z], qkv_w.at[s, z], *names) for names in LINE]
    down_own.wait()
    start_some((2,))

    own = [
        move.local(gate_in.at[zl, core], gate_w.at[s, zh, zl, core]),
        move.local(up_in.at[zl, core], up_w.at[s, zh, zl, core]),
    ]
    spread = []
    for src, dst in ((gate_in, gate_w), (up_in, up_w)):
        for names in (("core",), ("zl",), ("zl", "core")):
            to_zl = 1 - zl if "zl" in names else zl
            to_core = 1 - core if "core" in names else core
            spread.append(move.send(src.at[to_zl, to_core], dst.at[s, zh, zl, core], *names))
    out_own = move.quiet(out_in, out_w.at[x, z, core])
    out_sent = move.copy(out_in, out_w.at[x, z, core], "core")
    pl.when(mine)(out_own.start)
    pl.when(other)(out_sent.start)

    for made in line[:3]:
        made.wait_recv()
    gain_hops = [move.send(gains.at[s], gains.at[s], *names) for names in (("x",), ("y",))]
    turn_end(me, x_turn)
    gain_hops[0].wait_recv()
    sx = 2 * y + 1 - x
    gain_hops.append(move.send(gains.at[sx], gains.at[sx], "y"))
    for made in line[3:]:
        made.wait_recv()
    qkv_hops = plane_start(move, qkv_w, s, bands(width))
    pass_some((2,))

    out_line = [move.copy(out_w.at[x, z], out_w.at[x, z], *names) for names in LINE]
    pl.when(other)(out_sent.wait_send)

    @pl.when(mine)
    def _():
        out_own.wait()
        out_sent.wait_recv()
        for made in out_line:
            made.start()

    for made in own:
        made.wait()
    for made in spread:
        made.wait_recv()
    pairs = [
        move.send(ref.at[s, zh], ref.at[s, zh], "zh") for ref in (gate_w, up_w, down_w)
    ]

    for made in gain_hops[1:]:
        made.wait_recv()
    count = out_in.shape[0]
    for i in range(2):
        gain_rows[pl.ds(i, 1), :] = jnp.concatenate(
            [
                gains[a, b, c, 0:1, i * count : (i + 1) * count]
                for a in range(4)
                for b in range(4)
                for c in range(2)
            ],
            axis=1,
        )

    quarter = half_len // 2
    for q in range(2):

        def norm(at, q=q):
            field = x_own[q, at, :].astype(f32)
            inverse = lax.rsqrt(jnp.mean(field * field, axis=1, keepdims=True) + EPSILON)
            rows = pl.ds(pl.multiple_of(q * quarter + at.start, 16), at.size)
            normed[core, rows, :] = (field * inverse * gain_rows[0:1, :]).astype(low)

        by_rows(quarter, 16, norm)
    normed_move = move.send(normed.at[core], normed.at[core], "core")
    docs_move.wait_recv()
    row[...] = jnp.where(mine, docs_in[x], docs[x])
    col[...] = jnp.transpose(jnp.broadcast_to(row[...], (8, length)))[:, 0:1]

    qkv_rest = plane_pass(move, qkv_hops, qkv_w, y, x, bands(width))
    out_x = move.copy(out_w.at[x], out_w.at[x], "x")
    out_y = [move.copy(out_w.at[at], out_w.at[at], "y") for at in (x, 1 - x)]

    @pl.when(mine)
    def _():
        for made in out_line:
            made.wait()
        out_x.start()
        out_y[0].start()

    g_turn = turn_start(move, me, g_in, seeds.at[0])
    normed_move.wait_recv()
    for made in qkv_rest:
        made.wait_recv()
    weight = qkv_w.reshape(width, width)
    for i in range(length // QB):
        at = pl.ds(i * QB % half_len, QB)
        qkv[pl.ds(i * QB, QB), :] = nn(normed[i * QB // half_len, at, :], weight[...]).astype(low)
    start_some((0,))
    seed_moves = [
        move.later(seeds.at[0], seeds.at[1], "core"),
        move.later(seeds.at[0], seeds.at[2], "zl"),
    ]

    everything = pl.ds(0, length)
    for j in range(kvs):
        keys[j] = spun(head(qkv, everything, heads + j), cos_ref[...], sin_ref[...]).astype(low)

    def work(step, size):
        ahead_block(heads, kvs, step, size, qkv, cos_ref, sin_ref, row, col, mixed, keys)

    def block(step, carry):
        @pl.when(step == SPAN // QB - 1)
        def _():
            turn_end(me, g_turn)
            for made in seed_moves:
                made.start()
            start_some((1,))

        @pl.when(step == SPAN // QB)
        def _():
            pairs[0].wait_recv()
            start_some((3,))

        work(step, SPAN)
        return carry

    work(0, QB)

    @pl.when(mine)
    def _():
        out_x.wait_recv()
        out_y[1].start()

    for step in range(1, SPAN // QB - 1):
        work(step, (step + 1) * QB)
    lax.fori_loop(SPAN // QB - 1, length // QB, block, 0)
    for made in pairs[1:]:
        made.wait_recv()
    start_some((4, 5))

    @pl.when(mine)
    def _():
        out_x.wait_send()
        for made in out_y:
            made.wait_send()

    @pl.when(other)
    def _():
        for made in out_y:
            made.wait_recv()

    out_weight = out_w.reshape(width // 2, width)
    theirs, ours = (pl.multiple_of(c * half_len, half_len) for c in (1 - core, core))

    def project(start):
        for i in range(half_len // QB):
            at = pl.ds(pl.multiple_of(start + i * QB, QB), QB)
            part[pl.ds(i * QB, QB), :] = nn(mixed[at, :], out_weight[...])

    project(theirs)
    part_move = move.copy(part, part_got, "core")
    part_move.start()
    for i in range(half_len // QB):
        at = pl.ds(pl.multiple_of(ours + i * QB, QB), QB)
        hidden[pl.ds(i * QB, QB), :] = nn(mixed[at, :], out_weight[...])
    part_move.wait()
    for q in range(2):

        def norm(at, q=q):
            rows = pl.ds(pl.multiple_of(q * quarter + at.start, 16), at.size)
            field = x_own[q, at, :].astype(f32) + (hidden[rows, :] + part_got[rows, :])
            hidden[rows, :] = field
            inverse = lax.rsqrt(jnp.mean(field * field, axis=1, keepdims=True) + EPSILON)
            tokens[0, rows, :] = (field * inverse * gain_rows[1:2, :]).astype(low)

        by_rows(quarter, 16, norm)
    token_moves = [
        move.send(tokens.at[0], tokens.at[2], "zl"),
        move.send(tokens.at[0], tokens.at[1], "core"),
    ]
    pass_some((0, 1))
    seed_moves[1].wait_recv()
    seed_moves.append(move.send(seeds.at[2], seeds.at[3], "core"))
    pass_some((3, 4, 5))
    token_moves[0].wait_recv()
    token_moves.append(move.send(tokens.at[2], tokens.at[3], "core"))
    for made in rest + seed_moves[::2] + token_moves[1:]:
        made.wait_recv()
    move.finish()


def first_part(heads, kvs, x_in, g_in, qkv, gate, up, down, out, gain, docs, cosine, sine):
    f32, low = jnp.float32, jnp.bfloat16
    rows, width = out.shape
    half_len = 2 * x_in.shape[1]
    length = 2 * half_len
    hbm = pl.BlockSpec(memory_space=pl.ANY)
    vmem = pl.BlockSpec(memory_space=pltpu.VMEM)

    def made(shape, dtype=low):
        return jax.ShapeDtypeStruct(shape, dtype)

    return pl.pallas_call(
        functools.partial(first_kernel, heads, kvs),
        in_specs=[hbm] * 8 + [vmem] * 3,
        out_specs=[vmem] * 9 + [vmem] + [hbm] * 3,
        out_shape=[
            made(x_in.shape),
            made((2, half_len, width)),
            made((length, width)),
            made((length, heads * HD)),
            made((half_len, width), f32),
            made((4, 4, 2) + qkv.shape[1:]),
            made((2, 4, 2) + out.shape),
            made((2, width), f32),
            made((4,) + x_in.shape),
            made((4, half_len, width)),
            made((4, 2, 2, 2) + gate.shape[2:]),
            made((4, 2, 2, 2) + up.shape[2:]),
            made((4, 2) + down.shape),
        ],
        scratch_shapes=[
            pltpu.VMEM(docs.shape, docs.dtype),
            pltpu.VMEM(docs.shape[1:], docs.dtype),
            pltpu.VMEM(docs.shape[:0:-1], docs.dtype),
            pltpu.VMEM((4, 4, 2) + gain.shape, f32),
            pltpu.VMEM((kvs, length, HD), low),
            pltpu.VMEM((half_len, width), f32),
            pltpu.VMEM((half_len, width), f32),
            pltpu.SemaphoreType.DMA((96,)),
            pltpu.SemaphoreType.DMA((96,)),
        ],
        compiler_params=pltpu.CompilerParams(
            collective_id=1, has_side_effects=True, vmem_limit_bytes=60 << 20
        ),
        name="first",
    )(x_in, g_in, qkv, gate, up, down, out, gain, docs, cosine, sine)


def hidden_kernel(
    tokens,
    seeds,
    gate_w,
    up_w,
    down_w,
    act_out,
    gate_out,
    up_out,
    back_own,
    back_far,
    ahead_own,
    ahead_far,
    backs,
    aheads,
    back_got,
    ahead_got,
    sends,
    recvs,
):
    f32, low = jnp.float32, jnp.bfloat16
    me = coordinates()
    move = Mover(me, sends, recvs)

    @pl.when(pl.program_id(0) == 0)
    def _():
        greet(me, (("core",),))

    half_len = backs.shape[1]
    per = half_len // QB
    i = pl.program_id(0)
    moves = [
        (
            move.copy(backs.at[1], back_got.at[turn], "core"),
            move.copy(aheads.at[1], ahead_got.at[turn], "core"),
        )
        for turn in range(2)
    ]

    def fold(turn, back_ref, ahead_ref):
        for made in moves[turn]:
            made.wait()

        def work(at):
            back_ref[at, :] = (backs[0, at, :] + back_got[turn, at, :]).astype(back_ref.dtype)
            ahead_ref[at, :] = (aheads[0, at, :] + ahead_got[turn, at, :]).astype(ahead_ref.dtype)

        by_rows(half_len, 16, work)

    slot = 3 - i // per
    rows = pl.ds(pl.multiple_of(i % per * QB, QB), QB)
    token, seed = tokens[...], seeds[...]
    gate, upward = nn(token, gate_w[...]), nn(token, up_w[...])
    sigma = 1.0 / (1.0 + jnp.exp(-gate))
    silu = gate * sigma
    activated = (silu * upward).astype(low)
    act_out[...] = activated
    grad = nt(seed, down_w[...])
    up_low = (grad * silu).astype(low)
    gate_low = (grad * upward * sigma * (1.0 + gate * (1.0 - sigma))).astype(low)
    up_out[...] = up_low
    gate_out[...] = gate_low
    aheads[slot % 2, rows, :] = nn(activated, down_w[...])
    backs[slot % 2, rows, :] = nt(gate_low, gate_w[...]) + nt(up_low, up_w[...])
    for turn in range(2):

        @pl.when(i == (2 * turn + 1) * per - 1)
        def _(turn=turn):
            for made in moves[turn]:
                made.start()

    @pl.when(i == 2 * per - 1)
    def _():
        fold(0, back_far, ahead_far)

    @pl.when(i == 4 * per - 1)
    def _():
        fold(1, back_own, ahead_own)


def hidden_part(tokens, seeds, gate_w, up_w, down_w):
    f32, low = jnp.float32, jnp.bfloat16
    half_len, width = tokens.shape[1:]
    wide = gate_w.shape[1]
    per = half_len // QB
    vmem = pl.BlockSpec(memory_space=pltpu.VMEM)

    def banded(columns):
        return pl.BlockSpec((QB, columns), lambda i: ((3 - i // per) * per + i % per, 0))

    def made(rows, columns, dtype=low):
        return jax.ShapeDtypeStruct((rows, columns), dtype)

    return pl.pallas_call(
        hidden_kernel,
        grid=(4 * per,),
        in_specs=[banded(width)] * 2 + [vmem] * 3,
        out_specs=[banded(wide)] * 3 + [vmem] * 4,
        out_shape=[made(4 * half_len, wide)] * 3
        + [
            made(half_len, width, f32),
            made(half_len, width),
            made(half_len, width, f32),
            made(half_len, width),
        ],
        scratch_shapes=[
            pltpu.VMEM((2, half_len, width), f32),
            pltpu.VMEM((2, half_len, width), f32),
            pltpu.VMEM((2, half_len, width), f32),
            pltpu.VMEM((2, half_len, width), f32),
            pltpu.SemaphoreType.DMA((4,)),
            pltpu.SemaphoreType.DMA((4,)),
        ],
        compiler_params=pltpu.CompilerParams(
            collective_id=2, has_side_effects=True, vmem_limit_bytes=63 << 20
        ),
        cost_estimate=pl.CostEstimate(
            flops=2 * 6 * 4 * half_len * width * wide,
            bytes_accessed=40 << 20,
            transcendentals=4 * half_len * wide,
        ),
        name="hidden",
    )(tokens.reshape(-1, width), seeds.reshape(-1, width), gate_w, up_w, down_w)


def hop(value, *names):
    flip = sum(BITS[name] for name in names)
    return lax.ppermute(value, AXES, [(i, i ^ flip) for i in range(32)])


def after(value, *others):
    return lax.optimization_barrier((value,) + others)[0]


def in_order(mine, other, place, axis=0):
    first = jnp.where(place == 0, mine, other)
    second = jnp.where(place == 0, other, mine)
    return jnp.concatenate([first, second], axis=axis)


def pick(value, place, axis=0):
    return lax.dynamic_index_in_dim(value, place, axis, keepdims=False)


def fast_body(
    layer_input,
    cotangent,
    token_mask,
    document_ids,
    attn_gain,
    w_query,
    w_key,
    w_value,
    w_output,
    mlp_gain,
    w_gate,
    w_up,
    w_down,
):
    f32, low = jnp.float32, jnp.bfloat16
    y, x, zh, zl, core = (lax.axis_index(name) for name in AXES)
    device = sum(lax.axis_index(name) * BITS[name] for name in AXES)
    quarter, width = layer_input.shape[1:]
    half_len = 2 * quarter
    length = 2 * half_len
    rows = w_query.shape[0]
    units = w_gate.shape[1]
    heads, kvs = HEADS // 2, KV // 2
    cosine, sine = rope_tables(length, HD)

    def halves(weight):
        return weight.reshape(rows, 2, -1)

    masked = cotangent * token_mask.astype(low)[:, :, None]
    qkv = jnp.concatenate([halves(w) for w in (w_query, w_key, w_value)], axis=2)
    qkv = jnp.moveaxis(qkv, 1, 0)
    gate_in, up_in = (
        jnp.transpose(w.reshape(rows, units // 512, 2, 2, 128), (2, 3, 0, 1, 4)).reshape(
            2, 2, rows, -1
        )
        for w in (w_gate, w_up)
    )
    gain = jnp.concatenate([attn_gain, mlp_gain]).astype(f32)
    gain = jnp.broadcast_to(jnp.pad(gain, (0, 128 - 2 * rows)), (8, 128))
    own, normed, pair, mixed, hidden, qkv_w, out_w, gains, seeds, tokens, gate_w, up_w, down_w = (
        first_part(
            heads,
            kvs,
            layer_input,
            masked,
            qkv,
            gate_in,
            up_in,
            w_down,
            w_output,
            gain,
            document_ids[:, None],
            cosine,
            sine,
        )
    )
    qkv_w, out_w = qkv_w.reshape(width, -1), out_w.reshape(-1, width)
    gate_w, up_w = gate_w.reshape(width, -1), up_w.reshape(width, -1)
    down_w = down_w.reshape(-1, width)
    seeds = seeds.reshape(4, half_len, width)
    documents = pick(jnp.where(core == y, document_ids, hop(document_ids, "core")), x)
    row, col = documents[None, :], documents[:, None]
    activated, gate_low, up_low, back_own, back_far, ahead_own, ahead_far = hidden_part(
        tokens, seeds, gate_w, up_w, down_w
    )
    grad_qkv, steep, gain_two, y_low, grad_out_w, *sums = attend_behind(
        heads,
        kvs,
        hidden,
        seeds[0],
        back_own,
        gains,
        cosine,
        sine,
        row,
        col,
        pair,
        mixed,
        out_w,
        back_far,
        ahead_own,
        ahead_far.reshape(2, quarter, width),
        tokens.reshape(-1, width),
        seeds.reshape(-1, width),
        activated,
        gate_low,
        up_low,
    )
    hidden_grads = [None, None]
    hidden_grads[0], hidden_grads[1], grad_down, grad_qkv, grad_output, output, grad_input, gain = (
        sum_tail(
            sums[0].reshape(2, -1, units // 4),
            sums[1].reshape(2, -1, units // 4),
            sums[2].reshape(2, -1, width),
            grad_qkv,
            normed,
            qkv_w,
            own,
            steep,
            gains,
            gain_two,
            grad_out_w.reshape(2, 4, 2, rows, width),
            y_low,
        )
    )
    hidden_grads = [
        jnp.transpose(total.reshape(2, 2, rows, -1, 128), (2, 3, 0, 1, 4)).reshape(rows, units)
        for total in hidden_grads
    ]
    cols = heads * HD

    def columns(start, size):
        return jnp.moveaxis(grad_qkv[:, :, start : start + size], 0, 1).reshape(rows, -1)

    q_grad = columns(0, cols)
    k_grad = columns(cols, kvs * HD)
    v_grad = columns(cols + kvs * HD, kvs * HD)
    gain_one = lax.dynamic_slice_in_dim(gain, device * rows, rows, 1)

    return (
        output,
        grad_input,
        gain_one[0],
        q_grad,
        k_grad,
        v_grad,
        grad_output,
        gain_one[1],
        hidden_grads[0],
        hidden_grads[1],
        grad_down,
    )


def solution(mesh):
    fast = dict(mesh.shape) == {"seq": 4, "batch": 8}
    if fast:
        grid = Mesh(mesh.devices.reshape((2,) * 5), AXES)
        seq, batch = ("y", "x"), ("zh", "zl", "core")
    else:
        grid, seq, batch = mesh, ("seq",), ("batch",)
    weight = P(seq + batch, None)
    gain = P(seq + batch)
    token = P(batch, seq, None)
    return jax.shard_map(
        fast_body if fast else body,
        mesh=grid,
        in_specs=(token, token, P(batch, seq), P(batch, None), gain)
        + (weight,) * 4
        + (gain,)
        + (weight,) * 3,
        out_specs=(token, token, gain) + (weight,) * 4 + (gain,) + (weight,) * 3,
        check_vma=False,
    )
```

```python
import functools
import math

import jax
import jax.numpy as jnp
import numpy as np
from jax import lax
from jax.experimental import pallas as pl
from jax.experimental.pallas import tpu as pltpu
from jax.sharding import Mesh
from jax.sharding import PartitionSpec as P

HEADS = 16
KV = 8
HD = 96


EPSILON = 1e-05
ROPE_BASE = 10000.0


def inverse_rms(field):
    return lax.rsqrt(jnp.mean(field * field, axis=-1, keepdims=True) + EPSILON)


def half_turn(field):
    middle = field.shape[-1] // 2
    return jnp.concatenate([-field[..., middle:], field[..., :middle]], axis=-1)


def rope_tables(length, width):
    middle = width // 2
    freqs = ROPE_BASE ** (-2.0 * jnp.arange(middle, dtype=jnp.float32) / width)
    angles = jnp.arange(length, dtype=jnp.float32)[:, None] * freqs[None, :]
    cosine = jnp.concatenate([jnp.cos(angles), jnp.cos(angles)], axis=-1)
    sine = jnp.concatenate([jnp.sin(angles), jnp.sin(angles)], axis=-1)
    return (cosine, sine)


def rotate_ahead(field, cosine, sine):
    return field * cosine[:, None, :] + half_turn(field) * sine[:, None, :]


def rotate_behind(field, cosine, sine):
    return field * cosine[:, None, :] - half_turn(field) * sine[:, None, :]


def outer_sum(left, right):
    return lax.dot_general(
        left, right, (((0,), (0,)), ((), ())), preferred_element_type=jnp.float32
    )


def back_product(left, right):
    return lax.dot_general(
        left, right, (((1,), (1,)), ((), ())), preferred_element_type=jnp.float32
    )


def fetch_attention(attn_gain, w_query, w_key, w_value, w_output):
    return (
        lax.all_gather(attn_gain, ("seq", "batch"), axis=0, tiled=True),
        lax.all_gather(w_query, ("seq", "batch"), axis=0, tiled=True),
        lax.all_gather(w_key, ("seq", "batch"), axis=0, tiled=True),
        lax.all_gather(w_value, ("seq", "batch"), axis=0, tiled=True),
        lax.all_gather(w_output, ("seq", "batch"), axis=0, tiled=True),
    )


def fetch_feedforward(mlp_gain, w_gate, w_up, w_down):
    return (
        lax.all_gather(mlp_gain, ("seq", "batch"), axis=0, tiled=True),
        lax.all_gather(w_gate, ("seq", "batch"), axis=0, tiled=True),
        lax.all_gather(w_up, ("seq", "batch"), axis=0, tiled=True),
        lax.all_gather(w_down, ("seq", "batch"), axis=0, tiled=True),
    )


def block_scores(query_block, keys, documents, start, block, scale):
    length = keys.shape[0]
    scores = (
        jnp.einsum("qjhd,kjd->jhqk", query_block, keys, preferred_element_type=jnp.float32) * scale
    )
    key_pos = jnp.arange(length, dtype=jnp.int32)
    query_pos = start + jnp.arange(block, dtype=jnp.int32)
    query_docs = lax.dynamic_slice_in_dim(documents, start, block, 0)
    allowed = (key_pos[None, :] <= query_pos[:, None]) & (query_docs[:, None] == documents[None, :])
    return jnp.where(allowed[None, None], scores, -1e30)


def attention_forward(queries, keys, values, documents, block, scale):
    length = queries.shape[0]
    count = length // block

    def one_block(index):
        start = index * block
        query_block = lax.dynamic_slice_in_dim(queries, start, block, 0)
        scores = block_scores(query_block, keys, documents, start, block, scale)
        peak_score = jnp.max(scores, axis=-1, keepdims=True)
        weights = jnp.exp(scores - peak_score)
        totals = jnp.sum(weights, axis=-1, keepdims=True)
        probs = (weights / totals).astype(jnp.bfloat16)
        result = jnp.einsum("jhqk,kjd->qjhd", probs, values, preferred_element_type=jnp.float32)
        return (
            result.astype(jnp.bfloat16).reshape(block, -1),
            (peak_score + jnp.log(totals))[..., 0],
        )

    results, sums = lax.map(one_block, jnp.arange(count, dtype=jnp.int32))
    return (results.reshape(length, -1), sums)


def attention_backward(queries, keys, values, documents, sums, grad_out, block, scale):
    length = queries.shape[0]
    count = length // block

    def one_block(carry, member):
        grad_keys, grad_values = carry
        index, sums_block = member
        start = index * block
        query_block = lax.dynamic_slice_in_dim(queries, start, block, 0)
        grad_block = lax.dynamic_slice_in_dim(grad_out, start, block, 0)
        scores = block_scores(query_block, keys, documents, start, block, scale)
        probs = jnp.exp(scores - sums_block[..., None])
        grad_probs = jnp.einsum(
            "qjhd,kjd->jhqk", grad_block, values, preferred_element_type=jnp.float32
        )
        centre = jnp.sum(probs * grad_probs, axis=-1, keepdims=True)
        grad_scores = (probs * (grad_probs - centre)).astype(jnp.bfloat16)
        grad_query = (
            jnp.einsum("jhqk,kjd->qjhd", grad_scores, keys, preferred_element_type=jnp.float32)
            * scale
        )
        grad_keys = (
            grad_keys
            + jnp.einsum(
                "jhqk,qjhd->kjd", grad_scores, query_block, preferred_element_type=jnp.float32
            )
            * scale
        )
        grad_values = grad_values + jnp.einsum(
            "jhqk,qjhd->kjd",
            probs.astype(jnp.bfloat16),
            grad_block,
            preferred_element_type=jnp.float32,
        )
        return ((grad_keys, grad_values), grad_query)

    empty = jnp.zeros(keys.shape, jnp.float32)
    (grad_keys, grad_values), grad_query = lax.scan(
        one_block, (empty, empty), (jnp.arange(count, dtype=jnp.int32), sums)
    )
    return (
        grad_query.reshape(length, queries.shape[1] * queries.shape[2], queries.shape[3]),
        grad_keys,
        grad_values,
    )


def body(
    layer_input,
    cotangent,
    token_mask,
    document_ids,
    attn_gain,
    w_query,
    w_key,
    w_value,
    w_output,
    mlp_gain,
    w_gate,
    w_up,
    w_down,
):
    parts = lax.axis_size("seq")
    micro_count = layer_input.shape[0]
    shard = layer_input.shape[1]
    length = shard * parts
    heads_here = HEADS // parts
    kv_here = max(1, KV // parts)
    copies = parts * kv_here // KV
    per_kv = heads_here // kv_here
    block = min(512, length)
    scale = 1.0 / math.sqrt(HD)
    cosine, sine = rope_tables(length, HD)
    attn_set = None
    mlp_set = None
    attn_total = None
    mlp_total = None
    outputs = []
    input_grads = []
    kept = {
        "normed": [],
        "normed_two": [],
        "activated": [],
        "seed_low": [],
        "gate_low": [],
        "up_low": [],
        "grad_low": [],
        "mixed": [],
        "query_back": [],
        "key_back": [],
        "value_back": [],
    }
    gain_one_total = None
    gain_two_total = None
    for micro in range(micro_count):
        attn_set = fetch_attention(attn_gain, w_query, w_key, w_value, w_output)
        mlp_set = fetch_feedforward(mlp_gain, w_gate, w_up, w_down)
        gain_one = attn_set[0].astype(jnp.float32)
        gain_two = mlp_set[0].astype(jnp.float32)
        documents = document_ids[micro]
        inputs = layer_input[micro].astype(jnp.float32)
        inv_one = inverse_rms(inputs)
        unit_one = inputs * inv_one
        normed = (unit_one * gain_one).astype(jnp.bfloat16)
        queries = jnp.dot(normed, attn_set[1], preferred_element_type=jnp.float32).astype(
            jnp.bfloat16
        )
        keys_lin = jnp.dot(normed, attn_set[2], preferred_element_type=jnp.float32).astype(
            jnp.bfloat16
        )
        values_lin = jnp.dot(normed, attn_set[3], preferred_element_type=jnp.float32).astype(
            jnp.bfloat16
        )
        queries = queries.reshape(shard, parts, heads_here * HD)
        key_slots = jnp.repeat(keys_lin.reshape(shard, KV, HD), copies, axis=1).reshape(
            shard, parts, kv_here * HD
        )
        value_slots = jnp.repeat(values_lin.reshape(shard, KV, HD), copies, axis=1).reshape(
            shard, parts, kv_here * HD
        )
        pairs = jnp.concatenate([key_slots, value_slots], axis=-1)
        query_heads, pair_heads = (
            lax.all_to_all(queries, "seq", split_axis=1, concat_axis=0, tiled=True),
            lax.all_to_all(pairs, "seq", split_axis=1, concat_axis=0, tiled=True),
        )
        query_rot = rotate_ahead(
            query_heads.reshape(length, heads_here, HD).astype(jnp.float32), cosine, sine
        )
        query_rot = query_rot.astype(jnp.bfloat16).reshape(length, kv_here, per_kv, HD)
        key_heads = pair_heads[:, 0, : kv_here * HD].reshape(length, kv_here, HD)
        key_rot = rotate_ahead(key_heads.astype(jnp.float32), cosine, sine).astype(jnp.bfloat16)
        value_heads = pair_heads[:, 0, kv_here * HD :].reshape(length, kv_here, HD)
        attended, sums = attention_forward(query_rot, key_rot, value_heads, documents, block, scale)
        mixed = lax.all_to_all(
            attended.reshape(length, 1, heads_here * HD),
            "seq",
            split_axis=0,
            concat_axis=1,
            tiled=True,
        )
        mixed = mixed.reshape(shard, HEADS * HD)
        hidden_state = inputs + jnp.dot(mixed, attn_set[4], preferred_element_type=jnp.float32)
        inv_two = inverse_rms(hidden_state)
        unit_two = hidden_state * inv_two
        normed_two = (unit_two * gain_two).astype(jnp.bfloat16)
        gate = jnp.dot(normed_two, mlp_set[1], preferred_element_type=jnp.float32)
        upward = jnp.dot(normed_two, mlp_set[2], preferred_element_type=jnp.float32)
        sigma = jax.nn.sigmoid(gate)
        activated = (gate * sigma * upward).astype(jnp.bfloat16)
        output = hidden_state + jnp.dot(activated, mlp_set[3], preferred_element_type=jnp.float32)
        outputs.append(output.astype(jnp.bfloat16))
        seed = cotangent[micro].astype(jnp.float32) * token_mask[micro].astype(jnp.float32)[:, None]
        seed_low = seed.astype(jnp.bfloat16)
        grad_act = back_product(seed_low, mlp_set[3])
        grad_up_low = (grad_act * gate * sigma).astype(jnp.bfloat16)
        grad_gate_low = (grad_act * upward * sigma * (1.0 + gate * (1.0 - sigma))).astype(
            jnp.bfloat16
        )
        grad_normed_two = back_product(grad_gate_low, mlp_set[1]) + back_product(
            grad_up_low, mlp_set[2]
        )
        grad_gain_two = jnp.sum(grad_normed_two * unit_two, axis=0)
        scaled_two = grad_normed_two * gain_two
        grad_hidden = seed + inv_two * (
            scaled_two - unit_two * jnp.mean(scaled_two * unit_two, axis=-1, keepdims=True)
        )
        gain_two_total = grad_gain_two if gain_two_total is None else gain_two_total + grad_gain_two
        kept["normed_two"].append(normed_two)
        kept["activated"].append(activated)
        kept["seed_low"].append(seed_low)
        kept["gate_low"].append(grad_gate_low)
        kept["up_low"].append(grad_up_low)
        grad_low = grad_hidden.astype(jnp.bfloat16)
        grad_mixed = (
            back_product(grad_low, attn_set[4])
            .astype(jnp.bfloat16)
            .reshape(shard, parts, heads_here * HD)
        )
        grad_heads = lax.all_to_all(
            grad_mixed, "seq", split_axis=1, concat_axis=0, tiled=True
        ).reshape(length, kv_here, per_kv, HD)
        grad_query_rot, grad_key_rot, grad_values = attention_backward(
            query_rot, key_rot, value_heads, documents, sums, grad_heads, block, scale
        )
        grad_query_heads = (
            rotate_behind(grad_query_rot, cosine, sine)
            .astype(jnp.bfloat16)
            .reshape(length, 1, heads_here * HD)
        )
        grad_key_heads = rotate_behind(grad_key_rot, cosine, sine)
        grad_pairs = jnp.concatenate(
            [
                grad_key_heads.reshape(length, kv_here * HD),
                grad_values.reshape(length, kv_here * HD),
            ],
            axis=-1,
        )
        query_back = lax.all_to_all(
            grad_query_heads, "seq", split_axis=0, concat_axis=1, tiled=True
        ).reshape(shard, HEADS * HD)
        pair_back = lax.all_to_all(
            grad_pairs.reshape(length, 1, 2 * kv_here * HD).astype(jnp.bfloat16),
            "seq",
            split_axis=0,
            concat_axis=1,
            tiled=True,
        ).astype(jnp.float32)
        key_back = pair_back[:, :, : kv_here * HD].reshape(shard, KV, copies, HD).sum(axis=2)
        value_back = pair_back[:, :, kv_here * HD :].reshape(shard, KV, copies, HD).sum(axis=2)
        key_back = key_back.reshape(shard, KV * HD).astype(jnp.bfloat16)
        value_back = value_back.reshape(shard, KV * HD).astype(jnp.bfloat16)
        grad_normed = (
            back_product(query_back, attn_set[1])
            + back_product(key_back, attn_set[2])
            + back_product(value_back, attn_set[3])
        )
        grad_gain_one = jnp.sum(grad_normed * unit_one, axis=0)
        scaled_one = grad_normed * gain_one
        grad_input = grad_hidden + inv_one * (
            scaled_one - unit_one * jnp.mean(scaled_one * unit_one, axis=-1, keepdims=True)
        )
        input_grads.append(grad_input.astype(jnp.bfloat16))
        gain_one_total = grad_gain_one if gain_one_total is None else gain_one_total + grad_gain_one
        kept["normed"].append(normed)
        kept["mixed"].append(mixed)
        kept["grad_low"].append(grad_low)
        kept["query_back"].append(query_back)
        kept["key_back"].append(key_back)
        kept["value_back"].append(value_back)
    rows = {name: jnp.concatenate(values, axis=0) for name, values in kept.items()}
    attn_total = (
        lax.psum_scatter(gain_one_total, ("seq", "batch"), scatter_dimension=0, tiled=True),
        lax.psum_scatter(
            outer_sum(rows["normed"], rows["query_back"]),
            ("seq", "batch"),
            scatter_dimension=0,
            tiled=True,
        ),
        lax.psum_scatter(
            outer_sum(rows["normed"], rows["key_back"]),
            ("seq", "batch"),
            scatter_dimension=0,
            tiled=True,
        ),
        lax.psum_scatter(
            outer_sum(rows["normed"], rows["value_back"]),
            ("seq", "batch"),
            scatter_dimension=0,
            tiled=True,
        ),
        lax.psum_scatter(
            outer_sum(rows["mixed"], rows["grad_low"]),
            ("seq", "batch"),
            scatter_dimension=0,
            tiled=True,
        ),
    )
    mlp_total = (
        lax.psum_scatter(gain_two_total, ("seq", "batch"), scatter_dimension=0, tiled=True),
        lax.psum_scatter(
            outer_sum(rows["normed_two"], rows["gate_low"]),
            ("seq", "batch"),
            scatter_dimension=0,
            tiled=True,
        ),
        lax.psum_scatter(
            outer_sum(rows["normed_two"], rows["up_low"]),
            ("seq", "batch"),
            scatter_dimension=0,
            tiled=True,
        ),
        lax.psum_scatter(
            outer_sum(rows["activated"], rows["seed_low"]),
            ("seq", "batch"),
            scatter_dimension=0,
            tiled=True,
        ),
    )
    return (
        jnp.stack(outputs, axis=0),
        jnp.stack(input_grads, axis=0),
        attn_total[0],
        attn_total[1],
        attn_total[2],
        attn_total[3],
        attn_total[4],
        mlp_total[0],
        mlp_total[1],
        mlp_total[2],
        mlp_total[3],
    )


AXES = ("y", "x", "zh", "zl", "core")
BITS = {"y": 16, "x": 8, "zh": 4, "zl": 2, "core": 1}
MESH = pl.DeviceIdType.MESH


def coordinates():
    return tuple(lax.axis_index(name) for name in AXES)


def peer(me, *names):
    return tuple(1 - at if name in names else at for name, at in zip(AXES, me))


def greet(me, groups):
    barrier = pltpu.get_barrier_semaphore()
    for names in groups:
        pl.semaphore_signal(barrier, 1, device_id=peer(me, *names), device_id_type=MESH)
    pl.semaphore_wait(barrier, len(groups))


class Mover:
    def __init__(self, me, sends, recvs):
        self.me, self.sends, self.recvs, self.used = me, sends, recvs, 0
        self.started = []

    def next(self):
        number = self.used
        self.used += 1
        assert number < self.sends.shape[0]
        return number

    def copy(self, src, dst, *names, device=None):
        number = self.next()
        return pltpu.make_async_remote_copy(
            src_ref=src,
            dst_ref=dst,
            send_sem=self.sends.at[number],
            recv_sem=self.recvs.at[number],
            device_id=peer(self.me, *names) if device is None else device,
            device_id_type=MESH,
        )

    def later(self, src, dst, *names):
        made = self.copy(src, dst, *names)
        self.started.append(made)
        return made

    def send(self, src, dst, *names):
        made = self.later(src, dst, *names)
        made.start()
        return made

    def local(self, src, dst):
        made = self.quiet(src, dst)
        made.start()
        return made

    def quiet(self, src, dst):
        number = self.next()
        return pltpu.make_async_copy(src, dst, self.recvs.at[number])

    def finish(self):
        for made in self.started:
            made.wait_send()


HEAD_GROUPS = (
    ("core",),
    ("zl",),
    ("zh",),
    ("zh", "zl"),
    ("zl", "core"),
    ("x",),
    ("y",),
    ("y", "core"),
    ("y", "core", "x"),
)
LINE = (("zl",), ("zh",), ("zh", "zl"))


def turn_start(move, me, src, dst):
    y, x, zh, zl, core = me
    stays = y == core
    made = []
    for flip in (1, 0):
        place = x if flip == 0 else 1 - x
        from_, to = src.at[place], dst.at[x]
        copy = move.copy(from_, to, device=(core, place, zh, zl, y))
        if flip == 0:
            own = move.quiet(from_, to)
            pl.when(stays)(own.start)
            pl.when(jnp.logical_not(stays))(copy.start)
            made.append((copy, own))
        else:
            copy.start()
            made.append((copy, None))
    return made


def turn_end(me, made):
    stays = me[0] == me[4]
    for copy, own in made:
        if own is None:
            copy.wait()
        else:
            pl.when(stays)(own.wait)
            pl.when(jnp.logical_not(stays))(copy.wait)


def plane_make(move, ref, s, parts):
    made = []
    for part in parts:
        piece = ref.at[s, ..., part]
        made += [move.later(piece, piece, "x"), move.later(piece, piece, "y")]
    return made


def plane_start(move, ref, s, parts):
    made = plane_make(move, ref, s, parts)
    for one in made:
        one.start()
    return made


def plane_pass(move, made, ref, y, x, parts):
    made[0].wait_recv()
    first = ref.at[2 * y + 1 - x, ..., parts[0]]
    rest = [move.send(first, first, "y")]
    made[3].wait_recv()
    second = ref.at[2 * (1 - y) + x, ..., parts[1]]
    rest.append(move.send(second, second, "x"))
    made[1].wait_recv()
    made[2].wait_recv()
    return rest


def by_rows(count, chunk, work):
    def step(i, carry):
        work(pl.ds(pl.multiple_of(i * chunk, chunk), chunk))
        return carry

    lax.fori_loop(0, count // chunk, step, 0)


class PlaneSum:
    def __init__(self, move, total, held, y, x):
        self.move, self.total = move, total
        self.mid, self.far, self.near, self.last = (held.at[i] for i in range(4))
        self.own = self.far
        half = total.shape[-1] // 2
        self.left, self.right = pl.ds(0, half), pl.ds(half, half)
        self.at = (2 * y + x, 2 * y + 1 - x, 2 * (1 - y) + x, 2 * (1 - y) + 1 - x)

    def start(self):
        move, total, left, right = self.move, self.total, self.left, self.right
        s, sx, sy, sd = self.at
        self.far_moves = [
            move.send(total.at[sd, :, left], self.far.at[:, left], "y"),
            move.send(total.at[sd, :, right], self.far.at[:, right], "x"),
        ]
        self.loads = [
            move.local(total.at[sx, :, left], self.mid.at[:, left]),
            move.local(total.at[sy, :, right], self.mid.at[:, right]),
        ]
        self.own_load = move.quiet(total.at[s], self.own)
        self.near_moves = [
            move.copy(total.at[sy, :, left], self.near.at[:, left], "y"),
            move.copy(total.at[sx, :, right], self.near.at[:, right], "x"),
        ]
        self.last_moves = [
            move.copy(self.mid.at[:, left], self.last.at[:, left], "x"),
            move.copy(self.mid.at[:, right], self.last.at[:, right], "y"),
        ]

    def start_near(self):
        for made in self.near_moves:
            made.start()

    def pass_on(self):
        for made in self.loads:
            made.wait()
        for made in self.far_moves:
            made.wait_recv()
        rows = self.mid.shape[0]
        mid, far = self.mid, self.far

        def work(at):
            added = mid[at, :].astype(jnp.float32) + far[at, :].astype(jnp.float32)
            mid[at, :] = added.astype(jnp.bfloat16)

        by_rows(rows, 16, work)
        for made in self.last_moves:
            made.start()
        self.own_load.start()

    def end(self, write):
        if self.own_load is not None:
            self.own_load.wait()
        for made in self.near_moves + self.last_moves:
            made.wait()
        own, near, last = self.own, self.near, self.last

        def work(at):
            value = own[at, :].astype(jnp.float32) + near[at, :].astype(jnp.float32)
            write(at, value + last[at, :].astype(jnp.float32))

        by_rows(own.shape[0], 16, work)


class PlaneSumHere(PlaneSum):
    def __init__(self, move, total, held, y, x):
        self.move, self.total = move, total
        self.far, self.near, self.last = (held.at[i] for i in range(3))
        half = total.shape[-1] // 2
        self.left, self.right = left, right = pl.ds(0, half), pl.ds(half, half)
        self.at = s, sx, sy, sd = (2 * y + x, 2 * y + 1 - x, 2 * (1 - y) + x, 3 - 2 * y - x)
        self.own, self.mids = total.at[s], (total.at[sx], total.at[sy])
        self.far_moves = [
            move.later(total.at[sd, :, left], self.far.at[:, left], "y"),
            move.later(total.at[sd, :, right], self.far.at[:, right], "x"),
        ]
        self.near_moves = [
            move.copy(total.at[sy, :, left], self.near.at[:, left], "y"),
            move.copy(total.at[sx, :, right], self.near.at[:, right], "x"),
        ]
        self.last_moves = [
            move.copy(total.at[sx, :, left], self.last.at[:, left], "x"),
            move.copy(total.at[sy, :, right], self.last.at[:, right], "y"),
        ]
        self.own_load = None

    def start(self):
        for made in self.far_moves:
            made.start()

    def pass_on(self):
        for made in self.far_moves:
            made.wait_recv()
        far = self.far

        def work(at):
            for mid, part in zip(self.mids, (self.left, self.right)):
                added = mid[at, part].astype(jnp.float32) + far[at, part].astype(jnp.float32)
                mid[at, part] = added.astype(jnp.bfloat16)

        by_rows(far.shape[0], 16, work)
        for made in self.last_moves:
            made.start()


def tail_kernel(
    gate_hbm,
    up_hbm,
    down_hbm,
    grad_hbm,
    normed_hbm,
    qkv_hbm,
    x_hbm,
    steep_hbm,
    gain_rows,
    gain_two,
    out_hbm,
    y_in,
    gate_grad,
    up_grad,
    down_out,
    query_grad,
    key_grad,
    value_grad,
    out_out,
    y_out,
    x_out,
    gain_out,
    gate_in,
    up_in,
    down_in,
    grad_in,
    normed,
    qkv_w,
    x_own,
    steep,
    out_in,
    gate_out,
    up_out,
    qkv_out,
    pair_low,
    pair_got,
    down_low,
    down_got,
    quarter,
    part,
    part_got,
    x_low,
    qkv_in,
    qkv_held,
    qkv_sum,
    qkv_low,
    qkv_got,
    out_got,
    out_x,
    out_line,
    out_line_got,
    rows_sent,
    gain_got,
    sends,
    recvs,
):
    f32, low = jnp.float32, jnp.bfloat16
    me = coordinates()
    y, x, zh, zl, core = me
    z = 2 * zh + zl
    mine = y == core
    other = jnp.logical_not(mine)
    move = Mover(me, sends, recvs)
    loads = [
        move.local(src, dst)
        for src, dst in (
            (normed_hbm, normed),
            (grad_hbm, grad_in),
            (qkv_hbm, qkv_w),
            (gate_hbm, gate_in),
            (up_hbm, up_in),
            (down_hbm, down_in),
            (x_hbm, x_own),
            (steep_hbm, steep),
            (out_hbm, out_in),
        )
    ]
    greet(me, HEAD_GROUPS)
    qkv = PlaneSumHere(move, qkv_in, qkv_held, y, x)
    out_y = move.copy(out_in, out_got, "y")
    half_len = part.shape[0]
    block_rows = qkv_in.shape[1]

    def weigh(at):
        lanes = pl.ds(pl.multiple_of(at * block_rows, 128), block_rows)
        total = tn(normed[0, :, lanes], grad_in[pl.ds(0, half_len), :])
        total = total + tn(normed[1, :, lanes], grad_in[pl.ds(half_len, half_len), :])
        qkv_in[at] = total.astype(low)

    for made in loads[:2]:
        made.wait()
    weigh(qkv.at[3])
    qkv.start()

    weigh(qkv.at[1])
    weigh(qkv.at[2])
    qkv.start_near()

    for made in loads[2:6]:
        made.wait()
    pair_rows = pair_got.shape[1]

    def lower(src, dst, skip, count):
        def work(at):
            dst[at, :] = src[skip, at, :].astype(low)

        by_rows(count, 32, work)

    pairs = []
    for i, src in enumerate((gate_in, up_in)):
        lower(src, pair_low.at[i], 1 - zh, pair_rows)
        pairs.append(move.send(pair_low.at[i], pair_got.at[i], "zh"))
    lower(down_in, down_low, 1 - zh, down_low.shape[0])
    pairs.append(move.send(down_low, down_got, "zh"))

    theirs, ours = (pl.multiple_of(c * half_len, half_len) for c in (1 - core, core))

    def project(start):
        for i in range(half_len // QB):
            at = pl.ds(pl.multiple_of(start + i * QB, QB), QB)
            part[pl.ds(i * QB, QB), :] = nt(grad_in[at, :], qkv_w[...])

    project(theirs)
    part_move = move.copy(part, part_got, "core")
    part_move.start()
    weigh(qkv.at[0])
    qkv.pass_on()
    for made in loads[6:]:
        made.wait()
    pl.when(other)(out_y.start)
    y_turn = turn_start(move, me, y_in, y_out)
    part_move.wait()
    project(ours)
    gain_out[...] = jnp.zeros_like(gain_out)
    gain_out[1:2, :] = gain_two[...]
    piece = half_len // 2
    for q in range(2):

        def norm_back(at, q=q):
            every = pl.ds(pl.multiple_of(q * piece + at.start, 16), at.size)
            grad = part[every, :] + part_got[every, :]
            field = x_own[q, at, :].astype(f32)
            inverse = lax.rsqrt(jnp.mean(field * field, axis=1, keepdims=True) + EPSILON)
            unit = field * inverse
            gain_out[0:1, :] += jnp.sum(grad * unit, axis=0, keepdims=True)
            scaled = grad * gain_rows[0:1, :]
            centre = jnp.mean(scaled * unit, axis=1, keepdims=True)
            value = steep[every, :] + inverse * (scaled - unit * centre)
            x_low[q, at, :] = value.astype(low)

        by_rows(piece, 16, norm_back)
    x_turn = turn_start(move, me, x_low, x_out)

    gain_moves = [
        move.copy(gain_out, gain_got.at[turn], name)
        for turn, name in enumerate(("core", "x", "y", "zl", "zh"))
    ]

    def gain_round(turn):
        if turn > 0:
            gain_moves[turn - 1].wait()
            gain_out[...] = gain_out[...] + gain_got[turn - 1]
        if turn < len(gain_moves):
            gain_moves[turn].start()

    gain_round(0)
    out_shape = out_in.shape
    blocks = [(a, b) for a in range(out_shape[1]) for b in range(out_shape[2])]

    def keep(at, value):
        qkv_sum[at, :] = value
        qkv_low[at, :] = value.astype(low)

    qkv.end(keep)
    count = qkv_got.shape[1]
    line = []
    for k, names in enumerate(LINE):
        to = z ^ (1, 2, 3)[k]
        start = pl.multiple_of(to * count, count)
        line.append(move.send(qkv_low.at[pl.ds(start, count)], qkv_got.at[k], *names))

    gain_round(1)

    out_x_move = move.copy(out_got.at[1 - x], out_x, "x")

    @pl.when(mine)
    def _():
        out_y.wait_recv()

        def half(at_x):
            def work(i, carry):
                a, b = i // out_shape[2], i % out_shape[2]
                value = out_in[at_x, a, b].astype(f32) + out_got[at_x, a, b].astype(f32)
                out_got[at_x, a, b] = value.astype(low)
                return carry

            lax.fori_loop(0, len(blocks), work, 0)

        half(1 - x)
        out_x_move.start()
        half(x)

    gain_round(2)

    spread = []
    for i, (src, dst) in enumerate(((gate_in, gate_out), (up_in, up_out))):
        pairs[i].wait_recv()
        got, full = pair_got.at[i], quarter.at[i]

        def work(at, src=src, got=got, full=full):
            full[at, :] = src[zh, at, :] + got[at, :].astype(f32)

        by_rows(pair_rows, 32, work)
        share = pair_rows // 4
        for names in (("core",), ("zl",), ("zl", "core")):
            to_zl = 1 - zl if "zl" in names else zl
            to_core = 1 - core if "core" in names else core
            start = pl.multiple_of((2 * to_zl + to_core) * share, share)
            spread.append(move.send(full.at[pl.ds(start, share)], dst.at[zl, core], *names))
        start = pl.multiple_of((2 * zl + core) * share, share)
        dst[zl, core] = full[pl.ds(start, share), :]
    pairs[2].wait_recv()

    def work(at):
        down_out[at, :] = down_in[zh, at, :] + down_got[at, :].astype(f32)

    by_rows(down_out.shape[0], 32, work)

    gain_round(3)
    out_moves = []
    for k, names in enumerate(LINE):
        to = z ^ (1, 2, 3)[k]
        out_moves.append(move.copy(out_line.at[to], out_line_got.at[k], *names))

    @pl.when(mine)
    def _():
        out_x_move.wait()

        def work(i, carry):
            a, b = i // out_shape[2], i % out_shape[2]
            value = out_got[x, a, b].astype(f32) + out_x[a, b].astype(f32)
            out_line[a, b] = value.astype(low)
            return carry

        lax.fori_loop(0, len(blocks), work, 0)
        for made in out_moves:
            made.start()

    gain_round(4)
    for made in line:
        made.wait_recv()
    start = pl.multiple_of(z * count, count)
    total = qkv_sum[pl.ds(start, count), :]
    for k in range(3):
        total = total + qkv_got[k].astype(f32)
    rows = count // 2
    qkv_sum[pl.ds(0, count), :] = total
    theirs = pl.multiple_of((1 - core) * rows, rows)
    swap = move.send(qkv_sum.at[pl.ds(theirs, rows)], qkv_out.at[core], "core")
    qkv_out[core] = qkv_sum[pl.ds(pl.multiple_of(core * rows, rows), rows), :]

    out_swap = move.copy(rows_sent, out_out, "core")

    @pl.when(mine)
    def _():
        for made in out_moves:
            made.wait()
        for at in range(2):
            total = out_line[z, at].astype(f32)
            for k in range(3):
                total = total + out_line_got[k, at].astype(f32)

            @pl.when(core == at)
            def _(total=total):
                out_out[...] = total

            @pl.when(core != at)
            def _(total=total):
                rows_sent[...] = total

        out_swap.start()
        out_swap.wait_send()

    @pl.when(other)
    def _():
        out_y.wait_send()
        out_swap.wait_recv()

    gain_round(5)
    turn_end(me, y_turn)
    turn_end(me, x_turn)
    swap.wait_recv()
    for made in spread:
        made.wait_recv()
    for parts, grad in ((gate_out, gate_grad), (up_out, up_grad)):
        for i in range(grad.shape[1] // 128):
            lanes = slice(i // 4 * 128, i // 4 * 128 + 128)
            grad[:, i * 128 : (i + 1) * 128] = parts[i // 2 % 2, i % 2, :, lanes]
    at = 0
    for grad in (query_grad, key_grad, value_grad):
        size = grad.shape[1] // 2
        for c in range(2):
            grad[:, c * size : (c + 1) * size] = qkv_out[c, :, at : at + size]
        at += size
    move.finish()


def sum_tail(gate, up, down, grad, normed, qkv_w, x_own, steep, gain_rows, gain_two, out, y_in):
    f32, low = jnp.float32, jnp.bfloat16
    hbm = pl.BlockSpec(memory_space=pl.ANY)
    vmem = pl.BlockSpec(memory_space=pltpu.VMEM)
    wide, width = gate.shape[-1], grad.shape[-1]
    rows = out.shape[-2]
    half_len = steep.shape[0]
    pair_rows, down_rows = gate.shape[1], down.shape[1]
    return pl.pallas_call(
        tail_kernel,
        in_specs=[hbm] * 8 + [vmem] * 2 + [hbm] * 2,
        out_specs=[vmem] * 7 + [hbm, hbm, vmem],
        out_shape=[
            jax.ShapeDtypeStruct((rows, 4 * wide), f32),
            jax.ShapeDtypeStruct((rows, 4 * wide), f32),
            jax.ShapeDtypeStruct((down_rows, width), f32),
            jax.ShapeDtypeStruct((rows, width), f32),
            jax.ShapeDtypeStruct((rows, width // 2), f32),
            jax.ShapeDtypeStruct((rows, width // 2), f32),
            jax.ShapeDtypeStruct((rows, width), f32),
            jax.ShapeDtypeStruct(y_in.shape, low),
            jax.ShapeDtypeStruct(y_in.shape, low),
            jax.ShapeDtypeStruct((2, width), f32),
        ],
        scratch_shapes=[
            pltpu.VMEM(one.shape, one.dtype)
            for one in (gate, up, down, grad, normed, qkv_w, x_own, steep, out)
        ]
        + [
            pltpu.VMEM((2, 2, rows, wide), f32),
            pltpu.VMEM((2, 2, rows, wide), f32),
            pltpu.VMEM((2, rows, width), f32),
            pltpu.VMEM((2, pair_rows, wide), low),
            pltpu.VMEM((2, pair_rows, wide), low),
            pltpu.VMEM((down_rows, width), low),
            pltpu.VMEM((down_rows, width), low),
            pltpu.VMEM((2, pair_rows, wide), f32),
            pltpu.VMEM((half_len, width), f32),
            pltpu.VMEM((half_len, width), f32),
            pltpu.VMEM(y_in.shape, low),
            pltpu.VMEM((4, 8 * rows, width), low),
            pltpu.VMEM((3, 8 * rows, width), low),
            pltpu.VMEM((8 * rows, width), f32),
            pltpu.VMEM((8 * rows, width), low),
            pltpu.VMEM((3, 2 * rows, width), low),
            pltpu.VMEM(out.shape, low),
            pltpu.VMEM(out.shape[1:], low),
            pltpu.VMEM(out.shape[1:], low),
            pltpu.VMEM((3,) + out.shape[2:], low),
            pltpu.VMEM((rows, width), f32),
            pltpu.VMEM((5, 2, width), f32),
            pltpu.SemaphoreType.DMA((64,)),
            pltpu.SemaphoreType.DMA((64,)),
        ],
        compiler_params=pltpu.CompilerParams(
            collective_id=4, has_side_effects=True, vmem_limit_bytes=63 << 20
        ),
        name="tail",
    )(gate, up, down, grad, normed, qkv_w, x_own, steep, gain_rows, gain_two, out, y_in)


QB = 256
SPAN = 768


def turned(field, back):
    middle = HD // 2
    left, right = field[:, :middle], field[:, middle:]
    if back:
        return jnp.concatenate([right, -left], axis=1)
    return jnp.concatenate([-right, left], axis=1)


def spun(field, cosine, sine, back=False):
    field = field.astype(jnp.float32)
    return field * cosine + turned(field, back) * sine


def nt(left, right):
    return lax.dot_general(left, right, (((1,), (1,)), ((), ())), preferred_element_type=jnp.float32)


def nn(left, right):
    return jnp.dot(left, right, preferred_element_type=jnp.float32)


def tn(left, right):
    return lax.dot_general(left, right, (((0,), (0,)), ((), ())), preferred_element_type=jnp.float32)


def head(ref, rows, number):
    return ref[rows, HD * number : HD * (number + 1)]


def ahead_block(
    heads, kvs, step, size, qkv_ref, cos_ref, sin_ref, row_ref, col_ref, out_ref, keys
):
    low, f32 = jnp.bfloat16, jnp.float32
    start, base = step * QB, (step + 1) * QB - size
    if not isinstance(step, int):
        start, base = pl.multiple_of(start, QB), pl.multiple_of(base, QB)
    here, span = pl.ds(start, QB), pl.ds(base, size)
    key_place = base + lax.broadcasted_iota(jnp.int32, (size, QB), 0)
    place = start + lax.broadcasted_iota(jnp.int32, (size, QB), 1)
    allowed = (key_place <= place) & (col_ref[span, :] == row_ref[:, here])
    bias = jnp.where(allowed, 0.0, -1e30).astype(f32)
    scale = (1.0 / math.sqrt(HD)) * math.log2(math.e)
    cosine, sine = cos_ref[here, :], sin_ref[here, :]
    results = []
    for h in range(heads):
        j = h * kvs // heads
        query = spun(head(qkv_ref, here, h), cosine, sine).astype(low)
        scores = nt(keys[j, span, :], query) * scale + bias
        peak = jnp.max(scores, axis=0, keepdims=True)
        weights = jnp.exp2(scores - peak)
        total = jnp.sum(weights, axis=0, keepdims=True)
        probs = (weights * (1.0 / total)).astype(low)
        results.append(tn(probs, head(qkv_ref, span, heads + kvs + j)).astype(low))
    out_ref[here, :] = jnp.concatenate(results, axis=1)


def behind_block(
    heads,
    kvs,
    step,
    size,
    qkv_ref,
    grad_ref,
    cos_ref,
    sin_ref,
    row_ref,
    col_ref,
    gq_ref,
    keys,
    gks,
    gvs,
):
    low, f32 = jnp.bfloat16, jnp.float32
    start, base = step * QB, (step + 1) * QB - size
    if not isinstance(step, int):
        start, base = pl.multiple_of(start, QB), pl.multiple_of(base, QB)
    here, span = pl.ds(start, QB), pl.ds(base, size)
    key_place = base + lax.broadcasted_iota(jnp.int32, (size, QB), 0)
    place = start + lax.broadcasted_iota(jnp.int32, (size, QB), 1)
    allowed = (key_place <= place) & (col_ref[span, :] == row_ref[:, here])
    bias = jnp.where(allowed, 0.0, -1e30).astype(f32)
    width = 1.0 / math.sqrt(HD)
    scale = width * math.log2(math.e)
    cosine, sine = cos_ref[here, :], sin_ref[here, :]
    results = []
    for h in range(heads):
        j = h * kvs // heads
        query = spun(head(qkv_ref, here, h), cosine, sine).astype(low)
        key, value = keys[j, span, :], head(qkv_ref, span, heads + kvs + j)
        grad = head(grad_ref, here, h)
        scores = nt(key, query) * scale + bias
        peak = jnp.max(scores, axis=0, keepdims=True)
        weights = jnp.exp2(scores - peak)
        total = jnp.sum(weights, axis=0, keepdims=True)
        probs = weights * (1.0 / total)
        slope = nt(value, grad)
        centre = jnp.sum(probs * slope, axis=0, keepdims=True)
        gs = (probs * (slope - centre)).astype(low)
        gvs[j, span, :] += nn(probs.astype(low), grad)
        gks[j, span, :] += nn(gs, query)
        results.append(spun(tn(gs, key) * width, cosine, sine, True).astype(low))
    gq_ref[here, : HD * heads] = jnp.concatenate(results, axis=1)


def behind_kernel(
    heads,
    kvs,
    gain_rows,
    cos_ref,
    sin_ref,
    row_ref,
    col_ref,
    hidden_in,
    back_in,
    qkv_in,
    mixed_in,
    out_in,
    back_far,
    ahead_own,
    ahead_far,
    tokens,
    seeds,
    act_in,
    gate_in,
    up_in,
    gain_ref,
    grad_out,
    steep_out,
    y_low,
    out_grad,
    gate_out,
    up_out,
    down_out,
    hidden,
    seed,
    back_own,
    grad_ref,
    steep,
    steep_low,
    back_got,
    ahead_got,
    gate_sum,
    up_sum,
    down_sum,
    gate_held,
    up_held,
    down_held,
    sends,
    recvs,
):
    f32, low = jnp.float32, jnp.bfloat16
    me = coordinates()
    y, x, zh, zl, core = me
    greet(me, (("x",), ("y",), ("core",), ("zl",)))
    move = Mover(me, sends, recvs)
    back_move = move.send(back_far, back_got, "zl")
    ahead_move = move.later(ahead_far, ahead_got, "zl")
    swap = move.later(steep_low.at[core], steep_low.at[core], "core")
    gate, up, down = sums = [
        PlaneSumHere(move, total, held, y, x)
        for total, held in (
            (gate_sum, gate_held), (up_sum, up_held), (down_sum, down_held)
        )
    ]
    s, sx, sy, sd = gate.at
    order = (sd, sx, sy, s)
    half_len, width = hidden.shape
    count, wide = gate_in.shape
    block = gate_sum.shape[1]

    def wide_part(gates, ups, pieces):
        def column(i):
            lanes = pl.ds(pl.multiple_of(order[i] * block, 128), block)
            return move.quiet(tokens.at[:, lanes], pieces.at[i % 2])

        columns = [column(i) for i in range(4)]
        columns[0].start()
        loads = [move.local(gate_in, gates), move.local(up_in, ups)]
        for i in range(4):
            columns[i].wait()
            if i < 3:
                columns[i + 1].start()
            if i == 0:
                loads[0].wait()
            gate_sum[order[i]] = tn(pieces[i % 2], gates[...]).astype(low)
            if i == 0:
                gate.start()
                loads[1].wait()
            up_sum[order[i]] = tn(pieces[i % 2], ups[...]).astype(low)
            if i == 0:
                up.start()
            if i == 2:
                gate.start_near()
                up.start_near()

    half_loads = [
        move.quiet(hidden_in, hidden),
        move.quiet(back_in, back_own),
        move.quiet(seeds.at[pl.ds(0, half_len)], seed),
    ]
    half_stores = [move.quiet(steep, steep_out), move.quiet(grad_ref, grad_out)]
    pl.run_scoped(
        wide_part,
        pltpu.VMEM((count, wide), low),
        pltpu.VMEM((count, wide), low),
        pltpu.VMEM((2, count, block), low),
    )
    for made in half_loads:
        made.start()
    deep = down_sum.shape[1]

    def deep_part(rows, pieces):
        def column(i):
            lanes = pl.ds(pl.multiple_of(order[i] * deep, 128), deep)
            return move.quiet(act_in.at[:, lanes], pieces.at[i % 2])

        columns = [column(i) for i in range(4)]
        columns[0].start()
        move.local(seeds, rows).wait()
        for i in range(4):
            columns[i].wait()
            if i < 3:
                columns[i + 1].start()
            down_sum[order[i]] = tn(pieces[i % 2], rows[...]).astype(low)
            if i == 0:
                down.start()
            if i == 2:
                down.start_near()

    pl.run_scoped(
        deep_part,
        pltpu.VMEM((count, width), low),
        pltpu.VMEM((2, count, deep), low),
    )
    gate.pass_on()
    up.pass_on()

    def heads_part(qkv_ref, out_w, keys, gks, gvs):
        loads = [move.local(qkv_in, qkv_ref), move.local(out_in, out_w)]
        gain_ref[...] = jnp.zeros_like(gain_ref)
        for made in half_loads:
            made.wait()
        back_move.wait_recv()
        ahead_move.start()

        def norm_back(at):
            grad = back_own[at, :] + back_got[at, :].astype(f32)
            field = hidden[at, :]
            inverse = lax.rsqrt(jnp.mean(field * field, axis=1, keepdims=True) + EPSILON)
            unit = field * inverse
            gain_ref[...] += jnp.sum(grad * unit, axis=0, keepdims=True)
            scaled = grad * gain_rows[1:2, :]
            centre = jnp.mean(scaled * unit, axis=1, keepdims=True)
            value = seed[at, :].astype(f32) + inverse * (scaled - unit * centre)
            steep[at, :] = value
            steep_low[core, at, :] = value.astype(low)

        by_rows(half_len, 16, norm_back)
        swap.start()
        half_stores[0].start()
        for made in loads:
            made.wait()
        everything = pl.ds(0, 2 * half_len)
        for j in range(kvs):
            keys[j] = spun(
                head(qkv_ref, everything, heads + j), cos_ref[...], sin_ref[...]
            ).astype(low)
        gks[...] = jnp.zeros_like(gks)
        gvs[...] = jnp.zeros_like(gvs)
        swap.wait_recv()
        per = half_len // QB
        for i in range(2 * per):
            at = pl.ds(i % per * QB, QB)
            part = nt(steep_low[i // per, at, :], out_w[...]).astype(low)
            grad_ref[pl.ds(i * QB, QB), : heads * HD] = part
        down.pass_on()

        def work(step, size):
            behind_block(
                heads, kvs, step, size, qkv_ref, grad_ref, cos_ref, sin_ref, row_ref, col_ref,
                grad_ref, keys, gks, gvs,
            )

        def one(step, carry):
            work(step, SPAN)
            return carry

        for step in range(SPAN // QB - 1):
            work(step, (step + 1) * QB)
        lax.fori_loop(SPAN // QB - 1, 2 * half_len // QB, one, 0)
        scale = 1.0 / math.sqrt(HD)
        gk = [
            spun(gks[j] * scale, cos_ref[...], sin_ref[...], True).astype(low)
            for j in range(kvs)
        ]
        gv = [gvs[j].astype(low) for j in range(kvs)]
        grad_ref[:, HD * heads :] = jnp.concatenate(gk + gv, axis=1)
        half_stores[1].start()

    pl.run_scoped(
        heads_part,
        pltpu.VMEM(qkv_in.shape, low),
        pltpu.VMEM(out_in.shape, low),
        pltpu.VMEM((kvs, 2 * half_len, HD), low),
        pltpu.VMEM((kvs, 2 * half_len, HD), f32),
        pltpu.VMEM((kvs, 2 * half_len, HD), f32),
    )

    def last_part(mixed, own, out_made, gate_made, up_made, down_made):
        loads = [move.local(mixed_in, mixed), move.local(ahead_own, own)]
        loads[0].wait()
        rows = mixed.shape[1] // 4
        for i in range(4):
            lanes = pl.ds(i * rows, rows)
            total = tn(mixed[pl.ds(0, half_len), lanes], steep_low[0])
            total = total + tn(mixed[pl.ds(half_len, half_len), lanes], steep_low[1])
            out_made[pl.ds(i * rows, rows), :] = total.astype(low)
        stores = [move.local(out_made, out_grad)]
        ahead_move.wait_recv()
        loads[1].wait()
        quarter = half_len // 2
        for q in range(2):

            def add(at, q=q):
                every = pl.ds(pl.multiple_of(q * quarter + at.start, 16), at.size)
                value = hidden[every, :] + own[every, :] + ahead_got[q, at, :].astype(f32)
                ahead_got[q, at, :] = value.astype(low)

            by_rows(quarter, 16, add)
        stores.append(move.local(ahead_got, y_low))
        for plane, made, out in zip(
            sums, (gate_made, up_made, down_made), (gate_out, up_out, down_out)
        ):

            def write(at, value, made=made):
                made[at, :] = value

            plane.end(write)
            stores.append(move.local(made, out))
        for made in half_stores + stores:
            made.wait()

    pl.run_scoped(
        last_part,
        pltpu.VMEM(mixed_in.shape, low),
        pltpu.VMEM((half_len, width), f32),
        pltpu.VMEM(out_grad.shape, low),
        pltpu.VMEM(gate_out.shape, f32),
        pltpu.VMEM(up_out.shape, f32),
        pltpu.VMEM(down_out.shape, f32),
    )
    move.finish()


def attend_behind(heads, kvs, *operands):
    f32, low = jnp.float32, jnp.bfloat16
    half_len, width = operands[5].shape
    length = 2 * half_len
    wide = operands[-1].shape[1]
    hbm = pl.BlockSpec(memory_space=pl.ANY)
    vmem = pl.BlockSpec(memory_space=pltpu.VMEM)
    shapes = [(width // 4, wide), (width // 4, wide), (wide // 4, width)]

    def made(*shape, dtype=low):
        return jax.ShapeDtypeStruct(shape, dtype)

    return pl.pallas_call(
        functools.partial(behind_kernel, heads, kvs),
        in_specs=[vmem] * 5 + [hbm] * 13,
        out_specs=[vmem] + [hbm] * 7,
        out_shape=[
            made(1, width, dtype=f32),
            made(length, width),
            made(half_len, width, dtype=f32),
            made(2, half_len // 2, width),
            made(heads * HD, width),
        ]
        + [made(*shape, dtype=f32) for shape in shapes],
        scratch_shapes=[
            pltpu.VMEM((half_len, width), f32),
            pltpu.VMEM((half_len, width), low),
            pltpu.VMEM((half_len, width), f32),
            pltpu.VMEM((length, width), low),
            pltpu.VMEM((half_len, width), f32),
            pltpu.VMEM((2, half_len, width), low),
            pltpu.VMEM((half_len, width), low),
            pltpu.VMEM((2, half_len // 2, width), low),
        ]
        + [pltpu.VMEM((4,) + shape, low) for shape in shapes]
        + [pltpu.VMEM((3,) + shape, low) for shape in shapes]
        + [pltpu.SemaphoreType.DMA((64,)), pltpu.SemaphoreType.DMA((64,))],
        compiler_params=pltpu.CompilerParams(
            collective_id=3, has_side_effects=True, vmem_limit_bytes=63 << 20
        ),
        cost_estimate=pl.CostEstimate(
            flops=10 * heads * length * SPAN * HD,
            bytes_accessed=9 << 20,
            transcendentals=heads * length * SPAN,
        ),
        name="behind",
    )(*operands)


def bands(size):
    return (pl.ds(0, size // 2), pl.ds(size // 2, size // 2))


def first_kernel(
    heads,
    kvs,
    x_in,
    g_in,
    query_in,
    key_in,
    value_in,
    gate_raw,
    up_raw,
    down_in,
    out_in,
    gain_in,
    docs_in,
    cos_ref,
    sin_ref,
    x_out,
    normed_out,
    qkv_out,
    mixed_out,
    hidden_out,
    qkv_w_out,
    out_w_out,
    gain_rows,
    row,
    col,
    seeds,
    tokens,
    gate_w,
    up_w,
    down_w,
    x_own,
    normed,
    qkv,
    mixed,
    hidden,
    qkv_w,
    out_w,
    token,
    qkv_in,
    gate_in,
    up_in,
    docs,
    gains,
    keys,
    part,
    part_got,
    sends,
    recvs,
):
    f32, low = jnp.float32, jnp.bfloat16
    me = coordinates()
    y, x, zh, zl, core = me
    s, z = y * 2 + x, zh * 2 + zl
    mine = y == core
    other = jnp.logical_not(mine)
    width = qkv_w.shape[-1]
    length = qkv.shape[0]
    half_len = length // 2
    at = 0
    for ref in (query_in, key_in, value_in):
        size = ref.shape[1] // 2
        for c in range(2):
            qkv_in[c, :, at : at + size] = ref[:, c * size : (c + 1) * size]
        at += size
    for raw, parts in ((gate_raw, gate_in), (up_raw, up_in)):
        for i in range(raw.shape[1] // 128):
            lanes = slice(i // 4 * 128, i // 4 * 128 + 128)
            parts[i // 2 % 2, i % 2, :, lanes] = raw[:, i * 128 : (i + 1) * 128]
    greet(me, HEAD_GROUPS)
    move = Mover(me, sends, recvs)
    stores = []

    wides = [
        (ref.at[:, at], bands(ref.shape[-1]))
        for at in (zh, 1 - zh)
        for ref in (gate_w, up_w, down_w)
    ]
    hops = [plane_make(move, ref, s, parts) for ref, parts in wides]
    rest = []

    def start_some(which):
        for i in which:
            for made in hops[i]:
                made.start()

    def pass_some(which):
        for i in which:
            rest.extend(plane_pass(move, hops[i], wides[i][0], y, x, wides[i][1]))

    down_own = move.local(down_in, down_w.at[s, zh])
    own = [
        move.local(qkv_in.at[core], qkv_w.at[s, z, core]),
        move.local(gain_in, gains.at[s, z, core]),
    ]
    first = [
        move.send(qkv_in.at[1 - core], qkv_w.at[s, z, core], "core"),
        move.send(gain_in, gains.at[s, z, core], "core"),
    ]
    docs_move = move.send(docs_in, docs, "core")
    x_turn = turn_start(move, me, x_in, x_own)
    for made in own:
        made.wait()
    for made in first:
        made.wait_recv()
    line = [move.send(gains.at[s, z], gains.at[s, z], *names) for names in LINE]
    line += [move.send(qkv_w.at[s, z], qkv_w.at[s, z], *names) for names in LINE]
    down_own.wait()
    start_some((2,))

    own = [
        move.local(gate_in.at[zl, core], gate_w.at[s, zh, zl, core]),
        move.local(up_in.at[zl, core], up_w.at[s, zh, zl, core]),
    ]
    spread = []
    for src, dst in ((gate_in, gate_w), (up_in, up_w)):
        for names in (("core",), ("zl",), ("zl", "core")):
            to_zl = 1 - zl if "zl" in names else zl
            to_core = 1 - core if "core" in names else core
            spread.append(move.send(src.at[to_zl, to_core], dst.at[s, zh, zl, core], *names))
    out_own = move.quiet(out_in, out_w.at[x, z, core])
    out_sent = move.copy(out_in, out_w.at[x, z, core], "core")
    pl.when(mine)(out_own.start)
    pl.when(other)(out_sent.start)

    for made in line[:3]:
        made.wait_recv()
    gain_hops = [move.send(gains.at[s], gains.at[s], *names) for names in (("x",), ("y",))]
    turn_end(me, x_turn)
    stores.append(move.local(x_own, x_out))
    gain_hops[0].wait_recv()
    sx = 2 * y + 1 - x
    gain_hops.append(move.send(gains.at[sx], gains.at[sx], "y"))
    for made in line[3:]:
        made.wait_recv()
    qkv_hops = plane_start(move, qkv_w, s, bands(width))
    pass_some((2,))

    out_line = [move.copy(out_w.at[x, z], out_w.at[x, z], *names) for names in LINE]
    pl.when(other)(out_sent.wait_send)

    @pl.when(mine)
    def _():
        out_own.wait()
        out_sent.wait_recv()
        for made in out_line:
            made.start()

    for made in own:
        made.wait()
    for made in spread:
        made.wait_recv()
    pairs = [
        move.send(ref.at[s, zh], ref.at[s, zh], "zh") for ref in (gate_w, up_w, down_w)
    ]

    for made in gain_hops[1:]:
        made.wait_recv()
    count = out_in.shape[0]
    for i in range(2):
        gain_rows[pl.ds(i, 1), :] = jnp.concatenate(
            [
                gains[a, b, c, 0:1, i * count : (i + 1) * count]
                for a in range(4)
                for b in range(4)
                for c in range(2)
            ],
            axis=1,
        )

    quarter = half_len // 2
    for q in range(2):

        def norm(at, q=q):
            field = x_own[q, at, :].astype(f32)
            inverse = lax.rsqrt(jnp.mean(field * field, axis=1, keepdims=True) + EPSILON)
            rows = pl.ds(pl.multiple_of(q * quarter + at.start, 16), at.size)
            normed[core, rows, :] = (field * inverse * gain_rows[0:1, :]).astype(low)

        by_rows(quarter, 16, norm)
    normed_move = move.send(normed.at[core], normed.at[core], "core")
    docs_move.wait_recv()
    row[...] = jnp.where(mine, docs_in[x], docs[x])
    col[...] = jnp.transpose(jnp.broadcast_to(row[...], (8, length)))[:, 0:1]

    qkv_rest = plane_pass(move, qkv_hops, qkv_w, y, x, bands(width))
    out_x = move.copy(out_w.at[x], out_w.at[x], "x")
    out_y = [move.copy(out_w.at[at], out_w.at[at], "y") for at in (x, 1 - x)]

    @pl.when(mine)
    def _():
        for made in out_line:
            made.wait()
        out_x.start()
        out_y[0].start()

    g_turn = turn_start(move, me, g_in, seeds.at[0])
    normed_move.wait_recv()
    for made in qkv_rest:
        made.wait_recv()
    stores += [move.local(normed, normed_out), move.local(qkv_w, qkv_w_out)]
    weight = qkv_w.reshape(width, width)
    for i in range(length // QB):
        at = pl.ds(i * QB % half_len, QB)
        qkv[pl.ds(i * QB, QB), :] = nn(normed[i * QB // half_len, at, :], weight[...]).astype(low)
    stores.append(move.local(qkv, qkv_out))
    start_some((0,))
    seed_moves = [
        move.later(seeds.at[0], seeds.at[1], "core"),
        move.later(seeds.at[0], seeds.at[2], "zl"),
    ]

    everything = pl.ds(0, length)
    for j in range(kvs):
        keys[j] = spun(head(qkv, everything, heads + j), cos_ref[...], sin_ref[...]).astype(low)

    def work(step, size):
        ahead_block(heads, kvs, step, size, qkv, cos_ref, sin_ref, row, col, mixed, keys)

    def block(step, carry):
        @pl.when(step == SPAN // QB - 1)
        def _():
            turn_end(me, g_turn)
            for made in seed_moves:
                made.start()
            start_some((1,))

        @pl.when(step == SPAN // QB)
        def _():
            pairs[0].wait_recv()
            start_some((3,))

        work(step, SPAN)
        return carry

    work(0, QB)

    @pl.when(mine)
    def _():
        out_x.wait_recv()
        out_y[1].start()

    for step in range(1, SPAN // QB - 1):
        work(step, (step + 1) * QB)
    lax.fori_loop(SPAN // QB - 1, length // QB, block, 0)
    stores.append(move.local(mixed, mixed_out))
    for made in pairs[1:]:
        made.wait_recv()
    start_some((4, 5))

    @pl.when(mine)
    def _():
        out_x.wait_send()
        for made in out_y:
            made.wait_send()

    @pl.when(other)
    def _():
        for made in out_y:
            made.wait_recv()

    stores.append(move.local(out_w, out_w_out))

    out_weight = out_w.reshape(width // 2, width)
    theirs, ours = (pl.multiple_of(c * half_len, half_len) for c in (1 - core, core))

    def project(start):
        for i in range(half_len // QB):
            at = pl.ds(pl.multiple_of(start + i * QB, QB), QB)
            part[pl.ds(i * QB, QB), :] = nn(mixed[at, :], out_weight[...])

    project(theirs)
    part_move = move.copy(part, part_got, "core")
    part_move.start()
    for i in range(half_len // QB):
        at = pl.ds(pl.multiple_of(ours + i * QB, QB), QB)
        hidden[pl.ds(i * QB, QB), :] = nn(mixed[at, :], out_weight[...])
    part_move.wait()
    for q in range(2):

        def norm(at, q=q):
            rows = pl.ds(pl.multiple_of(q * quarter + at.start, 16), at.size)
            field = x_own[q, at, :].astype(f32) + (hidden[rows, :] + part_got[rows, :])
            hidden[rows, :] = field
            inverse = lax.rsqrt(jnp.mean(field * field, axis=1, keepdims=True) + EPSILON)
            token[rows, :] = (field * inverse * gain_rows[1:2, :]).astype(low)

        by_rows(quarter, 16, norm)
    token_moves = [
        move.send(token, tokens.at[2], "zl"),
        move.send(token, tokens.at[1], "core"),
    ]
    stores += [move.local(token, tokens.at[0]), move.local(hidden, hidden_out)]
    pass_some((0, 1))
    seed_moves[1].wait_recv()
    seed_moves.append(move.send(seeds.at[2], seeds.at[3], "core"))
    pass_some((3, 4, 5))
    token_moves[0].wait_recv()
    token_moves.append(move.send(tokens.at[2], tokens.at[3], "core"))
    for made in rest + seed_moves[::2] + token_moves[1:]:
        made.wait_recv()
    for made in stores:
        made.wait()
    move.finish()


def first_part(
    heads, kvs, x_in, g_in, query, key, value, gate, up, down, out, gain, docs, cosine, sine
):
    f32, low = jnp.float32, jnp.bfloat16
    rows, width = out.shape
    half_len = 2 * x_in.shape[1]
    length = 2 * half_len
    hbm = pl.BlockSpec(memory_space=pl.ANY)
    vmem = pl.BlockSpec(memory_space=pltpu.VMEM)

    def made(shape, dtype=low):
        return jax.ShapeDtypeStruct(shape, dtype)

    qkv_shape = (2, rows, width)
    quarter = (2, 2, rows, gate.shape[1] // 4)
    kept = [
        made(x_in.shape),
        made((2, half_len, width)),
        made((length, width)),
        made((length, heads * HD)),
        made((half_len, width), f32),
        made((4, 4) + qkv_shape),
        made((2, 4, 2) + out.shape),
    ]
    return pl.pallas_call(
        functools.partial(first_kernel, heads, kvs),
        in_specs=[hbm] * 2 + [vmem] * 5 + [hbm] * 3 + [vmem] * 3,
        out_specs=[hbm] * 7 + [vmem] * 3 + [hbm] * 5,
        out_shape=kept
        + [
            made((2, width), f32),
            made((1, length), docs.dtype),
            made((length, 1), docs.dtype),
            made((4,) + x_in.shape),
            made((4, half_len, width)),
            made((4, 2) + quarter),
            made((4, 2) + quarter),
            made((4, 2) + down.shape),
        ],
        scratch_shapes=[pltpu.VMEM(one.shape, one.dtype) for one in kept]
        + [
            pltpu.VMEM((half_len, width), low),
            pltpu.VMEM(qkv_shape, low),
            pltpu.VMEM(quarter, low),
            pltpu.VMEM(quarter, low),
            pltpu.VMEM(docs.shape, docs.dtype),
            pltpu.VMEM((4, 4, 2) + gain.shape, f32),
            pltpu.VMEM((kvs, length, HD), low),
            pltpu.VMEM((half_len, width), f32),
            pltpu.VMEM((half_len, width), f32),
            pltpu.SemaphoreType.DMA((112,)),
            pltpu.SemaphoreType.DMA((112,)),
        ],
        compiler_params=pltpu.CompilerParams(
            collective_id=1, has_side_effects=True, vmem_limit_bytes=60 << 20
        ),
        name="first",
    )(x_in, g_in, query, key, value, gate, up, down, out, gain, docs, cosine, sine)


def hidden_kernel(
    tokens,
    seeds,
    gate_w,
    up_w,
    down_w,
    act_out,
    gate_out,
    up_out,
    back_own,
    back_far,
    ahead_own,
    ahead_far,
    backs,
    aheads,
    back_got,
    ahead_got,
    sends,
    recvs,
):
    f32, low = jnp.float32, jnp.bfloat16
    me = coordinates()
    move = Mover(me, sends, recvs)

    @pl.when(pl.program_id(0) == 0)
    def _():
        greet(me, (("core",),))

    half_len = backs.shape[1]
    per = half_len // QB
    i = pl.program_id(0)
    moves = [
        (
            move.copy(backs.at[1], back_got.at[turn], "core"),
            move.copy(aheads.at[1], ahead_got.at[turn], "core"),
        )
        for turn in range(2)
    ]

    def fold(turn, back_ref, ahead_ref):
        for made in moves[turn]:
            made.wait()

        def work(at):
            back_ref[at, :] = (backs[0, at, :] + back_got[turn, at, :]).astype(back_ref.dtype)
            ahead_ref[at, :] = (aheads[0, at, :] + ahead_got[turn, at, :]).astype(ahead_ref.dtype)

        by_rows(half_len, 16, work)

    slot = 3 - i // per
    rows = pl.ds(pl.multiple_of(i % per * QB, QB), QB)
    token, seed = tokens[...], seeds[...]
    gate, upward = nn(token, gate_w[...]), nn(token, up_w[...])
    sigma = 1.0 / (1.0 + jnp.exp(-gate))
    silu = gate * sigma
    activated = (silu * upward).astype(low)
    act_out[...] = activated
    grad = nt(seed, down_w[...])
    up_low = (grad * silu).astype(low)
    gate_low = (grad * upward * sigma * (1.0 + gate * (1.0 - sigma))).astype(low)
    up_out[...] = up_low
    gate_out[...] = gate_low
    aheads[slot % 2, rows, :] = nn(activated, down_w[...])
    backs[slot % 2, rows, :] = nt(gate_low, gate_w[...]) + nt(up_low, up_w[...])
    for turn in range(2):

        @pl.when(i == (2 * turn + 1) * per - 1)
        def _(turn=turn):
            for made in moves[turn]:
                made.start()

    @pl.when(i == 2 * per - 1)
    def _():
        fold(0, back_far, ahead_far)

    @pl.when(i == 4 * per - 1)
    def _():
        fold(1, back_own, ahead_own)


def hidden_part(tokens, seeds, gate_w, up_w, down_w):
    f32, low = jnp.float32, jnp.bfloat16
    half_len, width = tokens.shape[1:]
    wide = gate_w.shape[1]
    per = half_len // QB
    vmem = pl.BlockSpec(memory_space=pltpu.VMEM)

    def banded(columns):
        return pl.BlockSpec((QB, columns), lambda i: ((3 - i // per) * per + i % per, 0))

    def made(rows, columns, dtype=low):
        return jax.ShapeDtypeStruct((rows, columns), dtype)

    return pl.pallas_call(
        hidden_kernel,
        grid=(4 * per,),
        in_specs=[banded(width)] * 2 + [vmem] * 3,
        out_specs=[banded(wide)] * 3 + [vmem] * 4,
        out_shape=[made(4 * half_len, wide)] * 3
        + [
            made(half_len, width, f32),
            made(half_len, width),
            made(half_len, width, f32),
            made(half_len, width),
        ],
        scratch_shapes=[
            pltpu.VMEM((2, half_len, width), f32),
            pltpu.VMEM((2, half_len, width), f32),
            pltpu.VMEM((2, half_len, width), f32),
            pltpu.VMEM((2, half_len, width), f32),
            pltpu.SemaphoreType.DMA((4,)),
            pltpu.SemaphoreType.DMA((4,)),
        ],
        compiler_params=pltpu.CompilerParams(
            collective_id=2, has_side_effects=True, vmem_limit_bytes=63 << 20
        ),
        cost_estimate=pl.CostEstimate(
            flops=2 * 6 * 4 * half_len * width * wide,
            bytes_accessed=40 << 20,
            transcendentals=4 * half_len * wide,
        ),
        name="hidden",
    )(tokens.reshape(-1, width), seeds.reshape(-1, width), gate_w, up_w, down_w)


def rope_constants(length, width):
    freqs = ROPE_BASE ** (-2.0 * np.arange(width // 2) / width)
    angles = np.tile(np.arange(length)[:, None] * freqs[None, :], 2)
    return np.cos(angles).astype(np.float32), np.sin(angles).astype(np.float32)


def fast_body(
    layer_input,
    cotangent,
    token_mask,
    document_ids,
    attn_gain,
    w_query,
    w_key,
    w_value,
    w_output,
    mlp_gain,
    w_gate,
    w_up,
    w_down,
):
    f32, low = jnp.float32, jnp.bfloat16
    y, x, zh, zl, core = (lax.axis_index(name) for name in AXES)
    device = sum(lax.axis_index(name) * BITS[name] for name in AXES)
    quarter, width = layer_input.shape[1:]
    half_len = 2 * quarter
    length = 2 * half_len
    rows = w_query.shape[0]
    units = w_gate.shape[1]
    heads, kvs = HEADS // 2, KV // 2
    cosine, sine = (jnp.asarray(table) for table in rope_constants(length, HD))

    masked = cotangent * token_mask.astype(low)[:, :, None]
    gain = jnp.concatenate([attn_gain, mlp_gain]).astype(f32)
    gain = jnp.broadcast_to(jnp.pad(gain, (0, 128 - 2 * rows)), (8, 128))
    (
        own,
        normed,
        pair,
        mixed,
        hidden,
        qkv_w,
        out_w,
        gains,
        row,
        col,
        seeds,
        tokens,
        gate_w,
        up_w,
        down_w,
    ) = first_part(
        heads,
        kvs,
        layer_input,
        masked,
        w_query,
        w_key,
        w_value,
        w_gate,
        w_up,
        w_down,
        w_output,
        gain,
        document_ids[:, None],
        cosine,
        sine,
    )
    qkv_w, out_w = qkv_w.reshape(width, -1), out_w.reshape(-1, width)
    gate_w, up_w = gate_w.reshape(width, -1), up_w.reshape(width, -1)
    down_w = down_w.reshape(-1, width)
    seeds = seeds.reshape(4, half_len, width)
    activated, gate_low, up_low, back_own, back_far, ahead_own, ahead_far = hidden_part(
        tokens, seeds, gate_w, up_w, down_w
    )
    gain_two, grad_qkv, steep, y_low, grad_out_w, *sums = attend_behind(
        heads,
        kvs,
        gains,
        cosine,
        sine,
        row,
        col,
        hidden,
        back_own,
        pair,
        mixed,
        out_w,
        back_far,
        ahead_own,
        ahead_far.reshape(2, quarter, width),
        tokens.reshape(-1, width),
        seeds.reshape(-1, width),
        activated,
        gate_low,
        up_low,
    )
    (
        gate_grad,
        up_grad,
        down_grad,
        query_grad,
        key_grad,
        value_grad,
        out_grad,
        output,
        grad_input,
        gain,
    ) = sum_tail(
        sums[0].reshape(2, -1, units // 4),
        sums[1].reshape(2, -1, units // 4),
        sums[2].reshape(2, -1, width),
        grad_qkv,
        normed,
        qkv_w,
        own,
        steep,
        gains,
        gain_two,
        grad_out_w.reshape(2, 4, 2, rows, width),
        y_low,
    )
    gain_one = lax.dynamic_slice_in_dim(gain, device * rows, rows, 1)

    return (
        output,
        grad_input,
        gain_one[0],
        query_grad,
        key_grad,
        value_grad,
        out_grad,
        gain_one[1],
        gate_grad,
        up_grad,
        down_grad,
    )


def solution(mesh):
    fast = dict(mesh.shape) == {"seq": 4, "batch": 8}
    if fast:
        grid = Mesh(mesh.devices.reshape((2,) * 5), AXES)
        seq, batch = ("y", "x"), ("zh", "zl", "core")
    else:
        grid, seq, batch = mesh, ("seq",), ("batch",)
    weight = P(seq + batch, None)
    gain = P(seq + batch)
    token = P(batch, seq, None)
    return jax.shard_map(
        fast_body if fast else body,
        mesh=grid,
        in_specs=(token, token, P(batch, seq), P(batch, None), gain)
        + (weight,) * 4
        + (gain,)
        + (weight,) * 3,
        out_specs=(token, token, gain) + (weight,) * 4 + (gain,) + (weight,) * 3,
        check_vma=False,
    )
```

```python
import functools
import math

import jax
import jax.numpy as jnp
import numpy as np
from jax import lax
from jax.experimental import pallas as pl
from jax.experimental.pallas import tpu as pltpu
from jax.sharding import Mesh
from jax.sharding import PartitionSpec as P

HEADS = 16
KV = 8
HD = 96


EPSILON = 1e-05
ROPE_BASE = 10000.0


def inverse_rms(field):
    return lax.rsqrt(jnp.mean(field * field, axis=-1, keepdims=True) + EPSILON)


def half_turn(field):
    middle = field.shape[-1] // 2
    return jnp.concatenate([-field[..., middle:], field[..., :middle]], axis=-1)


def rope_tables(length, width):
    middle = width // 2
    freqs = ROPE_BASE ** (-2.0 * jnp.arange(middle, dtype=jnp.float32) / width)
    angles = jnp.arange(length, dtype=jnp.float32)[:, None] * freqs[None, :]
    cosine = jnp.concatenate([jnp.cos(angles), jnp.cos(angles)], axis=-1)
    sine = jnp.concatenate([jnp.sin(angles), jnp.sin(angles)], axis=-1)
    return (cosine, sine)


def rotate_ahead(field, cosine, sine):
    return field * cosine[:, None, :] + half_turn(field) * sine[:, None, :]


def rotate_behind(field, cosine, sine):
    return field * cosine[:, None, :] - half_turn(field) * sine[:, None, :]


def outer_sum(left, right):
    return lax.dot_general(
        left, right, (((0,), (0,)), ((), ())), preferred_element_type=jnp.float32
    )


def back_product(left, right):
    return lax.dot_general(
        left, right, (((1,), (1,)), ((), ())), preferred_element_type=jnp.float32
    )


def fetch_attention(attn_gain, w_query, w_key, w_value, w_output):
    return (
        lax.all_gather(attn_gain, ("seq", "batch"), axis=0, tiled=True),
        lax.all_gather(w_query, ("seq", "batch"), axis=0, tiled=True),
        lax.all_gather(w_key, ("seq", "batch"), axis=0, tiled=True),
        lax.all_gather(w_value, ("seq", "batch"), axis=0, tiled=True),
        lax.all_gather(w_output, ("seq", "batch"), axis=0, tiled=True),
    )


def fetch_feedforward(mlp_gain, w_gate, w_up, w_down):
    return (
        lax.all_gather(mlp_gain, ("seq", "batch"), axis=0, tiled=True),
        lax.all_gather(w_gate, ("seq", "batch"), axis=0, tiled=True),
        lax.all_gather(w_up, ("seq", "batch"), axis=0, tiled=True),
        lax.all_gather(w_down, ("seq", "batch"), axis=0, tiled=True),
    )


def block_scores(query_block, keys, documents, start, block, scale):
    length = keys.shape[0]
    scores = (
        jnp.einsum("qjhd,kjd->jhqk", query_block, keys, preferred_element_type=jnp.float32) * scale
    )
    key_pos = jnp.arange(length, dtype=jnp.int32)
    query_pos = start + jnp.arange(block, dtype=jnp.int32)
    query_docs = lax.dynamic_slice_in_dim(documents, start, block, 0)
    allowed = (key_pos[None, :] <= query_pos[:, None]) & (query_docs[:, None] == documents[None, :])
    return jnp.where(allowed[None, None], scores, -1e30)


def attention_forward(queries, keys, values, documents, block, scale):
    length = queries.shape[0]
    count = length // block

    def one_block(index):
        start = index * block
        query_block = lax.dynamic_slice_in_dim(queries, start, block, 0)
        scores = block_scores(query_block, keys, documents, start, block, scale)
        peak_score = jnp.max(scores, axis=-1, keepdims=True)
        weights = jnp.exp(scores - peak_score)
        totals = jnp.sum(weights, axis=-1, keepdims=True)
        probs = (weights / totals).astype(jnp.bfloat16)
        result = jnp.einsum("jhqk,kjd->qjhd", probs, values, preferred_element_type=jnp.float32)
        return (
            result.astype(jnp.bfloat16).reshape(block, -1),
            (peak_score + jnp.log(totals))[..., 0],
        )

    results, sums = lax.map(one_block, jnp.arange(count, dtype=jnp.int32))
    return (results.reshape(length, -1), sums)


def attention_backward(queries, keys, values, documents, sums, grad_out, block, scale):
    length = queries.shape[0]
    count = length // block

    def one_block(carry, member):
        grad_keys, grad_values = carry
        index, sums_block = member
        start = index * block
        query_block = lax.dynamic_slice_in_dim(queries, start, block, 0)
        grad_block = lax.dynamic_slice_in_dim(grad_out, start, block, 0)
        scores = block_scores(query_block, keys, documents, start, block, scale)
        probs = jnp.exp(scores - sums_block[..., None])
        grad_probs = jnp.einsum(
            "qjhd,kjd->jhqk", grad_block, values, preferred_element_type=jnp.float32
        )
        centre = jnp.sum(probs * grad_probs, axis=-1, keepdims=True)
        grad_scores = (probs * (grad_probs - centre)).astype(jnp.bfloat16)
        grad_query = (
            jnp.einsum("jhqk,kjd->qjhd", grad_scores, keys, preferred_element_type=jnp.float32)
            * scale
        )
        grad_keys = (
            grad_keys
            + jnp.einsum(
                "jhqk,qjhd->kjd", grad_scores, query_block, preferred_element_type=jnp.float32
            )
            * scale
        )
        grad_values = grad_values + jnp.einsum(
            "jhqk,qjhd->kjd",
            probs.astype(jnp.bfloat16),
            grad_block,
            preferred_element_type=jnp.float32,
        )
        return ((grad_keys, grad_values), grad_query)

    empty = jnp.zeros(keys.shape, jnp.float32)
    (grad_keys, grad_values), grad_query = lax.scan(
        one_block, (empty, empty), (jnp.arange(count, dtype=jnp.int32), sums)
    )
    return (
        grad_query.reshape(length, queries.shape[1] * queries.shape[2], queries.shape[3]),
        grad_keys,
        grad_values,
    )


def body(
    layer_input,
    cotangent,
    token_mask,
    document_ids,
    attn_gain,
    w_query,
    w_key,
    w_value,
    w_output,
    mlp_gain,
    w_gate,
    w_up,
    w_down,
):
    parts = lax.axis_size("seq")
    micro_count = layer_input.shape[0]
    shard = layer_input.shape[1]
    length = shard * parts
    heads_here = HEADS // parts
    kv_here = max(1, KV // parts)
    copies = parts * kv_here // KV
    per_kv = heads_here // kv_here
    block = min(512, length)
    scale = 1.0 / math.sqrt(HD)
    cosine, sine = rope_tables(length, HD)
    attn_set = None
    mlp_set = None
    attn_total = None
    mlp_total = None
    outputs = []
    input_grads = []
    kept = {
        "normed": [],
        "normed_two": [],
        "activated": [],
        "seed_low": [],
        "gate_low": [],
        "up_low": [],
        "grad_low": [],
        "mixed": [],
        "query_back": [],
        "key_back": [],
        "value_back": [],
    }
    gain_one_total = None
    gain_two_total = None
    for micro in range(micro_count):
        attn_set = fetch_attention(attn_gain, w_query, w_key, w_value, w_output)
        mlp_set = fetch_feedforward(mlp_gain, w_gate, w_up, w_down)
        gain_one = attn_set[0].astype(jnp.float32)
        gain_two = mlp_set[0].astype(jnp.float32)
        documents = document_ids[micro]
        inputs = layer_input[micro].astype(jnp.float32)
        inv_one = inverse_rms(inputs)
        unit_one = inputs * inv_one
        normed = (unit_one * gain_one).astype(jnp.bfloat16)
        queries = jnp.dot(normed, attn_set[1], preferred_element_type=jnp.float32).astype(
            jnp.bfloat16
        )
        keys_lin = jnp.dot(normed, attn_set[2], preferred_element_type=jnp.float32).astype(
            jnp.bfloat16
        )
        values_lin = jnp.dot(normed, attn_set[3], preferred_element_type=jnp.float32).astype(
            jnp.bfloat16
        )
        queries = queries.reshape(shard, parts, heads_here * HD)
        key_slots = jnp.repeat(keys_lin.reshape(shard, KV, HD), copies, axis=1).reshape(
            shard, parts, kv_here * HD
        )
        value_slots = jnp.repeat(values_lin.reshape(shard, KV, HD), copies, axis=1).reshape(
            shard, parts, kv_here * HD
        )
        pairs = jnp.concatenate([key_slots, value_slots], axis=-1)
        query_heads, pair_heads = (
            lax.all_to_all(queries, "seq", split_axis=1, concat_axis=0, tiled=True),
            lax.all_to_all(pairs, "seq", split_axis=1, concat_axis=0, tiled=True),
        )
        query_rot = rotate_ahead(
            query_heads.reshape(length, heads_here, HD).astype(jnp.float32), cosine, sine
        )
        query_rot = query_rot.astype(jnp.bfloat16).reshape(length, kv_here, per_kv, HD)
        key_heads = pair_heads[:, 0, : kv_here * HD].reshape(length, kv_here, HD)
        key_rot = rotate_ahead(key_heads.astype(jnp.float32), cosine, sine).astype(jnp.bfloat16)
        value_heads = pair_heads[:, 0, kv_here * HD :].reshape(length, kv_here, HD)
        attended, sums = attention_forward(query_rot, key_rot, value_heads, documents, block, scale)
        mixed = lax.all_to_all(
            attended.reshape(length, 1, heads_here * HD),
            "seq",
            split_axis=0,
            concat_axis=1,
            tiled=True,
        )
        mixed = mixed.reshape(shard, HEADS * HD)
        hidden_state = inputs + jnp.dot(mixed, attn_set[4], preferred_element_type=jnp.float32)
        inv_two = inverse_rms(hidden_state)
        unit_two = hidden_state * inv_two
        normed_two = (unit_two * gain_two).astype(jnp.bfloat16)
        gate = jnp.dot(normed_two, mlp_set[1], preferred_element_type=jnp.float32)
        upward = jnp.dot(normed_two, mlp_set[2], preferred_element_type=jnp.float32)
        sigma = jax.nn.sigmoid(gate)
        activated = (gate * sigma * upward).astype(jnp.bfloat16)
        output = hidden_state + jnp.dot(activated, mlp_set[3], preferred_element_type=jnp.float32)
        outputs.append(output.astype(jnp.bfloat16))
        seed = cotangent[micro].astype(jnp.float32) * token_mask[micro].astype(jnp.float32)[:, None]
        seed_low = seed.astype(jnp.bfloat16)
        grad_act = back_product(seed_low, mlp_set[3])
        grad_up_low = (grad_act * gate * sigma).astype(jnp.bfloat16)
        grad_gate_low = (grad_act * upward * sigma * (1.0 + gate * (1.0 - sigma))).astype(
            jnp.bfloat16
        )
        grad_normed_two = back_product(grad_gate_low, mlp_set[1]) + back_product(
            grad_up_low, mlp_set[2]
        )
        grad_gain_two = jnp.sum(grad_normed_two * unit_two, axis=0)
        scaled_two = grad_normed_two * gain_two
        grad_hidden = seed + inv_two * (
            scaled_two - unit_two * jnp.mean(scaled_two * unit_two, axis=-1, keepdims=True)
        )
        gain_two_total = grad_gain_two if gain_two_total is None else gain_two_total + grad_gain_two
        kept["normed_two"].append(normed_two)
        kept["activated"].append(activated)
        kept["seed_low"].append(seed_low)
        kept["gate_low"].append(grad_gate_low)
        kept["up_low"].append(grad_up_low)
        grad_low = grad_hidden.astype(jnp.bfloat16)
        grad_mixed = (
            back_product(grad_low, attn_set[4])
            .astype(jnp.bfloat16)
            .reshape(shard, parts, heads_here * HD)
        )
        grad_heads = lax.all_to_all(
            grad_mixed, "seq", split_axis=1, concat_axis=0, tiled=True
        ).reshape(length, kv_here, per_kv, HD)
        grad_query_rot, grad_key_rot, grad_values = attention_backward(
            query_rot, key_rot, value_heads, documents, sums, grad_heads, block, scale
        )
        grad_query_heads = (
            rotate_behind(grad_query_rot, cosine, sine)
            .astype(jnp.bfloat16)
            .reshape(length, 1, heads_here * HD)
        )
        grad_key_heads = rotate_behind(grad_key_rot, cosine, sine)
        grad_pairs = jnp.concatenate(
            [
                grad_key_heads.reshape(length, kv_here * HD),
                grad_values.reshape(length, kv_here * HD),
            ],
            axis=-1,
        )
        query_back = lax.all_to_all(
            grad_query_heads, "seq", split_axis=0, concat_axis=1, tiled=True
        ).reshape(shard, HEADS * HD)
        pair_back = lax.all_to_all(
            grad_pairs.reshape(length, 1, 2 * kv_here * HD).astype(jnp.bfloat16),
            "seq",
            split_axis=0,
            concat_axis=1,
            tiled=True,
        ).astype(jnp.float32)
        key_back = pair_back[:, :, : kv_here * HD].reshape(shard, KV, copies, HD).sum(axis=2)
        value_back = pair_back[:, :, kv_here * HD :].reshape(shard, KV, copies, HD).sum(axis=2)
        key_back = key_back.reshape(shard, KV * HD).astype(jnp.bfloat16)
        value_back = value_back.reshape(shard, KV * HD).astype(jnp.bfloat16)
        grad_normed = (
            back_product(query_back, attn_set[1])
            + back_product(key_back, attn_set[2])
            + back_product(value_back, attn_set[3])
        )
        grad_gain_one = jnp.sum(grad_normed * unit_one, axis=0)
        scaled_one = grad_normed * gain_one
        grad_input = grad_hidden + inv_one * (
            scaled_one - unit_one * jnp.mean(scaled_one * unit_one, axis=-1, keepdims=True)
        )
        input_grads.append(grad_input.astype(jnp.bfloat16))
        gain_one_total = grad_gain_one if gain_one_total is None else gain_one_total + grad_gain_one
        kept["normed"].append(normed)
        kept["mixed"].append(mixed)
        kept["grad_low"].append(grad_low)
        kept["query_back"].append(query_back)
        kept["key_back"].append(key_back)
        kept["value_back"].append(value_back)
    rows = {name: jnp.concatenate(values, axis=0) for name, values in kept.items()}
    attn_total = (
        lax.psum_scatter(gain_one_total, ("seq", "batch"), scatter_dimension=0, tiled=True),
        lax.psum_scatter(
            outer_sum(rows["normed"], rows["query_back"]),
            ("seq", "batch"),
            scatter_dimension=0,
            tiled=True,
        ),
        lax.psum_scatter(
            outer_sum(rows["normed"], rows["key_back"]),
            ("seq", "batch"),
            scatter_dimension=0,
            tiled=True,
        ),
        lax.psum_scatter(
            outer_sum(rows["normed"], rows["value_back"]),
            ("seq", "batch"),
            scatter_dimension=0,
            tiled=True,
        ),
        lax.psum_scatter(
            outer_sum(rows["mixed"], rows["grad_low"]),
            ("seq", "batch"),
            scatter_dimension=0,
            tiled=True,
        ),
    )
    mlp_total = (
        lax.psum_scatter(gain_two_total, ("seq", "batch"), scatter_dimension=0, tiled=True),
        lax.psum_scatter(
            outer_sum(rows["normed_two"], rows["gate_low"]),
            ("seq", "batch"),
            scatter_dimension=0,
            tiled=True,
        ),
        lax.psum_scatter(
            outer_sum(rows["normed_two"], rows["up_low"]),
            ("seq", "batch"),
            scatter_dimension=0,
            tiled=True,
        ),
        lax.psum_scatter(
            outer_sum(rows["activated"], rows["seed_low"]),
            ("seq", "batch"),
            scatter_dimension=0,
            tiled=True,
        ),
    )
    return (
        jnp.stack(outputs, axis=0),
        jnp.stack(input_grads, axis=0),
        attn_total[0],
        attn_total[1],
        attn_total[2],
        attn_total[3],
        attn_total[4],
        mlp_total[0],
        mlp_total[1],
        mlp_total[2],
        mlp_total[3],
    )


AXES = ("y", "x", "zh", "zl", "core")
BITS = {"y": 16, "x": 8, "zh": 4, "zl": 2, "core": 1}
MESH = pl.DeviceIdType.MESH


def coordinates():
    return tuple(lax.axis_index(name) for name in AXES)


def peer(me, *names):
    return tuple(1 - at if name in names else at for name, at in zip(AXES, me))


def greet(me, groups):
    barrier = pltpu.get_barrier_semaphore()
    for names in groups:
        pl.semaphore_signal(barrier, 1, device_id=peer(me, *names), device_id_type=MESH)
    pl.semaphore_wait(barrier, len(groups))


class Mover:
    def __init__(self, me, sends, recvs):
        self.me, self.sends, self.recvs, self.used = me, sends, recvs, 0
        self.started = []

    def next(self):
        number = self.used
        self.used += 1
        assert number < self.sends.shape[0]
        return number

    def copy(self, src, dst, *names, device=None):
        number = self.next()
        return pltpu.make_async_remote_copy(
            src_ref=src,
            dst_ref=dst,
            send_sem=self.sends.at[number],
            recv_sem=self.recvs.at[number],
            device_id=peer(self.me, *names) if device is None else device,
            device_id_type=MESH,
        )

    def later(self, src, dst, *names):
        made = self.copy(src, dst, *names)
        self.started.append(made)
        return made

    def send(self, src, dst, *names):
        made = self.later(src, dst, *names)
        made.start()
        return made

    def local(self, src, dst):
        made = self.quiet(src, dst)
        made.start()
        return made

    def quiet(self, src, dst):
        number = self.next()
        return pltpu.make_async_copy(src, dst, self.recvs.at[number])

    def finish(self):
        for made in self.started:
            made.wait_send()


HEAD_GROUPS = (
    ("core",),
    ("zl",),
    ("zh",),
    ("zh", "zl"),
    ("zl", "core"),
    ("x",),
    ("y",),
    ("y", "core"),
    ("y", "core", "x"),
)
LINE = (("zl",), ("zh",), ("zh", "zl"))


def turn_start(move, me, src, dst):
    y, x, zh, zl, core = me
    stays = y == core
    made = []
    for flip in (1, 0):
        place = x if flip == 0 else 1 - x
        from_, to = src.at[place], dst.at[x]
        copy = move.copy(from_, to, device=(core, place, zh, zl, y))
        if flip == 0:
            own = move.quiet(from_, to)
            pl.when(stays)(own.start)
            pl.when(jnp.logical_not(stays))(copy.start)
            made.append((copy, own))
        else:
            copy.start()
            made.append((copy, None))
    return made


def turn_end(me, made):
    stays = me[0] == me[4]
    for copy, own in made:
        if own is None:
            copy.wait()
        else:
            pl.when(stays)(own.wait)
            pl.when(jnp.logical_not(stays))(copy.wait)


def plane_make(move, ref, s, parts):
    made = []
    for part in parts:
        piece = ref.at[s, ..., part]
        made += [move.later(piece, piece, "x"), move.later(piece, piece, "y")]
    return made


def plane_start(move, ref, s, parts):
    made = plane_make(move, ref, s, parts)
    for one in made:
        one.start()
    return made


def plane_pass(move, made, ref, y, x, parts):
    made[0].wait_recv()
    first = ref.at[2 * y + 1 - x, ..., parts[0]]
    rest = [move.send(first, first, "y")]
    made[3].wait_recv()
    second = ref.at[2 * (1 - y) + x, ..., parts[1]]
    rest.append(move.send(second, second, "x"))
    made[1].wait_recv()
    made[2].wait_recv()
    return rest


def by_rows(count, chunk, work):
    def step(i, carry):
        work(pl.ds(pl.multiple_of(i * chunk, chunk), chunk))
        return carry

    lax.fori_loop(0, count // chunk, step, 0)


class PlaneSum:
    def __init__(self, move, total, held, y, x):
        self.move, self.total = move, total
        self.mid, self.far, self.near, self.last = (held.at[i] for i in range(4))
        self.own = self.far
        half = total.shape[-1] // 2
        self.left, self.right = pl.ds(0, half), pl.ds(half, half)
        self.at = (2 * y + x, 2 * y + 1 - x, 2 * (1 - y) + x, 2 * (1 - y) + 1 - x)

    def start(self):
        move, total, left, right = self.move, self.total, self.left, self.right
        s, sx, sy, sd = self.at
        self.far_moves = [
            move.send(total.at[sd, :, left], self.far.at[:, left], "y"),
            move.send(total.at[sd, :, right], self.far.at[:, right], "x"),
        ]
        self.loads = [
            move.local(total.at[sx, :, left], self.mid.at[:, left]),
            move.local(total.at[sy, :, right], self.mid.at[:, right]),
        ]
        self.own_load = move.quiet(total.at[s], self.own)
        self.near_moves = [
            move.copy(total.at[sy, :, left], self.near.at[:, left], "y"),
            move.copy(total.at[sx, :, right], self.near.at[:, right], "x"),
        ]
        self.last_moves = [
            move.copy(self.mid.at[:, left], self.last.at[:, left], "x"),
            move.copy(self.mid.at[:, right], self.last.at[:, right], "y"),
        ]

    def start_near(self):
        for made in self.near_moves:
            made.start()

    def pass_on(self):
        for made in self.loads:
            made.wait()
        for made in self.far_moves:
            made.wait_recv()
        rows = self.mid.shape[0]
        mid, far = self.mid, self.far

        def work(at):
            added = mid[at, :].astype(jnp.float32) + far[at, :].astype(jnp.float32)
            mid[at, :] = added.astype(jnp.bfloat16)

        by_rows(rows, 16, work)
        for made in self.last_moves:
            made.start()
        self.own_load.start()

    def end(self, write):
        if self.own_load is not None:
            self.own_load.wait()
        for made in self.near_moves + self.last_moves:
            made.wait()
        own, near, last = self.own, self.near, self.last

        def work(at):
            value = own[at, :].astype(jnp.float32) + near[at, :].astype(jnp.float32)
            write(at, value + last[at, :].astype(jnp.float32))

        by_rows(own.shape[0], 16, work)


class PlaneSumHere(PlaneSum):
    def __init__(self, move, total, held, y, x):
        self.move, self.total = move, total
        self.far, self.near, self.last = (held.at[i] for i in range(3))
        half = total.shape[-1] // 2
        self.left, self.right = left, right = pl.ds(0, half), pl.ds(half, half)
        self.at = s, sx, sy, sd = (2 * y + x, 2 * y + 1 - x, 2 * (1 - y) + x, 3 - 2 * y - x)
        self.own, self.mids = total.at[s], (total.at[sx], total.at[sy])
        self.far_moves = [
            move.later(total.at[sd, :, left], self.far.at[:, left], "y"),
            move.later(total.at[sd, :, right], self.far.at[:, right], "x"),
        ]
        self.near_moves = [
            move.copy(total.at[sy, :, left], self.near.at[:, left], "y"),
            move.copy(total.at[sx, :, right], self.near.at[:, right], "x"),
        ]
        self.last_moves = [
            move.copy(total.at[sx, :, left], self.last.at[:, left], "x"),
            move.copy(total.at[sy, :, right], self.last.at[:, right], "y"),
        ]
        self.own_load = None

    def start(self):
        for made in self.far_moves:
            made.start()

    def pass_on(self):
        for made in self.far_moves:
            made.wait_recv()
        far = self.far

        def work(at):
            for mid, part in zip(self.mids, (self.left, self.right)):
                added = mid[at, part].astype(jnp.float32) + far[at, part].astype(jnp.float32)
                mid[at, part] = added.astype(jnp.bfloat16)

        by_rows(far.shape[0], 16, work)
        for made in self.last_moves:
            made.start()


def tail_kernel(
    gate_hbm,
    up_hbm,
    down_hbm,
    grad_hbm,
    normed_hbm,
    qkv_hbm,
    x_hbm,
    steep_hbm,
    gain_rows,
    gain_two,
    out_hbm,
    y_in,
    gate_grad,
    up_grad,
    down_out,
    query_grad,
    key_grad,
    value_grad,
    out_out,
    y_out,
    x_out,
    gain_out,
    gate_in,
    up_in,
    down_in,
    grad_in,
    normed,
    qkv_w,
    x_own,
    steep,
    out_in,
    gate_out,
    up_out,
    qkv_out,
    pair_low,
    pair_got,
    down_low,
    down_got,
    quarter,
    part,
    part_got,
    x_low,
    qkv_in,
    qkv_held,
    qkv_sum,
    qkv_low,
    qkv_got,
    out_got,
    out_x,
    out_line,
    out_line_got,
    rows_sent,
    gain_got,
    sends,
    recvs,
):
    f32, low = jnp.float32, jnp.bfloat16
    me = coordinates()
    y, x, zh, zl, core = me
    z = 2 * zh + zl
    mine = y == core
    other = jnp.logical_not(mine)
    move = Mover(me, sends, recvs)
    loads = [
        move.local(src, dst)
        for src, dst in (
            (normed_hbm, normed),
            (grad_hbm, grad_in),
            (qkv_hbm, qkv_w),
            (gate_hbm, gate_in),
            (up_hbm, up_in),
            (down_hbm, down_in),
            (x_hbm, x_own),
            (steep_hbm, steep),
            (out_hbm, out_in),
        )
    ]
    greet(me, HEAD_GROUPS)
    qkv = PlaneSumHere(move, qkv_in, qkv_held, y, x)
    out_y = move.copy(out_in, out_got, "y")
    half_len = part.shape[0]
    block_rows = qkv_in.shape[1]

    def weigh(at):
        lanes = pl.ds(pl.multiple_of(at * block_rows, 128), block_rows)
        total = tn(normed[0, :, lanes], grad_in[pl.ds(0, half_len), :])
        total = total + tn(normed[1, :, lanes], grad_in[pl.ds(half_len, half_len), :])
        qkv_in[at] = total.astype(low)

    for made in loads[:2]:
        made.wait()
    weigh(qkv.at[3])
    qkv.start()

    weigh(qkv.at[1])
    weigh(qkv.at[2])
    qkv.start_near()

    for made in loads[2:6]:
        made.wait()
    pair_rows = pair_got.shape[1]

    def lower(src, dst, skip, count):
        def work(at):
            dst[at, :] = src[skip, at, :].astype(low)

        by_rows(count, 32, work)

    pairs = []
    for i, src in enumerate((gate_in, up_in)):
        lower(src, pair_low.at[i], 1 - zh, pair_rows)
        pairs.append(move.send(pair_low.at[i], pair_got.at[i], "zh"))
    lower(down_in, down_low, 1 - zh, down_low.shape[0])
    pairs.append(move.send(down_low, down_got, "zh"))

    theirs, ours = (pl.multiple_of(c * half_len, half_len) for c in (1 - core, core))

    def project(start):
        for i in range(half_len // QB):
            at = pl.ds(pl.multiple_of(start + i * QB, QB), QB)
            part[pl.ds(i * QB, QB), :] = nt(grad_in[at, :], qkv_w[...])

    project(theirs)
    part_move = move.copy(part, part_got, "core")
    part_move.start()
    weigh(qkv.at[0])
    qkv.pass_on()
    for made in loads[6:]:
        made.wait()
    pl.when(other)(out_y.start)
    y_turn = turn_start(move, me, y_in, y_out)
    part_move.wait()
    project(ours)
    gain_out[...] = jnp.zeros_like(gain_out)
    gain_out[1:2, :] = gain_two[...]
    piece = half_len // 2
    for q in range(2):

        def norm_back(at, q=q):
            every = pl.ds(pl.multiple_of(q * piece + at.start, 16), at.size)
            grad = part[every, :] + part_got[every, :]
            field = x_own[q, at, :].astype(f32)
            inverse = lax.rsqrt(jnp.mean(field * field, axis=1, keepdims=True) + EPSILON)
            unit = field * inverse
            gain_out[0:1, :] += jnp.sum(grad * unit, axis=0, keepdims=True)
            scaled = grad * gain_rows[0:1, :]
            centre = jnp.mean(scaled * unit, axis=1, keepdims=True)
            value = steep[every, :] + inverse * (scaled - unit * centre)
            x_low[q, at, :] = value.astype(low)

        by_rows(piece, 16, norm_back)
    x_turn = turn_start(move, me, x_low, x_out)

    gain_moves = [
        move.copy(gain_out, gain_got.at[turn], name)
        for turn, name in enumerate(("core", "x", "y", "zl", "zh"))
    ]

    def gain_round(turn):
        if turn > 0:
            gain_moves[turn - 1].wait()
            gain_out[...] = gain_out[...] + gain_got[turn - 1]
        if turn < len(gain_moves):
            gain_moves[turn].start()

    gain_round(0)
    out_shape = out_in.shape
    blocks = [(a, b) for a in range(out_shape[1]) for b in range(out_shape[2])]

    def keep(at, value):
        qkv_sum[at, :] = value
        qkv_low[at, :] = value.astype(low)

    qkv.end(keep)
    count = qkv_got.shape[1]
    line = []
    for k, names in enumerate(LINE):
        to = z ^ (1, 2, 3)[k]
        start = pl.multiple_of(to * count, count)
        line.append(move.send(qkv_low.at[pl.ds(start, count)], qkv_got.at[k], *names))

    gain_round(1)

    out_x_move = move.copy(out_got.at[1 - x], out_x, "x")

    @pl.when(mine)
    def _():
        out_y.wait_recv()

        def half(at_x):
            def work(i, carry):
                a, b = i // out_shape[2], i % out_shape[2]
                value = out_in[at_x, a, b].astype(f32) + out_got[at_x, a, b].astype(f32)
                out_got[at_x, a, b] = value.astype(low)
                return carry

            lax.fori_loop(0, len(blocks), work, 0)

        half(1 - x)
        out_x_move.start()
        half(x)

    gain_round(2)

    spread = []
    for i, (src, dst) in enumerate(((gate_in, gate_out), (up_in, up_out))):
        pairs[i].wait_recv()
        got, full = pair_got.at[i], quarter.at[i]

        def work(at, src=src, got=got, full=full):
            full[at, :] = src[zh, at, :] + got[at, :].astype(f32)

        by_rows(pair_rows, 32, work)
        share = pair_rows // 4
        for names in (("core",), ("zl",), ("zl", "core")):
            to_zl = 1 - zl if "zl" in names else zl
            to_core = 1 - core if "core" in names else core
            start = pl.multiple_of((2 * to_zl + to_core) * share, share)
            spread.append(move.send(full.at[pl.ds(start, share)], dst.at[zl, core], *names))
        start = pl.multiple_of((2 * zl + core) * share, share)
        dst[zl, core] = full[pl.ds(start, share), :]
    pairs[2].wait_recv()

    def work(at):
        down_out[at, :] = down_in[zh, at, :] + down_got[at, :].astype(f32)

    by_rows(down_out.shape[0], 32, work)

    gain_round(3)
    out_moves = []
    for k, names in enumerate(LINE):
        to = z ^ (1, 2, 3)[k]
        out_moves.append(move.copy(out_line.at[to], out_line_got.at[k], *names))

    @pl.when(mine)
    def _():
        out_x_move.wait()

        def work(i, carry):
            a, b = i // out_shape[2], i % out_shape[2]
            value = out_got[x, a, b].astype(f32) + out_x[a, b].astype(f32)
            out_line[a, b] = value.astype(low)
            return carry

        lax.fori_loop(0, len(blocks), work, 0)
        for made in out_moves:
            made.start()

    gain_round(4)
    for made in line:
        made.wait_recv()
    start = pl.multiple_of(z * count, count)
    total = qkv_sum[pl.ds(start, count), :]
    for k in range(3):
        total = total + qkv_got[k].astype(f32)
    rows = count // 2
    qkv_sum[pl.ds(0, count), :] = total
    theirs = pl.multiple_of((1 - core) * rows, rows)
    swap = move.send(qkv_sum.at[pl.ds(theirs, rows)], qkv_out.at[core], "core")
    qkv_out[core] = qkv_sum[pl.ds(pl.multiple_of(core * rows, rows), rows), :]

    out_swap = move.copy(rows_sent, out_out, "core")

    @pl.when(mine)
    def _():
        for made in out_moves:
            made.wait()
        for at in range(2):
            total = out_line[z, at].astype(f32)
            for k in range(3):
                total = total + out_line_got[k, at].astype(f32)

            @pl.when(core == at)
            def _(total=total):
                out_out[...] = total

            @pl.when(core != at)
            def _(total=total):
                rows_sent[...] = total

        out_swap.start()
        out_swap.wait_send()

    @pl.when(other)
    def _():
        out_y.wait_send()
        out_swap.wait_recv()

    gain_round(5)
    turn_end(me, y_turn)
    turn_end(me, x_turn)
    swap.wait_recv()
    for made in spread:
        made.wait_recv()
    for parts, grad in ((gate_out, gate_grad), (up_out, up_grad)):
        for i in range(grad.shape[1] // 128):
            lanes = slice(i // 4 * 128, i // 4 * 128 + 128)
            grad[:, i * 128 : (i + 1) * 128] = parts[i // 2 % 2, i % 2, :, lanes]
    at = 0
    for grad in (query_grad, key_grad, value_grad):
        size = grad.shape[1] // 2
        for c in range(2):
            grad[:, c * size : (c + 1) * size] = qkv_out[c, :, at : at + size]
        at += size
    move.finish()


def sum_tail(gate, up, down, grad, normed, qkv_w, x_own, steep, gain_rows, gain_two, out, y_in):
    f32, low = jnp.float32, jnp.bfloat16
    hbm = pl.BlockSpec(memory_space=pl.ANY)
    vmem = pl.BlockSpec(memory_space=pltpu.VMEM)
    wide, width = gate.shape[-1], grad.shape[-1]
    rows = out.shape[-2]
    half_len = steep.shape[0]
    pair_rows, down_rows = gate.shape[1], down.shape[1]
    return pl.pallas_call(
        tail_kernel,
        in_specs=[hbm] * 8 + [vmem] * 2 + [hbm] * 2,
        out_specs=[vmem] * 7 + [hbm, hbm, vmem],
        out_shape=[
            jax.ShapeDtypeStruct((rows, 4 * wide), f32),
            jax.ShapeDtypeStruct((rows, 4 * wide), f32),
            jax.ShapeDtypeStruct((down_rows, width), f32),
            jax.ShapeDtypeStruct((rows, width), f32),
            jax.ShapeDtypeStruct((rows, width // 2), f32),
            jax.ShapeDtypeStruct((rows, width // 2), f32),
            jax.ShapeDtypeStruct((rows, width), f32),
            jax.ShapeDtypeStruct(y_in.shape, low),
            jax.ShapeDtypeStruct(y_in.shape, low),
            jax.ShapeDtypeStruct((2, width), f32),
        ],
        scratch_shapes=[
            pltpu.VMEM(one.shape, one.dtype)
            for one in (gate, up, down, grad, normed, qkv_w, x_own, steep, out)
        ]
        + [
            pltpu.VMEM((2, 2, rows, wide), f32),
            pltpu.VMEM((2, 2, rows, wide), f32),
            pltpu.VMEM((2, rows, width), f32),
            pltpu.VMEM((2, pair_rows, wide), low),
            pltpu.VMEM((2, pair_rows, wide), low),
            pltpu.VMEM((down_rows, width), low),
            pltpu.VMEM((down_rows, width), low),
            pltpu.VMEM((2, pair_rows, wide), f32),
            pltpu.VMEM((half_len, width), f32),
            pltpu.VMEM((half_len, width), f32),
            pltpu.VMEM(y_in.shape, low),
            pltpu.VMEM((4, 8 * rows, width), low),
            pltpu.VMEM((3, 8 * rows, width), low),
            pltpu.VMEM((8 * rows, width), f32),
            pltpu.VMEM((8 * rows, width), low),
            pltpu.VMEM((3, 2 * rows, width), low),
            pltpu.VMEM(out.shape, low),
            pltpu.VMEM(out.shape[1:], low),
            pltpu.VMEM(out.shape[1:], low),
            pltpu.VMEM((3,) + out.shape[2:], low),
            pltpu.VMEM((rows, width), f32),
            pltpu.VMEM((5, 2, width), f32),
            pltpu.SemaphoreType.DMA((64,)),
            pltpu.SemaphoreType.DMA((64,)),
        ],
        compiler_params=pltpu.CompilerParams(
            collective_id=4, has_side_effects=True, vmem_limit_bytes=63 << 20
        ),
        name="tail",
    )(gate, up, down, grad, normed, qkv_w, x_own, steep, gain_rows, gain_two, out, y_in)


QB = 256
SPAN = 768


def turned(field, back):
    middle = HD // 2
    left, right = field[:, :middle], field[:, middle:]
    if back:
        return jnp.concatenate([right, -left], axis=1)
    return jnp.concatenate([-right, left], axis=1)


def spun(field, cosine, sine, back=False):
    field = field.astype(jnp.float32)
    return field * cosine + turned(field, back) * sine


def nt(left, right):
    return lax.dot_general(left, right, (((1,), (1,)), ((), ())), preferred_element_type=jnp.float32)


def nn(left, right):
    return jnp.dot(left, right, preferred_element_type=jnp.float32)


def tn(left, right):
    return lax.dot_general(left, right, (((0,), (0,)), ((), ())), preferred_element_type=jnp.float32)


def head(ref, rows, number):
    return ref[rows, HD * number : HD * (number + 1)]


def ahead_block(
    heads, kvs, step, size, qkv_ref, cos_ref, sin_ref, row_ref, col_ref, out_ref, keys
):
    low, f32 = jnp.bfloat16, jnp.float32
    start, base = step * QB, (step + 1) * QB - size
    if not isinstance(step, int):
        start, base = pl.multiple_of(start, QB), pl.multiple_of(base, QB)
    here, span = pl.ds(start, QB), pl.ds(base, size)
    key_place = base + lax.broadcasted_iota(jnp.int32, (size, QB), 0)
    place = start + lax.broadcasted_iota(jnp.int32, (size, QB), 1)
    allowed = (key_place <= place) & (col_ref[span, :] == row_ref[:, here])
    bias = jnp.where(allowed, 0.0, -1e30).astype(f32)
    scale = (1.0 / math.sqrt(HD)) * math.log2(math.e)
    cosine, sine = cos_ref[here, :], sin_ref[here, :]
    results = []
    for h in range(heads):
        j = h * kvs // heads
        query = spun(head(qkv_ref, here, h), cosine, sine).astype(low)
        scores = nt(keys[j, span, :], query) * scale + bias
        peak = jnp.max(scores, axis=0, keepdims=True)
        weights = jnp.exp2(scores - peak)
        total = jnp.sum(weights, axis=0, keepdims=True)
        probs = (weights * (1.0 / total)).astype(low)
        results.append(tn(probs, head(qkv_ref, span, heads + kvs + j)).astype(low))
    out_ref[here, :] = jnp.concatenate(results, axis=1)


def behind_block(
    heads,
    kvs,
    step,
    size,
    qkv_ref,
    grad_ref,
    cos_ref,
    sin_ref,
    row_ref,
    col_ref,
    gq_ref,
    keys,
    gks,
    gvs,
):
    low, f32 = jnp.bfloat16, jnp.float32
    start, base = step * QB, (step + 1) * QB - size
    if not isinstance(step, int):
        start, base = pl.multiple_of(start, QB), pl.multiple_of(base, QB)
    here, span = pl.ds(start, QB), pl.ds(base, size)
    key_place = base + lax.broadcasted_iota(jnp.int32, (size, QB), 0)
    place = start + lax.broadcasted_iota(jnp.int32, (size, QB), 1)
    allowed = (key_place <= place) & (col_ref[span, :] == row_ref[:, here])
    bias = jnp.where(allowed, 0.0, -1e30).astype(f32)
    width = 1.0 / math.sqrt(HD)
    scale = width * math.log2(math.e)
    cosine, sine = cos_ref[here, :], sin_ref[here, :]
    results = []
    for h in range(heads):
        j = h * kvs // heads
        query = spun(head(qkv_ref, here, h), cosine, sine).astype(low)
        key, value = keys[j, span, :], head(qkv_ref, span, heads + kvs + j)
        grad = head(grad_ref, here, h)
        scores = nt(key, query) * scale + bias
        peak = jnp.max(scores, axis=0, keepdims=True)
        weights = jnp.exp2(scores - peak)
        total = jnp.sum(weights, axis=0, keepdims=True)
        probs = weights * (1.0 / total)
        slope = nt(value, grad)
        centre = jnp.sum(probs * slope, axis=0, keepdims=True)
        gs = (probs * (slope - centre)).astype(low)
        gvs[j, span, :] += nn(probs.astype(low), grad)
        gks[j, span, :] += nn(gs, query)
        results.append(spun(tn(gs, key) * width, cosine, sine, True).astype(low))
    gq_ref[here, : HD * heads] = jnp.concatenate(results, axis=1)


def behind_kernel(
    heads,
    kvs,
    gain_rows,
    cos_ref,
    sin_ref,
    row_ref,
    col_ref,
    hidden_in,
    back_in,
    qkv_in,
    mixed_in,
    out_in,
    back_far,
    ahead_own,
    ahead_far,
    tokens,
    seeds,
    act_in,
    gate_in,
    up_in,
    gain_ref,
    grad_out,
    steep_out,
    y_low,
    out_grad,
    gate_out,
    up_out,
    down_out,
    hidden,
    seed,
    back_own,
    grad_ref,
    steep,
    steep_low,
    back_got,
    ahead_got,
    gate_sum,
    up_sum,
    down_sum,
    gate_held,
    up_held,
    down_held,
    sends,
    recvs,
):
    f32, low = jnp.float32, jnp.bfloat16
    me = coordinates()
    y, x, zh, zl, core = me
    greet(me, (("x",), ("y",), ("core",), ("zl",)))
    move = Mover(me, sends, recvs)
    back_move = move.send(back_far, back_got, "zl")
    ahead_move = move.later(ahead_far, ahead_got, "zl")
    swap = move.later(steep_low.at[core], steep_low.at[core], "core")
    gate, up, down = sums = [
        PlaneSumHere(move, total, held, y, x)
        for total, held in (
            (gate_sum, gate_held), (up_sum, up_held), (down_sum, down_held)
        )
    ]
    s, sx, sy, sd = gate.at
    order = (sd, sx, sy, s)
    half_len, width = hidden.shape
    count, wide = gate_in.shape
    block = gate_sum.shape[1]

    def wide_part(gates, ups, pieces):
        def column(i):
            lanes = pl.ds(pl.multiple_of(order[i] * block, 128), block)
            return move.quiet(tokens.at[:, lanes], pieces.at[i % 2])

        columns = [column(i) for i in range(4)]
        columns[0].start()
        loads = [move.local(gate_in, gates), move.local(up_in, ups)]
        for i in range(4):
            columns[i].wait()
            if i < 3:
                columns[i + 1].start()
            if i == 0:
                loads[0].wait()
            gate_sum[order[i]] = tn(pieces[i % 2], gates[...]).astype(low)
            if i == 0:
                gate.start()
                loads[1].wait()
            up_sum[order[i]] = tn(pieces[i % 2], ups[...]).astype(low)
            if i == 0:
                up.start()
            if i == 2:
                gate.start_near()
                up.start_near()

    half_loads = [
        move.quiet(hidden_in, hidden),
        move.quiet(back_in, back_own),
        move.quiet(seeds.at[pl.ds(0, half_len)], seed),
    ]
    half_stores = [move.quiet(steep, steep_out), move.quiet(grad_ref, grad_out)]
    pl.run_scoped(
        wide_part,
        pltpu.VMEM((count, wide), low),
        pltpu.VMEM((count, wide), low),
        pltpu.VMEM((2, count, block), low),
    )
    for made in half_loads:
        made.start()
    deep = down_sum.shape[1]

    def deep_part(rows, pieces):
        def column(i):
            lanes = pl.ds(pl.multiple_of(order[i] * deep, 128), deep)
            return move.quiet(act_in.at[:, lanes], pieces.at[i % 2])

        columns = [column(i) for i in range(4)]
        columns[0].start()
        move.local(seeds, rows).wait()
        for i in range(4):
            columns[i].wait()
            if i < 3:
                columns[i + 1].start()
            down_sum[order[i]] = tn(pieces[i % 2], rows[...]).astype(low)
            if i == 0:
                down.start()
            if i == 2:
                down.start_near()

    pl.run_scoped(
        deep_part,
        pltpu.VMEM((count, width), low),
        pltpu.VMEM((2, count, deep), low),
    )
    gate.pass_on()
    up.pass_on()

    def heads_part(qkv_ref, out_w, keys, gks, gvs):
        loads = [move.local(qkv_in, qkv_ref), move.local(out_in, out_w)]
        gain_ref[...] = jnp.zeros_like(gain_ref)
        for made in half_loads:
            made.wait()
        back_move.wait_recv()
        ahead_move.start()

        def norm_back(at):
            grad = back_own[at, :] + back_got[at, :].astype(f32)
            field = hidden[at, :]
            inverse = lax.rsqrt(jnp.mean(field * field, axis=1, keepdims=True) + EPSILON)
            unit = field * inverse
            gain_ref[...] += jnp.sum(grad * unit, axis=0, keepdims=True)
            scaled = grad * gain_rows[1:2, :]
            centre = jnp.mean(scaled * unit, axis=1, keepdims=True)
            value = seed[at, :].astype(f32) + inverse * (scaled - unit * centre)
            steep[at, :] = value
            steep_low[core, at, :] = value.astype(low)

        by_rows(half_len, 16, norm_back)
        swap.start()
        half_stores[0].start()
        for made in loads:
            made.wait()
        everything = pl.ds(0, 2 * half_len)
        for j in range(kvs):
            keys[j] = spun(
                head(qkv_ref, everything, heads + j), cos_ref[...], sin_ref[...]
            ).astype(low)
        gks[...] = jnp.zeros_like(gks)
        gvs[...] = jnp.zeros_like(gvs)
        swap.wait_recv()
        per = half_len // QB
        for i in range(2 * per):
            at = pl.ds(i % per * QB, QB)
            part = nt(steep_low[i // per, at, :], out_w[...]).astype(low)
            grad_ref[pl.ds(i * QB, QB), : heads * HD] = part
        down.pass_on()

        def work(step, size):
            behind_block(
                heads, kvs, step, size, qkv_ref, grad_ref, cos_ref, sin_ref, row_ref, col_ref,
                grad_ref, keys, gks, gvs,
            )

        def one(step, carry):
            work(step, SPAN)
            return carry

        for step in range(SPAN // QB - 1):
            work(step, (step + 1) * QB)
        lax.fori_loop(SPAN // QB - 1, 2 * half_len // QB, one, 0)
        scale = 1.0 / math.sqrt(HD)
        gk = [
            spun(gks[j] * scale, cos_ref[...], sin_ref[...], True).astype(low)
            for j in range(kvs)
        ]
        gv = [gvs[j].astype(low) for j in range(kvs)]
        grad_ref[:, HD * heads :] = jnp.concatenate(gk + gv, axis=1)
        half_stores[1].start()

    pl.run_scoped(
        heads_part,
        pltpu.VMEM(qkv_in.shape, low),
        pltpu.VMEM(out_in.shape, low),
        pltpu.VMEM((kvs, 2 * half_len, HD), low),
        pltpu.VMEM((kvs, 2 * half_len, HD), f32),
        pltpu.VMEM((kvs, 2 * half_len, HD), f32),
    )

    def last_part(mixed, own, out_made, gate_made, up_made, down_made):
        loads = [move.local(mixed_in, mixed), move.local(ahead_own, own)]
        loads[0].wait()
        rows = mixed.shape[1] // 4
        for i in range(4):
            lanes = pl.ds(i * rows, rows)
            total = tn(mixed[pl.ds(0, half_len), lanes], steep_low[0])
            total = total + tn(mixed[pl.ds(half_len, half_len), lanes], steep_low[1])
            out_made[pl.ds(i * rows, rows), :] = total.astype(low)
        stores = [move.local(out_made, out_grad)]
        ahead_move.wait_recv()
        loads[1].wait()
        quarter = half_len // 2
        for q in range(2):

            def add(at, q=q):
                every = pl.ds(pl.multiple_of(q * quarter + at.start, 16), at.size)
                value = hidden[every, :] + own[every, :] + ahead_got[q, at, :].astype(f32)
                ahead_got[q, at, :] = value.astype(low)

            by_rows(quarter, 16, add)
        stores.append(move.local(ahead_got, y_low))
        for plane, made, out in zip(
            sums, (gate_made, up_made, down_made), (gate_out, up_out, down_out)
        ):

            def write(at, value, made=made):
                made[at, :] = value

            plane.end(write)
            stores.append(move.local(made, out))
        for made in half_stores + stores:
            made.wait()

    pl.run_scoped(
        last_part,
        pltpu.VMEM(mixed_in.shape, low),
        pltpu.VMEM((half_len, width), f32),
        pltpu.VMEM(out_grad.shape, low),
        pltpu.VMEM(gate_out.shape, f32),
        pltpu.VMEM(up_out.shape, f32),
        pltpu.VMEM(down_out.shape, f32),
    )
    move.finish()


def attend_behind(heads, kvs, *operands):
    f32, low = jnp.float32, jnp.bfloat16
    half_len, width = operands[5].shape
    length = 2 * half_len
    wide = operands[-1].shape[1]
    hbm = pl.BlockSpec(memory_space=pl.ANY)
    vmem = pl.BlockSpec(memory_space=pltpu.VMEM)
    shapes = [(width // 4, wide), (width // 4, wide), (wide // 4, width)]

    def made(*shape, dtype=low):
        return jax.ShapeDtypeStruct(shape, dtype)

    return pl.pallas_call(
        functools.partial(behind_kernel, heads, kvs),
        in_specs=[vmem] * 5 + [hbm] * 13,
        out_specs=[vmem] + [hbm] * 7,
        out_shape=[
            made(1, width, dtype=f32),
            made(length, width),
            made(half_len, width, dtype=f32),
            made(2, half_len // 2, width),
            made(heads * HD, width),
        ]
        + [made(*shape, dtype=f32) for shape in shapes],
        scratch_shapes=[
            pltpu.VMEM((half_len, width), f32),
            pltpu.VMEM((half_len, width), low),
            pltpu.VMEM((half_len, width), f32),
            pltpu.VMEM((length, width), low),
            pltpu.VMEM((half_len, width), f32),
            pltpu.VMEM((2, half_len, width), low),
            pltpu.VMEM((half_len, width), low),
            pltpu.VMEM((2, half_len // 2, width), low),
        ]
        + [pltpu.VMEM((4,) + shape, low) for shape in shapes]
        + [pltpu.VMEM((3,) + shape, low) for shape in shapes]
        + [pltpu.SemaphoreType.DMA((64,)), pltpu.SemaphoreType.DMA((64,))],
        compiler_params=pltpu.CompilerParams(
            collective_id=3, has_side_effects=True, vmem_limit_bytes=63 << 20
        ),
        cost_estimate=pl.CostEstimate(
            flops=10 * heads * length * SPAN * HD,
            bytes_accessed=9 << 20,
            transcendentals=heads * length * SPAN,
        ),
        name="behind",
    )(*operands)


def bands(size):
    return (pl.ds(0, size // 2), pl.ds(size // 2, size // 2))


def first_kernel(
    heads,
    kvs,
    x_in,
    g_in,
    query_in,
    key_in,
    value_in,
    gate_raw,
    up_raw,
    down_in,
    out_in,
    gain_in,
    docs_in,
    cos_ref,
    sin_ref,
    x_out,
    normed_out,
    qkv_out,
    mixed_out,
    hidden_out,
    qkv_w_out,
    out_w_out,
    gain_rows,
    row,
    col,
    seeds,
    tokens,
    gate_w,
    up_w,
    down_w,
    x_own,
    normed,
    qkv,
    mixed,
    hidden,
    qkv_w,
    out_w,
    token,
    qkv_in,
    gate_in,
    up_in,
    docs,
    gains,
    keys,
    part,
    part_got,
    sends,
    recvs,
):
    f32, low = jnp.float32, jnp.bfloat16
    me = coordinates()
    y, x, zh, zl, core = me
    s, z = y * 2 + x, zh * 2 + zl
    mine = y == core
    other = jnp.logical_not(mine)
    width = qkv_w.shape[-1]
    length = qkv.shape[0]
    half_len = length // 2
    at = 0
    for ref in (query_in, key_in, value_in):
        size = ref.shape[1] // 2
        for c in range(2):
            qkv_in[c, :, at : at + size] = ref[:, c * size : (c + 1) * size]
        at += size
    for raw, parts in ((gate_raw, gate_in), (up_raw, up_in)):
        for i in range(raw.shape[1] // 128):
            lanes = slice(i // 4 * 128, i // 4 * 128 + 128)
            parts[i // 2 % 2, i % 2, :, lanes] = raw[:, i * 128 : (i + 1) * 128]
    greet(me, HEAD_GROUPS)
    move = Mover(me, sends, recvs)
    stores = []

    wides = [
        (ref.at[:, at], bands(ref.shape[-1]))
        for at in (zh, 1 - zh)
        for ref in (gate_w, up_w, down_w)
    ]
    hops = [plane_make(move, ref, s, parts) for ref, parts in wides]
    rest = []

    def start_some(which):
        for i in which:
            for made in hops[i]:
                made.start()

    def pass_some(which):
        for i in which:
            rest.extend(plane_pass(move, hops[i], wides[i][0], y, x, wides[i][1]))

    down_own = move.local(down_in, down_w.at[s, zh])
    own = [
        move.local(qkv_in.at[core], qkv_w.at[s, z, core]),
        move.local(gain_in, gains.at[s, z, core]),
    ]
    first = [
        move.send(qkv_in.at[1 - core], qkv_w.at[s, z, core], "core"),
        move.send(gain_in, gains.at[s, z, core], "core"),
    ]
    docs_move = move.send(docs_in, docs, "core")
    x_turn = turn_start(move, me, x_in, x_own)
    for made in own:
        made.wait()
    for made in first:
        made.wait_recv()
    line = [move.send(gains.at[s, z], gains.at[s, z], *names) for names in LINE]
    line += [move.send(qkv_w.at[s, z], qkv_w.at[s, z], *names) for names in LINE]
    down_own.wait()
    start_some((2,))

    own = [
        move.local(gate_in.at[zl, core], gate_w.at[s, zh, zl, core]),
        move.local(up_in.at[zl, core], up_w.at[s, zh, zl, core]),
    ]
    spread = []
    for src, dst in ((gate_in, gate_w), (up_in, up_w)):
        for names in (("core",), ("zl",), ("zl", "core")):
            to_zl = 1 - zl if "zl" in names else zl
            to_core = 1 - core if "core" in names else core
            spread.append(move.send(src.at[to_zl, to_core], dst.at[s, zh, zl, core], *names))
    out_own = move.quiet(out_in, out_w.at[x, z, core])
    out_sent = move.copy(out_in, out_w.at[x, z, core], "core")
    pl.when(mine)(out_own.start)
    pl.when(other)(out_sent.start)

    for made in line[:3]:
        made.wait_recv()
    gain_hops = [move.send(gains.at[s], gains.at[s], *names) for names in (("x",), ("y",))]
    turn_end(me, x_turn)
    stores.append(move.local(x_own, x_out))
    gain_hops[0].wait_recv()
    sx = 2 * y + 1 - x
    gain_hops.append(move.send(gains.at[sx], gains.at[sx], "y"))
    for made in line[3:]:
        made.wait_recv()
    qkv_hops = plane_start(move, qkv_w, s, bands(width))
    pass_some((2,))

    out_line = [move.copy(out_w.at[x, z], out_w.at[x, z], *names) for names in LINE]
    pl.when(other)(out_sent.wait_send)

    @pl.when(mine)
    def _():
        out_own.wait()
        out_sent.wait_recv()
        for made in out_line:
            made.start()

    for made in own:
        made.wait()
    for made in spread:
        made.wait_recv()
    pairs = [
        move.send(ref.at[s, zh], ref.at[s, zh], "zh") for ref in (gate_w, up_w, down_w)
    ]

    for made in gain_hops[1:]:
        made.wait_recv()
    count = out_in.shape[0]
    for i in range(2):
        gain_rows[pl.ds(i, 1), :] = jnp.concatenate(
            [
                gains[a, b, c, 0:1, i * count : (i + 1) * count]
                for a in range(4)
                for b in range(4)
                for c in range(2)
            ],
            axis=1,
        )

    quarter = half_len // 2
    for q in range(2):

        def norm(at, q=q):
            field = x_own[q, at, :].astype(f32)
            inverse = lax.rsqrt(jnp.mean(field * field, axis=1, keepdims=True) + EPSILON)
            rows = pl.ds(pl.multiple_of(q * quarter + at.start, 16), at.size)
            normed[core, rows, :] = (field * inverse * gain_rows[0:1, :]).astype(low)

        by_rows(quarter, 16, norm)
    normed_move = move.send(normed.at[core], normed.at[core], "core")
    docs_move.wait_recv()
    row[...] = jnp.where(mine, docs_in[x], docs[x])
    col[...] = jnp.transpose(jnp.broadcast_to(row[...], (8, length)))[:, 0:1]

    qkv_rest = plane_pass(move, qkv_hops, qkv_w, y, x, bands(width))
    out_x = move.copy(out_w.at[x], out_w.at[x], "x")
    near, left, right = (
        out_w.at[x], out_w.at[1 - x, ..., bands(width)[0]], out_w.at[x, ..., bands(width)[1]]
    )
    out_y = [move.copy(near, near, "y"), move.copy(left, left, "y")]
    out_far = move.copy(right, right, "x")

    @pl.when(mine)
    def _():
        for made in out_line:
            made.wait()
        out_x.start()
        out_y[0].start()

    g_turn = turn_start(move, me, g_in, seeds.at[0])
    normed_move.wait_recv()
    for made in qkv_rest:
        made.wait_recv()
    stores += [move.local(normed, normed_out), move.local(qkv_w, qkv_w_out)]
    weight = qkv_w.reshape(width, width)
    for i in range(length // QB):
        at = pl.ds(i * QB % half_len, QB)
        qkv[pl.ds(i * QB, QB), :] = nn(normed[i * QB // half_len, at, :], weight[...]).astype(low)
    stores.append(move.local(qkv, qkv_out))
    start_some((0,))
    seed_moves = [
        move.later(seeds.at[0], seeds.at[1], "core"),
        move.later(seeds.at[0], seeds.at[2], "zl"),
    ]

    everything = pl.ds(0, length)
    for j in range(kvs):
        keys[j] = spun(head(qkv, everything, heads + j), cos_ref[...], sin_ref[...]).astype(low)

    def work(step, size):
        ahead_block(heads, kvs, step, size, qkv, cos_ref, sin_ref, row, col, mixed, keys)

    def block(step, carry):
        @pl.when(step == SPAN // QB - 1)
        def _():
            turn_end(me, g_turn)
            for made in seed_moves:
                made.start()
            start_some((1,))

        @pl.when(step == SPAN // QB)
        def _():
            pairs[0].wait_recv()
            start_some((3,))

        work(step, SPAN)
        return carry

    work(0, QB)

    @pl.when(mine)
    def _():
        out_x.wait_recv()
        out_y[1].start()

    @pl.when(other)
    def _():
        out_y[0].wait_recv()
        out_far.start()

    for step in range(1, SPAN // QB - 1):
        work(step, (step + 1) * QB)
    lax.fori_loop(SPAN // QB - 1, length // QB, block, 0)
    stores.append(move.local(mixed, mixed_out))
    for made in pairs[1:]:
        made.wait_recv()
    start_some((4, 5))

    @pl.when(mine)
    def _():
        out_x.wait_send()
        for made in out_y:
            made.wait_send()

    @pl.when(other)
    def _():
        out_y[1].wait_recv()
        out_far.wait()

    stores.append(move.local(out_w, out_w_out))

    out_weight = out_w.reshape(width // 2, width)
    theirs, ours = (pl.multiple_of(c * half_len, half_len) for c in (1 - core, core))

    def project(start):
        for i in range(half_len // QB):
            at = pl.ds(pl.multiple_of(start + i * QB, QB), QB)
            part[pl.ds(i * QB, QB), :] = nn(mixed[at, :], out_weight[...])

    project(theirs)
    part_move = move.copy(part, part_got, "core")
    part_move.start()
    for i in range(half_len // QB):
        at = pl.ds(pl.multiple_of(ours + i * QB, QB), QB)
        hidden[pl.ds(i * QB, QB), :] = nn(mixed[at, :], out_weight[...])
    part_move.wait()
    for q in range(2):

        def norm(at, q=q):
            rows = pl.ds(pl.multiple_of(q * quarter + at.start, 16), at.size)
            field = x_own[q, at, :].astype(f32) + (hidden[rows, :] + part_got[rows, :])
            hidden[rows, :] = field
            inverse = lax.rsqrt(jnp.mean(field * field, axis=1, keepdims=True) + EPSILON)
            token[rows, :] = (field * inverse * gain_rows[1:2, :]).astype(low)

        by_rows(quarter, 16, norm)
    token_moves = [
        move.send(token, tokens.at[2], "zl"),
        move.send(token, tokens.at[1], "core"),
    ]
    stores += [move.local(token, tokens.at[0]), move.local(hidden, hidden_out)]
    pass_some((0, 1))
    seed_moves[1].wait_recv()
    seed_moves.append(move.send(seeds.at[2], seeds.at[3], "core"))
    pass_some((3, 4, 5))
    token_moves[0].wait_recv()
    token_moves.append(move.send(tokens.at[2], tokens.at[3], "core"))
    for made in rest + seed_moves[::2] + token_moves[1:]:
        made.wait_recv()
    for made in stores:
        made.wait()
    move.finish()


def first_part(
    heads, kvs, x_in, g_in, query, key, value, gate, up, down, out, gain, docs, cosine, sine
):
    f32, low = jnp.float32, jnp.bfloat16
    rows, width = out.shape
    half_len = 2 * x_in.shape[1]
    length = 2 * half_len
    hbm = pl.BlockSpec(memory_space=pl.ANY)
    vmem = pl.BlockSpec(memory_space=pltpu.VMEM)

    def made(shape, dtype=low):
        return jax.ShapeDtypeStruct(shape, dtype)

    qkv_shape = (2, rows, width)
    quarter = (2, 2, rows, gate.shape[1] // 4)
    kept = [
        made(x_in.shape),
        made((2, half_len, width)),
        made((length, width)),
        made((length, heads * HD)),
        made((half_len, width), f32),
        made((4, 4) + qkv_shape),
        made((2, 4, 2) + out.shape),
    ]
    return pl.pallas_call(
        functools.partial(first_kernel, heads, kvs),
        in_specs=[hbm] * 2 + [vmem] * 5 + [hbm] * 3 + [vmem] * 3,
        out_specs=[hbm] * 7 + [vmem] * 3 + [hbm] * 5,
        out_shape=kept
        + [
            made((2, width), f32),
            made((1, length), docs.dtype),
            made((length, 1), docs.dtype),
            made((4,) + x_in.shape),
            made((4, half_len, width)),
            made((4, 2) + quarter),
            made((4, 2) + quarter),
            made((4, 2) + down.shape),
        ],
        scratch_shapes=[pltpu.VMEM(one.shape, one.dtype) for one in kept]
        + [
            pltpu.VMEM((half_len, width), low),
            pltpu.VMEM(qkv_shape, low),
            pltpu.VMEM(quarter, low),
            pltpu.VMEM(quarter, low),
            pltpu.VMEM(docs.shape, docs.dtype),
            pltpu.VMEM((4, 4, 2) + gain.shape, f32),
            pltpu.VMEM((kvs, length, HD), low),
            pltpu.VMEM((half_len, width), f32),
            pltpu.VMEM((half_len, width), f32),
            pltpu.SemaphoreType.DMA((112,)),
            pltpu.SemaphoreType.DMA((112,)),
        ],
        compiler_params=pltpu.CompilerParams(
            collective_id=1, has_side_effects=True, vmem_limit_bytes=60 << 20
        ),
        name="first",
    )(x_in, g_in, query, key, value, gate, up, down, out, gain, docs, cosine, sine)


def hidden_kernel(
    tokens,
    seeds,
    gate_w,
    up_w,
    down_w,
    act_out,
    gate_out,
    up_out,
    back_own,
    back_far,
    ahead_own,
    ahead_far,
    backs,
    aheads,
    back_got,
    ahead_got,
    sends,
    recvs,
):
    f32, low = jnp.float32, jnp.bfloat16
    me = coordinates()
    move = Mover(me, sends, recvs)

    @pl.when(pl.program_id(0) == 0)
    def _():
        greet(me, (("core",),))

    half_len = backs.shape[1]
    per = half_len // QB
    i = pl.program_id(0)
    moves = [
        (
            move.copy(backs.at[1], back_got.at[turn], "core"),
            move.copy(aheads.at[1], ahead_got.at[turn], "core"),
        )
        for turn in range(2)
    ]

    def fold(turn, back_ref, ahead_ref):
        for made in moves[turn]:
            made.wait()

        def work(at):
            back_ref[at, :] = (backs[0, at, :] + back_got[turn, at, :]).astype(back_ref.dtype)
            ahead_ref[at, :] = (aheads[0, at, :] + ahead_got[turn, at, :]).astype(ahead_ref.dtype)

        by_rows(half_len, 16, work)

    slot = 3 - i // per
    rows = pl.ds(pl.multiple_of(i % per * QB, QB), QB)
    token, seed = tokens[...], seeds[...]
    gate, upward = nn(token, gate_w[...]), nn(token, up_w[...])
    sigma = 1.0 / (1.0 + jnp.exp(-gate))
    silu = gate * sigma
    activated = (silu * upward).astype(low)
    act_out[...] = activated
    grad = nt(seed, down_w[...])
    up_low = (grad * silu).astype(low)
    gate_low = (grad * upward * sigma * (1.0 + gate * (1.0 - sigma))).astype(low)
    up_out[...] = up_low
    gate_out[...] = gate_low
    aheads[slot % 2, rows, :] = nn(activated, down_w[...])
    backs[slot % 2, rows, :] = nt(gate_low, gate_w[...]) + nt(up_low, up_w[...])
    for turn in range(2):

        @pl.when(i == (2 * turn + 1) * per - 1)
        def _(turn=turn):
            for made in moves[turn]:
                made.start()

    @pl.when(i == 2 * per - 1)
    def _():
        fold(0, back_far, ahead_far)

    @pl.when(i == 4 * per - 1)
    def _():
        fold(1, back_own, ahead_own)


def hidden_part(tokens, seeds, gate_w, up_w, down_w):
    f32, low = jnp.float32, jnp.bfloat16
    half_len, width = tokens.shape[1:]
    wide = gate_w.shape[1]
    per = half_len // QB
    vmem = pl.BlockSpec(memory_space=pltpu.VMEM)

    def banded(columns):
        return pl.BlockSpec((QB, columns), lambda i: ((3 - i // per) * per + i % per, 0))

    def made(rows, columns, dtype=low):
        return jax.ShapeDtypeStruct((rows, columns), dtype)

    return pl.pallas_call(
        hidden_kernel,
        grid=(4 * per,),
        in_specs=[banded(width)] * 2 + [vmem] * 3,
        out_specs=[banded(wide)] * 3 + [vmem] * 4,
        out_shape=[made(4 * half_len, wide)] * 3
        + [
            made(half_len, width, f32),
            made(half_len, width),
            made(half_len, width, f32),
            made(half_len, width),
        ],
        scratch_shapes=[
            pltpu.VMEM((2, half_len, width), f32),
            pltpu.VMEM((2, half_len, width), f32),
            pltpu.VMEM((2, half_len, width), f32),
            pltpu.VMEM((2, half_len, width), f32),
            pltpu.SemaphoreType.DMA((4,)),
            pltpu.SemaphoreType.DMA((4,)),
        ],
        compiler_params=pltpu.CompilerParams(
            collective_id=2, has_side_effects=True, vmem_limit_bytes=63 << 20
        ),
        cost_estimate=pl.CostEstimate(
            flops=2 * 6 * 4 * half_len * width * wide,
            bytes_accessed=40 << 20,
            transcendentals=4 * half_len * wide,
        ),
        name="hidden",
    )(tokens.reshape(-1, width), seeds.reshape(-1, width), gate_w, up_w, down_w)


def rope_constants(length, width):
    freqs = ROPE_BASE ** (-2.0 * np.arange(width // 2) / width)
    angles = np.tile(np.arange(length)[:, None] * freqs[None, :], 2)
    return np.cos(angles).astype(np.float32), np.sin(angles).astype(np.float32)


def fast_body(
    layer_input,
    cotangent,
    token_mask,
    document_ids,
    attn_gain,
    w_query,
    w_key,
    w_value,
    w_output,
    mlp_gain,
    w_gate,
    w_up,
    w_down,
):
    f32, low = jnp.float32, jnp.bfloat16
    y, x, zh, zl, core = (lax.axis_index(name) for name in AXES)
    device = sum(lax.axis_index(name) * BITS[name] for name in AXES)
    quarter, width = layer_input.shape[1:]
    half_len = 2 * quarter
    length = 2 * half_len
    rows = w_query.shape[0]
    units = w_gate.shape[1]
    heads, kvs = HEADS // 2, KV // 2
    cosine, sine = (jnp.asarray(table) for table in rope_constants(length, HD))

    masked = cotangent * token_mask.astype(low)[:, :, None]
    gain = jnp.concatenate([attn_gain, mlp_gain]).astype(f32)
    gain = jnp.broadcast_to(jnp.pad(gain, (0, 128 - 2 * rows)), (8, 128))
    (
        own,
        normed,
        pair,
        mixed,
        hidden,
        qkv_w,
        out_w,
        gains,
        row,
        col,
        seeds,
        tokens,
        gate_w,
        up_w,
        down_w,
    ) = first_part(
        heads,
        kvs,
        layer_input,
        masked,
        w_query,
        w_key,
        w_value,
        w_gate,
        w_up,
        w_down,
        w_output,
        gain,
        document_ids[:, None],
        cosine,
        sine,
    )
    qkv_w, out_w = qkv_w.reshape(width, -1), out_w.reshape(-1, width)
    gate_w, up_w = gate_w.reshape(width, -1), up_w.reshape(width, -1)
    down_w = down_w.reshape(-1, width)
    seeds = seeds.reshape(4, half_len, width)
    activated, gate_low, up_low, back_own, back_far, ahead_own, ahead_far = hidden_part(
        tokens, seeds, gate_w, up_w, down_w
    )
    gain_two, grad_qkv, steep, y_low, grad_out_w, *sums = attend_behind(
        heads,
        kvs,
        gains,
        cosine,
        sine,
        row,
        col,
        hidden,
        back_own,
        pair,
        mixed,
        out_w,
        back_far,
        ahead_own,
        ahead_far.reshape(2, quarter, width),
        tokens.reshape(-1, width),
        seeds.reshape(-1, width),
        activated,
        gate_low,
        up_low,
    )
    (
        gate_grad,
        up_grad,
        down_grad,
        query_grad,
        key_grad,
        value_grad,
        out_grad,
        output,
        grad_input,
        gain,
    ) = sum_tail(
        sums[0].reshape(2, -1, units // 4),
        sums[1].reshape(2, -1, units // 4),
        sums[2].reshape(2, -1, width),
        grad_qkv,
        normed,
        qkv_w,
        own,
        steep,
        gains,
        gain_two,
        grad_out_w.reshape(2, 4, 2, rows, width),
        y_low,
    )
    gain_one = lax.dynamic_slice_in_dim(gain, device * rows, rows, 1)

    return (
        output,
        grad_input,
        gain_one[0],
        query_grad,
        key_grad,
        value_grad,
        out_grad,
        gain_one[1],
        gate_grad,
        up_grad,
        down_grad,
    )


def solution(mesh):
    fast = dict(mesh.shape) == {"seq": 4, "batch": 8}
    if fast:
        grid = Mesh(mesh.devices.reshape((2,) * 5), AXES)
        seq, batch = ("y", "x"), ("zh", "zl", "core")
    else:
        grid, seq, batch = mesh, ("seq",), ("batch",)
    weight = P(seq + batch, None)
    gain = P(seq + batch)
    token = P(batch, seq, None)
    return jax.shard_map(
        fast_body if fast else body,
        mesh=grid,
        in_specs=(token, token, P(batch, seq), P(batch, None), gain)
        + (weight,) * 4
        + (gain,)
        + (weight,) * 3,
        out_specs=(token, token, gain) + (weight,) * 4 + (gain,) + (weight,) * 3,
        check_vma=False,
    )
```

```python
import functools
import math

import jax
import jax.numpy as jnp
import numpy as np
from jax import lax
from jax.experimental import pallas as pl
from jax.experimental.pallas import tpu as pltpu
from jax.sharding import Mesh
from jax.sharding import PartitionSpec as P

HEADS = 16
KV = 8
HD = 96


EPSILON = 1e-05
ROPE_BASE = 10000.0


def inverse_rms(field):
    return lax.rsqrt(jnp.mean(field * field, axis=-1, keepdims=True) + EPSILON)


def half_turn(field):
    middle = field.shape[-1] // 2
    return jnp.concatenate([-field[..., middle:], field[..., :middle]], axis=-1)


def rope_tables(length, width):
    middle = width // 2
    freqs = ROPE_BASE ** (-2.0 * jnp.arange(middle, dtype=jnp.float32) / width)
    angles = jnp.arange(length, dtype=jnp.float32)[:, None] * freqs[None, :]
    cosine = jnp.concatenate([jnp.cos(angles), jnp.cos(angles)], axis=-1)
    sine = jnp.concatenate([jnp.sin(angles), jnp.sin(angles)], axis=-1)
    return (cosine, sine)


def rotate_ahead(field, cosine, sine):
    return field * cosine[:, None, :] + half_turn(field) * sine[:, None, :]


def rotate_behind(field, cosine, sine):
    return field * cosine[:, None, :] - half_turn(field) * sine[:, None, :]


def outer_sum(left, right):
    return lax.dot_general(
        left, right, (((0,), (0,)), ((), ())), preferred_element_type=jnp.float32
    )


def back_product(left, right):
    return lax.dot_general(
        left, right, (((1,), (1,)), ((), ())), preferred_element_type=jnp.float32
    )


def fetch_attention(attn_gain, w_query, w_key, w_value, w_output):
    return (
        lax.all_gather(attn_gain, ("seq", "batch"), axis=0, tiled=True),
        lax.all_gather(w_query, ("seq", "batch"), axis=0, tiled=True),
        lax.all_gather(w_key, ("seq", "batch"), axis=0, tiled=True),
        lax.all_gather(w_value, ("seq", "batch"), axis=0, tiled=True),
        lax.all_gather(w_output, ("seq", "batch"), axis=0, tiled=True),
    )


def fetch_feedforward(mlp_gain, w_gate, w_up, w_down):
    return (
        lax.all_gather(mlp_gain, ("seq", "batch"), axis=0, tiled=True),
        lax.all_gather(w_gate, ("seq", "batch"), axis=0, tiled=True),
        lax.all_gather(w_up, ("seq", "batch"), axis=0, tiled=True),
        lax.all_gather(w_down, ("seq", "batch"), axis=0, tiled=True),
    )


def block_scores(query_block, keys, documents, start, block, scale):
    length = keys.shape[0]
    scores = (
        jnp.einsum("qjhd,kjd->jhqk", query_block, keys, preferred_element_type=jnp.float32) * scale
    )
    key_pos = jnp.arange(length, dtype=jnp.int32)
    query_pos = start + jnp.arange(block, dtype=jnp.int32)
    query_docs = lax.dynamic_slice_in_dim(documents, start, block, 0)
    allowed = (key_pos[None, :] <= query_pos[:, None]) & (query_docs[:, None] == documents[None, :])
    return jnp.where(allowed[None, None], scores, -1e30)


def attention_forward(queries, keys, values, documents, block, scale):
    length = queries.shape[0]
    count = length // block

    def one_block(index):
        start = index * block
        query_block = lax.dynamic_slice_in_dim(queries, start, block, 0)
        scores = block_scores(query_block, keys, documents, start, block, scale)
        peak_score = jnp.max(scores, axis=-1, keepdims=True)
        weights = jnp.exp(scores - peak_score)
        totals = jnp.sum(weights, axis=-1, keepdims=True)
        probs = (weights / totals).astype(jnp.bfloat16)
        result = jnp.einsum("jhqk,kjd->qjhd", probs, values, preferred_element_type=jnp.float32)
        return (
            result.astype(jnp.bfloat16).reshape(block, -1),
            (peak_score + jnp.log(totals))[..., 0],
        )

    results, sums = lax.map(one_block, jnp.arange(count, dtype=jnp.int32))
    return (results.reshape(length, -1), sums)


def attention_backward(queries, keys, values, documents, sums, grad_out, block, scale):
    length = queries.shape[0]
    count = length // block

    def one_block(carry, member):
        grad_keys, grad_values = carry
        index, sums_block = member
        start = index * block
        query_block = lax.dynamic_slice_in_dim(queries, start, block, 0)
        grad_block = lax.dynamic_slice_in_dim(grad_out, start, block, 0)
        scores = block_scores(query_block, keys, documents, start, block, scale)
        probs = jnp.exp(scores - sums_block[..., None])
        grad_probs = jnp.einsum(
            "qjhd,kjd->jhqk", grad_block, values, preferred_element_type=jnp.float32
        )
        centre = jnp.sum(probs * grad_probs, axis=-1, keepdims=True)
        grad_scores = (probs * (grad_probs - centre)).astype(jnp.bfloat16)
        grad_query = (
            jnp.einsum("jhqk,kjd->qjhd", grad_scores, keys, preferred_element_type=jnp.float32)
            * scale
        )
        grad_keys = (
            grad_keys
            + jnp.einsum(
                "jhqk,qjhd->kjd", grad_scores, query_block, preferred_element_type=jnp.float32
            )
            * scale
        )
        grad_values = grad_values + jnp.einsum(
            "jhqk,qjhd->kjd",
            probs.astype(jnp.bfloat16),
            grad_block,
            preferred_element_type=jnp.float32,
        )
        return ((grad_keys, grad_values), grad_query)

    empty = jnp.zeros(keys.shape, jnp.float32)
    (grad_keys, grad_values), grad_query = lax.scan(
        one_block, (empty, empty), (jnp.arange(count, dtype=jnp.int32), sums)
    )
    return (
        grad_query.reshape(length, queries.shape[1] * queries.shape[2], queries.shape[3]),
        grad_keys,
        grad_values,
    )


def body(
    layer_input,
    cotangent,
    token_mask,
    document_ids,
    attn_gain,
    w_query,
    w_key,
    w_value,
    w_output,
    mlp_gain,
    w_gate,
    w_up,
    w_down,
):
    parts = lax.axis_size("seq")
    micro_count = layer_input.shape[0]
    shard = layer_input.shape[1]
    length = shard * parts
    heads_here = HEADS // parts
    kv_here = max(1, KV // parts)
    copies = parts * kv_here // KV
    per_kv = heads_here // kv_here
    block = min(512, length)
    scale = 1.0 / math.sqrt(HD)
    cosine, sine = rope_tables(length, HD)
    attn_set = None
    mlp_set = None
    attn_total = None
    mlp_total = None
    outputs = []
    input_grads = []
    kept = {
        "normed": [],
        "normed_two": [],
        "activated": [],
        "seed_low": [],
        "gate_low": [],
        "up_low": [],
        "grad_low": [],
        "mixed": [],
        "query_back": [],
        "key_back": [],
        "value_back": [],
    }
    gain_one_total = None
    gain_two_total = None
    for micro in range(micro_count):
        attn_set = fetch_attention(attn_gain, w_query, w_key, w_value, w_output)
        mlp_set = fetch_feedforward(mlp_gain, w_gate, w_up, w_down)
        gain_one = attn_set[0].astype(jnp.float32)
        gain_two = mlp_set[0].astype(jnp.float32)
        documents = document_ids[micro]
        inputs = layer_input[micro].astype(jnp.float32)
        inv_one = inverse_rms(inputs)
        unit_one = inputs * inv_one
        normed = (unit_one * gain_one).astype(jnp.bfloat16)
        queries = jnp.dot(normed, attn_set[1], preferred_element_type=jnp.float32).astype(
            jnp.bfloat16
        )
        keys_lin = jnp.dot(normed, attn_set[2], preferred_element_type=jnp.float32).astype(
            jnp.bfloat16
        )
        values_lin = jnp.dot(normed, attn_set[3], preferred_element_type=jnp.float32).astype(
            jnp.bfloat16
        )
        queries = queries.reshape(shard, parts, heads_here * HD)
        key_slots = jnp.repeat(keys_lin.reshape(shard, KV, HD), copies, axis=1).reshape(
            shard, parts, kv_here * HD
        )
        value_slots = jnp.repeat(values_lin.reshape(shard, KV, HD), copies, axis=1).reshape(
            shard, parts, kv_here * HD
        )
        pairs = jnp.concatenate([key_slots, value_slots], axis=-1)
        query_heads, pair_heads = (
            lax.all_to_all(queries, "seq", split_axis=1, concat_axis=0, tiled=True),
            lax.all_to_all(pairs, "seq", split_axis=1, concat_axis=0, tiled=True),
        )
        query_rot = rotate_ahead(
            query_heads.reshape(length, heads_here, HD).astype(jnp.float32), cosine, sine
        )
        query_rot = query_rot.astype(jnp.bfloat16).reshape(length, kv_here, per_kv, HD)
        key_heads = pair_heads[:, 0, : kv_here * HD].reshape(length, kv_here, HD)
        key_rot = rotate_ahead(key_heads.astype(jnp.float32), cosine, sine).astype(jnp.bfloat16)
        value_heads = pair_heads[:, 0, kv_here * HD :].reshape(length, kv_here, HD)
        attended, sums = attention_forward(query_rot, key_rot, value_heads, documents, block, scale)
        mixed = lax.all_to_all(
            attended.reshape(length, 1, heads_here * HD),
            "seq",
            split_axis=0,
            concat_axis=1,
            tiled=True,
        )
        mixed = mixed.reshape(shard, HEADS * HD)
        hidden_state = inputs + jnp.dot(mixed, attn_set[4], preferred_element_type=jnp.float32)
        inv_two = inverse_rms(hidden_state)
        unit_two = hidden_state * inv_two
        normed_two = (unit_two * gain_two).astype(jnp.bfloat16)
        gate = jnp.dot(normed_two, mlp_set[1], preferred_element_type=jnp.float32)
        upward = jnp.dot(normed_two, mlp_set[2], preferred_element_type=jnp.float32)
        sigma = jax.nn.sigmoid(gate)
        activated = (gate * sigma * upward).astype(jnp.bfloat16)
        output = hidden_state + jnp.dot(activated, mlp_set[3], preferred_element_type=jnp.float32)
        outputs.append(output.astype(jnp.bfloat16))
        seed = cotangent[micro].astype(jnp.float32) * token_mask[micro].astype(jnp.float32)[:, None]
        seed_low = seed.astype(jnp.bfloat16)
        grad_act = back_product(seed_low, mlp_set[3])
        grad_up_low = (grad_act * gate * sigma).astype(jnp.bfloat16)
        grad_gate_low = (grad_act * upward * sigma * (1.0 + gate * (1.0 - sigma))).astype(
            jnp.bfloat16
        )
        grad_normed_two = back_product(grad_gate_low, mlp_set[1]) + back_product(
            grad_up_low, mlp_set[2]
        )
        grad_gain_two = jnp.sum(grad_normed_two * unit_two, axis=0)
        scaled_two = grad_normed_two * gain_two
        grad_hidden = seed + inv_two * (
            scaled_two - unit_two * jnp.mean(scaled_two * unit_two, axis=-1, keepdims=True)
        )
        gain_two_total = grad_gain_two if gain_two_total is None else gain_two_total + grad_gain_two
        kept["normed_two"].append(normed_two)
        kept["activated"].append(activated)
        kept["seed_low"].append(seed_low)
        kept["gate_low"].append(grad_gate_low)
        kept["up_low"].append(grad_up_low)
        grad_low = grad_hidden.astype(jnp.bfloat16)
        grad_mixed = (
            back_product(grad_low, attn_set[4])
            .astype(jnp.bfloat16)
            .reshape(shard, parts, heads_here * HD)
        )
        grad_heads = lax.all_to_all(
            grad_mixed, "seq", split_axis=1, concat_axis=0, tiled=True
        ).reshape(length, kv_here, per_kv, HD)
        grad_query_rot, grad_key_rot, grad_values = attention_backward(
            query_rot, key_rot, value_heads, documents, sums, grad_heads, block, scale
        )
        grad_query_heads = (
            rotate_behind(grad_query_rot, cosine, sine)
            .astype(jnp.bfloat16)
            .reshape(length, 1, heads_here * HD)
        )
        grad_key_heads = rotate_behind(grad_key_rot, cosine, sine)
        grad_pairs = jnp.concatenate(
            [
                grad_key_heads.reshape(length, kv_here * HD),
                grad_values.reshape(length, kv_here * HD),
            ],
            axis=-1,
        )
        query_back = lax.all_to_all(
            grad_query_heads, "seq", split_axis=0, concat_axis=1, tiled=True
        ).reshape(shard, HEADS * HD)
        pair_back = lax.all_to_all(
            grad_pairs.reshape(length, 1, 2 * kv_here * HD).astype(jnp.bfloat16),
            "seq",
            split_axis=0,
            concat_axis=1,
            tiled=True,
        ).astype(jnp.float32)
        key_back = pair_back[:, :, : kv_here * HD].reshape(shard, KV, copies, HD).sum(axis=2)
        value_back = pair_back[:, :, kv_here * HD :].reshape(shard, KV, copies, HD).sum(axis=2)
        key_back = key_back.reshape(shard, KV * HD).astype(jnp.bfloat16)
        value_back = value_back.reshape(shard, KV * HD).astype(jnp.bfloat16)
        grad_normed = (
            back_product(query_back, attn_set[1])
            + back_product(key_back, attn_set[2])
            + back_product(value_back, attn_set[3])
        )
        grad_gain_one = jnp.sum(grad_normed * unit_one, axis=0)
        scaled_one = grad_normed * gain_one
        grad_input = grad_hidden + inv_one * (
            scaled_one - unit_one * jnp.mean(scaled_one * unit_one, axis=-1, keepdims=True)
        )
        input_grads.append(grad_input.astype(jnp.bfloat16))
        gain_one_total = grad_gain_one if gain_one_total is None else gain_one_total + grad_gain_one
        kept["normed"].append(normed)
        kept["mixed"].append(mixed)
        kept["grad_low"].append(grad_low)
        kept["query_back"].append(query_back)
        kept["key_back"].append(key_back)
        kept["value_back"].append(value_back)
    rows = {name: jnp.concatenate(values, axis=0) for name, values in kept.items()}
    attn_total = (
        lax.psum_scatter(gain_one_total, ("seq", "batch"), scatter_dimension=0, tiled=True),
        lax.psum_scatter(
            outer_sum(rows["normed"], rows["query_back"]),
            ("seq", "batch"),
            scatter_dimension=0,
            tiled=True,
        ),
        lax.psum_scatter(
            outer_sum(rows["normed"], rows["key_back"]),
            ("seq", "batch"),
            scatter_dimension=0,
            tiled=True,
        ),
        lax.psum_scatter(
            outer_sum(rows["normed"], rows["value_back"]),
            ("seq", "batch"),
            scatter_dimension=0,
            tiled=True,
        ),
        lax.psum_scatter(
            outer_sum(rows["mixed"], rows["grad_low"]),
            ("seq", "batch"),
            scatter_dimension=0,
            tiled=True,
        ),
    )
    mlp_total = (
        lax.psum_scatter(gain_two_total, ("seq", "batch"), scatter_dimension=0, tiled=True),
        lax.psum_scatter(
            outer_sum(rows["normed_two"], rows["gate_low"]),
            ("seq", "batch"),
            scatter_dimension=0,
            tiled=True,
        ),
        lax.psum_scatter(
            outer_sum(rows["normed_two"], rows["up_low"]),
            ("seq", "batch"),
            scatter_dimension=0,
            tiled=True,
        ),
        lax.psum_scatter(
            outer_sum(rows["activated"], rows["seed_low"]),
            ("seq", "batch"),
            scatter_dimension=0,
            tiled=True,
        ),
    )
    return (
        jnp.stack(outputs, axis=0),
        jnp.stack(input_grads, axis=0),
        attn_total[0],
        attn_total[1],
        attn_total[2],
        attn_total[3],
        attn_total[4],
        mlp_total[0],
        mlp_total[1],
        mlp_total[2],
        mlp_total[3],
    )


AXES = ("y", "x", "zh", "zl", "core")
BITS = {"y": 16, "x": 8, "zh": 4, "zl": 2, "core": 1}
MESH = pl.DeviceIdType.MESH


def coordinates():
    return tuple(lax.axis_index(name) for name in AXES)


def peer(me, *names):
    return tuple(1 - at if name in names else at for name, at in zip(AXES, me))


def greet(me, groups):
    barrier = pltpu.get_barrier_semaphore()
    for names in groups:
        pl.semaphore_signal(barrier, 1, device_id=peer(me, *names), device_id_type=MESH)
    pl.semaphore_wait(barrier, len(groups))


class Mover:
    def __init__(self, me, sends, recvs):
        self.me, self.sends, self.recvs, self.used = me, sends, recvs, 0
        self.started = []

    def next(self):
        number = self.used
        self.used += 1
        assert number < self.sends.shape[0]
        return number

    def copy(self, src, dst, *names, device=None):
        number = self.next()
        return pltpu.make_async_remote_copy(
            src_ref=src,
            dst_ref=dst,
            send_sem=self.sends.at[number],
            recv_sem=self.recvs.at[number],
            device_id=peer(self.me, *names) if device is None else device,
            device_id_type=MESH,
        )

    def later(self, src, dst, *names):
        made = self.copy(src, dst, *names)
        self.started.append(made)
        return made

    def send(self, src, dst, *names):
        made = self.later(src, dst, *names)
        made.start()
        return made

    def local(self, src, dst):
        made = self.quiet(src, dst)
        made.start()
        return made

    def quiet(self, src, dst):
        number = self.next()
        return pltpu.make_async_copy(src, dst, self.recvs.at[number])

    def finish(self):
        for made in self.started:
            made.wait_send()


HEAD_GROUPS = (
    ("core",),
    ("zl",),
    ("zh",),
    ("zh", "zl"),
    ("zl", "core"),
    ("x",),
    ("y",),
    ("y", "core"),
    ("y", "core", "x"),
)
LINE = (("zl",), ("zh",), ("zh", "zl"))


def turn_start(move, me, src, dst):
    y, x, zh, zl, core = me
    stays = y == core
    made = []
    for flip in (1, 0):
        place = x if flip == 0 else 1 - x
        from_, to = src.at[place], dst.at[x]
        copy = move.copy(from_, to, device=(core, place, zh, zl, y))
        if flip == 0:
            own = move.quiet(from_, to)
            pl.when(stays)(own.start)
            pl.when(jnp.logical_not(stays))(copy.start)
            made.append((copy, own))
        else:
            copy.start()
            made.append((copy, None))
    return made


def turn_end(me, made):
    stays = me[0] == me[4]
    for copy, own in made:
        if own is None:
            copy.wait()
        else:
            pl.when(stays)(own.wait)
            pl.when(jnp.logical_not(stays))(copy.wait)


def plane_make(move, ref, s, parts):
    made = []
    for part in parts:
        piece = ref.at[s, ..., part]
        made += [move.later(piece, piece, "x"), move.later(piece, piece, "y")]
    return made


def plane_start(move, ref, s, parts):
    made = plane_make(move, ref, s, parts)
    for one in made:
        one.start()
    return made


def plane_pass(move, made, ref, y, x, parts):
    made[0].wait_recv()
    first = ref.at[2 * y + 1 - x, ..., parts[0]]
    rest = [move.send(first, first, "y")]
    made[3].wait_recv()
    second = ref.at[2 * (1 - y) + x, ..., parts[1]]
    rest.append(move.send(second, second, "x"))
    made[1].wait_recv()
    made[2].wait_recv()
    return rest


def by_rows(count, chunk, work):
    def step(i, carry):
        work(pl.ds(pl.multiple_of(i * chunk, chunk), chunk))
        return carry

    lax.fori_loop(0, count // chunk, step, 0)


class PlaneSum:
    def __init__(self, move, total, held, y, x):
        self.move, self.total = move, total
        self.mid, self.far, self.near, self.last = (held.at[i] for i in range(4))
        self.own = self.far
        half = total.shape[-1] // 2
        self.left, self.right = pl.ds(0, half), pl.ds(half, half)
        self.at = (2 * y + x, 2 * y + 1 - x, 2 * (1 - y) + x, 2 * (1 - y) + 1 - x)

    def start(self):
        move, total, left, right = self.move, self.total, self.left, self.right
        s, sx, sy, sd = self.at
        self.far_moves = [
            move.send(total.at[sd, :, left], self.far.at[:, left], "y"),
            move.send(total.at[sd, :, right], self.far.at[:, right], "x"),
        ]
        self.loads = [
            move.local(total.at[sx, :, left], self.mid.at[:, left]),
            move.local(total.at[sy, :, right], self.mid.at[:, right]),
        ]
        self.own_load = move.quiet(total.at[s], self.own)
        self.near_moves = [
            move.copy(total.at[sy, :, left], self.near.at[:, left], "y"),
            move.copy(total.at[sx, :, right], self.near.at[:, right], "x"),
        ]
        self.last_moves = [
            move.copy(self.mid.at[:, left], self.last.at[:, left], "x"),
            move.copy(self.mid.at[:, right], self.last.at[:, right], "y"),
        ]

    def start_near(self):
        for made in self.near_moves:
            made.start()

    def pass_on(self):
        for made in self.loads:
            made.wait()
        for made in self.far_moves:
            made.wait_recv()
        rows = self.mid.shape[0]
        mid, far = self.mid, self.far

        def work(at):
            added = mid[at, :].astype(jnp.float32) + far[at, :].astype(jnp.float32)
            mid[at, :] = added.astype(jnp.bfloat16)

        by_rows(rows, 16, work)
        for made in self.last_moves:
            made.start()
        self.own_load.start()

    def end(self, write):
        if self.own_load is not None:
            self.own_load.wait()
        for made in self.near_moves + self.last_moves:
            made.wait()
        own, near, last = self.own, self.near, self.last

        def work(at):
            value = own[at, :].astype(jnp.float32) + near[at, :].astype(jnp.float32)
            write(at, value + last[at, :].astype(jnp.float32))

        by_rows(own.shape[0], 16, work)


class PlaneSumHere(PlaneSum):
    def __init__(self, move, total, held, y, x):
        self.move, self.total = move, total
        self.far, self.near, self.last = (held.at[i] for i in range(3))
        half = total.shape[-1] // 2
        self.left, self.right = left, right = pl.ds(0, half), pl.ds(half, half)
        self.at = s, sx, sy, sd = (2 * y + x, 2 * y + 1 - x, 2 * (1 - y) + x, 3 - 2 * y - x)
        self.own, self.mids = total.at[s], (total.at[sx], total.at[sy])
        self.far_moves = [
            move.later(total.at[sd, :, left], self.far.at[:, left], "y"),
            move.later(total.at[sd, :, right], self.far.at[:, right], "x"),
        ]
        self.near_moves = [
            move.copy(total.at[sy, :, left], self.near.at[:, left], "y"),
            move.copy(total.at[sx, :, right], self.near.at[:, right], "x"),
        ]
        self.last_moves = [
            move.copy(total.at[sx, :, left], self.last.at[:, left], "x"),
            move.copy(total.at[sy, :, right], self.last.at[:, right], "y"),
        ]
        self.own_load = None

    def start(self):
        for made in self.far_moves:
            made.start()

    def pass_on(self):
        for made in self.far_moves:
            made.wait_recv()
        far = self.far

        def work(at):
            for mid, part in zip(self.mids, (self.left, self.right)):
                added = mid[at, part].astype(jnp.float32) + far[at, part].astype(jnp.float32)
                mid[at, part] = added.astype(jnp.bfloat16)

        by_rows(far.shape[0], 16, work)
        for made in self.last_moves:
            made.start()


def tail_kernel(
    gate_hbm,
    up_hbm,
    down_hbm,
    grad_hbm,
    normed_hbm,
    qkv_hbm,
    x_hbm,
    steep_hbm,
    gain_rows,
    gain_two,
    out_hbm,
    y_in,
    gate_grad,
    up_grad,
    down_out,
    query_grad,
    key_grad,
    value_grad,
    out_out,
    y_out,
    x_out,
    gain_out,
    gate_in,
    up_in,
    down_in,
    grad_in,
    normed,
    qkv_w,
    x_own,
    steep,
    out_in,
    gate_out,
    up_out,
    qkv_out,
    pair_low,
    pair_got,
    down_low,
    down_got,
    quarter,
    part,
    part_got,
    x_low,
    qkv_in,
    qkv_held,
    qkv_sum,
    qkv_low,
    qkv_got,
    out_got,
    out_x,
    out_line,
    out_line_got,
    rows_sent,
    gain_got,
    sends,
    recvs,
):
    f32, low = jnp.float32, jnp.bfloat16
    me = coordinates()
    y, x, zh, zl, core = me
    z = 2 * zh + zl
    mine = y == core
    other = jnp.logical_not(mine)
    move = Mover(me, sends, recvs)
    loads = [
        move.local(src, dst)
        for src, dst in (
            (normed_hbm, normed),
            (grad_hbm, grad_in),
            (qkv_hbm, qkv_w),
            (gate_hbm, gate_in),
            (up_hbm, up_in),
            (down_hbm, down_in),
            (x_hbm, x_own),
            (steep_hbm, steep),
            (out_hbm, out_in),
        )
    ]
    greet(me, HEAD_GROUPS)
    qkv = PlaneSumHere(move, qkv_in, qkv_held, y, x)
    out_y = move.copy(out_in, out_got, "y")
    half_len = part.shape[0]
    block_rows = qkv_in.shape[1]

    def weigh(at):
        lanes = pl.ds(pl.multiple_of(at * block_rows, 128), block_rows)
        total = tn(normed[0, :, lanes], grad_in[pl.ds(0, half_len), :])
        total = total + tn(normed[1, :, lanes], grad_in[pl.ds(half_len, half_len), :])
        qkv_in[at] = total.astype(low)

    for made in loads[:2]:
        made.wait()
    weigh(qkv.at[3])
    qkv.start()

    weigh(qkv.at[1])
    weigh(qkv.at[2])
    qkv.start_near()

    for made in loads[2:6]:
        made.wait()
    pair_rows = pair_got.shape[1]

    def lower(src, dst, skip, count):
        def work(at):
            dst[at, :] = src[skip, at, :].astype(low)

        by_rows(count, 32, work)

    pairs = []
    for i, src in enumerate((gate_in, up_in)):
        lower(src, pair_low.at[i], 1 - zh, pair_rows)
        pairs.append(move.send(pair_low.at[i], pair_got.at[i], "zh"))
    lower(down_in, down_low, 1 - zh, down_low.shape[0])
    pairs.append(move.send(down_low, down_got, "zh"))

    theirs, ours = (pl.multiple_of(c * half_len, half_len) for c in (1 - core, core))

    def project(start):
        for i in range(half_len // QB):
            at = pl.ds(pl.multiple_of(start + i * QB, QB), QB)
            part[pl.ds(i * QB, QB), :] = nt(grad_in[at, :], qkv_w[...])

    project(theirs)
    part_move = move.copy(part, part_got, "core")
    part_move.start()
    weigh(qkv.at[0])
    qkv.pass_on()
    for made in loads[6:]:
        made.wait()
    pl.when(other)(out_y.start)
    part_move.wait()
    project(ours)
    gain_out[...] = jnp.zeros_like(gain_out)
    gain_out[1:2, :] = gain_two[...]
    piece = half_len // 2
    for q in range(2):

        def norm_back(at, q=q):
            every = pl.ds(pl.multiple_of(q * piece + at.start, 16), at.size)
            grad = part[every, :] + part_got[every, :]
            field = x_own[q, at, :].astype(f32)
            inverse = lax.rsqrt(jnp.mean(field * field, axis=1, keepdims=True) + EPSILON)
            unit = field * inverse
            gain_out[0:1, :] += jnp.sum(grad * unit, axis=0, keepdims=True)
            scaled = grad * gain_rows[0:1, :]
            centre = jnp.mean(scaled * unit, axis=1, keepdims=True)
            value = steep[every, :] + inverse * (scaled - unit * centre)
            x_low[q, at, :] = value.astype(low)

        by_rows(piece, 16, norm_back)
    x_turn = turn_start(move, me, x_low, x_out)

    gain_moves = [
        move.copy(gain_out, gain_got.at[turn], name)
        for turn, name in enumerate(("core", "x", "y", "zl", "zh"))
    ]

    def gain_round(turn):
        if turn > 0:
            gain_moves[turn - 1].wait()
            gain_out[...] = gain_out[...] + gain_got[turn - 1]
        if turn < len(gain_moves):
            gain_moves[turn].start()

    gain_round(0)
    out_shape = out_in.shape
    blocks = [(a, b) for a in range(out_shape[1]) for b in range(out_shape[2])]

    def keep(at, value):
        qkv_sum[at, :] = value
        qkv_low[at, :] = value.astype(low)

    qkv.end(keep)
    count = qkv_got.shape[1]
    line = []
    for k, names in enumerate(LINE):
        to = z ^ (1, 2, 3)[k]
        start = pl.multiple_of(to * count, count)
        line.append(move.send(qkv_low.at[pl.ds(start, count)], qkv_got.at[k], *names))

    gain_round(1)

    out_x_move = move.copy(out_got.at[1 - x], out_x, "x")

    @pl.when(mine)
    def _():
        out_y.wait_recv()

        def half(at_x):
            def work(i, carry):
                a, b = i // out_shape[2], i % out_shape[2]
                value = out_in[at_x, a, b].astype(f32) + out_got[at_x, a, b].astype(f32)
                out_got[at_x, a, b] = value.astype(low)
                return carry

            lax.fori_loop(0, len(blocks), work, 0)

        half(1 - x)
        out_x_move.start()
        half(x)

    pl.when(other)(out_y.wait_send)
    y_turn = turn_start(move, me, y_in, y_out)
    gain_round(2)

    spread = []
    for i, (src, dst) in enumerate(((gate_in, gate_out), (up_in, up_out))):
        pairs[i].wait_recv()
        got, full = pair_got.at[i], quarter.at[i]

        def work(at, src=src, got=got, full=full):
            full[at, :] = src[zh, at, :] + got[at, :].astype(f32)

        by_rows(pair_rows, 32, work)
        share = pair_rows // 4
        for names in (("core",), ("zl",), ("zl", "core")):
            to_zl = 1 - zl if "zl" in names else zl
            to_core = 1 - core if "core" in names else core
            start = pl.multiple_of((2 * to_zl + to_core) * share, share)
            spread.append(move.send(full.at[pl.ds(start, share)], dst.at[zl, core], *names))
        start = pl.multiple_of((2 * zl + core) * share, share)
        dst[zl, core] = full[pl.ds(start, share), :]
    pairs[2].wait_recv()

    def work(at):
        down_out[at, :] = down_in[zh, at, :] + down_got[at, :].astype(f32)

    by_rows(down_out.shape[0], 32, work)

    gain_round(3)
    out_moves = []
    for k, names in enumerate(LINE):
        to = z ^ (1, 2, 3)[k]
        out_moves.append(move.copy(out_line.at[to], out_line_got.at[k], *names))

    @pl.when(mine)
    def _():
        out_x_move.wait()

        def work(i, carry):
            a, b = i // out_shape[2], i % out_shape[2]
            value = out_got[x, a, b].astype(f32) + out_x[a, b].astype(f32)
            out_line[a, b] = value.astype(low)
            return carry

        lax.fori_loop(0, len(blocks), work, 0)
        for made in out_moves:
            made.start()

    gain_round(4)
    for made in line:
        made.wait_recv()
    start = pl.multiple_of(z * count, count)
    total = qkv_sum[pl.ds(start, count), :]
    for k in range(3):
        total = total + qkv_got[k].astype(f32)
    rows = count // 2
    qkv_sum[pl.ds(0, count), :] = total
    theirs = pl.multiple_of((1 - core) * rows, rows)
    swap = move.send(qkv_sum.at[pl.ds(theirs, rows)], qkv_out.at[core], "core")
    qkv_out[core] = qkv_sum[pl.ds(pl.multiple_of(core * rows, rows), rows), :]

    out_swap = move.copy(rows_sent, out_out, "core")

    @pl.when(mine)
    def _():
        for made in out_moves:
            made.wait()
        for at in range(2):
            total = out_line[z, at].astype(f32)
            for k in range(3):
                total = total + out_line_got[k, at].astype(f32)

            @pl.when(core == at)
            def _(total=total):
                out_out[...] = total

            @pl.when(core != at)
            def _(total=total):
                rows_sent[...] = total

        out_swap.start()
        out_swap.wait_send()

    @pl.when(other)
    def _():
        out_swap.wait_recv()

    gain_round(5)
    turn_end(me, y_turn)
    turn_end(me, x_turn)
    swap.wait_recv()
    for made in spread:
        made.wait_recv()
    for parts, grad in ((gate_out, gate_grad), (up_out, up_grad)):
        for i in range(grad.shape[1] // 128):
            lanes = slice(i // 4 * 128, i // 4 * 128 + 128)
            grad[:, i * 128 : (i + 1) * 128] = parts[i // 2 % 2, i % 2, :, lanes]
    at = 0
    for grad in (query_grad, key_grad, value_grad):
        size = grad.shape[1] // 2
        for c in range(2):
            grad[:, c * size : (c + 1) * size] = qkv_out[c, :, at : at + size]
        at += size
    move.finish()


def sum_tail(gate, up, down, grad, normed, qkv_w, x_own, steep, gain_rows, gain_two, out, y_in):
    f32, low = jnp.float32, jnp.bfloat16
    hbm = pl.BlockSpec(memory_space=pl.ANY)
    vmem = pl.BlockSpec(memory_space=pltpu.VMEM)
    wide, width = gate.shape[-1], grad.shape[-1]
    rows = out.shape[-2]
    half_len = steep.shape[0]
    pair_rows, down_rows = gate.shape[1], down.shape[1]
    return pl.pallas_call(
        tail_kernel,
        in_specs=[hbm] * 8 + [vmem] * 2 + [hbm] * 2,
        out_specs=[vmem] * 7 + [hbm, hbm, vmem],
        out_shape=[
            jax.ShapeDtypeStruct((rows, 4 * wide), f32),
            jax.ShapeDtypeStruct((rows, 4 * wide), f32),
            jax.ShapeDtypeStruct((down_rows, width), f32),
            jax.ShapeDtypeStruct((rows, width), f32),
            jax.ShapeDtypeStruct((rows, width // 2), f32),
            jax.ShapeDtypeStruct((rows, width // 2), f32),
            jax.ShapeDtypeStruct((rows, width), f32),
            jax.ShapeDtypeStruct(y_in.shape, low),
            jax.ShapeDtypeStruct(y_in.shape, low),
            jax.ShapeDtypeStruct((2, width), f32),
        ],
        scratch_shapes=[
            pltpu.VMEM(one.shape, one.dtype)
            for one in (gate, up, down, grad, normed, qkv_w, x_own, steep, out)
        ]
        + [
            pltpu.VMEM((2, 2, rows, wide), f32),
            pltpu.VMEM((2, 2, rows, wide), f32),
            pltpu.VMEM((2, rows, width), f32),
            pltpu.VMEM((2, pair_rows, wide), low),
            pltpu.VMEM((2, pair_rows, wide), low),
            pltpu.VMEM((down_rows, width), low),
            pltpu.VMEM((down_rows, width), low),
            pltpu.VMEM((2, pair_rows, wide), f32),
            pltpu.VMEM((half_len, width), f32),
            pltpu.VMEM((half_len, width), f32),
            pltpu.VMEM(y_in.shape, low),
            pltpu.VMEM((4, 8 * rows, width), low),
            pltpu.VMEM((3, 8 * rows, width), low),
            pltpu.VMEM((8 * rows, width), f32),
            pltpu.VMEM((8 * rows, width), low),
            pltpu.VMEM((3, 2 * rows, width), low),
            pltpu.VMEM(out.shape, low),
            pltpu.VMEM(out.shape[1:], low),
            pltpu.VMEM(out.shape[1:], low),
            pltpu.VMEM((3,) + out.shape[2:], low),
            pltpu.VMEM((rows, width), f32),
            pltpu.VMEM((5, 2, width), f32),
            pltpu.SemaphoreType.DMA((64,)),
            pltpu.SemaphoreType.DMA((64,)),
        ],
        compiler_params=pltpu.CompilerParams(
            collective_id=4, has_side_effects=True, vmem_limit_bytes=63 << 20
        ),
        name="tail",
    )(gate, up, down, grad, normed, qkv_w, x_own, steep, gain_rows, gain_two, out, y_in)


QB = 256
SPAN = 768


def turned(field, back):
    middle = HD // 2
    left, right = field[:, :middle], field[:, middle:]
    if back:
        return jnp.concatenate([right, -left], axis=1)
    return jnp.concatenate([-right, left], axis=1)


def spun(field, cosine, sine, back=False):
    field = field.astype(jnp.float32)
    return field * cosine + turned(field, back) * sine


def nt(left, right):
    return lax.dot_general(left, right, (((1,), (1,)), ((), ())), preferred_element_type=jnp.float32)


def nn(left, right):
    return jnp.dot(left, right, preferred_element_type=jnp.float32)


def tn(left, right):
    return lax.dot_general(left, right, (((0,), (0,)), ((), ())), preferred_element_type=jnp.float32)


def head(ref, rows, number):
    return ref[rows, HD * number : HD * (number + 1)]


def ahead_block(
    heads, kvs, step, size, qkv_ref, cos_ref, sin_ref, row_ref, col_ref, out_ref, keys
):
    low, f32 = jnp.bfloat16, jnp.float32
    start, base = step * QB, (step + 1) * QB - size
    if not isinstance(step, int):
        start, base = pl.multiple_of(start, QB), pl.multiple_of(base, QB)
    here, span = pl.ds(start, QB), pl.ds(base, size)
    key_place = base + lax.broadcasted_iota(jnp.int32, (size, QB), 0)
    place = start + lax.broadcasted_iota(jnp.int32, (size, QB), 1)
    allowed = (key_place <= place) & (col_ref[span, :] == row_ref[:, here])
    bias = jnp.where(allowed, 0.0, -1e30).astype(f32)
    scale = (1.0 / math.sqrt(HD)) * math.log2(math.e)
    cosine, sine = cos_ref[here, :], sin_ref[here, :]
    results = []
    for h in range(heads):
        j = h * kvs // heads
        query = spun(head(qkv_ref, here, h), cosine, sine).astype(low)
        scores = nt(keys[j, span, :], query) * scale + bias
        peak = jnp.max(scores, axis=0, keepdims=True)
        weights = jnp.exp2(scores - peak)
        total = jnp.sum(weights, axis=0, keepdims=True)
        probs = (weights * (1.0 / total)).astype(low)
        results.append(tn(probs, head(qkv_ref, span, heads + kvs + j)).astype(low))
    out_ref[here, :] = jnp.concatenate(results, axis=1)


def behind_block(
    heads,
    kvs,
    step,
    size,
    qkv_ref,
    grad_ref,
    cos_ref,
    sin_ref,
    row_ref,
    col_ref,
    gq_ref,
    keys,
    gks,
    gvs,
):
    low, f32 = jnp.bfloat16, jnp.float32
    start, base = step * QB, (step + 1) * QB - size
    if not isinstance(step, int):
        start, base = pl.multiple_of(start, QB), pl.multiple_of(base, QB)
    here, span = pl.ds(start, QB), pl.ds(base, size)
    key_place = base + lax.broadcasted_iota(jnp.int32, (size, QB), 0)
    place = start + lax.broadcasted_iota(jnp.int32, (size, QB), 1)
    allowed = (key_place <= place) & (col_ref[span, :] == row_ref[:, here])
    bias = jnp.where(allowed, 0.0, -1e30).astype(f32)
    width = 1.0 / math.sqrt(HD)
    scale = width * math.log2(math.e)
    cosine, sine = cos_ref[here, :], sin_ref[here, :]
    results = []
    for h in range(heads):
        j = h * kvs // heads
        query = spun(head(qkv_ref, here, h), cosine, sine).astype(low)
        key, value = keys[j, span, :], head(qkv_ref, span, heads + kvs + j)
        grad = head(grad_ref, here, h)
        scores = nt(key, query) * scale + bias
        peak = jnp.max(scores, axis=0, keepdims=True)
        weights = jnp.exp2(scores - peak)
        total = jnp.sum(weights, axis=0, keepdims=True)
        probs = weights * (1.0 / total)
        slope = nt(value, grad)
        centre = jnp.sum(probs * slope, axis=0, keepdims=True)
        gs = (probs * (slope - centre)).astype(low)
        gvs[j, span, :] += nn(probs.astype(low), grad)
        gks[j, span, :] += nn(gs, query)
        results.append(spun(tn(gs, key) * width, cosine, sine, True).astype(low))
    gq_ref[here, : HD * heads] = jnp.concatenate(results, axis=1)


def behind_kernel(
    heads,
    kvs,
    gain_rows,
    cos_ref,
    sin_ref,
    row_ref,
    col_ref,
    hidden_in,
    back_in,
    qkv_in,
    mixed_in,
    out_in,
    back_far,
    ahead_own,
    ahead_far,
    tokens,
    seeds,
    act_in,
    gate_in,
    up_in,
    gain_ref,
    grad_out,
    steep_out,
    y_low,
    out_grad,
    gate_out,
    up_out,
    down_out,
    hidden,
    seed,
    back_own,
    grad_ref,
    steep,
    steep_low,
    back_got,
    ahead_got,
    gate_sum,
    up_sum,
    down_sum,
    gate_held,
    up_held,
    down_held,
    sends,
    recvs,
):
    f32, low = jnp.float32, jnp.bfloat16
    me = coordinates()
    y, x, zh, zl, core = me
    greet(me, (("x",), ("y",), ("core",), ("zl",)))
    move = Mover(me, sends, recvs)
    back_move = move.send(back_far, back_got, "zl")
    ahead_move = move.later(ahead_far, ahead_got, "zl")
    swap = move.later(steep_low.at[core], steep_low.at[core], "core")
    gate, up, down = sums = [
        PlaneSumHere(move, total, held, y, x)
        for total, held in (
            (gate_sum, gate_held), (up_sum, up_held), (down_sum, down_held)
        )
    ]
    s, sx, sy, sd = gate.at
    order = (sd, sx, sy, s)
    half_len, width = hidden.shape
    count, wide = gate_in.shape
    block = gate_sum.shape[1]

    def wide_part(gates, ups, pieces):
        def column(i):
            lanes = pl.ds(pl.multiple_of(order[i] * block, 128), block)
            return move.quiet(tokens.at[:, lanes], pieces.at[i % 2])

        columns = [column(i) for i in range(4)]
        columns[0].start()
        loads = [move.local(gate_in, gates), move.local(up_in, ups)]
        for i in range(4):
            columns[i].wait()
            if i < 3:
                columns[i + 1].start()
            if i == 0:
                loads[0].wait()
            gate_sum[order[i]] = tn(pieces[i % 2], gates[...]).astype(low)
            if i == 0:
                gate.start()
                loads[1].wait()
            up_sum[order[i]] = tn(pieces[i % 2], ups[...]).astype(low)
            if i == 0:
                up.start()
            if i == 2:
                gate.start_near()
                up.start_near()

    half_loads = [
        move.quiet(hidden_in, hidden),
        move.quiet(back_in, back_own),
        move.quiet(seeds.at[pl.ds(0, half_len)], seed),
    ]
    half_stores = [move.quiet(steep, steep_out), move.quiet(grad_ref, grad_out)]
    pl.run_scoped(
        wide_part,
        pltpu.VMEM((count, wide), low),
        pltpu.VMEM((count, wide), low),
        pltpu.VMEM((2, count, block), low),
    )
    for made in half_loads:
        made.start()
    deep = down_sum.shape[1]

    def deep_part(rows, pieces):
        def column(i):
            lanes = pl.ds(pl.multiple_of(order[i] * deep, 128), deep)
            return move.quiet(act_in.at[:, lanes], pieces.at[i % 2])

        columns = [column(i) for i in range(4)]
        columns[0].start()
        move.local(seeds, rows).wait()
        for i in range(4):
            columns[i].wait()
            if i < 3:
                columns[i + 1].start()
            down_sum[order[i]] = tn(pieces[i % 2], rows[...]).astype(low)
            if i == 0:
                down.start()
            if i == 2:
                down.start_near()

    pl.run_scoped(
        deep_part,
        pltpu.VMEM((count, width), low),
        pltpu.VMEM((2, count, deep), low),
    )
    gate.pass_on()
    up.pass_on()

    def heads_part(qkv_ref, out_w, keys, gks, gvs):
        loads = [move.local(qkv_in, qkv_ref), move.local(out_in, out_w)]
        gain_ref[...] = jnp.zeros_like(gain_ref)
        for made in half_loads:
            made.wait()
        back_move.wait_recv()
        ahead_move.start()

        def norm_back(at):
            grad = back_own[at, :] + back_got[at, :].astype(f32)
            field = hidden[at, :]
            inverse = lax.rsqrt(jnp.mean(field * field, axis=1, keepdims=True) + EPSILON)
            unit = field * inverse
            gain_ref[...] += jnp.sum(grad * unit, axis=0, keepdims=True)
            scaled = grad * gain_rows[1:2, :]
            centre = jnp.mean(scaled * unit, axis=1, keepdims=True)
            value = seed[at, :].astype(f32) + inverse * (scaled - unit * centre)
            steep[at, :] = value
            steep_low[core, at, :] = value.astype(low)

        by_rows(half_len, 16, norm_back)
        swap.start()
        half_stores[0].start()
        for made in loads:
            made.wait()
        everything = pl.ds(0, 2 * half_len)
        for j in range(kvs):
            keys[j] = spun(
                head(qkv_ref, everything, heads + j), cos_ref[...], sin_ref[...]
            ).astype(low)
        gks[...] = jnp.zeros_like(gks)
        gvs[...] = jnp.zeros_like(gvs)
        swap.wait_recv()
        per = half_len // QB
        for i in range(2 * per):
            at = pl.ds(i % per * QB, QB)
            part = nt(steep_low[i // per, at, :], out_w[...]).astype(low)
            grad_ref[pl.ds(i * QB, QB), : heads * HD] = part
        down.pass_on()

        def work(step, size):
            behind_block(
                heads, kvs, step, size, qkv_ref, grad_ref, cos_ref, sin_ref, row_ref, col_ref,
                grad_ref, keys, gks, gvs,
            )

        def one(step, carry):
            work(step, SPAN)
            return carry

        for step in range(SPAN // QB - 1):
            work(step, (step + 1) * QB)
        lax.fori_loop(SPAN // QB - 1, 2 * half_len // QB, one, 0)
        scale = 1.0 / math.sqrt(HD)
        gk = [
            spun(gks[j] * scale, cos_ref[...], sin_ref[...], True).astype(low)
            for j in range(kvs)
        ]
        gv = [gvs[j].astype(low) for j in range(kvs)]
        grad_ref[:, HD * heads :] = jnp.concatenate(gk + gv, axis=1)
        half_stores[1].start()

    pl.run_scoped(
        heads_part,
        pltpu.VMEM(qkv_in.shape, low),
        pltpu.VMEM(out_in.shape, low),
        pltpu.VMEM((kvs, 2 * half_len, HD), low),
        pltpu.VMEM((kvs, 2 * half_len, HD), f32),
        pltpu.VMEM((kvs, 2 * half_len, HD), f32),
    )

    def last_part(mixed, own, out_made, gate_made, up_made, down_made):
        loads = [move.local(mixed_in, mixed), move.local(ahead_own, own)]
        loads[0].wait()
        rows = mixed.shape[1] // 4
        for i in range(4):
            lanes = pl.ds(i * rows, rows)
            total = tn(mixed[pl.ds(0, half_len), lanes], steep_low[0])
            total = total + tn(mixed[pl.ds(half_len, half_len), lanes], steep_low[1])
            out_made[pl.ds(i * rows, rows), :] = total.astype(low)
        stores = [move.local(out_made, out_grad)]
        ahead_move.wait_recv()
        loads[1].wait()
        quarter = half_len // 2
        for q in range(2):

            def add(at, q=q):
                every = pl.ds(pl.multiple_of(q * quarter + at.start, 16), at.size)
                value = hidden[every, :] + own[every, :] + ahead_got[q, at, :].astype(f32)
                ahead_got[q, at, :] = value.astype(low)

            by_rows(quarter, 16, add)
        stores.append(move.local(ahead_got, y_low))
        for plane, made, out in zip(
            sums, (gate_made, up_made, down_made), (gate_out, up_out, down_out)
        ):

            def write(at, value, made=made):
                made[at, :] = value

            plane.end(write)
            stores.append(move.local(made, out))
        for made in half_stores + stores:
            made.wait()

    pl.run_scoped(
        last_part,
        pltpu.VMEM(mixed_in.shape, low),
        pltpu.VMEM((half_len, width), f32),
        pltpu.VMEM(out_grad.shape, low),
        pltpu.VMEM(gate_out.shape, f32),
        pltpu.VMEM(up_out.shape, f32),
        pltpu.VMEM(down_out.shape, f32),
    )
    move.finish()


def attend_behind(heads, kvs, *operands):
    f32, low = jnp.float32, jnp.bfloat16
    half_len, width = operands[5].shape
    length = 2 * half_len
    wide = operands[-1].shape[1]
    hbm = pl.BlockSpec(memory_space=pl.ANY)
    vmem = pl.BlockSpec(memory_space=pltpu.VMEM)
    shapes = [(width // 4, wide), (width // 4, wide), (wide // 4, width)]

    def made(*shape, dtype=low):
        return jax.ShapeDtypeStruct(shape, dtype)

    return pl.pallas_call(
        functools.partial(behind_kernel, heads, kvs),
        in_specs=[vmem] * 5 + [hbm] * 13,
        out_specs=[vmem] + [hbm] * 7,
        out_shape=[
            made(1, width, dtype=f32),
            made(length, width),
            made(half_len, width, dtype=f32),
            made(2, half_len // 2, width),
            made(heads * HD, width),
        ]
        + [made(*shape, dtype=f32) for shape in shapes],
        scratch_shapes=[
            pltpu.VMEM((half_len, width), f32),
            pltpu.VMEM((half_len, width), low),
            pltpu.VMEM((half_len, width), f32),
            pltpu.VMEM((length, width), low),
            pltpu.VMEM((half_len, width), f32),
            pltpu.VMEM((2, half_len, width), low),
            pltpu.VMEM((half_len, width), low),
            pltpu.VMEM((2, half_len // 2, width), low),
        ]
        + [pltpu.VMEM((4,) + shape, low) for shape in shapes]
        + [pltpu.VMEM((3,) + shape, low) for shape in shapes]
        + [pltpu.SemaphoreType.DMA((64,)), pltpu.SemaphoreType.DMA((64,))],
        compiler_params=pltpu.CompilerParams(
            collective_id=3, has_side_effects=True, vmem_limit_bytes=63 << 20
        ),
        cost_estimate=pl.CostEstimate(
            flops=10 * heads * length * SPAN * HD,
            bytes_accessed=9 << 20,
            transcendentals=heads * length * SPAN,
        ),
        name="behind",
    )(*operands)


def bands(size):
    return (pl.ds(0, size // 2), pl.ds(size // 2, size // 2))


def first_kernel(
    heads,
    kvs,
    x_in,
    g_in,
    query_in,
    key_in,
    value_in,
    gate_raw,
    up_raw,
    down_in,
    out_in,
    gain_in,
    docs_in,
    cos_ref,
    sin_ref,
    x_out,
    normed_out,
    qkv_out,
    mixed_out,
    hidden_out,
    qkv_w_out,
    out_w_out,
    gain_rows,
    row,
    col,
    seeds,
    tokens,
    gate_w,
    up_w,
    down_w,
    x_own,
    normed,
    qkv,
    mixed,
    hidden,
    qkv_w,
    out_w,
    token,
    qkv_in,
    gate_in,
    up_in,
    docs,
    gains,
    keys,
    part,
    part_got,
    sends,
    recvs,
):
    f32, low = jnp.float32, jnp.bfloat16
    me = coordinates()
    y, x, zh, zl, core = me
    s, z = y * 2 + x, zh * 2 + zl
    mine = y == core
    other = jnp.logical_not(mine)
    width = qkv_w.shape[-1]
    length = qkv.shape[0]
    half_len = length // 2
    at = 0
    for ref in (query_in, key_in, value_in):
        size = ref.shape[1] // 2
        for c in range(2):
            qkv_in[c, :, at : at + size] = ref[:, c * size : (c + 1) * size]
        at += size
    for raw, parts in ((gate_raw, gate_in), (up_raw, up_in)):
        for i in range(raw.shape[1] // 128):
            lanes = slice(i // 4 * 128, i // 4 * 128 + 128)
            parts[i // 2 % 2, i % 2, :, lanes] = raw[:, i * 128 : (i + 1) * 128]
    greet(me, HEAD_GROUPS)
    move = Mover(me, sends, recvs)
    stores = []

    wides = [
        (ref.at[:, at], bands(ref.shape[-1]))
        for at in (zh, 1 - zh)
        for ref in (gate_w, up_w, down_w)
    ]
    hops = [plane_make(move, ref, s, parts) for ref, parts in wides]
    rest = []

    def start_some(which):
        for i in which:
            for made in hops[i]:
                made.start()

    def pass_some(which):
        for i in which:
            rest.extend(plane_pass(move, hops[i], wides[i][0], y, x, wides[i][1]))

    down_own = move.local(down_in, down_w.at[s, zh])
    own = [
        move.local(qkv_in.at[core], qkv_w.at[s, z, core]),
        move.local(gain_in, gains.at[s, z, core]),
    ]
    first = [
        move.send(qkv_in.at[1 - core], qkv_w.at[s, z, core], "core"),
        move.send(gain_in, gains.at[s, z, core], "core"),
    ]
    docs_move = move.send(docs_in, docs, "core")
    x_turn = turn_start(move, me, x_in, x_own)
    for made in own:
        made.wait()
    for made in first:
        made.wait_recv()
    line = [move.send(gains.at[s, z], gains.at[s, z], *names) for names in LINE]
    line += [move.send(qkv_w.at[s, z], qkv_w.at[s, z], *names) for names in LINE]
    down_own.wait()
    start_some((2,))

    own = [
        move.local(gate_in.at[zl, core], gate_w.at[s, zh, zl, core]),
        move.local(up_in.at[zl, core], up_w.at[s, zh, zl, core]),
    ]
    spread = []
    for src, dst in ((gate_in, gate_w), (up_in, up_w)):
        for names in (("core",), ("zl",), ("zl", "core")):
            to_zl = 1 - zl if "zl" in names else zl
            to_core = 1 - core if "core" in names else core
            spread.append(move.send(src.at[to_zl, to_core], dst.at[s, zh, zl, core], *names))
    out_own = move.quiet(out_in, out_w.at[x, z, core])
    out_sent = move.copy(out_in, out_w.at[x, z, core], "core")
    pl.when(mine)(out_own.start)
    pl.when(other)(out_sent.start)

    for made in line[:3]:
        made.wait_recv()
    gain_hops = [move.send(gains.at[s], gains.at[s], *names) for names in (("x",), ("y",))]
    turn_end(me, x_turn)
    stores.append(move.local(x_own, x_out))
    gain_hops[0].wait_recv()
    sx = 2 * y + 1 - x
    gain_hops.append(move.send(gains.at[sx], gains.at[sx], "y"))
    for made in line[3:]:
        made.wait_recv()
    qkv_hops = plane_start(move, qkv_w, s, bands(width))
    pass_some((2,))

    out_line = [move.copy(out_w.at[x, z], out_w.at[x, z], *names) for names in LINE]
    pl.when(other)(out_sent.wait_send)

    @pl.when(mine)
    def _():
        out_own.wait()
        out_sent.wait_recv()
        for made in out_line:
            made.start()

    for made in own:
        made.wait()
    for made in spread:
        made.wait_recv()
    pairs = [
        move.send(ref.at[s, zh], ref.at[s, zh], "zh") for ref in (gate_w, up_w, down_w)
    ]

    for made in gain_hops[1:]:
        made.wait_recv()
    count = out_in.shape[0]
    for i in range(2):
        gain_rows[pl.ds(i, 1), :] = jnp.concatenate(
            [
                gains[a, b, c, 0:1, i * count : (i + 1) * count]
                for a in range(4)
                for b in range(4)
                for c in range(2)
            ],
            axis=1,
        )

    quarter = half_len // 2
    for q in range(2):

        def norm(at, q=q):
            field = x_own[q, at, :].astype(f32)
            inverse = lax.rsqrt(jnp.mean(field * field, axis=1, keepdims=True) + EPSILON)
            rows = pl.ds(pl.multiple_of(q * quarter + at.start, 16), at.size)
            normed[core, rows, :] = (field * inverse * gain_rows[0:1, :]).astype(low)

        by_rows(quarter, 16, norm)
    normed_move = move.send(normed.at[core], normed.at[core], "core")
    docs_move.wait_recv()
    row[...] = jnp.where(mine, docs_in[x], docs[x])
    col[...] = jnp.transpose(jnp.broadcast_to(row[...], (8, length)))[:, 0:1]

    qkv_rest = plane_pass(move, qkv_hops, qkv_w, y, x, bands(width))
    out_x = move.copy(out_w.at[x], out_w.at[x], "x")
    near, left, right = (
        out_w.at[x], out_w.at[1 - x, ..., bands(width)[0]], out_w.at[x, ..., bands(width)[1]]
    )
    out_y = [move.copy(near, near, "y"), move.copy(left, left, "y")]
    out_far = move.copy(right, right, "x")

    @pl.when(mine)
    def _():
        for made in out_line:
            made.wait()
        out_x.start()
        out_y[0].start()

    g_turn = turn_start(move, me, g_in, seeds.at[0])
    normed_move.wait_recv()
    for made in qkv_rest:
        made.wait_recv()
    stores += [move.local(normed, normed_out), move.local(qkv_w, qkv_w_out)]
    weight = qkv_w.reshape(width, width)
    for i in range(length // QB):
        at = pl.ds(i * QB % half_len, QB)
        qkv[pl.ds(i * QB, QB), :] = nn(normed[i * QB // half_len, at, :], weight[...]).astype(low)
    stores.append(move.local(qkv, qkv_out))
    start_some((0,))
    seed_moves = [
        move.later(seeds.at[0], seeds.at[1], "core"),
        move.later(seeds.at[0], seeds.at[2], "zl"),
    ]

    everything = pl.ds(0, length)
    for j in range(kvs):
        keys[j] = spun(head(qkv, everything, heads + j), cos_ref[...], sin_ref[...]).astype(low)

    def work(step, size):
        ahead_block(heads, kvs, step, size, qkv, cos_ref, sin_ref, row, col, mixed, keys)

    def block(step, carry):
        @pl.when(step == SPAN // QB - 1)
        def _():
            turn_end(me, g_turn)
            for made in seed_moves:
                made.start()
            start_some((1,))

        work(step, SPAN)
        return carry

    work(0, QB)

    @pl.when(mine)
    def _():
        out_x.wait_recv()
        out_y[1].start()

    @pl.when(other)
    def _():
        out_y[0].wait_recv()
        out_far.start()

    for step in range(1, SPAN // QB - 1):
        work(step, (step + 1) * QB)
    lax.fori_loop(SPAN // QB - 1, length // QB, block, 0)
    stores.append(move.local(mixed, mixed_out))
    for made in pairs:
        made.wait_recv()
    start_some((3, 4, 5))

    @pl.when(mine)
    def _():
        out_x.wait_send()
        for made in out_y:
            made.wait_send()

    @pl.when(other)
    def _():
        out_y[1].wait_recv()
        out_far.wait()

    stores.append(move.local(out_w, out_w_out))

    out_weight = out_w.reshape(width // 2, width)
    theirs, ours = (pl.multiple_of(c * half_len, half_len) for c in (1 - core, core))

    def project(start):
        for i in range(half_len // QB):
            at = pl.ds(pl.multiple_of(start + i * QB, QB), QB)
            part[pl.ds(i * QB, QB), :] = nn(mixed[at, :], out_weight[...])

    project(theirs)
    part_move = move.copy(part, part_got, "core")
    part_move.start()
    for i in range(half_len // QB):
        at = pl.ds(pl.multiple_of(ours + i * QB, QB), QB)
        hidden[pl.ds(i * QB, QB), :] = nn(mixed[at, :], out_weight[...])
    part_move.wait()
    for q in range(2):

        def norm(at, q=q):
            rows = pl.ds(pl.multiple_of(q * quarter + at.start, 16), at.size)
            field = x_own[q, at, :].astype(f32) + (hidden[rows, :] + part_got[rows, :])
            hidden[rows, :] = field
            inverse = lax.rsqrt(jnp.mean(field * field, axis=1, keepdims=True) + EPSILON)
            token[rows, :] = (field * inverse * gain_rows[1:2, :]).astype(low)

        by_rows(quarter, 16, norm)
    token_moves = [
        move.send(token, tokens.at[2], "zl"),
        move.send(token, tokens.at[1], "core"),
    ]
    stores += [move.local(token, tokens.at[0]), move.local(hidden, hidden_out)]
    pass_some((0, 1))
    seed_moves[1].wait_recv()
    seed_moves.append(move.send(seeds.at[2], seeds.at[3], "core"))
    pass_some((3, 4, 5))
    token_moves[0].wait_recv()
    token_moves.append(move.send(tokens.at[2], tokens.at[3], "core"))
    for made in rest + seed_moves[::2] + token_moves[1:]:
        made.wait_recv()
    for made in stores:
        made.wait()
    move.finish()


def first_part(
    heads, kvs, x_in, g_in, query, key, value, gate, up, down, out, gain, docs, cosine, sine
):
    f32, low = jnp.float32, jnp.bfloat16
    rows, width = out.shape
    half_len = 2 * x_in.shape[1]
    length = 2 * half_len
    hbm = pl.BlockSpec(memory_space=pl.ANY)
    vmem = pl.BlockSpec(memory_space=pltpu.VMEM)

    def made(shape, dtype=low):
        return jax.ShapeDtypeStruct(shape, dtype)

    qkv_shape = (2, rows, width)
    quarter = (2, 2, rows, gate.shape[1] // 4)
    kept = [
        made(x_in.shape),
        made((2, half_len, width)),
        made((length, width)),
        made((length, heads * HD)),
        made((half_len, width), f32),
        made((4, 4) + qkv_shape),
        made((2, 4, 2) + out.shape),
    ]
    return pl.pallas_call(
        functools.partial(first_kernel, heads, kvs),
        in_specs=[hbm] * 2 + [vmem] * 5 + [hbm] * 3 + [vmem] * 3,
        out_specs=[hbm] * 7 + [vmem] * 3 + [hbm] * 5,
        out_shape=kept
        + [
            made((2, width), f32),
            made((1, length), docs.dtype),
            made((length, 1), docs.dtype),
            made((4,) + x_in.shape),
            made((4, half_len, width)),
            made((4, 2) + quarter),
            made((4, 2) + quarter),
            made((4, 2) + down.shape),
        ],
        scratch_shapes=[pltpu.VMEM(one.shape, one.dtype) for one in kept]
        + [
            pltpu.VMEM((half_len, width), low),
            pltpu.VMEM(qkv_shape, low),
            pltpu.VMEM(quarter, low),
            pltpu.VMEM(quarter, low),
            pltpu.VMEM(docs.shape, docs.dtype),
            pltpu.VMEM((4, 4, 2) + gain.shape, f32),
            pltpu.VMEM((kvs, length, HD), low),
            pltpu.VMEM((half_len, width), f32),
            pltpu.VMEM((half_len, width), f32),
            pltpu.SemaphoreType.DMA((112,)),
            pltpu.SemaphoreType.DMA((112,)),
        ],
        compiler_params=pltpu.CompilerParams(
            collective_id=1, has_side_effects=True, vmem_limit_bytes=60 << 20
        ),
        name="first",
    )(x_in, g_in, query, key, value, gate, up, down, out, gain, docs, cosine, sine)


def hidden_kernel(
    tokens,
    seeds,
    gate_w,
    up_w,
    down_w,
    act_out,
    gate_out,
    up_out,
    back_own,
    back_far,
    ahead_own,
    ahead_far,
    backs,
    aheads,
    back_got,
    ahead_got,
    sends,
    recvs,
):
    f32, low = jnp.float32, jnp.bfloat16
    me = coordinates()
    move = Mover(me, sends, recvs)

    @pl.when(pl.program_id(0) == 0)
    def _():
        greet(me, (("core",),))

    half_len = backs.shape[1]
    per = half_len // QB
    i = pl.program_id(0)
    moves = [
        (
            move.copy(backs.at[1], back_got.at[turn], "core"),
            move.copy(aheads.at[1], ahead_got.at[turn], "core"),
        )
        for turn in range(2)
    ]

    def fold(turn, back_ref, ahead_ref):
        for made in moves[turn]:
            made.wait()

        def work(at):
            back_ref[at, :] = (backs[0, at, :] + back_got[turn, at, :]).astype(back_ref.dtype)
            ahead_ref[at, :] = (aheads[0, at, :] + ahead_got[turn, at, :]).astype(ahead_ref.dtype)

        by_rows(half_len, 16, work)

    slot = 3 - i // per
    rows = pl.ds(pl.multiple_of(i % per * QB, QB), QB)
    token, seed = tokens[...], seeds[...]
    gate, upward = nn(token, gate_w[...]), nn(token, up_w[...])
    sigma = 1.0 / (1.0 + jnp.exp(-gate))
    silu = gate * sigma
    activated = (silu * upward).astype(low)
    act_out[...] = activated
    grad = nt(seed, down_w[...])
    up_low = (grad * silu).astype(low)
    gate_low = (grad * upward * sigma * (1.0 + gate * (1.0 - sigma))).astype(low)
    up_out[...] = up_low
    gate_out[...] = gate_low
    aheads[slot % 2, rows, :] = nn(activated, down_w[...])
    backs[slot % 2, rows, :] = nt(gate_low, gate_w[...]) + nt(up_low, up_w[...])
    for turn in range(2):

        @pl.when(i == (2 * turn + 1) * per - 1)
        def _(turn=turn):
            for made in moves[turn]:
                made.start()

    @pl.when(i == 2 * per - 1)
    def _():
        fold(0, back_far, ahead_far)

    @pl.when(i == 4 * per - 1)
    def _():
        fold(1, back_own, ahead_own)


def hidden_part(tokens, seeds, gate_w, up_w, down_w):
    f32, low = jnp.float32, jnp.bfloat16
    half_len, width = tokens.shape[1:]
    wide = gate_w.shape[1]
    per = half_len // QB
    vmem = pl.BlockSpec(memory_space=pltpu.VMEM)

    def banded(columns):
        return pl.BlockSpec((QB, columns), lambda i: ((3 - i // per) * per + i % per, 0))

    def made(rows, columns, dtype=low):
        return jax.ShapeDtypeStruct((rows, columns), dtype)

    return pl.pallas_call(
        hidden_kernel,
        grid=(4 * per,),
        in_specs=[banded(width)] * 2 + [vmem] * 3,
        out_specs=[banded(wide)] * 3 + [vmem] * 4,
        out_shape=[made(4 * half_len, wide)] * 3
        + [
            made(half_len, width, f32),
            made(half_len, width),
            made(half_len, width, f32),
            made(half_len, width),
        ],
        scratch_shapes=[
            pltpu.VMEM((2, half_len, width), f32),
            pltpu.VMEM((2, half_len, width), f32),
            pltpu.VMEM((2, half_len, width), f32),
            pltpu.VMEM((2, half_len, width), f32),
            pltpu.SemaphoreType.DMA((4,)),
            pltpu.SemaphoreType.DMA((4,)),
        ],
        compiler_params=pltpu.CompilerParams(
            collective_id=2, has_side_effects=True, vmem_limit_bytes=63 << 20
        ),
        cost_estimate=pl.CostEstimate(
            flops=2 * 6 * 4 * half_len * width * wide,
            bytes_accessed=40 << 20,
            transcendentals=4 * half_len * wide,
        ),
        name="hidden",
    )(tokens.reshape(-1, width), seeds.reshape(-1, width), gate_w, up_w, down_w)


def rope_constants(length, width):
    freqs = ROPE_BASE ** (-2.0 * np.arange(width // 2) / width)
    angles = np.tile(np.arange(length)[:, None] * freqs[None, :], 2)
    return np.cos(angles).astype(np.float32), np.sin(angles).astype(np.float32)


def fast_body(
    layer_input,
    cotangent,
    token_mask,
    document_ids,
    attn_gain,
    w_query,
    w_key,
    w_value,
    w_output,
    mlp_gain,
    w_gate,
    w_up,
    w_down,
):
    f32, low = jnp.float32, jnp.bfloat16
    y, x, zh, zl, core = (lax.axis_index(name) for name in AXES)
    device = sum(lax.axis_index(name) * BITS[name] for name in AXES)
    quarter, width = layer_input.shape[1:]
    half_len = 2 * quarter
    length = 2 * half_len
    rows = w_query.shape[0]
    units = w_gate.shape[1]
    heads, kvs = HEADS // 2, KV // 2
    cosine, sine = (jnp.asarray(table) for table in rope_constants(length, HD))

    masked = cotangent * token_mask.astype(low)[:, :, None]
    gain = jnp.concatenate([attn_gain, mlp_gain]).astype(f32)
    gain = jnp.broadcast_to(jnp.pad(gain, (0, 128 - 2 * rows)), (8, 128))
    (
        own,
        normed,
        pair,
        mixed,
        hidden,
        qkv_w,
        out_w,
        gains,
        row,
        col,
        seeds,
        tokens,
        gate_w,
        up_w,
        down_w,
    ) = first_part(
        heads,
        kvs,
        layer_input,
        masked,
        w_query,
        w_key,
        w_value,
        w_gate,
        w_up,
        w_down,
        w_output,
        gain,
        document_ids[:, None],
        cosine,
        sine,
    )
    qkv_w, out_w = qkv_w.reshape(width, -1), out_w.reshape(-1, width)
    gate_w, up_w = gate_w.reshape(width, -1), up_w.reshape(width, -1)
    down_w = down_w.reshape(-1, width)
    seeds = seeds.reshape(4, half_len, width)
    activated, gate_low, up_low, back_own, back_far, ahead_own, ahead_far = hidden_part(
        tokens, seeds, gate_w, up_w, down_w
    )
    gain_two, grad_qkv, steep, y_low, grad_out_w, *sums = attend_behind(
        heads,
        kvs,
        gains,
        cosine,
        sine,
        row,
        col,
        hidden,
        back_own,
        pair,
        mixed,
        out_w,
        back_far,
        ahead_own,
        ahead_far.reshape(2, quarter, width),
        tokens.reshape(-1, width),
        seeds.reshape(-1, width),
        activated,
        gate_low,
        up_low,
    )
    (
        gate_grad,
        up_grad,
        down_grad,
        query_grad,
        key_grad,
        value_grad,
        out_grad,
        output,
        grad_input,
        gain,
    ) = sum_tail(
        sums[0].reshape(2, -1, units // 4),
        sums[1].reshape(2, -1, units // 4),
        sums[2].reshape(2, -1, width),
        grad_qkv,
        normed,
        qkv_w,
        own,
        steep,
        gains,
        gain_two,
        grad_out_w.reshape(2, 4, 2, rows, width),
        y_low,
    )
    gain_one = lax.dynamic_slice_in_dim(gain, device * rows, rows, 1)

    return (
        output,
        grad_input,
        gain_one[0],
        query_grad,
        key_grad,
        value_grad,
        out_grad,
        gain_one[1],
        gate_grad,
        up_grad,
        down_grad,
    )


def solution(mesh):
    fast = dict(mesh.shape) == {"seq": 4, "batch": 8}
    if fast:
        grid = Mesh(mesh.devices.reshape((2,) * 5), AXES)
        seq, batch = ("y", "x"), ("zh", "zl", "core")
    else:
        grid, seq, batch = mesh, ("seq",), ("batch",)
    weight = P(seq + batch, None)
    gain = P(seq + batch)
    token = P(batch, seq, None)
    return jax.shard_map(
        fast_body if fast else body,
        mesh=grid,
        in_specs=(token, token, P(batch, seq), P(batch, None), gain)
        + (weight,) * 4
        + (gain,)
        + (weight,) * 3,
        out_specs=(token, token, gain) + (weight,) * 4 + (gain,) + (weight,) * 3,
        check_vma=False,
    )
```
